32 devices in a mesh: dp: 16 (over z, y, x), mp: 2 (over core).
Axes of the slice: x: 2, y: 2, z: 4, core: 2. Of those that a mesh axis runs over, the one named last changes fastest.
Arguments:
- tokens: bfloat16 [49152, 1024], P(('dp', 'mp')), may hold values from -6 to 6
- slot_lengths: int32 [16, 1], P('dp'), may hold values from 512 to 3072, as said below
- gain_one: bfloat16 [1024], replicated, may hold values from 0.5 to 1.5
- shift_one: bfloat16 [1024], replicated, may hold values from -3 to 3
- w_qkv: bfloat16 [1024, 3, 1024], P('dp', None, 'mp'), may hold values from -0.25 to 0.25
- bias_qv: bfloat16 [2, 1024], P(None, 'mp'), may hold values from -3 to 3
- w_out: bfloat16 [1024, 1024], P('mp', 'dp'), may hold values from -1 to 1
- bias_out: bfloat16 [1024], replicated, may hold values from -3 to 3
- gain_two: bfloat16 [1024], replicated, may hold values from 0.5 to 1.5
- shift_two: bfloat16 [1024], replicated, may hold values from -3 to 3
- w_up: bfloat16 [1024, 4096], P('dp', 'mp'), may hold values from -0.1875 to 0.1875
- bias_up: bfloat16 [4096], P('mp'), may hold values from -3 to 3
- w_down: bfloat16 [4096, 1024], P('mp', 'dp'), may hold values from -0.125 to 0.125
- bias_down: bfloat16 [1024], replicated, may hold values from -3 to 3
- cotangent: bfloat16 [49152, 1024], P(('dp', 'mp')), may hold values from -6 to 6
Outputs:
- output: bfloat16 [49152, 1024], P(('dp', 'mp'))
- grad_tokens: bfloat16 [49152, 1024], P(('dp', 'mp'))
- grad_gain_one: float32 [1024], replicated
- grad_shift_one: float32 [1024], replicated
- grad_w_qkv: float32 [1024, 3, 1024], P('dp', None, 'mp')
- grad_bias_qv: float32 [2, 1024], P(None, 'mp')
- grad_w_out: float32 [1024, 1024], P('mp', 'dp')
- grad_bias_out: float32 [1024], replicated
- grad_gain_two: float32 [1024], replicated
- grad_shift_two: float32 [1024], replicated
- grad_w_up: float32 [1024, 4096], P('dp', 'mp')
- grad_bias_up: float32 [4096], P('mp')
- grad_w_down: float32 [4096, 1024], P('mp', 'dp')
- grad_bias_down: float32 [1024], replicated
The draws below stay inside these ranges and needn't reach their ends.
Inputs may be any that keep to these rules, and one draw needn't show every extreme that they name: `slot_lengths`: each entry is 512 or 3072: the slot holds one sequence of 3072 tokens or sequences of 512 tokens one after another; both values occur in every draw.
All inputs are finite; a program needn't handle non-finite values.
Results may differ from the reference program's by a relative error of at most 0.02.
Values may be sent and summed in bfloat16 or wider, within the bound.
A program may use at most 256 MiB of HBM per device.

```python
import jax
import jax.numpy as jnp
from jax import lax

D = 1024
H = 16
HD = 64
FF = 4096
SHORT = 512
LONG_LEN = 3072
SLOTS = 1
DP_GROUPS = 16
TOKENS = 49152


def draw_slot_lengths(key, part):
    slot_kind = jax.random.randint(jax.random.fold_in(key, 11), (DP_GROUPS, SLOTS), 0, 2)
    shuffled = jax.random.permutation(jax.random.fold_in(key, 12), DP_GROUPS)
    slot_kind = slot_kind.at[shuffled[0], 0].set(1)
    slot_kind = slot_kind.at[shuffled[1], 0].set(0)
    return jnp.where(slot_kind == 1, LONG_LEN, SHORT).astype(jnp.int32)


def raised(result, key, source, target, shards_of, factor):
    def block_of(dim):
        return (jnp.arange(result.shape[dim]) // (result.shape[dim] // shards_of)).reshape((-1,) + (1,) * (result.ndim - 1 - dim))

    near = jax.random.permutation(key, shards_of)[block_of(target)]
    far = (block_of(target) + shards_of // 2) % shards_of
    return jnp.where((block_of(source) == near) | (block_of(source) == far), factor * result, result)


def block_scale(own_key, shape, shards, low, high):
    loudness = 1.0
    for axis_at, parts in shards:
        draws = jax.random.uniform(jax.random.fold_in(jax.random.fold_in(own_key, 6), axis_at), (parts,), jnp.float32, low / len(shards), high / len(shards))
        loudness = loudness * jnp.repeat(jnp.exp(draws), shape[axis_at] // parts).reshape((-1,) + (1,) * (len(shape) - 1 - axis_at))
    return loudness


def bell_draw(rng, dims, scale, reach, split=(), kind=jnp.bfloat16):
    level = block_scale(rng, dims, split, -0.22, 0.18) if split else 1.0
    drawn = jax.random.normal(rng, dims, jnp.float32) * scale * level
    return jnp.minimum(jnp.maximum(drawn, -reach), reach).astype(kind)


def noise_with(key, dims, width, limit, split, heavy, kind=jnp.bfloat16):
    entries = width * jax.random.normal(key, dims, jnp.float32)
    if split:
        entries = entries * block_scale(key, dims, split, -0.22, 0.18)
    return jnp.clip(raised(entries, jax.random.fold_in(key, 3), *heavy), -limit, limit).astype(kind)


def setup_inputs(seed: int = 0) -> dict:
    keys = jax.random.split(jax.random.key(seed), 16)
    tokens = bell_draw(keys[0], (TOKENS, D), 1.0, 6.0, ((0, 32),))
    slot_lengths = draw_slot_lengths(jax.random.fold_in(keys[15], 71), 0)
    gain_one = jnp.clip(1.0 + 0.1 * jax.random.normal(keys[2], (D,), jnp.float32), 0.5, 1.5).astype(jnp.bfloat16)
    shift_one = bell_draw(keys[3], (D,), 0.5, 3.0)
    w_qkv = bell_draw(keys[4], (D, 3, D), (D // 2) ** -0.5, 0.25, ((0, 16), (2, 2)))
    bias_qv = bell_draw(keys[5], (2, D), 0.5, 3.0, ((1, 2),))
    w_out = bell_draw(keys[6], (D, D), (D // 32) ** -0.5, 1.0, ((0, 2), (1, 16)))
    bias_out = bell_draw(keys[7], (D,), 0.5, 3.0)
    gain_two = jnp.clip(1.0 + 0.1 * jax.random.normal(keys[8], (D,), jnp.float32), 0.5, 1.5).astype(jnp.bfloat16)
    shift_two = bell_draw(keys[9], (D,), 0.5, 3.0)
    w_up = bell_draw(keys[10], (D, FF), D ** -0.5, 0.1875, ((0, 16), (1, 2)))
    bias_up = bell_draw(keys[11], (FF,), 0.5, 3.0, ((0, 2),))
    w_down = bell_draw(keys[12], (FF, D), (FF // 2) ** -0.5, 0.125, ((0, 2), (1, 16)))
    bias_down = bell_draw(keys[13], (D,), 0.5, 3.0)
    cotangent = noise_with(keys[14], (TOKENS, D), 1.0, 6.0, ((0, 32),), (0, 1, 32, 2.75))
    return dict(tokens=tokens, slot_lengths=slot_lengths, gain_one=gain_one, shift_one=shift_one, w_qkv=w_qkv, bias_qv=bias_qv, w_out=w_out, bias_out=bias_out, gain_two=gain_two, shift_two=shift_two, w_up=w_up, bias_up=bias_up, w_down=w_down, bias_down=bias_down, cotangent=cotangent)


@jax.custom_vjp
def low(v):
    return lax.optimization_barrier(v.astype(jnp.bfloat16)).astype(jnp.float32)

@jax.custom_vjp
def low_back(v):
    return v

def low_keep(v):
    return (low(v), None)

def low_pass(kept, grad):
    return (grad,)

def back_keep(v):
    return (v, None)

def back_low(kept, grad):
    return (low(grad),)
low.defvjp(low_keep, low_pass)
low_back.defvjp(back_keep, back_low)
norm_eps = 1e-05
highest = lax.Precision.HIGHEST

def matmul(left_side, right_side):
    return jnp.dot(left_side, right_side, precision=highest, preferred_element_type=jnp.float32)

def layer_norm(values, gain_vec, shift_vec):
    average = lax.optimization_barrier(jnp.mean(values, axis=-1, keepdims=True))
    centred = values - average
    variance = lax.optimization_barrier(jnp.mean(centred * centred, axis=-1, keepdims=True))
    return centred * lax.rsqrt(variance + norm_eps) * gain_vec + shift_vec

def gelu_tanh(values):
    inner = 0.7978845608028654 * (values + 0.044715 * values * values * values)
    return 0.5 * values * (1.0 + jnp.tanh(inner))

def head_attention(queries, key_rows, values, allowed):
    scores = low_back(matmul(queries, key_rows.T) * HD ** (-0.5))
    kept_scores = jnp.where(allowed, scores, jnp.zeros_like(scores))
    row_max = lax.optimization_barrier(jnp.max(jnp.where(allowed, scores, jnp.full_like(scores, -30000.0)), axis=-1, keepdims=True))
    weights = jnp.where(allowed, jnp.exp(kept_scores - row_max), jnp.zeros_like(scores))
    attn_probs = weights / lax.optimization_barrier(jnp.sum(weights, axis=-1, keepdims=True))
    return matmul(low(attn_probs), values)

def slot_forward(slot_tokens, slot_length, params):
    gain_one, shift_one, w_qkv, bias_qv, w_out, bias_out, gain_two, shift_two, w_up, bias_up, w_down, bias_down = params
    position = jnp.arange(LONG_LEN, dtype=jnp.int32)
    starts = position - position % slot_length.astype(jnp.int32)
    allowed = (starts[:, None] == starts[None, :]) & (position[:, None] >= position[None, :])
    normed_one = low(layer_norm(slot_tokens, gain_one, shift_one))
    packed = jnp.einsum('td,dcf->tcf', normed_one, w_qkv, precision=highest)
    zero_bias = jnp.zeros_like(bias_qv[0])
    packed = packed + jnp.stack([bias_qv[0], zero_bias, bias_qv[1]])[None]
    packed = low(low_back(packed))
    per_head = packed.reshape(LONG_LEN, 3, H, HD).transpose(1, 2, 0, 3)

    def one_head(triple):
        return head_attention(triple[0], triple[1], triple[2], allowed)
    attended = lax.map(jax.checkpoint(one_head), (per_head[0], per_head[1], per_head[2]))
    attended = low(low_back(attended.transpose(1, 0, 2).reshape(LONG_LEN, D)))
    hidden = slot_tokens + low_back(matmul(attended, w_out) + bias_out)
    normed_two = low(layer_norm(hidden, gain_two, shift_two))
    preact = low_back(matmul(normed_two, w_up) + bias_up)
    active = low(gelu_tanh(preact))
    return hidden + low_back(matmul(active, w_down) + bias_down)

def forward(tokens, params, slot_lengths):
    slot_rows = tokens.reshape(-1, LONG_LEN, D)
    lengths = slot_lengths.reshape(-1).astype(jnp.int32)
    slot_step = jax.checkpoint(slot_forward)

    def scan_step(running, slot_item):
        return (running, slot_step(slot_item[0], slot_item[1], params))
    _, outputs = lax.scan(scan_step, jnp.zeros((), tokens.dtype), (slot_rows, lengths))
    return outputs.reshape(-1, D)

def reference(tokens, slot_lengths, gain_one, shift_one, w_qkv, bias_qv, w_out, bias_out, gain_two, shift_two, w_up, bias_up, w_down, bias_down, cotangent):
    params = tuple((tensor.astype(jnp.float32) for tensor in (gain_one, shift_one, w_qkv, bias_qv, w_out, bias_out, gain_two, shift_two, w_up, bias_up, w_down, bias_down)))

    def wrapped(token_values, weights):
        return forward(token_values, weights, slot_lengths)
    output, pullback = jax.vjp(wrapped, tokens.astype(jnp.float32), params)
    grad_tokens, weight_grads = pullback(cotangent.astype(jnp.float32))
    return (output.astype(jnp.bfloat16), grad_tokens.astype(jnp.bfloat16), weight_grads[0], weight_grads[1], weight_grads[2], weight_grads[3], weight_grads[4], weight_grads[5], weight_grads[6], weight_grads[7], weight_grads[8], weight_grads[9], weight_grads[10], weight_grads[11])
```

```python
import functools
import math

import jax
import jax.numpy as jnp
from jax import lax
from jax.experimental import pallas as pl
from jax.experimental.pallas import tpu as pltpu
from jax.sharding import PartitionSpec as P

HD = 64
LONG_LEN = 3072
BT = 512
VMEM_CAP = 60 * 1024 * 1024

f32 = jnp.float32
bf16 = jnp.bfloat16
norm_eps = 1e-05
masked_score = -1e30
gelu_coeff = 0.7978845608028654
score_scale = HD ** (-0.5)
score_scale_2 = HD ** (-0.5) * math.log2(math.e)
safe_sum = 1e30


def dot_nt(left, right):
    return lax.dot_general(left, right, (((1,), (1,)), ((), ())), preferred_element_type=f32)


def dot_nn(left, right):
    return lax.dot_general(left, right, (((1,), (0,)), ((), ())), preferred_element_type=f32)


def dot_tn(left, right):
    return lax.dot_general(left, right, (((0,), (0,)), ((), ())), preferred_element_type=f32)


def params(semantics=1):
    return pltpu.CompilerParams(
        vmem_limit_bytes=VMEM_CAP, dimension_semantics=("arbitrary",) * semantics
    )


def cost(flops, nbytes, exps=0):
    return pl.CostEstimate(flops=int(flops), bytes_accessed=int(nbytes), transcendentals=int(exps))


def head_lanes(block, head):
    lane_head = lax.broadcasted_iota(jnp.int32, block.shape, 1) // HD
    return jnp.where(lane_head == head, block, jnp.zeros_like(block))


def pack_heads(columns):
    lane = lax.broadcasted_iota(jnp.int32, columns[0].shape, 1)
    pairs = [
        jnp.where(lane < HD, columns[2 * i], columns[2 * i + 1]) for i in range(len(columns) // 2)
    ]
    return pairs[0] if len(pairs) == 1 else jnp.concatenate(pairs, axis=1)


def attend_forward_kernel(
    heads, lens_ref, q_ref, k_ref, v_ref, out_ref, exact_ref, lse_ref, vm_ref, m_ref, l_ref, acc_ref
):
    step = pl.program_id(0)
    block = q_ref.shape[0]
    tokens = k_ref.shape[0]

    @pl.when(step == 0)
    def _():
        for j in range(tokens // block):
            value = v_ref[j * block : (j + 1) * block, :]
            for h in range(heads):
                vm_ref[j, h * block : (h + 1) * block, :] = head_lanes(value, h)

    query = q_ref[...]
    masked = [head_lanes(query, h) for h in range(heads)]

    def probs(scores, top):
        total, parts = None, []
        for t in range(block // 128):
            part = jnp.exp2(scores[:, t * 128 : (t + 1) * 128] * score_scale_2 - top)
            total = part if total is None else total + part
            parts.append(part.astype(bf16))
        return parts, total

    def key_block(j):
        return k_ref[pl.ds(pl.multiple_of(j * block, block), block), :]

    def diagonal(j):
        keys = key_block(j)
        low = []
        for h in range(heads):
            scores = dot_nt(masked[h], keys)
            row = lax.broadcasted_iota(jnp.int32, scores.shape, 0)
            col = lax.broadcasted_iota(jnp.int32, scores.shape, 1)
            scores = jnp.where(row >= col, scores, masked_score)
            top = jnp.max(scores, axis=1, keepdims=True) * score_scale_2
            top = jnp.broadcast_to(top, (block, 128))
            m_ref[h] = top
            parts, l_ref[h] = probs(scores, top)
            low += parts
        acc_ref[...] = dot_nn(jnp.concatenate(low, axis=1), vm_ref[j])

    def fixed_top(j):
        keys = key_block(j)
        low = []
        for h in range(heads):
            parts, total = probs(dot_nt(masked[h], keys), m_ref[h])
            l_ref[h] += total
            low += parts
        acc_ref[...] += dot_nn(jnp.concatenate(low, axis=1), vm_ref[j])

    def running_top(j):
        keys = key_block(j)
        low, shrink = [], []
        for h in range(heads):
            scores = dot_nt(masked[h], keys)
            old = m_ref[h]
            top = jnp.maximum(old, jnp.max(scores, axis=1, keepdims=True) * score_scale_2)
            factor = jnp.exp2(old - top)
            m_ref[h] = top
            parts, total = probs(scores, top)
            l_ref[h] = l_ref[h] * factor + total
            low += parts
            shrink.append(factor)
        acc_ref[...] = acc_ref[...] * pack_heads(shrink) + dot_nn(
            jnp.concatenate(low, axis=1), vm_ref[j]
        )

    earlier = jnp.where(lens_ref[0] == LONG_LEN, step, 0)
    diagonal(step)
    lax.fori_loop(0, earlier, lambda j, c: (fixed_top(j), c)[1], 0)
    largest = jnp.max(l_ref[...])

    @pl.when(jnp.logical_not(largest < safe_sum))
    def _():
        diagonal(step)
        lax.fori_loop(0, earlier, lambda j, c: (running_top(j), c)[1], 0)

    lane = lax.broadcasted_iota(jnp.int32, (block, 128), 1)
    rows = jnp.zeros((block, 128), f32)
    inverse = []
    for h in range(heads):
        total = jnp.sum(l_ref[h], axis=1, keepdims=True)
        rows = jnp.where(lane == h, m_ref[h][:, :1] + jnp.log2(total), rows)
        inverse.append(jnp.broadcast_to(1.0 / total, (block, 128)))
    result = acc_ref[...] * pack_heads(inverse)
    out_ref[...] = result.astype(bf16)
    exact_ref[...] = result
    lse_ref[...] = rows.T[:8, :]


def attend_forward(packed, lengths):
    tokens, width = packed.shape[0], packed.shape[1] // 3
    heads = width // HD
    pairs = (tokens // BT) * (tokens // BT + 1) // 2
    return pl.pallas_call(
        functools.partial(attend_forward_kernel, heads),
        grid_spec=pltpu.PrefetchScalarGridSpec(
            num_scalar_prefetch=1,
            grid=(tokens // BT,),
            in_specs=[
                pl.BlockSpec((BT, width), lambda i, n: (i, 0)),
                pl.BlockSpec((tokens, width), lambda i, n: (0, 1)),
                pl.BlockSpec((tokens, width), lambda i, n: (0, 2)),
            ],
            out_specs=[
                pl.BlockSpec((BT, width), lambda i, n: (i, 0)),
                pl.BlockSpec((BT, width), lambda i, n: (i, 0)),
                pl.BlockSpec((8, BT), lambda i, n: (0, i)),
            ],
            scratch_shapes=[
                pltpu.VMEM((tokens // BT, heads * BT, width), bf16),
                pltpu.VMEM((heads, BT, 128), f32),
                pltpu.VMEM((heads, BT, 128), f32),
                pltpu.VMEM((BT, width), f32),
            ],
        ),
        out_shape=[
            jax.ShapeDtypeStruct((tokens, width), bf16),
            jax.ShapeDtypeStruct((tokens, width), f32),
            jax.ShapeDtypeStruct((8, tokens), f32),
        ],
        compiler_params=params(),
        cost_estimate=cost(16 * pairs * BT * BT * 64 * heads, 10 * tokens * width, pairs * BT * BT),
        name="attend_forward",
    )(lengths, packed, packed, packed)


def attend_backward_kernel(
    heads,
    lens_ref,
    q_ref,
    k_ref,
    v_ref,
    do_ref,
    lse_ref,
    delta_ref,
    dq_ref,
    dk_ref,
    dv_ref,
    qm_ref,
    dom_ref,
    km_ref,
    vm_ref,
    dqa_ref,
    dka_ref,
    dva_ref,
):
    step = pl.program_id(0)
    count = pl.num_programs(0)
    block = k_ref.shape[0]

    @pl.when(step == 0)
    def _():
        for t in range(q_ref.shape[0] // block):
            rows = slice(t * block, (t + 1) * block)
            for h in range(heads):
                place = slice(h * block, (h + 1) * block)
                qm_ref[t, place, :] = head_lanes(q_ref[rows, :], h)
                dom_ref[t, place, :] = head_lanes(do_ref[rows, :], h)
        dqa_ref[...] = jnp.zeros(dqa_ref.shape, f32)

    for h in range(heads):
        place = slice(h * block, (h + 1) * block)
        km_ref[place, :] = head_lanes(k_ref[...], h)
        vm_ref[place, :] = head_lanes(v_ref[...], h)
    dka_ref[...] = jnp.zeros(dka_ref.shape, f32)
    dva_ref[...] = jnp.zeros(dva_ref.shape, f32)

    def pair(i, on_diagonal):
        rows = pl.ds(pl.multiple_of(i * block, block), block)
        query, grad = q_ref[rows, :], do_ref[rows, :]
        low, slopes = [], []
        for h in range(heads):
            place = slice(h * block, (h + 1) * block)
            scores = dot_nt(km_ref[place, :], query)
            prob = jnp.exp2(scores * score_scale_2 - lse_ref[h : h + 1, rows])
            if on_diagonal:
                key = lax.broadcasted_iota(jnp.int32, scores.shape, 0)
                tok = lax.broadcasted_iota(jnp.int32, scores.shape, 1)
                prob = jnp.where(tok >= key, prob, 0.0)
            grad_prob = dot_nt(vm_ref[place, :], grad)
            slope = prob * (grad_prob - delta_ref[h : h + 1, rows])
            low.append(prob.astype(bf16))
            slopes.append(slope.astype(bf16))
        dva_ref[...] += dot_nn(jnp.concatenate(low, axis=1), dom_ref[i])
        dka_ref[...] += dot_nn(jnp.concatenate(slopes, axis=1), qm_ref[i])
        dqa_ref[rows, :] += dot_tn(jnp.concatenate(slopes, axis=0), km_ref[...])

    pair(step, True)
    last = jnp.where(lens_ref[0] == LONG_LEN, count, step + 1)
    lax.fori_loop(step + 1, last, lambda i, c: (pair(i, False), c)[1], 0)
    dk_ref[...] = (dka_ref[...] * score_scale).astype(bf16)
    dv_ref[...] = dva_ref[...].astype(bf16)

    @pl.when(step == count - 1)
    def _():
        dq_ref[...] = (dqa_ref[...] * score_scale).astype(bf16)


def attend_backward(packed, grad_attended, lse, delta, lengths):
    tokens, width = grad_attended.shape
    heads = width // HD
    blocks = tokens // BT
    pairs = blocks * (blocks + 1) // 2
    whole = pl.BlockSpec((tokens, width), lambda j, n: (0, 0))
    stats = pl.BlockSpec((8, tokens), lambda j, n: (0, 0))
    tile = pl.BlockSpec((BT, width), lambda j, n: (j, 0))
    return pl.pallas_call(
        functools.partial(attend_backward_kernel, heads),
        grid_spec=pltpu.PrefetchScalarGridSpec(
            num_scalar_prefetch=1,
            grid=(blocks,),
            in_specs=[
                whole,
                pl.BlockSpec((BT, width), lambda j, n: (j, 1)),
                pl.BlockSpec((BT, width), lambda j, n: (j, 2)),
                whole,
                stats,
                stats,
            ],
            out_specs=[whole, tile, tile],
            scratch_shapes=[
                pltpu.VMEM((blocks, heads * BT, width), bf16),
                pltpu.VMEM((blocks, heads * BT, width), bf16),
                pltpu.VMEM((heads * BT, width), bf16),
                pltpu.VMEM((heads * BT, width), bf16),
                pltpu.VMEM((tokens, width), f32),
                pltpu.VMEM((BT, width), f32),
                pltpu.VMEM((BT, width), f32),
            ],
        ),
        out_shape=[jax.ShapeDtypeStruct((tokens, width), bf16)] * 3,
        compiler_params=params(),
        cost_estimate=cost(40 * pairs * BT * BT * 64 * heads, 16 * tokens * width, pairs * BT * BT),
        name="attend_backward",
    )(lengths, packed, packed, packed, grad_attended, lse, delta)


def swap_mp(block):
    return lax.ppermute(block, "mp", [(0, 1), (1, 0)])


def flip_dp(block, bits):
    return lax.ppermute(block, "dp", [(i, i ^ bits) for i in range(16)])


def gather_blocks(shard):
    half = shard.shape[1] // 2
    first = [shard] + [flip_dp(shard, k) for k in (4, 8, 12)]
    column = jnp.stack([part[:, :half] for part in first])
    other = jnp.stack([part[:, half:] for part in first])
    column_low = jnp.concatenate([column, flip_dp(column, 1)])
    other_low = jnp.concatenate([other, flip_dp(other, 2)])
    return [column_low, flip_dp(column_low, 2), other_low, flip_dp(other_low, 1)]


def block_of(piece, slot):
    mid, depth = slot // 4, slot % 4
    return depth * 4 + (mid, mid + 2, mid * 2, mid * 2 + 1)[piece]


def plain_spans(cols):
    half = cols // 2
    return ([(0, half)], [(half, half)])


def qkv_spans(cols):
    third = cols // 3
    half = third // 2
    return ([(c * third, half) for c in range(3)], [(c * third + half, half) for c in range(3)])


def load_weight(pieces, weight_ref, sems, me, spans):
    copies = []
    for p in range(4):
        for s in range(8):
            row = pl.multiple_of((me ^ block_of(p, s)) * 64, 64)
            start = 0
            for at, cols in spans[p // 2]:
                copies.append(
                    pltpu.make_async_copy(
                        pieces[p].at[s, :, pl.ds(start, cols)],
                        weight_ref.at[pl.ds(row, 64), pl.ds(at, cols)],
                        sems.at[len(copies)],
                    )
                )
                start += cols
    return copies


def sum_blocks(keep_a, send_a, keep_b, send_b):
    keep_a = (keep_a.astype(f32) + flip_dp(send_a, 2).astype(f32)).astype(bf16)
    keep_b = (keep_b.astype(f32) + flip_dp(send_b, 1).astype(f32)).astype(bf16)
    sums = []
    for part, bits in ((keep_a, 1), (keep_b, 2)):
        part = (part[:256].astype(f32) + flip_dp(part[256:], bits).astype(f32)).astype(bf16)
        total = part[:64].astype(f32)
        for z in (1, 2, 3):
            total = total + flip_dp(part[64 * z : 64 * (z + 1)], 4 * z).astype(f32)
        sums.append(total)
    return jnp.concatenate(sums, axis=1)


def sum_small(vectors):
    for bits in (1, 2, 4, 8):
        vectors = vectors + flip_dp(vectors, bits)
    return vectors


def turned(values, out_ref, me):
    flipped = values.T
    for a in range(16):
        r = me ^ a
        slot = ((r >> 1) & 1) * 8 + (r & 1) * 4 + (r >> 2)
        out_ref[pl.ds(pl.multiple_of(slot * 64, 64), 64), :] = flipped[a * 64 : (a + 1) * 64, :]


ANY = pl.BlockSpec(memory_space=pl.ANY)


def normalized(values):
    average = jnp.mean(values, axis=-1, keepdims=True)
    centred = values - average
    variance = jnp.mean(centred * centred, axis=-1, keepdims=True)
    inverse = lax.rsqrt(variance + norm_eps)
    return centred * inverse, inverse


def grid_call(kernel, steps, scalars, ins, outs, scratch, flops, name, exps=0):
    arrays = [a for a, _ in ins]
    nbytes = sum(a.size * a.dtype.itemsize for a in arrays)
    nbytes += sum(o.size * o.dtype.itemsize for o, _ in outs)
    return pl.pallas_call(
        kernel,
        grid_spec=pltpu.PrefetchScalarGridSpec(
            num_scalar_prefetch=1,
            grid=(steps,),
            in_specs=[s for _, s in ins],
            out_specs=[s for _, s in outs],
            scratch_shapes=scratch,
        ),
        out_shape=[o for o, _ in outs],
        compiler_params=params(),
        cost_estimate=cost(flops, nbytes, exps),
        name=name,
    )(scalars, *arrays)


def shape(rows, cols, dtype=bf16):
    return jax.ShapeDtypeStruct((rows, cols), dtype)


def row_tile(rows, cols):
    return pl.BlockSpec((rows, cols), lambda i, s: (i, 0))


def whole(rows, cols):
    return pl.BlockSpec((rows, cols), lambda i, s: (0, 0))


def own_tile(cols, tiles):
    return pl.BlockSpec((BT, cols), lambda i, s: (jnp.clip(i - tiles * s[1], 0, tiles - 1), 0))


def other_tile(cols, tiles):
    return pl.BlockSpec(
        (BT, cols), lambda i, s: (jnp.clip(i - tiles * (1 - s[1]), 0, tiles - 1), 0)
    )


def pick_rows(s_ref, own_ref, other_ref, tiles):
    mine = (pl.program_id(0) // tiles) == s_ref[1]
    return jnp.where(mine, own_ref[...], other_ref[...])


def qkv_first_kernel(tiles, s_ref, own, other, gain, shift, bias, p0, p1, p2, p3, rows_out, turned_out, out, w, sems):
    copies = load_weight((p0, p1, p2, p3), w, sems, s_ref[0], qkv_spans(w.shape[1]))

    @pl.when(pl.program_id(0) == 0)
    def _():
        for copy in copies:
            copy.start()

    values = pick_rows(s_ref, own, other, tiles).astype(f32)
    scaled, _ = normalized(values)
    normed = (scaled * gain[...] + shift[...]).astype(bf16)
    rows_out[...] = normed
    turned(normed, turned_out, s_ref[0])

    @pl.when(pl.program_id(0) == 0)
    def _():
        for copy in copies:
            copy.wait()

    out[...] = (dot_nn(normed, w[...]) + bias[...]).astype(bf16)


def qkv_second_kernel(s_ref, rows, bias, p0, p1, p2, p3, out, w, sems):
    copies = load_weight((p0, p1, p2, p3), w, sems, s_ref[0], qkv_spans(w.shape[1]))

    @pl.when(pl.program_id(0) == 0)
    def _():
        for copy in copies:
            copy.start()
        for copy in copies:
            copy.wait()

    out[...] = (dot_nn(rows[...], w[...]) + bias[...]).astype(bf16)


def weight_scratch(*cols):
    made = []
    for c in cols:
        made += [pltpu.VMEM((1024, c), bf16), pltpu.SemaphoreType.DMA((96,))]
    return made


def project_kernel(s_ref, a0, a1, p0, p1, p2, p3, out, w, sems):
    copies = load_weight((p0, p1, p2, p3), w, sems, s_ref[0], plain_spans(w.shape[1]))

    @pl.when(pl.program_id(0) == 0)
    def _():
        for copy in copies:
            copy.start()
        for copy in copies:
            copy.wait()

    half = a0.shape[1]
    out[...] = (dot_nt(a0[...], w[:, :half]) + dot_nt(a1[...], w[:, half:])).astype(bf16)


def project_norm_kernel(s_ref, a0, a1, p0, p1, p2, p3, toks, came, bias, gain, shift, hid_out, normed_out, w, sems):
    copies = load_weight((p0, p1, p2, p3), w, sems, s_ref[0], plain_spans(w.shape[1]))

    @pl.when(pl.program_id(0) == 0)
    def _():
        for copy in copies:
            copy.start()
        for copy in copies:
            copy.wait()

    half = a0.shape[1]
    partial = dot_nt(a0[...], w[:, :half]) + dot_nt(a1[...], w[:, half:])
    hidden = toks[...].astype(f32) + (partial + came[...].astype(f32) + bias[...])
    hid_out[...] = hidden
    scaled, _ = normalized(hidden)
    normed_out[...] = (scaled * gain[...] + shift[...]).astype(bf16)


def feed_kernel(s_ref, x_ref, c_ref, bias, u0, u1, u2, u3, d0, d1, d2, d3,
                act, gpre, ffn, gnorm, x_turned, c_turned, bsum, wu, semu, wd, semd):
    copies = load_weight((u0, u1, u2, u3), wu, semu, s_ref[0], plain_spans(wu.shape[1]))
    copies += load_weight((d0, d1, d2, d3), wd, semd, s_ref[0], plain_spans(wd.shape[1]))

    @pl.when(pl.program_id(0) == 0)
    def _():
        for copy in copies:
            copy.start()
        bsum[...] = jnp.zeros(bsum.shape, f32)

    x, c = x_ref[...], c_ref[...]
    turned(x, x_turned, s_ref[0])
    turned(c, c_turned, s_ref[0])

    @pl.when(pl.program_id(0) == 0)
    def _():
        for copy in copies:
            copy.wait()

    width = 512
    for part in range(wu.shape[1] // width):
        cols = slice(part * width, (part + 1) * width)
        value = dot_nn(x, wu[:, cols]) + bias[:, cols]
        upstream = dot_nn(c, wd[:, cols])
        square = value * value
        bent = jnp.tanh(value * (gelu_coeff + (gelu_coeff * 0.044715) * square))
        half_up = 0.5 + 0.5 * bent
        act[:, cols] = (value * half_up).astype(bf16)
        slope = half_up + value * (half_up * (1.0 - bent)) * (
            gelu_coeff + (3.0 * 0.044715 * gelu_coeff) * square
        )
        grad = (upstream * slope).astype(bf16)
        gpre[:, cols] = grad
        bsum[:, cols] += jnp.sum(grad.astype(f32).reshape(-1, 8, width), axis=0)
    ffn[...] = dot_nt(act[...], wd[...]).astype(bf16)
    gnorm[...] = dot_nt(gpre[...], wu[...]).astype(bf16)


def column_sum(values):
    return jnp.sum(values.reshape(-1, 8, values.shape[-1]), axis=0)


def middle_kernel(s_ref, hid, f_own, f_came, g_own, g_came, cot, bias, gain, out, gattn, sums):
    @pl.when(pl.program_id(0) == 0)
    def _():
        sums[...] = jnp.zeros(sums.shape, f32)

    hidden = hid[...]
    grad_out = cot[...].astype(f32)
    out[...] = (hidden + (f_own[...].astype(f32) + f_came[...].astype(f32) + bias[...])).astype(bf16)
    scaled, inverse = normalized(hidden)
    grad_norm = g_own[...].astype(f32) + g_came[...].astype(f32)
    through = grad_norm * gain[...]
    centre = jnp.mean(through, axis=-1, keepdims=True)
    along = jnp.mean(through * scaled, axis=-1, keepdims=True)
    grad = (grad_out + inverse * (through - centre - scaled * along)).astype(bf16)
    gattn[...] = grad
    sums[0:8, :] += column_sum(grad_norm * scaled)
    sums[8:16, :] += column_sum(grad_norm)
    sums[16:24, :] += column_sum(grad.astype(f32))
    sums[24:32, :] += column_sum(grad_out)


def grad_attended_kernel(tiles, s_ref, own, other, e0, e1, p0, p1, p2, p3, do0, do1, dl0, dl1, g_turned, w, sems):
    copies = load_weight((p0, p1, p2, p3), w, sems, s_ref[0], plain_spans(w.shape[1]))

    @pl.when(pl.program_id(0) == 0)
    def _():
        for copy in copies:
            copy.start()

    grad = pick_rows(s_ref, own, other, tiles)
    turned(grad, g_turned, s_ref[0])

    @pl.when(pl.program_id(0) == 0)
    def _():
        for copy in copies:
            copy.wait()

    half = e0.shape[1]
    result = dot_nn(grad, w[...]).astype(bf16)
    head = lax.broadcasted_iota(jnp.int32, (8, half), 0)
    lane = lax.broadcasted_iota(jnp.int32, (8, half), 1) // HD
    pick = jnp.where(head == lane, 1.0, 0.0).astype(f32)
    for exact, do_out, delta_out, start in ((e0, do0, dl0, 0), (e1, do1, dl1, half)):
        part = result[:, start : start + half]
        do_out[...] = part
        delta_out[...] = lax.dot_general(
            pick,
            part.astype(f32) * exact[...],
            (((1,), (1,)), ((), ())),
            precision=lax.Precision.HIGHEST,
            preferred_element_type=f32,
        )


def grad_rows_kernel(parts, *refs):
    s_ref, refs = refs[0], refs[1:]
    grads, refs = refs[:parts], refs[parts:]
    p = refs[:8]
    out, wa, sema, wb, semb = refs[8:]
    spans = qkv_spans(wa.shape[1])
    copies = load_weight(p[:4], wa, sema, s_ref[0], spans)
    copies += load_weight(p[4:], wb, semb, s_ref[0], spans)

    @pl.when(pl.program_id(0) == 0)
    def _():
        for copy in copies:
            copy.start()
        for copy in copies:
            copy.wait()

    out[...] = grad_rows(grads, wa, wb).astype(bf16)


def grad_rows(grads, wa, wb):
    first = jnp.concatenate([g[...] for g in grads[:3]], axis=1)
    second = jnp.concatenate([g[...] for g in grads[3:]], axis=1)
    return dot_nt(first, wa[...]) + dot_nt(second, wb[...])


def grad_tokens_kernel(*refs):
    s_ref, refs = refs[0], refs[1:]
    grads, p, refs = refs[:6], refs[6:14], refs[14:]
    toks, came, gattn, gain, out, sums, wa, sema, wb, semb = refs
    spans = qkv_spans(wa.shape[1])
    copies = load_weight(p[:4], wa, sema, s_ref[0], spans)
    copies += load_weight(p[4:], wb, semb, s_ref[0], spans)

    @pl.when(pl.program_id(0) == 0)
    def _():
        for copy in copies:
            copy.start()
        sums[...] = jnp.zeros(sums.shape, f32)
        for copy in copies:
            copy.wait()

    grad_norm = grad_rows(grads, wa, wb) + came[...].astype(f32)
    scaled, inverse = normalized(toks[...].astype(f32))
    through = grad_norm * gain[...]
    centre = jnp.mean(through, axis=-1, keepdims=True)
    along = jnp.mean(through * scaled, axis=-1, keepdims=True)
    grad_in = inverse * (through - centre - scaled * along)
    out[...] = (gattn[...].astype(f32) + grad_in).astype(bf16)
    sums[0:8, :] += column_sum(grad_norm * scaled)
    sums[8:16, :] += column_sum(grad_norm)


def weight_grad_kernel(lefts, rights, spans, *refs):
    refs = refs[1:]
    left, right = refs[:lefts], refs[lefts : lefts * (1 + rights)]
    outs, sums, total = refs[lefts * (1 + rights) : -2], refs[-2], refs[-1]
    step = pl.program_id(0)
    tiles = pl.num_programs(0) // lefts

    def add(k, fresh):
        at = 0
        for r in right[k * rights : (k + 1) * rights]:
            cols = slice(at, at + r.shape[1])
            term = dot_nn(left[k][...], r[...])
            count = column_sum(r[...].astype(f32))
            total[:, cols] = term if fresh else total[:, cols] + term
            sums[:, cols] = count if fresh else sums[:, cols] + count
            at += r.shape[1]

    @pl.when(step == 0)
    def _():
        add(0, True)

    for k in range(lefts):

        @pl.when((step > 0) & (step // tiles == k))
        def _():
            add(k, False)

    @pl.when(step == pl.num_programs(0) - 1)
    def _():
        keep_a, send_a, keep_b, send_b = outs
        to = 0
        for at, cols in spans[0]:
            here, there = slice(at, at + cols), slice(to, to + cols)
            keep_a[:, there] = total[0:512, here].astype(bf16)
            send_a[:, there] = total[512:1024, here].astype(bf16)
            to += cols
        to = 0
        for at, cols in spans[1]:
            here, there = slice(at, at + cols), slice(to, to + cols)
            keep_b[0:256, there] = total[0:256, here].astype(bf16)
            keep_b[256:512, there] = total[512:768, here].astype(bf16)
            send_b[0:256, there] = total[256:512, here].astype(bf16)
            send_b[256:512, there] = total[768:1024, here].astype(bf16)
            to += cols


def weight_grad(scalars, lefts, rights, spans_of, name):
    tiles = lefts[0].shape[1] // BT
    cols = sum(r.shape[1] for r in rights[0])
    ins = []
    for k, left in enumerate(lefts):
        ins.append(
            (
                left,
                pl.BlockSpec(
                    (1024, BT), lambda i, s, k=k: (0, jnp.clip(i - k * tiles, 0, tiles - 1))
                ),
            )
        )
    for k, group in enumerate(rights):
        for r in group:
            ins.append(
                (
                    r,
                    pl.BlockSpec(
                        (BT, r.shape[1]), lambda i, s, k=k: (jnp.clip(i - k * tiles, 0, tiles - 1), 0)
                    ),
                )
            )
    outs = [(shape(512, cols // 2), whole(512, cols // 2))] * 4
    outs.append((shape(8, cols, f32), whole(8, cols)))
    return grid_call(
        functools.partial(weight_grad_kernel, len(lefts), len(rights[0]), spans_of(cols)),
        tiles * len(lefts),
        scalars,
        ins,
        outs,
        [pltpu.VMEM((1024, cols), f32)],
        2 * 1024 * cols * BT * tiles * len(lefts),
        name,
    )


def wide(vector):
    return vector.astype(f32).reshape(1, -1)


def pieces_in(*groups):
    return [(piece, ANY) for group in groups for piece in group]


def layer_on_pairs(
    tokens,
    slot_lengths,
    gain_one,
    shift_one,
    w_qkv,
    bias_qv,
    w_out,
    bias_out,
    gain_two,
    shift_two,
    w_up,
    bias_up,
    w_down,
    bias_down,
    cotangent,
):
    own_rows, width = tokens.shape
    total_rows = 2 * own_rows
    tiles = own_rows // BT
    local = w_qkv.shape[2]
    half = local // 2
    hidden_cols = w_up.shape[1]
    me = lax.axis_index("dp").astype(jnp.int32)
    side = lax.axis_index("mp").astype(jnp.int32)
    scalars = jnp.stack([me, side])
    lengths = slot_lengths[0]

    def qkv_shard(g):
        quarter = half // 2
        part = w_qkv[:, :, g * half : (g + 1) * half]
        return jnp.concatenate(
            [part[:, :, :quarter].reshape(64, -1), part[:, :, quarter:].reshape(64, -1)], axis=1
        )

    tokens_other = swap_mp(tokens)
    qkv = [gather_blocks(qkv_shard(0)), gather_blocks(qkv_shard(1))]
    out_w = gather_blocks(w_out.T)
    up_w = gather_blocks(w_up)
    down_w = gather_blocks(w_down.T)
    cotangent_other = swap_mp(cotangent)

    zero_bias = jnp.zeros((half,), f32)
    biases = []
    for g in range(2):
        cols = slice(g * half, (g + 1) * half)
        biases.append(
            jnp.concatenate(
                [bias_qv[0, cols].astype(f32), zero_bias, bias_qv[1, cols].astype(f32)]
            ).reshape(1, -1)
        )

    def natural(i_cols):
        return pl.BlockSpec((BT, i_cols), lambda i, s: (i, 0))

    side_cols = 3 * half
    rows_one, rows_turned, packed_0 = grid_call(
        functools.partial(qkv_first_kernel, tiles),
        2 * tiles,
        scalars,
        [
            (tokens, own_tile(width, tiles)),
            (tokens_other, other_tile(width, tiles)),
            (wide(gain_one), whole(1, width)),
            (wide(shift_one), whole(1, width)),
            (biases[0], whole(1, side_cols)),
        ]
        + pieces_in(qkv[0]),
        [
            (shape(total_rows, width), natural(width)),
            (shape(width, total_rows), pl.BlockSpec((width, BT), lambda i, s: (0, i))),
            (shape(total_rows, side_cols), natural(side_cols)),
        ],
        weight_scratch(side_cols),
        2 * total_rows * width * side_cols,
        "qkv_first",
    )
    attended, exact, lse = [None, None], [None, None], [None, None]
    attended[0], exact[0], lse[0] = attend_forward(packed_0, lengths)
    (packed_1,) = grid_call(
        qkv_second_kernel,
        2 * tiles,
        scalars,
        [(rows_one, natural(width)), (biases[1], whole(1, side_cols))] + pieces_in(qkv[1]),
        [(shape(total_rows, side_cols), natural(side_cols))],
        weight_scratch(side_cols),
        2 * total_rows * width * side_cols,
        "qkv_second",
    )
    attended[1], exact[1], lse[1] = attend_forward(packed_1, lengths)
    packed = [packed_0, packed_1]

    def own_of_natural(cols):
        return pl.BlockSpec((BT, cols), lambda i, s: (s[1] * tiles + i, 0))

    def other_of_natural(cols):
        return pl.BlockSpec((BT, cols), lambda i, s: ((1 - s[1]) * tiles + i, 0))

    (partial_other,) = grid_call(
        project_kernel,
        tiles,
        scalars,
        [(attended[0], other_of_natural(half)), (attended[1], other_of_natural(half))]
        + pieces_in(out_w),
        [(shape(own_rows, width), row_tile(BT, width))],
        weight_scratch(local),
        2 * own_rows * width * local,
        "project_other",
    )
    partial_came = swap_mp(partial_other)
    hidden, normed_own = grid_call(
        project_norm_kernel,
        tiles,
        scalars,
        [(attended[0], own_of_natural(half)), (attended[1], own_of_natural(half))]
        + pieces_in(out_w)
        + [
            (tokens, row_tile(BT, width)),
            (partial_came, row_tile(BT, width)),
            (wide(bias_out), whole(1, width)),
            (wide(gain_two), whole(1, width)),
            (wide(shift_two), whole(1, width)),
        ],
        [
            (shape(own_rows, width, f32), row_tile(BT, width)),
            (shape(own_rows, width), row_tile(BT, width)),
        ],
        weight_scratch(local),
        2 * own_rows * width * local,
        "project_norm",
    )
    normed_other = swap_mp(normed_own)

    def feed(rows, cots):
        turn = pl.BlockSpec((width, BT), lambda i, s: (0, i))
        return grid_call(
            feed_kernel,
            tiles,
            scalars,
            [
                (rows, row_tile(BT, width)),
                (cots, row_tile(BT, width)),
                (wide(bias_up), whole(1, hidden_cols)),
            ]
            + pieces_in(up_w, down_w),
            [
                (shape(own_rows, hidden_cols), row_tile(BT, hidden_cols)),
                (shape(own_rows, hidden_cols), row_tile(BT, hidden_cols)),
                (shape(own_rows, width), row_tile(BT, width)),
                (shape(own_rows, width), row_tile(BT, width)),
                (shape(width, own_rows), turn),
                (shape(width, own_rows), turn),
                (shape(8, hidden_cols, f32), whole(8, hidden_cols)),
            ],
            weight_scratch(hidden_cols, hidden_cols),
            8 * own_rows * width * hidden_cols,
            "feed",
            own_rows * hidden_cols,
        )

    act_own, pre_own, ffn_own, norm_own, x_own, c_own, bsum_own = feed(normed_own, cotangent)
    act_oth, pre_oth, ffn_oth, norm_oth, x_oth, c_oth, bsum_oth = feed(normed_other, cotangent_other)
    norm_came = swap_mp(norm_oth)
    ffn_came = swap_mp(ffn_oth)
    down_parts = weight_grad(
        scalars, [c_own, c_oth], [[act_own], [act_oth]], plain_spans, "down_grad"
    )
    output, grad_attn, middle_sums = grid_call(
        middle_kernel,
        tiles,
        scalars,
        [
            (hidden, row_tile(BT, width)),
            (ffn_own, row_tile(BT, width)),
            (ffn_came, row_tile(BT, width)),
            (norm_own, row_tile(BT, width)),
            (norm_came, row_tile(BT, width)),
            (cotangent, row_tile(BT, width)),
            (wide(bias_down), whole(1, width)),
            (wide(gain_two), whole(1, width)),
        ],
        [
            (shape(own_rows, width), row_tile(BT, width)),
            (shape(own_rows, width), row_tile(BT, width)),
            (shape(32, width, f32), whole(32, width)),
        ],
        [],
        40 * own_rows * width,
        "middle",
    )
    grad_attn_other = swap_mp(grad_attn)
    up_parts = weight_grad(scalars, [x_own, x_oth], [[pre_own], [pre_oth]], plain_spans, "up_grad")
    do_0, do_1, delta_0, delta_1, g_turned = grid_call(
        functools.partial(grad_attended_kernel, tiles),
        2 * tiles,
        scalars,
        [
            (grad_attn, own_tile(width, tiles)),
            (grad_attn_other, other_tile(width, tiles)),
            (exact[0], natural(half)),
            (exact[1], natural(half)),
        ]
        + pieces_in(out_w),
        [
            (shape(total_rows, half), natural(half)),
            (shape(total_rows, half), natural(half)),
            (shape(8, total_rows, f32), pl.BlockSpec((8, BT), lambda i, s: (0, i))),
            (shape(8, total_rows, f32), pl.BlockSpec((8, BT), lambda i, s: (0, i))),
            (shape(width, total_rows), pl.BlockSpec((width, BT), lambda i, s: (0, i))),
        ],
        weight_scratch(local),
        2 * total_rows * width * local,
        "grad_attended",
    )
    out_parts = weight_grad(scalars, [g_turned], [attended], plain_spans, "out_grad")
    grads_0 = attend_backward(packed[0], do_0, lse[0], delta_0, lengths)
    grads_1 = attend_backward(packed[1], do_1, lse[1], delta_1, lengths)
    qkv_parts = [
        weight_grad(scalars, [rows_turned], [list(g)], qkv_spans, "qkv_grad")
        for g in (grads_0, grads_1)
    ]
    grads = list(grads_0) + list(grads_1)
    (rows_other,) = grid_call(
        functools.partial(grad_rows_kernel, 6),
        tiles,
        scalars,
        [(g, other_of_natural(half)) for g in grads] + pieces_in(qkv[0], qkv[1]),
        [(shape(own_rows, width), row_tile(BT, width))],
        weight_scratch(side_cols, side_cols),
        4 * own_rows * width * side_cols,
        "grad_rows",
    )
    rows_came = swap_mp(rows_other)
    grad_tokens, token_sums = grid_call(
        grad_tokens_kernel,
        tiles,
        scalars,
        [(g, own_of_natural(half)) for g in grads]
        + pieces_in(qkv[0], qkv[1])
        + [
            (tokens, row_tile(BT, width)),
            (rows_came, row_tile(BT, width)),
            (grad_attn, row_tile(BT, width)),
            (wide(gain_one), whole(1, width)),
        ],
        [
            (shape(own_rows, width), row_tile(BT, width)),
            (shape(16, width, f32), whole(16, width)),
        ],
        weight_scratch(side_cols, side_cols),
        4 * own_rows * width * side_cols,
        "grad_tokens",
    )

    grad_down = sum_blocks(*down_parts[:4]).T
    grad_up = sum_blocks(*up_parts[:4])
    grad_w_out = sum_blocks(*out_parts[:4]).T
    quarter = half // 2
    qkv_sums = [sum_blocks(*parts[:4]).reshape(64, 2, 3, quarter) for parts in qkv_parts]
    grad_w_qkv = jnp.concatenate(
        [part[:, a] for part in qkv_sums for a in range(2)], axis=2
    )

    early = middle_sums.reshape(4, 8, width).sum(axis=1)
    early = early + swap_mp(early)
    up_bias = (bsum_own + bsum_oth).sum(axis=0).reshape(-1, width)
    early = sum_small(jnp.concatenate([early, up_bias]))
    late = token_sums.reshape(2, 8, width).sum(axis=1)
    late = late + swap_mp(late)
    qv = jnp.stack(
        [
            jnp.concatenate([parts[4][:, c : c + half].sum(axis=0) for parts in qkv_parts])
            for c in (0, 2 * half)
        ]
    )
    late = sum_small(jnp.concatenate([late, qv.reshape(-1, width)]))
    return (
        output,
        grad_tokens,
        late[0],
        late[1],
        grad_w_qkv,
        late[2:].reshape(2, local),
        grad_w_out,
        early[2],
        early[0],
        early[1],
        grad_up,
        early[4:].reshape(-1),
        grad_down,
        early[3],
    )


def gelu_tanh(values):
    inner = gelu_coeff * (values + 0.044715 * values * values * values)
    return 0.5 * values * (1.0 + jnp.tanh(inner))


def gelu_slope(values):
    inner = gelu_coeff * (values + 0.044715 * values * values * values)
    bent = jnp.tanh(inner)
    return 0.5 * (1.0 + bent) + 0.5 * values * (1.0 - bent * bent) * gelu_coeff * (
        1.0 + 3.0 * 0.044715 * values * values
    )


def norm_forward(values, gain_vec, shift_vec):
    average = jnp.mean(values, axis=-1, keepdims=True)
    centred = values - average
    variance = jnp.mean(centred * centred, axis=-1, keepdims=True)
    inverse = lax.rsqrt(variance + norm_eps)
    scaled = centred * inverse
    return (scaled * gain_vec.astype(f32) + shift_vec.astype(f32), scaled, inverse)


def norm_backward(grad_out, scaled, inverse, gain_vec):
    grad_scaled = grad_out * gain_vec.astype(f32)
    centre_term = jnp.mean(grad_scaled, axis=-1, keepdims=True)
    slope_term = jnp.mean(grad_scaled * scaled, axis=-1, keepdims=True)
    grad_in = inverse * (grad_scaled - centre_term - scaled * slope_term)
    return (grad_in, jnp.sum(grad_out * scaled, axis=0), jnp.sum(grad_out, axis=0))


def layer_by_collectives(
    tokens,
    slot_lengths,
    gain_one,
    shift_one,
    w_qkv,
    bias_qv,
    w_out,
    bias_out,
    gain_two,
    shift_two,
    w_up,
    bias_up,
    w_down,
    bias_down,
    cotangent,
):
    w_qkv, w_out, w_up, w_down = (
        lax.all_gather(w_qkv, "dp", axis=0, tiled=True),
        lax.all_gather(w_out, "dp", axis=1, tiled=True),
        lax.all_gather(w_up, "dp", axis=0, tiled=True),
        lax.all_gather(w_down, "dp", axis=1, tiled=True),
    )
    lengths = slot_lengths[0]
    residual = tokens.astype(f32)
    normed_one, scaled_one, inverse_one = norm_forward(residual, gain_one, shift_one)
    rows_one = lax.all_gather(normed_one.astype(bf16), "mp", axis=0, tiled=True)
    packed = jnp.einsum("td,dcf->tcf", rows_one, w_qkv, preferred_element_type=f32)
    zero_bias = jnp.zeros_like(bias_qv[0])
    packed_bias = jnp.stack([bias_qv[0], zero_bias, bias_qv[1]]).astype(f32)
    packed = (packed + packed_bias[None]).astype(bf16)
    local = packed.shape[2]
    group = min(256, local)
    packed_groups, attended, exact_out, log_totals = [], [], [], []
    for at in range(0, local, group):
        part = packed[:, :, at : at + group].reshape(packed.shape[0], -1)
        low, exact, logs = attend_forward(part, lengths)
        packed_groups.append(part)
        attended.append(low)
        exact_out.append(exact)
        log_totals.append(logs)
    attended = jnp.concatenate(attended, axis=1)
    hidden = (
        residual
        + lax.psum_scatter(
            jnp.dot(attended, w_out, preferred_element_type=f32),
            "mp",
            scatter_dimension=0,
            tiled=True,
        )
        + bias_out.astype(f32)
    )
    normed_two, scaled_two, inverse_two = norm_forward(hidden, gain_two, shift_two)
    normed_low = normed_two.astype(bf16)
    rows_two = lax.all_gather(normed_low, "mp", axis=0, tiled=True)
    preact = jnp.dot(rows_two, w_up, preferred_element_type=f32) + bias_up.astype(
        f32
    )
    active = gelu_tanh(preact).astype(bf16)
    ffn_out = lax.psum_scatter(
        jnp.dot(active, w_down, preferred_element_type=f32).astype(bf16),
        "mp",
        scatter_dimension=0,
        tiled=True,
    ).astype(f32)
    output = (hidden + ffn_out + bias_down.astype(f32)).astype(bf16)
    grad_out = cotangent.astype(f32)
    grad_rows = lax.all_gather(cotangent, "mp", axis=0, tiled=True)
    grad_active = jnp.einsum("td,fd->tf", grad_rows, w_down, preferred_element_type=f32)
    grad_pre = (grad_active * gelu_slope(preact)).astype(bf16)
    grad_up = jnp.einsum("td,tf->df", rows_two, grad_pre, preferred_element_type=f32)
    grad_down = jnp.einsum("tf,td->fd", active, grad_rows, preferred_element_type=f32)
    grad_bias_up = jnp.sum(grad_pre.astype(f32), axis=0)
    grad_norm_two = lax.psum_scatter(
        jnp.einsum("tf,df->td", grad_pre, w_up, preferred_element_type=f32),
        "mp",
        scatter_dimension=0,
        tiled=True,
    )
    grad_in_two, grad_gain_two, grad_shift_two = norm_backward(
        grad_norm_two, scaled_two, inverse_two, gain_two
    )
    grad_hidden = grad_out + grad_in_two
    grad_attn = grad_hidden.astype(bf16)
    grad_attn_rows = lax.all_gather(grad_attn, "mp", axis=0, tiled=True)
    grad_w_out = jnp.einsum(
        "tf,td->fd", attended, grad_attn_rows, preferred_element_type=f32
    )
    grad_attended = jnp.einsum(
        "td,fd->tf", grad_attn_rows, w_out, preferred_element_type=f32
    ).astype(bf16)
    pieces = []
    for k, at in enumerate(range(0, local, group)):
        part = grad_attended[:, at : at + group]
        product = (part.astype(f32) * exact_out[k]).reshape(part.shape[0], -1, HD)
        delta = jnp.sum(product, axis=-1).T
        delta = jnp.pad(delta, ((0, 8 - delta.shape[0]), (0, 0)))
        grads = attend_backward(packed_groups[k], part, log_totals[k], delta, lengths)
        pieces.append(jnp.stack(grads, axis=1))
    grad_packed = jnp.concatenate(pieces, axis=2)
    grad_w_qkv = jnp.einsum(
        "td,tcf->dcf", rows_one, grad_packed, preferred_element_type=f32
    )
    grad_bias_qv = jnp.stack(
        [
            jnp.sum(grad_packed[:, 0].astype(f32), axis=0),
            jnp.sum(grad_packed[:, 2].astype(f32), axis=0),
        ]
    )
    grad_norm_one = lax.psum_scatter(
        jnp.einsum("tcf,dcf->td", grad_packed, w_qkv, preferred_element_type=f32),
        "mp",
        scatter_dimension=0,
        tiled=True,
    )
    grad_in_one, grad_gain_one, grad_shift_one = norm_backward(
        grad_norm_one, scaled_one, inverse_one, gain_one
    )
    grad_tokens = (grad_hidden + grad_in_one).astype(bf16)
    grad_bias_out = jnp.sum(grad_attn.astype(f32), axis=0)
    grad_bias_down = jnp.sum(grad_out, axis=0)
    grad_w_qkv, grad_w_out, grad_up, grad_down = (
        lax.psum_scatter(grad_w_qkv, "dp", scatter_dimension=0, tiled=True),
        lax.psum_scatter(grad_w_out, "dp", scatter_dimension=1, tiled=True),
        lax.psum_scatter(grad_up, "dp", scatter_dimension=0, tiled=True),
        lax.psum_scatter(grad_down, "dp", scatter_dimension=1, tiled=True),
    )
    small_grads = lax.psum(
        (
            grad_gain_one,
            grad_shift_one,
            grad_bias_out,
            grad_gain_two,
            grad_shift_two,
            grad_bias_down,
        ),
        ("dp", "mp"),
    )
    grad_bias_qv, grad_bias_up = lax.psum((grad_bias_qv, grad_bias_up), "dp")
    return (
        output,
        grad_tokens,
        small_grads[0],
        small_grads[1],
        grad_w_qkv,
        grad_bias_qv,
        grad_w_out,
        small_grads[2],
        small_grads[3],
        small_grads[4],
        grad_up,
        grad_bias_up,
        grad_down,
        small_grads[5],
    )


def solution(mesh):
    sizes = dict(mesh.shape)
    pairs = sizes == {"dp": 16, "mp": 2}
    layer = layer_on_pairs if pairs else layer_by_collectives
    return jax.shard_map(
        layer,
        mesh=mesh,
        in_specs=(
            P(("dp", "mp"), None),
            P("dp", None),
            P(),
            P(),
            P("dp", None, "mp"),
            P(None, "mp"),
            P("mp", "dp"),
            P(),
            P(),
            P(),
            P("dp", "mp"),
            P("mp"),
            P("mp", "dp"),
            P(),
            P(("dp", "mp"), None),
        ),
        out_specs=(
            P(("dp", "mp"), None),
            P(("dp", "mp"), None),
            P(),
            P(),
            P("dp", None, "mp"),
            P(None, "mp"),
            P("mp", "dp"),
            P(),
            P(),
            P(),
            P("dp", "mp"),
            P("mp"),
            P("mp", "dp"),
            P(),
        ),
        check_vma=False,
    )
```

```python
import functools
import math

import jax
import jax.numpy as jnp
from jax import lax
from jax.experimental import pallas as pl
from jax.experimental.pallas import tpu as pltpu
from jax.sharding import PartitionSpec as P

HD = 64
LONG_LEN = 3072
BT = 512
VMEM_CAP = 60 * 1024 * 1024

f32 = jnp.float32
bf16 = jnp.bfloat16
norm_eps = 1e-05
masked_score = -1e30
gelu_coeff = 0.7978845608028654
score_scale = HD ** (-0.5)
score_scale_2 = HD ** (-0.5) * math.log2(math.e)
safe_sum = 1e30


def dot_nt(left, right):
    return lax.dot_general(left, right, (((1,), (1,)), ((), ())), preferred_element_type=f32)


def dot_nn(left, right):
    return lax.dot_general(left, right, (((1,), (0,)), ((), ())), preferred_element_type=f32)


def dot_tn(left, right):
    return lax.dot_general(left, right, (((0,), (0,)), ((), ())), preferred_element_type=f32)


def params(axes=1, collective=None):
    if collective is None:
        return pltpu.CompilerParams(
            vmem_limit_bytes=VMEM_CAP, dimension_semantics=("arbitrary",) * axes
        )
    return pltpu.CompilerParams(
        vmem_limit_bytes=VMEM_CAP,
        dimension_semantics=("arbitrary",) * axes,
        collective_id=collective,
        has_side_effects=True,
    )


def cost(flops, nbytes, exps=0):
    return pl.CostEstimate(flops=int(flops), bytes_accessed=int(nbytes), transcendentals=int(exps))


ANY = pl.BlockSpec(memory_space=pl.ANY)


def bits_of_me():
    me = lax.axis_index("dp")
    return (me // 8, (me // 4) % 2, (me // 2) % 2, me % 2)


def flipped(bits, which):
    return tuple(1 - b if which & (8 >> k) else b for k, b in enumerate(bits))


def index_of(bits):
    return bits[0] * 8 + bits[1] * 4 + bits[2] * 2 + bits[3]


def across(which):
    return {"dp": index_of(flipped(bits_of_me(), which))}


def sibling():
    return {"mp": 1 - lax.axis_index("mp")}


MESH_ID = pl.DeviceIdType.MESH
HOPS = (1, 2, 4, 8, 12)


def greet(with_sibling):
    barrier = pltpu.get_barrier_semaphore()
    for hop in HOPS:
        pl.semaphore_signal(barrier, inc=1, device_id=across(hop), device_id_type=MESH_ID)
    if with_sibling:
        pl.semaphore_signal(barrier, inc=1, device_id=sibling(), device_id_type=MESH_ID)
    pl.semaphore_wait(barrier, len(HOPS) + (1 if with_sibling else 0))


def send(src, dst, sems, slot, device):
    return pltpu.make_async_remote_copy(
        src_ref=src,
        dst_ref=dst,
        send_sem=sems[0].at[slot],
        recv_sem=sems[1].at[slot],
        device_id=device,
        device_id_type=MESH_ID,
    )


def start_all(copies):
    for copy in copies:
        copy.start()


def wait_all(copies):
    for copy in copies:
        copy.wait()


def gather_z(src, dst, span, sems, base):
    bits = bits_of_me()
    z, yx = bits[0] * 2 + bits[1], bits[2] * 2 + bits[3]
    cols = pl.ds(*span)
    place = dst.at[z, yx, :, cols]
    copies = [
        send(src.at[:, cols], place, sems, base + k, across(4 * (k + 1))) for k in range(3)
    ]
    copies.append(pltpu.make_async_copy(src.at[:, cols], place, sems[2].at[base]))
    return copies


def gather_second(dst, span, route, sems, base):
    bits = bits_of_me()
    part = dst.at[:, bits[2] * 2 + bits[3], :, pl.ds(*span)]
    return [send(part, part, sems, base + 3, across((1, 2)[route]))]


def gather_third(dst, span, route, sems, base):
    copies = []
    for k, which in enumerate((0, (1, 2)[route])):
        bits = flipped(bits_of_me(), which)
        part = dst.at[:, bits[2] * 2 + bits[3], :, pl.ds(*span)]
        copies.append(send(part, part, sems, base + 4 + k, across((2, 1)[route])))
    return copies


def gather_sems(pieces):
    return [
        pltpu.SemaphoreType.DMA((6 * pieces,)),
        pltpu.SemaphoreType.DMA((6 * pieces,)),
        pltpu.SemaphoreType.DMA((6 * pieces,)),
    ]


def halves(cols, parts=1):
    half = cols // 2
    width = half // parts
    return [(r * half + c * width, width, r) for c in range(parts) for r in range(2)]


def head_lanes(block, head):
    lane_head = lax.broadcasted_iota(jnp.int32, block.shape, 1) // HD
    return jnp.where(lane_head == head, block, jnp.zeros_like(block))


def pack_heads(columns):
    lane = lax.broadcasted_iota(jnp.int32, columns[0].shape, 1)
    pairs = [
        jnp.where(lane < HD, columns[2 * i], columns[2 * i + 1]) for i in range(len(columns) // 2)
    ]
    return pairs[0] if len(pairs) == 1 else jnp.concatenate(pairs, axis=1)


def block_probs(scores, top):
    total, parts = None, []
    for t in range(scores.shape[1] // 128):
        part = jnp.exp2(scores[:, t * 128 : (t + 1) * 128] * score_scale_2 - top)
        total = part if total is None else total + part
        parts.append(part.astype(bf16))
    return parts, total


def attend_block(masked, keys, values, m_ref, l_ref, acc_ref):
    block = keys.shape[0]
    low = []
    for h, query in enumerate(masked):
        scores = dot_nt(query, keys)
        row = lax.broadcasted_iota(jnp.int32, scores.shape, 0)
        col = lax.broadcasted_iota(jnp.int32, scores.shape, 1)
        scores = jnp.where(row >= col, scores, masked_score)
        top = jnp.max(scores, axis=1, keepdims=True) * score_scale_2
        top = jnp.broadcast_to(top, (block, 128))
        m_ref[h] = top
        parts, l_ref[h] = block_probs(scores, top)
        low += parts
    acc_ref[...] = dot_nn(jnp.concatenate(low, axis=1), values)


def attend_finish(heads, m_ref, l_ref, acc_ref, out_ref, exact_ref, lse_ref):
    block = out_ref.shape[0]
    lane = lax.broadcasted_iota(jnp.int32, (block, 128), 1)
    rows = jnp.zeros((block, 128), f32)
    inverse = []
    for h in range(heads):
        total = jnp.sum(l_ref[h], axis=1, keepdims=True)
        rows = jnp.where(lane == h, m_ref[h][:, :1] + jnp.log2(total), rows)
        inverse.append(jnp.broadcast_to(1.0 / total, (block, 128)))
    result = acc_ref[...] * pack_heads(inverse)
    out_ref[...] = result.astype(bf16)
    exact_ref[...] = result
    lse_ref[...] = rows.T[:8, :]


def mask_values(v_ref, vm_ref, heads, block):
    for j in range(v_ref.shape[0] // block):
        value = v_ref[j * block : (j + 1) * block, :]
        for h in range(heads):
            vm_ref[j, h * block : (h + 1) * block, :] = head_lanes(value, h)


def attend_forward_kernel(heads, comm, lens_ref, q_ref, k_ref, v_ref, *refs):
    ins, refs = refs[: comm.ins], refs[comm.ins :]
    out_ref, exact_ref, lse_ref, big_ref = refs[:4]
    outs = refs[4 : 4 + comm.outs]
    vm_ref, m_ref, l_ref, acc_ref = refs[4 + comm.outs : 8 + comm.outs]
    sems = refs[8 + comm.outs :]
    step = pl.program_id(1)
    block = q_ref.shape[0]
    comm.before(pl.program_id(0) * pl.num_programs(1) + step, ins, outs, sems)

    @pl.when(step == 0)
    def _():
        mask_values(v_ref, vm_ref, heads, block)

    @pl.when((step == 0) & (pl.program_id(0) == 0))
    def _():
        big_ref[...] = jnp.zeros(big_ref.shape, f32)

    query = q_ref[...]
    masked = [head_lanes(query, h) for h in range(heads)]

    def key_block(j):
        return k_ref[pl.ds(pl.multiple_of(j * block, block), block), :]

    attend_block(masked, key_block(step), vm_ref[step], m_ref, l_ref, acc_ref)
    away = jnp.where(lens_ref[0] == LONG_LEN, 0.0, 1e30).astype(f32)

    def earlier(j, carry):
        keys = key_block(j)
        low = []
        for h in range(heads):
            parts, total = block_probs(dot_nt(masked[h], keys), m_ref[h] + away)
            l_ref[h] += total
            low += parts
        acc_ref[...] += dot_nn(jnp.concatenate(low, axis=1), vm_ref[j])
        return carry

    lax.fori_loop(0, step, earlier, 0)
    for h in range(heads):
        big_ref[...] = jnp.maximum(
            big_ref[...], jnp.max(l_ref[h].reshape(-1, 8, 128), axis=0)
        )
    attend_finish(heads, m_ref, l_ref, acc_ref, out_ref, exact_ref, lse_ref)
    comm.after(pl.program_id(0) * pl.num_programs(1) + step, ins, outs, sems)


def attend_safe_kernel(
    heads, lens_ref, q_ref, k_ref, v_ref, out_ref, exact_ref, lse_ref, vm_ref, m_ref, l_ref, acc_ref
):
    step = pl.program_id(1)
    block = q_ref.shape[0]

    @pl.when(step == 0)
    def _():
        mask_values(v_ref, vm_ref, heads, block)

    query = q_ref[...]
    masked = [head_lanes(query, h) for h in range(heads)]

    def key_block(j):
        return k_ref[pl.ds(pl.multiple_of(j * block, block), block), :]

    attend_block(masked, key_block(step), vm_ref[step], m_ref, l_ref, acc_ref)

    def earlier(j, carry):
        keys = key_block(j)
        low, shrink = [], []
        for h in range(heads):
            scores = dot_nt(masked[h], keys)
            old = m_ref[h]
            top = jnp.maximum(old, jnp.max(scores, axis=1, keepdims=True) * score_scale_2)
            factor = jnp.exp2(old - top)
            m_ref[h] = top
            parts, total = block_probs(scores, top)
            l_ref[h] = l_ref[h] * factor + total
            low += parts
            shrink.append(factor)
        acc_ref[...] = acc_ref[...] * pack_heads(shrink) + dot_nn(
            jnp.concatenate(low, axis=1), vm_ref[j]
        )
        return carry

    lax.fori_loop(0, jnp.where(lens_ref[0] == LONG_LEN, step, 0), earlier, 0)
    attend_finish(heads, m_ref, l_ref, acc_ref, out_ref, exact_ref, lse_ref)


class NoTransfers:
    ins = outs = 0

    def before(self, *args):
        pass

    def after(self, *args):
        pass


def attend_specs(tokens, width):
    groups = width // min(256, width)
    cols = width // groups
    ins = [
        pl.BlockSpec((BT, cols), lambda g, i, n: (i, g)),
        pl.BlockSpec((tokens, cols), lambda g, i, n: (0, groups + g)),
        pl.BlockSpec((tokens, cols), lambda g, i, n: (0, 2 * groups + g)),
    ]
    outs = [
        pl.BlockSpec((BT, cols), lambda g, i, n: (i, g)),
        pl.BlockSpec((BT, cols), lambda g, i, n: (i, g)),
        pl.BlockSpec((8, BT), lambda g, i, n: (g, i)),
    ]
    shapes = [
        jax.ShapeDtypeStruct((tokens, width), bf16),
        jax.ShapeDtypeStruct((tokens, width), f32),
        jax.ShapeDtypeStruct((8 * groups, tokens), f32),
    ]
    heads = cols // HD
    scratch = [
        pltpu.VMEM((tokens // BT, heads * BT, cols), bf16),
        pltpu.VMEM((heads, BT, 128), f32),
        pltpu.VMEM((heads, BT, 128), f32),
        pltpu.VMEM((BT, cols), f32),
    ]
    return groups, heads, ins, outs, shapes, scratch


def attend_cost(tokens, width, products):
    pairs = (tokens // BT) * (tokens // BT + 1) // 2
    work = products * 2 * pairs * BT * BT * width
    return cost(4 * work, 10 * tokens * width, pairs * BT * BT * width // HD)


def attend_safe(packed, lengths):
    tokens, width = packed.shape[0], packed.shape[1] // 3
    groups, heads, ins, outs, shapes, scratch = attend_specs(tokens, width)
    return pl.pallas_call(
        functools.partial(attend_safe_kernel, heads),
        grid_spec=pltpu.PrefetchScalarGridSpec(
            num_scalar_prefetch=1,
            grid=(groups, tokens // BT),
            in_specs=ins,
            out_specs=outs,
            scratch_shapes=scratch,
        ),
        out_shape=shapes,
        compiler_params=params(2),
        cost_estimate=attend_cost(tokens, width, 2),
        name="attend_safe",
    )(lengths, packed, packed, packed)


def attend_forward(packed, lengths, comm=NoTransfers(), moved=()):
    tokens, width = packed.shape[0], packed.shape[1] // 3
    groups, heads, ins, outs, shapes, scratch = attend_specs(tokens, width)
    low, exact, lse, big, *rest = pl.pallas_call(
        functools.partial(attend_forward_kernel, heads, comm),
        grid_spec=pltpu.PrefetchScalarGridSpec(
            num_scalar_prefetch=1,
            grid=(groups, tokens // BT),
            in_specs=ins + [ANY] * len(moved),
            out_specs=outs + [pl.BlockSpec((8, 128), lambda g, i, n: (0, 0))] + [ANY] * len(moved),
            scratch_shapes=scratch + (comm.scratch() if moved else []),
        ),
        out_shape=shapes
        + [jax.ShapeDtypeStruct((8, 128), f32)]
        + [jax.ShapeDtypeStruct(m.shape, m.dtype) for m in moved],
        input_output_aliases={4 + k: 4 + k for k in range(len(moved))},
        compiler_params=params(2, 2 if moved else None),
        cost_estimate=attend_cost(tokens, width, 2),
        name="attend_forward",
    )(lengths, packed, packed, packed, *moved)
    fits = jnp.max(big) < safe_sum
    low, exact, lse = lax.cond(
        fits,
        lambda low, exact, lse, packed: (low, exact, lse),
        lambda low, exact, lse, packed: tuple(attend_safe(packed, lengths)),
        low,
        exact,
        lse,
        packed,
    )
    return [low, exact, lse] + rest


def attend_backward_kernel(heads, comm, lens_ref, q_ref, k_ref, v_ref, do_ref, lse_ref, delta_ref, *refs):
    ins, refs = refs[: comm.ins], refs[comm.ins :]
    dq_ref, dk_ref, dv_ref = refs[:3]
    outs, refs = refs[3 : 3 + comm.outs], refs[3 + comm.outs :]
    qm_ref, dom_ref, km_ref, vm_ref, dqa_ref, dka_ref, dva_ref = refs[:7]
    scratch = refs[7:]
    step = pl.program_id(1)
    count = pl.num_programs(1)
    block = k_ref.shape[0]
    comm.before(pl.program_id(0) * count + step, ins, outs, scratch)

    @pl.when(step == 0)
    def _():
        for t in range(q_ref.shape[0] // block):
            rows = slice(t * block, (t + 1) * block)
            for h in range(heads):
                place = slice(h * block, (h + 1) * block)
                qm_ref[t, place, :] = head_lanes(q_ref[rows, :], h)
                dom_ref[t, place, :] = head_lanes(do_ref[rows, :], h)
        dqa_ref[...] = jnp.zeros(dqa_ref.shape, f32)

    for h in range(heads):
        place = slice(h * block, (h + 1) * block)
        km_ref[place, :] = head_lanes(k_ref[...], h)
        vm_ref[place, :] = head_lanes(v_ref[...], h)
    dka_ref[...] = jnp.zeros(dka_ref.shape, f32)
    dva_ref[...] = jnp.zeros(dva_ref.shape, f32)
    away = jnp.where(lens_ref[0] == LONG_LEN, 0.0, 1e30).astype(f32)

    def pair(i, on_diagonal):
        rows = pl.ds(pl.multiple_of(i * block, block), block)
        query, grad = q_ref[rows, :], do_ref[rows, :]
        low, slopes = [], []
        for h in range(heads):
            place = slice(h * block, (h + 1) * block)
            scores = dot_nt(km_ref[place, :], query)
            logs = lse_ref[h : h + 1, rows]
            if not on_diagonal:
                logs = logs + away
            prob = jnp.exp2(scores * score_scale_2 - logs)
            if on_diagonal:
                key = lax.broadcasted_iota(jnp.int32, scores.shape, 0)
                tok = lax.broadcasted_iota(jnp.int32, scores.shape, 1)
                prob = jnp.where(tok >= key, prob, 0.0)
            grad_prob = dot_nt(vm_ref[place, :], grad)
            slope = prob * (grad_prob - delta_ref[h : h + 1, rows])
            low.append(prob.astype(bf16))
            slopes.append(slope.astype(bf16))
        dva_ref[...] += dot_nn(jnp.concatenate(low, axis=1), dom_ref[i])
        dka_ref[...] += dot_nn(jnp.concatenate(slopes, axis=1), qm_ref[i])
        dqa_ref[rows, :] += dot_tn(jnp.concatenate(slopes, axis=0), km_ref[...])

    pair(step, True)
    lax.fori_loop(step + 1, count, lambda i, c: (pair(i, False), c)[1], 0)
    dk_ref[...] = (dka_ref[...] * score_scale).astype(bf16)
    dv_ref[...] = dva_ref[...].astype(bf16)

    @pl.when(step == count - 1)
    def _():
        dq_ref[...] = (dqa_ref[...] * score_scale).astype(bf16)

    comm.after(pl.program_id(0) * count + step, ins, outs, scratch)


def attend_backward(packed, grad_attended, lse, delta, lengths, comm=NoTransfers(), moved=()):
    tokens, width = grad_attended.shape
    groups = width // min(256, width)
    cols = width // groups
    heads = cols // HD
    blocks = tokens // BT
    column = pl.BlockSpec((tokens, cols), lambda g, j, n: (0, g))
    stats = pl.BlockSpec((8, tokens), lambda g, j, n: (g, 0))
    tile = pl.BlockSpec((BT, cols), lambda g, j, n: (j, g))
    move_ins, move_outs, move_shapes, move_scratch = comm.specs(moved) if moved else ([], [], [], [])
    return pl.pallas_call(
        functools.partial(attend_backward_kernel, heads, comm),
        grid_spec=pltpu.PrefetchScalarGridSpec(
            num_scalar_prefetch=1,
            grid=(groups, blocks),
            in_specs=[
                column,
                pl.BlockSpec((BT, cols), lambda g, j, n: (j, groups + g)),
                pl.BlockSpec((BT, cols), lambda g, j, n: (j, 2 * groups + g)),
                column,
                stats,
                stats,
            ]
            + move_ins,
            out_specs=[column, tile, tile] + move_outs,
            scratch_shapes=[
                pltpu.VMEM((blocks, heads * BT, cols), bf16),
                pltpu.VMEM((blocks, heads * BT, cols), bf16),
                pltpu.VMEM((heads * BT, cols), bf16),
                pltpu.VMEM((heads * BT, cols), bf16),
                pltpu.VMEM((tokens, cols), f32),
                pltpu.VMEM((BT, cols), f32),
                pltpu.VMEM((BT, cols), f32),
            ]
            + move_scratch,
        ),
        out_shape=[jax.ShapeDtypeStruct((tokens, width), bf16)] * 3 + move_shapes,
        compiler_params=params(2, 3 if moved else None),
        cost_estimate=attend_cost(tokens, width, 5),
        name="attend_backward",
    )(lengths, packed, packed, packed, grad_attended, lse, delta, *moved)


class AttendGather:
    ins = outs = 3

    def scratch(self):
        return gather_sems(6)

    def parts(self, outs):
        return [
            (ref, (at, width), route)
            for ref in (outs[0], outs[1], outs[2])
            for at, width, route in halves(ref.shape[3])
        ]

    def third(self, k, outs, sems):
        ref, span, route = self.parts(outs)[k]
        return gather_third(ref, span, route, sems, 6 * k)

    def second(self, k, outs, sems):
        ref, span, route = self.parts(outs)[k]
        return gather_second(ref, span, route, sems, 6 * k)

    def before(self, step, ins, outs, sems):
        @pl.when(step == 0)
        def _():
            greet(False)
            for k in (0, 1):
                start_all(self.third(k, outs, sems))
            for k in (2, 3, 4, 5):
                start_all(self.second(k, outs, sems))

        @pl.when(step == 6)
        def _():
            for k in (2, 3, 4, 5):
                wait_all(self.second(k, outs, sems))
            for k in (2, 3, 4, 5):
                start_all(self.third(k, outs, sems))

    def after(self, step, ins, outs, sems):
        @pl.when(step == 11)
        def _():
            for k in range(6):
                wait_all(self.third(k, outs, sems))


class SumPart:
    slots = 5

    def __init__(self, keep, sent, span, route, refs, sems, base):
        self.keep, self.sent, self.span, self.route = keep, sent, pl.ds(*span), route
        self.held, self.got_1, self.got_2, self.got_3 = refs
        self.sems, self.base = sems, base
        self.hops = ((2, 1), (1, 2))[route]

    @staticmethod
    def buffers(width):
        return [
            pltpu.VMEM((512, width), bf16),
            pltpu.VMEM((512, width), bf16),
            pltpu.VMEM((256, width), bf16),
            pltpu.VMEM((3, 64, width), bf16),
        ]

    def first(self):
        return [
            send(self.sent.at[:, self.span], self.got_1, self.sems, self.base, across(self.hops[0])),
            pltpu.make_async_copy(self.keep.at[:, self.span], self.held, self.sems[2].at[self.base]),
        ]

    def second(self):
        return [
            send(
                self.held.at[pl.ds(256, 256), :],
                self.got_2,
                self.sems,
                self.base + 1,
                across(self.hops[1]),
            )
        ]

    def third(self):
        return [
            send(
                self.held.at[pl.ds(64 * z, 64), :],
                self.got_3.at[z - 1],
                self.sems,
                self.base + 1 + z,
                across(4 * z),
            )
            for z in (1, 2, 3)
        ]

    def add(self, other, rows):
        def body(i, carry):
            at = pl.ds(pl.multiple_of(i * 64, 64), 64)
            self.held[at, :] = (self.held[at, :].astype(f32) + other[at, :].astype(f32)).astype(bf16)
            return carry

        lax.fori_loop(0, rows // 64, body, 0)

    def to_second(self):
        wait_all(self.first())
        self.add(self.got_1, 512)
        start_all(self.second())

    def to_third(self):
        wait_all(self.second())
        self.add(self.got_2, 256)
        start_all(self.third())

    def result(self):
        wait_all(self.third())
        total = self.held[0:64, :].astype(f32)
        for z in range(3):
            total = total + self.got_3[z].astype(f32)
        return total


def sum_sems(parts):
    return [
        pltpu.SemaphoreType.DMA((SumPart.slots * parts,)),
        pltpu.SemaphoreType.DMA((SumPart.slots * parts,)),
        pltpu.SemaphoreType.DMA((SumPart.slots * parts,)),
    ]


class SmallSum:
    def __init__(self, refs, sems):
        self.mine, self.got = refs
        self.sems = sems

    @staticmethod
    def scratch():
        return [
            pltpu.VMEM((6, 8, 1024), f32),
            pltpu.VMEM((5, 8, 1024), f32),
            pltpu.SemaphoreType.DMA((5,)),
            pltpu.SemaphoreType.DMA((5,)),
        ]

    def hop(self, k):
        device = sibling() if k == 0 else across((0, 1, 2, 4, 8)[k])
        return send(self.mine.at[k], self.got.at[k], self.sems, k, device)

    def begin(self, rows):
        self.mine[0] = rows
        self.hop(0).start()

    def advance(self, k, both):
        self.hop(k).wait()
        came = self.got[k]
        if k == 0:
            row = lax.broadcasted_iota(jnp.int32, came.shape, 0)
            came = jnp.where(row < both, came, 0.0)
        self.mine[k + 1] = self.mine[k] + came
        if k < 4:
            self.hop(k + 1).start()


class BackwardSum:
    def __init__(self, cols):
        self.cols = cols
        self.ins = 4 * len(cols) + 1
        self.outs = len(cols) + 1

    def specs(self, moved):
        vmem = [pl.BlockSpec((8, 1024), lambda g, j, n: (0, 0))]
        shapes = [jax.ShapeDtypeStruct((64, c), f32) for c in self.cols]
        outs = [pl.BlockSpec((64, c), lambda g, j, n: (0, 0)) for c in self.cols]
        scratch = []
        for c in self.cols:
            scratch += SumPart.buffers(c // 2) * 2
        scratch += sum_sems(2 * len(self.cols)) + SmallSum.scratch()
        return (
            [ANY] * (4 * len(self.cols)) + vmem,
            outs + vmem,
            shapes + [jax.ShapeDtypeStruct((8, 1024), f32)],
            scratch,
        )

    def parts(self, ins, scratch):
        count = 2 * len(self.cols)
        sems = scratch[4 * count : 4 * count + 3]
        made = []
        for k in range(count):
            width = self.cols[k // 2] // 2
            keep, sent = ins[2 * k], ins[2 * k + 1]
            refs = scratch[4 * k : 4 * k + 4]
            made.append(SumPart(keep, sent, (0, width), k % 2, refs, sems, SumPart.slots * k))
        rest = scratch[4 * count + 3 :]
        return made, SmallSum(rest[:2], rest[2:])

    def before(self, step, ins, outs, scratch):
        parts, small = self.parts(ins, scratch)

        @pl.when(step == 0)
        def _():
            greet(True)
            small.begin(ins[-1][...])
            for part in parts:
                start_all(part.first())

        for k in range(4):

            @pl.when(step == k + 1)
            def _():
                small.advance(k, 4)

        @pl.when(step == 2)
        def _():
            for part in parts[:2]:
                part.to_second()

        @pl.when(step == 5)
        def _():
            small.advance(4, 4)
            outs[-1][...] = small.mine[5]

        @pl.when(step == 6)
        def _():
            for part in parts[2:]:
                part.to_second()
            for part in parts[:2]:
                part.to_third()

        @pl.when(step == 8)
        def _():
            for part in parts[2:]:
                part.to_third()

    def after(self, step, ins, outs, scratch):
        parts, _ = self.parts(ins, scratch)

        @pl.when(step == 11)
        def _():
            for k, part in enumerate(parts):
                width = self.cols[k // 2] // 2
                outs[k // 2][:, (k % 2) * width : (k % 2 + 1) * width] = part.result()


def normalized(values):
    average = jnp.mean(values, axis=-1, keepdims=True)
    centred = values - average
    variance = jnp.mean(centred * centred, axis=-1, keepdims=True)
    inverse = lax.rsqrt(variance + norm_eps)
    return centred * inverse, inverse


def column_sum(values):
    return jnp.sum(values.reshape(-1, 8, values.shape[-1]), axis=0)


def turned(values, out_ref):
    flip = values.T
    bits = bits_of_me()
    for a in range(16):
        r = flipped(bits, a)
        slot = r[2] * 8 + r[3] * 4 + r[0] * 2 + r[1]
        out_ref[pl.ds(pl.multiple_of(slot * 64, 64), 64), :] = flip[a * 64 : (a + 1) * 64, :]


def shape(rows, cols, dtype=bf16):
    return jax.ShapeDtypeStruct((rows, cols), dtype)


def row_tile(cols):
    return pl.BlockSpec((BT, cols), lambda i: (i, 0))


def col_tile(rows):
    return pl.BlockSpec((rows, BT), lambda i: (0, i))


def whole(rows, cols):
    return pl.BlockSpec((rows, cols), lambda i: (0, 0))


def weight(cols):
    return pl.BlockSpec((1024, cols), lambda i: (0, 0), pipeline_mode=pl.Buffered(1))


def my_side():
    return lax.axis_index("mp")


def own_tile(cols, tiles):
    return pl.BlockSpec((BT, cols), lambda i: (jnp.clip(i - tiles * my_side(), 0, tiles - 1), 0))


def other_tile(cols, tiles):
    return pl.BlockSpec(
        (BT, cols), lambda i: (jnp.clip(i - tiles * (1 - my_side()), 0, tiles - 1), 0)
    )


def own_of_natural(cols, tiles):
    return pl.BlockSpec((BT, cols), lambda i: (my_side() * tiles + i, 0))


def other_of_natural(cols, tiles):
    return pl.BlockSpec((BT, cols), lambda i: ((1 - my_side()) * tiles + i, 0))


def grid_call(kernel, steps, ins, outs, scratch, flops, name, collective=None, aliases={}):
    arrays = [a for a, _ in ins]
    nbytes = sum(a.size * a.dtype.itemsize for a in arrays)
    nbytes += sum(o.size * o.dtype.itemsize for o, _ in outs)
    return pl.pallas_call(
        kernel,
        grid=(steps,),
        in_specs=[s for _, s in ins],
        out_specs=[s for _, s in outs],
        scratch_shapes=scratch,
        out_shape=[o for o, _ in outs],
        input_output_aliases=aliases,
        compiler_params=params(1, collective),
        cost_estimate=cost(flops, nbytes),
        name=name,
    )(*arrays)


def gather_kernel(qkv, up, qkv_out, up_out, *sems):
    pieces = [(qkv, qkv_out, (a, w), r) for a, w, r in halves(qkv.shape[1], 2)]
    pieces += [(up, up_out, (a, w), r) for a, w, r in halves(up.shape[1])]
    greet(False)

    def z(k):
        src, dst, span, _ = pieces[k]
        return gather_z(src, dst, span, sems, 6 * k)

    def second(k):
        _, dst, span, route = pieces[k]
        return gather_second(dst, span, route, sems, 6 * k)

    def third(k):
        _, dst, span, route = pieces[k]
        return gather_third(dst, span, route, sems, 6 * k)

    for k in range(6):
        start_all(z(k))
    for k in (0, 1, 2, 3):
        wait_all(z(k))
        start_all(second(k))
    for k in (0, 1, 2, 3):
        wait_all(second(k))
        start_all(third(k))
    for k in (4, 5):
        wait_all(z(k))
    for k in (0, 1, 2, 3):
        wait_all(third(k))


def gather_first(w_qkv, w_up):
    return pl.pallas_call(
        gather_kernel,
        in_specs=[ANY, ANY],
        out_specs=[ANY, ANY],
        out_shape=[
            jax.ShapeDtypeStruct((4, 4, 64, w_qkv.shape[1]), bf16),
            jax.ShapeDtypeStruct((4, 4, 64, w_up.shape[1]), bf16),
        ],
        scratch_shapes=gather_sems(6),
        compiler_params=pltpu.CompilerParams(
            vmem_limit_bytes=VMEM_CAP, collective_id=0, has_side_effects=True
        ),
        name="gather_first",
    )(w_qkv, w_up)


def qkv_kernel(tiles, own, other, gain, shift, bias, w, down, out_w, up_in, turned_out, out, up_out, down_out, wout_out, *sems):
    pieces = [(None, up_out, (a, c), r) for a, c, r in halves(up_out.shape[3])]
    pieces += [(down, down_out, (a, c), r) for a, c, r in halves(down.shape[1])]
    pieces += [(out_w, wout_out, (a, c), r) for a, c, r in halves(out_w.shape[1])]
    step = pl.program_id(0)

    def moves():
        copies = []
        for k, (src, dst, span, route) in enumerate(pieces):
            if src is None:
                copies += gather_second(dst, span, route, sems, 6 * k)
            else:
                copies += gather_z(src, dst, span, sems, 6 * k)
        return copies

    @pl.when(step == 0)
    def _():
        greet(False)
        start_all(moves())

    mine = (step // tiles) == my_side()
    values = jnp.where(mine, own[...], other[...]).astype(f32)
    scaled, _ = normalized(values)
    normed = (scaled * gain[...] + shift[...]).astype(bf16)
    turned(normed, turned_out)
    out[...] = (dot_nn(normed, w[...]) + bias[...]).astype(bf16)

    @pl.when(step == pl.num_programs(0) - 1)
    def _():
        wait_all(moves())


def project_kernel(a, w, out):
    out[...] = dot_nt(a[...], w[...]).astype(bf16)


def project_norm_kernel(a, w, toks, came, bias, gain, shift, hid_out, normed_out):
    partial = dot_nt(a[...], w[...])
    hidden = toks[...].astype(f32) + (partial + came[...].astype(f32) + bias[...])
    hid_out[...] = hidden
    scaled, _ = normalized(hidden)
    normed_out[...] = (scaled * gain[...] + shift[...]).astype(bf16)


def feed_kernel(x_ref, c_ref, bias, wu, wd, act, gpre, ffn, gnorm, x_turned, c_turned, bsum):
    @pl.when(pl.program_id(0) == 0)
    def _():
        bsum[...] = jnp.zeros(bsum.shape, f32)

    x, c = x_ref[...], c_ref[...]
    turned(x, x_turned)
    turned(c, c_turned)
    width = 512
    for part in range(wu.shape[1] // width):
        cols = slice(part * width, (part + 1) * width)
        value = dot_nn(x, wu[:, cols]) + bias[:, cols]
        upstream = dot_nn(c, wd[:, cols])
        square = value * value
        bent = jnp.tanh(value * (gelu_coeff + (gelu_coeff * 0.044715) * square))
        half_up = 0.5 + 0.5 * bent
        act[:, cols] = (value * half_up).astype(bf16)
        slope = half_up + value * (half_up * (1.0 - bent)) * (
            gelu_coeff + (3.0 * 0.044715 * gelu_coeff) * square
        )
        grad = (upstream * slope).astype(bf16)
        gpre[:, cols] = grad
        bsum[:, cols] += column_sum(grad.astype(f32))
    ffn[...] = dot_nt(act[...], wd[...]).astype(bf16)
    gnorm[...] = dot_nt(gpre[...], wu[...]).astype(bf16)


def middle_kernel(hid, f_own, f_came, g_own, g_came, cot, bias, gain, out, gattn, sums):
    @pl.when(pl.program_id(0) == 0)
    def _():
        sums[...] = jnp.zeros(sums.shape, f32)

    hidden = hid[...]
    grad_out = cot[...].astype(f32)
    out[...] = (hidden + (f_own[...].astype(f32) + f_came[...].astype(f32) + bias[...])).astype(bf16)
    scaled, inverse = normalized(hidden)
    grad_norm = g_own[...].astype(f32) + g_came[...].astype(f32)
    through = grad_norm * gain[...]
    centre = jnp.mean(through, axis=-1, keepdims=True)
    along = jnp.mean(through * scaled, axis=-1, keepdims=True)
    grad = (grad_out + inverse * (through - centre - scaled * along)).astype(bf16)
    gattn[...] = grad
    sums[0:8, :] += column_sum(grad_norm * scaled)
    sums[8:16, :] += column_sum(grad_norm)
    sums[16:24, :] += column_sum(grad.astype(f32))
    sums[24:32, :] += column_sum(grad_out)


def grad_attended_kernel(tiles, own, other, exact, w, do_out, delta_out, g_turned):
    mine = (pl.program_id(0) // tiles) == my_side()
    grad = jnp.where(mine, own[...], other[...])
    turned(grad, g_turned)
    part = dot_nn(grad, w[...]).astype(bf16)
    do_out[...] = part
    cols = part.shape[1]
    row = lax.broadcasted_iota(jnp.int32, (16, cols), 0)
    head = lax.broadcasted_iota(jnp.int32, (16, cols), 1) // HD
    pick = jnp.where(row == (head // 4) * 8 + head % 4, 1.0, 0.0).astype(f32)
    delta_out[...] = lax.dot_general(
        pick,
        part.astype(f32) * exact[...],
        (((1,), (1,)), ((), ())),
        precision=lax.Precision.HIGHEST,
        preferred_element_type=f32,
    )


class LastSum:
    def __init__(self, cols):
        self.spans = halves(cols, 2)

    def scratch(self):
        made = []
        for _, width, _ in self.spans:
            made += SumPart.buffers(width)
        return made + sum_sems(4) + SmallSum.scratch()

    def parts(self, ins, scratch):
        made = []
        half = 2 * self.spans[0][1]
        for k, (at, width, route) in enumerate(self.spans):
            keep, sent = ins[2 * route], ins[2 * route + 1]
            made.append(
                SumPart(
                    keep,
                    sent,
                    (at - route * half, width),
                    route,
                    scratch[4 * k : 4 * k + 4],
                    scratch[16:19],
                    SumPart.slots * k,
                )
            )
        return made, SmallSum(scratch[19:21], scratch[21:23])


def last_kernel(tiles, comm, dq, dk, dv, w, toks, gattn, gain, small, *refs):
    ins, refs = refs[:4], refs[4:]
    out, grad_w, small_out = refs[:3]
    sums, sent, came, send_sems, recv_sems = refs[3:8]
    parts, tiny = comm.parts(ins, refs[8:])
    step = pl.program_id(0)

    def swap(k):
        return send(sent.at[k], came.at[k], (send_sems, recv_sems), k, sibling())

    @pl.when(step == 0)
    def _():
        greet(True)
        sums[...] = jnp.zeros(sums.shape, f32)
        for part in parts:
            start_all(part.first())

    @pl.when(step == 2)
    def _():
        for part in parts[:2]:
            part.to_second()

    @pl.when(step == 4)
    def _():
        for part in parts[2:]:
            part.to_second()
        for part in parts[:2]:
            part.to_third()

    grads = jnp.concatenate([dq[...], dk[...], dv[...]], axis=1)
    rows = dot_nt(grads, w[...])

    for k in range(tiles):

        @pl.when(step == k)
        def _():
            sent[k] = rows.astype(bf16)
            swap(k).start()

        @pl.when(step == tiles + k)
        def _():
            swap(k).wait()
            grad_norm = rows + came[k].astype(f32)
            scaled, inverse = normalized(toks[...].astype(f32))
            through = grad_norm * gain[...]
            centre = jnp.mean(through, axis=-1, keepdims=True)
            along = jnp.mean(through * scaled, axis=-1, keepdims=True)
            grad_in = inverse * (through - centre - scaled * along)
            out[...] = (gattn[...].astype(f32) + grad_in).astype(bf16)
            sums[0:8, :] += column_sum(grad_norm * scaled)
            sums[8:16, :] += column_sum(grad_norm)

    @pl.when(step == pl.num_programs(0) - 1)
    def _():
        row = lax.broadcasted_iota(jnp.int32, (8, 1024), 0)
        first = jnp.sum(sums[0:8, :], axis=0, keepdims=True)
        second = jnp.sum(sums[8:16, :], axis=0, keepdims=True)
        tiny.begin(jnp.where(row == 0, first, jnp.where(row == 1, second, small[...])))
        for part in parts[2:]:
            part.to_third()
        for k in range(5):
            tiny.advance(k, 2)
        small_out[...] = tiny.mine[5]
        for part, (at, width, _) in zip(parts, comm.spans):
            grad_w[:, at : at + width] = part.result()


def weight_grad_kernel(lefts, rights, *refs):
    left, right = refs[:lefts], refs[lefts : lefts * (1 + rights)]
    outs, sums, total = refs[lefts * (1 + rights) : -2], refs[-2], refs[-1]
    step = pl.program_id(0)
    tiles = pl.num_programs(0) // lefts

    def add(k, fresh):
        at = 0
        for r in right[k * rights : (k + 1) * rights]:
            cols = slice(at, at + r.shape[1])
            term = dot_nn(left[k][...], r[...])
            total[:, cols] = term if fresh else total[:, cols] + term
            if rights > 1:
                count = column_sum(r[...].astype(f32))
                sums[:, cols] = count if fresh else sums[:, cols] + count
            at += r.shape[1]

    @pl.when(step == 0)
    def _():
        add(0, True)
        if rights == 1:
            sums[...] = jnp.zeros(sums.shape, f32)

    for k in range(lefts):

        @pl.when((step > 0) & (step // tiles == k))
        def _():
            add(k, False)

    @pl.when(step == pl.num_programs(0) - 1)
    def _():
        keep_a, send_a, keep_b, send_b = outs
        half = total.shape[1] // 2
        keep_a[...] = total[0:512, :half].astype(bf16)
        send_a[...] = total[512:1024, :half].astype(bf16)
        keep_b[0:256, :] = total[0:256, half:].astype(bf16)
        keep_b[256:512, :] = total[512:768, half:].astype(bf16)
        send_b[0:256, :] = total[256:512, half:].astype(bf16)
        send_b[256:512, :] = total[768:1024, half:].astype(bf16)


def weight_grad(lefts, rights, name):
    tiles = lefts[0].shape[1] // BT
    cols = sum(r.shape[1] for r in rights[0])

    def at(i, k):
        return jnp.clip(i - k * tiles, 0, tiles - 1)

    ins = []
    for k, left in enumerate(lefts):
        ins.append((left, pl.BlockSpec((1024, BT), lambda i, k=k: (0, at(i, k)))))
    for k, group in enumerate(rights):
        for r in group:
            ins.append((r, pl.BlockSpec((BT, r.shape[1]), lambda i, k=k: (at(i, k), 0))))
    outs = [(shape(512, cols // 2), whole(512, cols // 2))] * 4
    outs.append((shape(8, cols, f32), whole(8, cols)))
    return grid_call(
        functools.partial(weight_grad_kernel, len(lefts), len(rights[0])),
        tiles * len(lefts),
        ins,
        outs,
        [pltpu.VMEM((1024, cols), f32)],
        2 * 1024 * cols * BT * tiles * len(lefts),
        name,
    )


def swap_mp(block):
    return lax.ppermute(block, "mp", [(0, 1), (1, 0)])


def wide(vector):
    return vector.astype(f32).reshape(1, -1)


def layer_on_pairs(
    tokens,
    slot_lengths,
    gain_one,
    shift_one,
    w_qkv,
    bias_qv,
    w_out,
    bias_out,
    gain_two,
    shift_two,
    w_up,
    bias_up,
    w_down,
    bias_down,
    cotangent,
):
    own_rows, width = tokens.shape
    total_rows = 2 * own_rows
    tiles = own_rows // BT
    local = w_qkv.shape[2]
    hidden_cols = w_up.shape[1]
    side_cols = 3 * local
    lengths = slot_lengths[0]
    sums_in = whole(8, width)

    tokens_other = swap_mp(tokens)
    qkv_blocks, up_blocks = gather_first(w_qkv.reshape(64, side_cols), w_up)
    qkv_w = qkv_blocks.reshape(width, side_cols)
    bias = jnp.concatenate([bias_qv[0], jnp.zeros_like(bias_qv[0]), bias_qv[1]])
    rows_turned, packed, up_blocks, down_blocks, out_blocks = grid_call(
        functools.partial(qkv_kernel, tiles),
        2 * tiles,
        [
            (tokens, own_tile(width, tiles)),
            (tokens_other, other_tile(width, tiles)),
            (wide(gain_one), whole(1, width)),
            (wide(shift_one), whole(1, width)),
            (wide(bias), whole(1, side_cols)),
            (qkv_w, weight(side_cols)),
            (w_down.T, ANY),
            (w_out.T, ANY),
            (up_blocks, ANY),
        ],
        [
            (shape(width, total_rows), col_tile(width)),
            (shape(total_rows, side_cols), row_tile(side_cols)),
            (jax.ShapeDtypeStruct((4, 4, 64, hidden_cols), bf16), ANY),
            (jax.ShapeDtypeStruct((4, 4, 64, hidden_cols), bf16), ANY),
            (jax.ShapeDtypeStruct((4, 4, 64, local), bf16), ANY),
        ],
        gather_sems(6),
        2 * total_rows * width * side_cols,
        "qkv",
        1,
        {8: 2},
    )
    attended, exact, lse, up_blocks, down_blocks, out_blocks = attend_forward(
        packed, lengths, AttendGather(), (up_blocks, down_blocks, out_blocks)
    )
    up_w = up_blocks.reshape(width, hidden_cols)
    down_w = down_blocks.reshape(width, hidden_cols)
    out_w = out_blocks.reshape(width, local)
    cotangent_other = swap_mp(cotangent)

    (partial_other,) = grid_call(
        project_kernel,
        tiles,
        [(attended, other_of_natural(local, tiles)), (out_w, weight(local))],
        [(shape(own_rows, width), row_tile(width))],
        [],
        2 * own_rows * width * local,
        "project_other",
    )
    partial_came = swap_mp(partial_other)
    hidden, normed_own = grid_call(
        project_norm_kernel,
        tiles,
        [
            (attended, own_of_natural(local, tiles)),
            (out_w, weight(local)),
            (tokens, row_tile(width)),
            (partial_came, row_tile(width)),
            (wide(bias_out), whole(1, width)),
            (wide(gain_two), whole(1, width)),
            (wide(shift_two), whole(1, width)),
        ],
        [(shape(own_rows, width, f32), row_tile(width)), (shape(own_rows, width), row_tile(width))],
        [],
        2 * own_rows * width * local,
        "project_norm",
    )
    normed_other = swap_mp(normed_own)

    def feed(rows, cots):
        return grid_call(
            feed_kernel,
            tiles,
            [
                (rows, row_tile(width)),
                (cots, row_tile(width)),
                (wide(bias_up), whole(1, hidden_cols)),
                (up_w, weight(hidden_cols)),
                (down_w, weight(hidden_cols)),
            ],
            [
                (shape(own_rows, hidden_cols), row_tile(hidden_cols)),
                (shape(own_rows, hidden_cols), row_tile(hidden_cols)),
                (shape(own_rows, width), row_tile(width)),
                (shape(own_rows, width), row_tile(width)),
                (shape(width, own_rows), col_tile(width)),
                (shape(width, own_rows), col_tile(width)),
                (shape(8, hidden_cols, f32), whole(8, hidden_cols)),
            ],
            [],
            8 * own_rows * width * hidden_cols,
            "feed",
        )

    act_own, pre_own, ffn_own, norm_own, x_own, c_own, bsum_own = feed(normed_own, cotangent)
    act_oth, pre_oth, ffn_oth, norm_oth, x_oth, c_oth, bsum_oth = feed(normed_other, cotangent_other)
    norm_came = swap_mp(norm_oth)
    ffn_came = swap_mp(ffn_oth)
    down_parts = weight_grad([c_own, c_oth], [[act_own], [act_oth]], "down_grad")
    output, grad_attn, middle_sums = grid_call(
        middle_kernel,
        tiles,
        [
            (hidden, row_tile(width)),
            (ffn_own, row_tile(width)),
            (ffn_came, row_tile(width)),
            (norm_own, row_tile(width)),
            (norm_came, row_tile(width)),
            (cotangent, row_tile(width)),
            (wide(bias_down), whole(1, width)),
            (wide(gain_two), whole(1, width)),
        ],
        [
            (shape(own_rows, width), row_tile(width)),
            (shape(own_rows, width), row_tile(width)),
            (shape(32, width, f32), whole(32, width)),
        ],
        [],
        40 * own_rows * width,
        "middle",
    )
    grad_attn_other = swap_mp(grad_attn)
    up_parts = weight_grad([x_own, x_oth], [[pre_own], [pre_oth]], "up_grad")
    grad_attended, delta, g_turned = grid_call(
        functools.partial(grad_attended_kernel, tiles),
        2 * tiles,
        [
            (grad_attn, own_tile(width, tiles)),
            (grad_attn_other, other_tile(width, tiles)),
            (exact, row_tile(local)),
            (out_w, weight(local)),
        ],
        [
            (shape(total_rows, local), row_tile(local)),
            (shape(16, total_rows, f32), col_tile(16)),
            (shape(width, total_rows), col_tile(width)),
        ],
        [],
        2 * total_rows * width * local,
        "grad_attended",
    )
    half = local // 2
    out_parts = weight_grad([g_turned], [[attended]], "out_grad")
    early = middle_sums.reshape(4, 8, width).sum(axis=1)
    up_bias = (bsum_own + bsum_oth).sum(axis=0).reshape(-1, width)
    early = jnp.concatenate([early, up_bias, jnp.zeros((2, width), f32)])
    moved = tuple(down_parts[:4]) + tuple(up_parts[:4]) + tuple(out_parts[:4]) + (early,)
    grad_q, grad_k, grad_v, grad_down, grad_up, grad_w_out, early = attend_backward(
        packed,
        grad_attended,
        lse,
        delta,
        lengths,
        BackwardSum((hidden_cols, hidden_cols, local)),
        moved,
    )
    qkv_parts = weight_grad([rows_turned], [[grad_q, grad_k, grad_v]], "qkv_grad")
    qv = jnp.concatenate([qkv_parts[4][:, :local].sum(axis=0), qkv_parts[4][:, 2 * local :].sum(axis=0)])
    small = jnp.concatenate(
        [jnp.zeros((2, width), f32), qv.reshape(1, -1), jnp.zeros((5, width), f32)]
    )
    last = LastSum(side_cols)

    def two_way(cols):
        return pl.BlockSpec(
            (BT, cols), lambda i: (lax.rem(i + (1 - my_side()) * tiles, 2 * tiles), 0)
        )

    late_tile = pl.BlockSpec((BT, width), lambda i: (jnp.maximum(i - tiles, 0), 0))
    grad_tokens, grad_w_qkv, late = grid_call(
        functools.partial(last_kernel, tiles, last),
        2 * tiles,
        [(g, two_way(local)) for g in (grad_q, grad_k, grad_v)]
        + [
            (qkv_w, weight(side_cols)),
            (tokens, late_tile),
            (grad_attn, late_tile),
            (wide(gain_one), whole(1, width)),
            (small, sums_in),
        ]
        + [(p, ANY) for p in qkv_parts[:4]],
        [
            (shape(own_rows, width), late_tile),
            (shape(64, side_cols, f32), whole(64, side_cols)),
            (shape(8, width, f32), sums_in),
        ],
        [
            pltpu.VMEM((16, width), f32),
            pltpu.VMEM((tiles, BT, width), bf16),
            pltpu.VMEM((tiles, BT, width), bf16),
            pltpu.SemaphoreType.DMA((tiles,)),
            pltpu.SemaphoreType.DMA((tiles,)),
        ]
        + last.scratch(),
        2 * total_rows * width * side_cols,
        "last",
        4,
    )
    return (
        output,
        grad_tokens,
        late[0],
        late[1],
        grad_w_qkv.reshape(64, 3, local),
        late[2].reshape(2, local),
        grad_w_out.T,
        early[2],
        early[0],
        early[1],
        grad_up,
        early[4:6].reshape(-1),
        grad_down.T,
        early[3],
    )


def gelu_tanh(values):
    inner = gelu_coeff * (values + 0.044715 * values * values * values)
    return 0.5 * values * (1.0 + jnp.tanh(inner))


def gelu_slope(values):
    inner = gelu_coeff * (values + 0.044715 * values * values * values)
    bent = jnp.tanh(inner)
    return 0.5 * (1.0 + bent) + 0.5 * values * (1.0 - bent * bent) * gelu_coeff * (
        1.0 + 3.0 * 0.044715 * values * values
    )


def norm_forward(values, gain_vec, shift_vec):
    average = jnp.mean(values, axis=-1, keepdims=True)
    centred = values - average
    variance = jnp.mean(centred * centred, axis=-1, keepdims=True)
    inverse = lax.rsqrt(variance + norm_eps)
    scaled = centred * inverse
    return (scaled * gain_vec.astype(f32) + shift_vec.astype(f32), scaled, inverse)


def norm_backward(grad_out, scaled, inverse, gain_vec):
    grad_scaled = grad_out * gain_vec.astype(f32)
    centre_term = jnp.mean(grad_scaled, axis=-1, keepdims=True)
    slope_term = jnp.mean(grad_scaled * scaled, axis=-1, keepdims=True)
    grad_in = inverse * (grad_scaled - centre_term - scaled * slope_term)
    return (grad_in, jnp.sum(grad_out * scaled, axis=0), jnp.sum(grad_out, axis=0))


def layer_by_collectives(
    tokens,
    slot_lengths,
    gain_one,
    shift_one,
    w_qkv,
    bias_qv,
    w_out,
    bias_out,
    gain_two,
    shift_two,
    w_up,
    bias_up,
    w_down,
    bias_down,
    cotangent,
):
    w_qkv, w_out, w_up, w_down = (
        lax.all_gather(w_qkv, "dp", axis=0, tiled=True),
        lax.all_gather(w_out, "dp", axis=1, tiled=True),
        lax.all_gather(w_up, "dp", axis=0, tiled=True),
        lax.all_gather(w_down, "dp", axis=1, tiled=True),
    )
    lengths = slot_lengths[0]
    residual = tokens.astype(f32)
    normed_one, scaled_one, inverse_one = norm_forward(residual, gain_one, shift_one)
    rows_one = lax.all_gather(normed_one.astype(bf16), "mp", axis=0, tiled=True)
    packed = jnp.einsum("td,dcf->tcf", rows_one, w_qkv, preferred_element_type=f32)
    zero_bias = jnp.zeros_like(bias_qv[0])
    packed_bias = jnp.stack([bias_qv[0], zero_bias, bias_qv[1]]).astype(f32)
    packed = (packed + packed_bias[None]).astype(bf16)
    local = packed.shape[2]
    packed_rows = packed.reshape(packed.shape[0], -1)
    attended, exact_out, log_totals = attend_forward(packed_rows, lengths)
    hidden = (
        residual
        + lax.psum_scatter(
            jnp.dot(attended, w_out, preferred_element_type=f32),
            "mp",
            scatter_dimension=0,
            tiled=True,
        )
        + bias_out.astype(f32)
    )
    normed_two, scaled_two, inverse_two = norm_forward(hidden, gain_two, shift_two)
    normed_low = normed_two.astype(bf16)
    rows_two = lax.all_gather(normed_low, "mp", axis=0, tiled=True)
    preact = jnp.dot(rows_two, w_up, preferred_element_type=f32) + bias_up.astype(
        f32
    )
    active = gelu_tanh(preact).astype(bf16)
    ffn_out = lax.psum_scatter(
        jnp.dot(active, w_down, preferred_element_type=f32).astype(bf16),
        "mp",
        scatter_dimension=0,
        tiled=True,
    ).astype(f32)
    output = (hidden + ffn_out + bias_down.astype(f32)).astype(bf16)
    grad_out = cotangent.astype(f32)
    grad_rows = lax.all_gather(cotangent, "mp", axis=0, tiled=True)
    grad_active = jnp.einsum("td,fd->tf", grad_rows, w_down, preferred_element_type=f32)
    grad_pre = (grad_active * gelu_slope(preact)).astype(bf16)
    grad_up = jnp.einsum("td,tf->df", rows_two, grad_pre, preferred_element_type=f32)
    grad_down = jnp.einsum("tf,td->fd", active, grad_rows, preferred_element_type=f32)
    grad_bias_up = jnp.sum(grad_pre.astype(f32), axis=0)
    grad_norm_two = lax.psum_scatter(
        jnp.einsum("tf,df->td", grad_pre, w_up, preferred_element_type=f32),
        "mp",
        scatter_dimension=0,
        tiled=True,
    )
    grad_in_two, grad_gain_two, grad_shift_two = norm_backward(
        grad_norm_two, scaled_two, inverse_two, gain_two
    )
    grad_hidden = grad_out + grad_in_two
    grad_attn = grad_hidden.astype(bf16)
    grad_attn_rows = lax.all_gather(grad_attn, "mp", axis=0, tiled=True)
    grad_w_out = jnp.einsum(
        "tf,td->fd", attended, grad_attn_rows, preferred_element_type=f32
    )
    grad_attended = jnp.einsum(
        "td,fd->tf", grad_attn_rows, w_out, preferred_element_type=f32
    ).astype(bf16)
    product = (grad_attended.astype(f32) * exact_out).reshape(grad_attended.shape[0], -1, HD)
    delta = jnp.sum(product, axis=-1).T
    groups = log_totals.shape[0] // 8
    delta = delta.reshape(groups, -1, delta.shape[1])
    delta = jnp.pad(delta, ((0, 0), (0, 8 - delta.shape[1]), (0, 0))).reshape(8 * groups, -1)
    grads = attend_backward(packed_rows, grad_attended, log_totals, delta, lengths)
    grad_packed = jnp.stack(grads, axis=1)
    grad_w_qkv = jnp.einsum(
        "td,tcf->dcf", rows_one, grad_packed, preferred_element_type=f32
    )
    grad_bias_qv = jnp.stack(
        [
            jnp.sum(grad_packed[:, 0].astype(f32), axis=0),
            jnp.sum(grad_packed[:, 2].astype(f32), axis=0),
        ]
    )
    grad_norm_one = lax.psum_scatter(
        jnp.einsum("tcf,dcf->td", grad_packed, w_qkv, preferred_element_type=f32),
        "mp",
        scatter_dimension=0,
        tiled=True,
    )
    grad_in_one, grad_gain_one, grad_shift_one = norm_backward(
        grad_norm_one, scaled_one, inverse_one, gain_one
    )
    grad_tokens = (grad_hidden + grad_in_one).astype(bf16)
    grad_bias_out = jnp.sum(grad_attn.astype(f32), axis=0)
    grad_bias_down = jnp.sum(grad_out, axis=0)
    grad_w_qkv, grad_w_out, grad_up, grad_down = (
        lax.psum_scatter(grad_w_qkv, "dp", scatter_dimension=0, tiled=True),
        lax.psum_scatter(grad_w_out, "dp", scatter_dimension=1, tiled=True),
        lax.psum_scatter(grad_up, "dp", scatter_dimension=0, tiled=True),
        lax.psum_scatter(grad_down, "dp", scatter_dimension=1, tiled=True),
    )
    small_grads = lax.psum(
        (
            grad_gain_one,
            grad_shift_one,
            grad_bias_out,
            grad_gain_two,
            grad_shift_two,
            grad_bias_down,
        ),
        ("dp", "mp"),
    )
    grad_bias_qv, grad_bias_up = lax.psum((grad_bias_qv, grad_bias_up), "dp")
    return (
        output,
        grad_tokens,
        small_grads[0],
        small_grads[1],
        grad_w_qkv,
        grad_bias_qv,
        grad_w_out,
        small_grads[2],
        small_grads[3],
        small_grads[4],
        grad_up,
        grad_bias_up,
        grad_down,
        small_grads[5],
    )


def solution(mesh):
    pairs = dict(mesh.shape) == {"dp": 16, "mp": 2}
    layer = layer_on_pairs if pairs else layer_by_collectives
    return jax.shard_map(
        layer,
        mesh=mesh,
        in_specs=(
            P(("dp", "mp"), None),
            P("dp", None),
            P(),
            P(),
            P("dp", None, "mp"),
            P(None, "mp"),
            P("mp", "dp"),
            P(),
            P(),
            P(),
            P("dp", "mp"),
            P("mp"),
            P("mp", "dp"),
            P(),
            P(("dp", "mp"), None),
        ),
        out_specs=(
            P(("dp", "mp"), None),
            P(("dp", "mp"), None),
            P(),
            P(),
            P("dp", None, "mp"),
            P(None, "mp"),
            P("mp", "dp"),
            P(),
            P(),
            P(),
            P("dp", "mp"),
            P("mp"),
            P("mp", "dp"),
            P(),
        ),
        check_vma=False,
    )
```

```python
import functools
import math

import jax
import jax.numpy as jnp
from jax import lax
from jax.experimental import pallas as pl
from jax.experimental.pallas import tpu as pltpu
from jax.sharding import PartitionSpec as P

HD = 64
LONG_LEN = 3072
BT = 512
VMEM_CAP = 60 * 1024 * 1024

f32 = jnp.float32
bf16 = jnp.bfloat16
norm_eps = 1e-05
masked_score = -1e30
gelu_coeff = 0.7978845608028654
score_scale = HD ** (-0.5)
score_scale_2 = HD ** (-0.5) * math.log2(math.e)
safe_sum = 1e30


def dot_nt(left, right):
    return lax.dot_general(left, right, (((1,), (1,)), ((), ())), preferred_element_type=f32)


def dot_nn(left, right):
    return lax.dot_general(left, right, (((1,), (0,)), ((), ())), preferred_element_type=f32)


def dot_tn(left, right):
    return lax.dot_general(left, right, (((0,), (0,)), ((), ())), preferred_element_type=f32)


def params(axes=1, collective=None):
    if collective is None:
        return pltpu.CompilerParams(
            vmem_limit_bytes=VMEM_CAP, dimension_semantics=("arbitrary",) * axes
        )
    return pltpu.CompilerParams(
        vmem_limit_bytes=VMEM_CAP,
        dimension_semantics=("arbitrary",) * axes,
        collective_id=collective,
        has_side_effects=True,
    )


def cost(flops, nbytes, exps=0):
    return pl.CostEstimate(flops=int(flops), bytes_accessed=int(nbytes), transcendentals=int(exps))


ANY = pl.BlockSpec(memory_space=pl.ANY)


def bits_of_me():
    me = lax.axis_index("dp")
    return (me // 8, (me // 4) % 2, (me // 2) % 2, me % 2)


def flipped(bits, which):
    return tuple(1 - b if which & (8 >> k) else b for k, b in enumerate(bits))


def index_of(bits):
    return bits[0] * 8 + bits[1] * 4 + bits[2] * 2 + bits[3]


def across(which):
    return {"dp": index_of(flipped(bits_of_me(), which))}


def sibling():
    return {"mp": 1 - lax.axis_index("mp")}


MESH_ID = pl.DeviceIdType.MESH
HOPS = (1, 2, 4, 8, 12)


def greet(with_sibling):
    barrier = pltpu.get_barrier_semaphore()
    for hop in HOPS:
        pl.semaphore_signal(barrier, inc=1, device_id=across(hop), device_id_type=MESH_ID)
    if with_sibling:
        pl.semaphore_signal(barrier, inc=1, device_id=sibling(), device_id_type=MESH_ID)
    pl.semaphore_wait(barrier, len(HOPS) + (1 if with_sibling else 0))


def greet_sibling():
    barrier = pltpu.get_barrier_semaphore()
    pl.semaphore_signal(barrier, inc=1, device_id=sibling(), device_id_type=MESH_ID)
    pl.semaphore_wait(barrier, 1)


def send(src, dst, sems, slot, device):
    return pltpu.make_async_remote_copy(
        src_ref=src,
        dst_ref=dst,
        send_sem=sems[0].at[slot],
        recv_sem=sems[1].at[slot],
        device_id=device,
        device_id_type=MESH_ID,
    )


def start_all(copies):
    for copy in copies:
        copy.start()


def wait_all(copies):
    for copy in copies:
        copy.wait()


def gather_z(src, dst, span, sems, base):
    bits = bits_of_me()
    z, yx = bits[0] * 2 + bits[1], bits[2] * 2 + bits[3]
    cols = pl.ds(*span)
    place = dst.at[z, yx, :, cols]
    copies = [
        send(src.at[:, cols], place, sems, base + k, across(4 * (k + 1))) for k in range(3)
    ]
    copies.append(pltpu.make_async_copy(src.at[:, cols], place, sems[2].at[base]))
    return copies


def gather_second(dst, span, route, sems, base):
    bits = bits_of_me()
    part = dst.at[:, bits[2] * 2 + bits[3], :, pl.ds(*span)]
    return [send(part, part, sems, base + 3, across((1, 2)[route]))]


def gather_third(dst, span, route, sems, base):
    copies = []
    for k, which in enumerate((0, (1, 2)[route])):
        bits = flipped(bits_of_me(), which)
        part = dst.at[:, bits[2] * 2 + bits[3], :, pl.ds(*span)]
        copies.append(send(part, part, sems, base + 4 + k, across((2, 1)[route])))
    return copies


def gather_sems(pieces):
    return [
        pltpu.SemaphoreType.DMA((6 * pieces,)),
        pltpu.SemaphoreType.DMA((6 * pieces,)),
        pltpu.SemaphoreType.DMA((6 * pieces,)),
    ]


def halves(cols, parts=1):
    half = cols // 2
    width = half // parts
    return [(r * half + c * width, width, r) for c in range(parts) for r in range(2)]


def head_lanes(block, head):
    lane_head = lax.broadcasted_iota(jnp.int32, block.shape, 1) // HD
    return jnp.where(lane_head == head, block, jnp.zeros_like(block))


def pack_heads(columns):
    lane = lax.broadcasted_iota(jnp.int32, columns[0].shape, 1)
    pairs = [
        jnp.where(lane < HD, columns[2 * i], columns[2 * i + 1]) for i in range(len(columns) // 2)
    ]
    return pairs[0] if len(pairs) == 1 else jnp.concatenate(pairs, axis=1)


def block_probs(scores, top):
    total, parts = None, []
    for t in range(scores.shape[1] // 128):
        part = jnp.exp2(scores[:, t * 128 : (t + 1) * 128] * score_scale_2 - top)
        total = part if total is None else total + part
        parts.append(part.astype(bf16))
    return parts, total


def attend_block(masked, keys, values, m_ref, l_ref, acc_ref):
    block = keys.shape[0]
    low = []
    for h, query in enumerate(masked):
        scores = dot_nt(query, keys)
        row = lax.broadcasted_iota(jnp.int32, scores.shape, 0)
        col = lax.broadcasted_iota(jnp.int32, scores.shape, 1)
        scores = jnp.where(row >= col, scores, masked_score)
        top = jnp.max(scores, axis=1, keepdims=True) * score_scale_2
        top = jnp.broadcast_to(top, (block, 128))
        m_ref[h] = top
        parts, l_ref[h] = block_probs(scores, top)
        low += parts
    acc_ref[...] = dot_nn(jnp.concatenate(low, axis=1), values)


def attend_finish(heads, m_ref, l_ref, acc_ref, out_ref, exact_ref, lse_ref):
    block = out_ref.shape[0]
    lane = lax.broadcasted_iota(jnp.int32, (block, 128), 1)
    rows = jnp.zeros((block, 128), f32)
    inverse = []
    for h in range(heads):
        total = jnp.sum(l_ref[h], axis=1, keepdims=True)
        rows = jnp.where(lane == h, m_ref[h][:, :1] + jnp.log2(total), rows)
        inverse.append(jnp.broadcast_to(1.0 / total, (block, 128)))
    result = acc_ref[...] * pack_heads(inverse)
    out_ref[...] = result.astype(bf16)
    exact_ref[...] = result
    lse_ref[...] = rows.T[:8, :]


def mask_values(v_ref, vm_ref, heads, block):
    for j in range(v_ref.shape[0] // block):
        value = v_ref[j * block : (j + 1) * block, :]
        for h in range(heads):
            vm_ref[j, h * block : (h + 1) * block, :] = head_lanes(value, h)


def attend_forward_kernel(heads, comm, lens_ref, q_ref, k_ref, v_ref, *refs):
    ins, refs = refs[: comm.ins], refs[comm.ins :]
    out_ref, exact_ref, lse_ref, big_ref = refs[:4]
    outs = refs[4 : 4 + comm.outs]
    vm_ref, m_ref, l_ref, acc_ref = refs[4 + comm.outs : 8 + comm.outs]
    sems = refs[8 + comm.outs :]
    step = pl.program_id(1)
    block = q_ref.shape[0]
    comm.before(pl.program_id(0) * pl.num_programs(1) + step, ins, outs, sems)

    @pl.when(step == 0)
    def _():
        mask_values(v_ref, vm_ref, heads, block)

    @pl.when((step == 0) & (pl.program_id(0) == 0))
    def _():
        big_ref[...] = jnp.zeros(big_ref.shape, f32)

    query = q_ref[...]
    masked = [head_lanes(query, h) for h in range(heads)]

    def key_block(j):
        return k_ref[pl.ds(pl.multiple_of(j * block, block), block), :]

    attend_block(masked, key_block(step), vm_ref[step], m_ref, l_ref, acc_ref)
    away = jnp.where(lens_ref[0] == LONG_LEN, 0.0, 1e30).astype(f32)

    def earlier(j, carry):
        keys = key_block(j)
        low = []
        for h in range(heads):
            parts, total = block_probs(dot_nt(masked[h], keys), m_ref[h] + away)
            l_ref[h] += total
            low += parts
        acc_ref[...] += dot_nn(jnp.concatenate(low, axis=1), vm_ref[j])
        return carry

    lax.fori_loop(0, step, earlier, 0)
    for h in range(heads):
        big_ref[...] = jnp.maximum(
            big_ref[...], jnp.max(l_ref[h].reshape(-1, 8, 128), axis=0)
        )
    attend_finish(heads, m_ref, l_ref, acc_ref, out_ref, exact_ref, lse_ref)
    comm.after(pl.program_id(0) * pl.num_programs(1) + step, ins, outs, sems)


def attend_safe_kernel(
    heads,
    groups,
    lens_ref,
    big_ref,
    packed,
    low_in,
    exact_in,
    lse_in,
    low,
    exact,
    lse,
    q_ref,
    k_ref,
    v_ref,
    out_ref,
    exact_ref,
    lse_ref,
    vm_ref,
    m_ref,
    l_ref,
    acc_ref,
    sem,
):
    block, cols = q_ref.shape
    tokens = k_ref.shape[0]

    def fetch(src, dst):
        copy = pltpu.make_async_copy(src, dst, sem)
        copy.start()
        copy.wait()

    def one_query(group, step):
        rows = pl.ds(pl.multiple_of(step * block, block), block)
        here = pl.ds(group * cols, cols)
        fetch(packed.at[rows, here], q_ref)
        query = q_ref[...]
        masked = [head_lanes(query, h) for h in range(heads)]

        def key_block(j):
            return k_ref[pl.ds(pl.multiple_of(j * block, block), block), :]

        attend_block(masked, key_block(step), vm_ref[step], m_ref, l_ref, acc_ref)

        def earlier(j, carry):
            keys = key_block(j)
            parts_all, shrink = [], []
            for h in range(heads):
                scores = dot_nt(masked[h], keys)
                old = m_ref[h]
                top = jnp.maximum(old, jnp.max(scores, axis=1, keepdims=True) * score_scale_2)
                factor = jnp.exp2(old - top)
                m_ref[h] = top
                parts, total = block_probs(scores, top)
                l_ref[h] = l_ref[h] * factor + total
                parts_all += parts
                shrink.append(factor)
            acc_ref[...] = acc_ref[...] * pack_heads(shrink) + dot_nn(
                jnp.concatenate(parts_all, axis=1), vm_ref[j]
            )
            return carry

        lax.fori_loop(0, jnp.where(lens_ref[0] == LONG_LEN, step, 0), earlier, 0)
        attend_finish(heads, m_ref, l_ref, acc_ref, out_ref, exact_ref, lse_ref)
        fetch(out_ref, low.at[rows, here])
        fetch(exact_ref, exact.at[rows, here])
        fetch(lse_ref, lse.at[pl.ds(group * 8, 8), rows])

    @pl.when(jnp.logical_not(jnp.max(big_ref[...]) < safe_sum))
    def _():
        for group in range(groups):
            fetch(packed.at[:, pl.ds((groups + group) * cols, cols)], k_ref)
            fetch(packed.at[:, pl.ds((2 * groups + group) * cols, cols)], v_ref)
            mask_values(v_ref, vm_ref, heads, block)
            lax.fori_loop(
                0, tokens // block, lambda i, c, group=group: (one_query(group, i), c)[1], 0
            )


class NoTransfers:
    ins = outs = 0

    def before(self, *args):
        pass

    def after(self, *args):
        pass


def attend_specs(tokens, width):
    groups = width // min(256, width)
    cols = width // groups
    ins = [
        pl.BlockSpec((BT, cols), lambda g, i, n: (i, g)),
        pl.BlockSpec((tokens, cols), lambda g, i, n: (0, groups + g)),
        pl.BlockSpec((tokens, cols), lambda g, i, n: (0, 2 * groups + g)),
    ]
    outs = [
        pl.BlockSpec((BT, cols), lambda g, i, n: (i, g)),
        pl.BlockSpec((BT, cols), lambda g, i, n: (i, g)),
        pl.BlockSpec((8, BT), lambda g, i, n: (g, i)),
    ]
    shapes = [
        jax.ShapeDtypeStruct((tokens, width), bf16),
        jax.ShapeDtypeStruct((tokens, width), f32),
        jax.ShapeDtypeStruct((8 * groups, tokens), f32),
    ]
    heads = cols // HD
    scratch = [
        pltpu.VMEM((tokens // BT, heads * BT, cols), bf16),
        pltpu.VMEM((heads, BT, 128), f32),
        pltpu.VMEM((heads, BT, 128), f32),
        pltpu.VMEM((BT, cols), f32),
    ]
    return groups, heads, ins, outs, shapes, scratch


def attend_cost(tokens, width, products):
    pairs = (tokens // BT) * (tokens // BT + 1) // 2
    work = products * 2 * pairs * BT * BT * width
    return cost(4 * work, 10 * tokens * width, pairs * BT * BT * width // HD)


def attend_safe(packed, lengths, big, low, exact, lse):
    tokens, width = packed.shape[0], packed.shape[1] // 3
    groups, heads, _, _, shapes, scratch = attend_specs(tokens, width)
    cols = width // groups
    return pl.pallas_call(
        functools.partial(attend_safe_kernel, heads, groups),
        grid_spec=pltpu.PrefetchScalarGridSpec(
            num_scalar_prefetch=1,
            grid=(1,),
            in_specs=[pl.BlockSpec((8, 128), lambda i, n: (0, 0))] + [ANY] * 4,
            out_specs=[ANY] * 3,
            scratch_shapes=[
                pltpu.VMEM((BT, cols), bf16),
                pltpu.VMEM((tokens, cols), bf16),
                pltpu.VMEM((tokens, cols), bf16),
                pltpu.VMEM((BT, cols), bf16),
                pltpu.VMEM((BT, cols), f32),
                pltpu.VMEM((8, BT), f32),
            ]
            + scratch
            + [pltpu.SemaphoreType.DMA(())],
        ),
        out_shape=shapes,
        input_output_aliases={3: 0, 4: 1, 5: 2},
        compiler_params=params(1),
        cost_estimate=cost(1000, 100000),
        name="attend_safe",
    )(lengths, big, packed, low, exact, lse)


def attend_forward(packed, lengths, comm=NoTransfers(), moved=(), fresh=None):
    tokens, width = packed.shape[0], packed.shape[1] // 3
    groups, heads, ins, outs, shapes, scratch = attend_specs(tokens, width)
    low, exact, lse, big, *rest = pl.pallas_call(
        functools.partial(attend_forward_kernel, heads, comm),
        grid_spec=pltpu.PrefetchScalarGridSpec(
            num_scalar_prefetch=1,
            grid=(groups, tokens // BT),
            in_specs=ins + [ANY] * len(moved),
            out_specs=outs
            + [pl.BlockSpec((8, 128), lambda g, i, n: (0, 0))]
            + [ANY] * comm.outs,
            scratch_shapes=scratch + (comm.scratch() if moved else []),
        ),
        out_shape=shapes
        + [jax.ShapeDtypeStruct((8, 128), f32)]
        + [jax.ShapeDtypeStruct(m.shape, m.dtype) for m in moved[1:]]
        + ([fresh] if moved else []),
        input_output_aliases={5: 4} if moved else {},
        compiler_params=params(2, 2 if moved else None),
        cost_estimate=attend_cost(tokens, width, 2),
        name="attend_forward",
    )(lengths, packed, packed, packed, *moved)
    low, exact, lse = attend_safe(packed, lengths, big, low, exact, lse)
    return [low, exact, lse] + rest


def attend_backward_kernel(heads, comm, lens_ref, q_ref, k_ref, v_ref, do_ref, lse_ref, delta_ref, *refs):
    ins, refs = refs[: comm.ins], refs[comm.ins :]
    dq_ref, dk_ref, dv_ref = refs[:3]
    outs, refs = refs[3 : 3 + comm.outs], refs[3 + comm.outs :]
    qm_ref, dom_ref, km_ref, vm_ref, dqa_ref, dka_ref, dva_ref = refs[:7]
    scratch = refs[7:]
    step = pl.program_id(1)
    count = pl.num_programs(1)
    block = k_ref.shape[0]
    comm.before(pl.program_id(0) * count + step, ins, outs, scratch)

    @pl.when(step == 0)
    def _():
        for t in range(q_ref.shape[0] // block):
            rows = slice(t * block, (t + 1) * block)
            for h in range(heads):
                place = slice(h * block, (h + 1) * block)
                qm_ref[t, place, :] = head_lanes(q_ref[rows, :], h)
                dom_ref[t, place, :] = head_lanes(do_ref[rows, :], h)
        dqa_ref[...] = jnp.zeros(dqa_ref.shape, f32)

    for h in range(heads):
        place = slice(h * block, (h + 1) * block)
        km_ref[place, :] = head_lanes(k_ref[...], h)
        vm_ref[place, :] = head_lanes(v_ref[...], h)
    dka_ref[...] = jnp.zeros(dka_ref.shape, f32)
    dva_ref[...] = jnp.zeros(dva_ref.shape, f32)
    away = jnp.where(lens_ref[0] == LONG_LEN, 0.0, 1e30).astype(f32)

    def pair(i, on_diagonal):
        rows = pl.ds(pl.multiple_of(i * block, block), block)
        query, grad = q_ref[rows, :], do_ref[rows, :]
        low, slopes = [], []
        for h in range(heads):
            place = slice(h * block, (h + 1) * block)
            scores = dot_nt(km_ref[place, :], query)
            logs = lse_ref[h : h + 1, rows]
            if not on_diagonal:
                logs = logs + away
            prob = jnp.exp2(scores * score_scale_2 - logs)
            if on_diagonal:
                key = lax.broadcasted_iota(jnp.int32, scores.shape, 0)
                tok = lax.broadcasted_iota(jnp.int32, scores.shape, 1)
                prob = jnp.where(tok >= key, prob, 0.0)
            grad_prob = dot_nt(vm_ref[place, :], grad)
            slope = prob * (grad_prob - delta_ref[h : h + 1, rows])
            low.append(prob.astype(bf16))
            slopes.append(slope.astype(bf16))
        dva_ref[...] += dot_nn(jnp.concatenate(low, axis=1), dom_ref[i])
        dka_ref[...] += dot_nn(jnp.concatenate(slopes, axis=1), qm_ref[i])
        dqa_ref[rows, :] += dot_tn(jnp.concatenate(slopes, axis=0), km_ref[...])

    pair(step, True)
    lax.fori_loop(step + 1, count, lambda i, c: (pair(i, False), c)[1], 0)
    dk_ref[...] = (dka_ref[...] * score_scale).astype(bf16)
    dv_ref[...] = dva_ref[...].astype(bf16)

    @pl.when(step == count - 1)
    def _():
        dq_ref[...] = (dqa_ref[...] * score_scale).astype(bf16)

    comm.after(pl.program_id(0) * count + step, ins, outs, scratch)


def attend_backward(packed, grad_attended, lse, delta, lengths, comm=NoTransfers(), moved=()):
    tokens, width = grad_attended.shape
    groups = width // min(256, width)
    cols = width // groups
    heads = cols // HD
    blocks = tokens // BT
    column = pl.BlockSpec((tokens, cols), lambda g, j, n: (0, g))
    stats = pl.BlockSpec((8, tokens), lambda g, j, n: (g, 0))
    tile = pl.BlockSpec((BT, cols), lambda g, j, n: (j, g))
    move_ins, move_outs, move_shapes, move_scratch = comm.specs(moved) if moved else ([], [], [], [])
    return pl.pallas_call(
        functools.partial(attend_backward_kernel, heads, comm),
        grid_spec=pltpu.PrefetchScalarGridSpec(
            num_scalar_prefetch=1,
            grid=(groups, blocks),
            in_specs=[
                column,
                pl.BlockSpec((BT, cols), lambda g, j, n: (j, groups + g)),
                pl.BlockSpec((BT, cols), lambda g, j, n: (j, 2 * groups + g)),
                column,
                stats,
                stats,
            ]
            + move_ins,
            out_specs=[column, tile, tile] + move_outs,
            scratch_shapes=[
                pltpu.VMEM((blocks, heads * BT, cols), bf16),
                pltpu.VMEM((blocks, heads * BT, cols), bf16),
                pltpu.VMEM((heads * BT, cols), bf16),
                pltpu.VMEM((heads * BT, cols), bf16),
                pltpu.VMEM((tokens, cols), f32),
                pltpu.VMEM((BT, cols), f32),
                pltpu.VMEM((BT, cols), f32),
            ]
            + move_scratch,
        ),
        out_shape=[jax.ShapeDtypeStruct((tokens, width), bf16)] * 3 + move_shapes,
        compiler_params=params(2, 3 if moved else None),
        cost_estimate=attend_cost(tokens, width, 5),
        name="attend_backward",
    )(lengths, packed, packed, packed, grad_attended, lse, delta, *moved)


class AttendGather:
    ins, outs = 2, 2

    def scratch(self):
        return gather_sems(4)

    def pieces(self, ins, outs):
        up = [(None, outs[0], (at, width), route) for at, width, route in halves(outs[0].shape[3])]
        down = [(ins[0], outs[1], (at, width), route) for at, width, route in halves(ins[0].shape[1])]
        return up + down

    def hops(self, name, ks, ins, outs, sems):
        copies = []
        for k in ks:
            src, dst, span, route = self.pieces(ins, outs)[k]
            if name == "z":
                copies += gather_z(src, dst, span, sems, 6 * k)
            elif name == "second":
                copies += gather_second(dst, span, route, sems, 6 * k)
            else:
                copies += gather_third(dst, span, route, sems, 6 * k)
        return copies

    def before(self, step, ins, outs, sems):
        def hops(name, ks):
            return self.hops(name, ks, ins, outs, sems)

        @pl.when(step == 0)
        def _():
            greet(False)
            start_all(hops("z", (2, 3)))
            start_all(hops("second", (0, 1)))

        @pl.when(step == 3)
        def _():
            wait_all(hops("second", (0, 1)))
            start_all(hops("third", (0, 1)))

        @pl.when(step == 6)
        def _():
            wait_all(hops("z", (2, 3)))
            start_all(hops("second", (2, 3)))

        @pl.when(step == 9)
        def _():
            wait_all(hops("second", (2, 3)))
            start_all(hops("third", (2, 3)))

    def after(self, step, ins, outs, sems):
        @pl.when(step == 11)
        def _():
            wait_all(self.hops("third", (0, 1, 2, 3), ins, outs, sems))


class SumPart:
    slots = 5

    def __init__(self, grad, span, route, refs, sems, base):
        self.keep = grad.at[pl.ds(0, 512), pl.ds(*span)]
        self.sent = grad.at[pl.ds(512, 512), pl.ds(*span)]
        self.held, self.got_1, self.got_2, self.got_3 = refs
        self.sems, self.base = sems, base
        self.hops = ((2, 1), (1, 2))[route]

    @staticmethod
    def buffers(width):
        return [
            pltpu.VMEM((512, width), bf16),
            pltpu.VMEM((512, width), bf16),
            pltpu.VMEM((256, width), bf16),
            pltpu.VMEM((3, 64, width), bf16),
        ]

    def first(self):
        return [
            send(self.sent, self.got_1, self.sems, self.base, across(self.hops[0])),
            pltpu.make_async_copy(self.keep, self.held, self.sems[2].at[self.base]),
        ]

    def second(self):
        return [
            send(
                self.held.at[pl.ds(256, 256), :],
                self.got_2,
                self.sems,
                self.base + 1,
                across(self.hops[1]),
            )
        ]

    def third(self):
        return [
            send(
                self.held.at[pl.ds(64 * z, 64), :],
                self.got_3.at[z - 1],
                self.sems,
                self.base + 1 + z,
                across(4 * z),
            )
            for z in (1, 2, 3)
        ]

    def add(self, other, rows):
        def body(i, carry):
            at = pl.ds(pl.multiple_of(i * 64, 64), 64)
            self.held[at, :] = (self.held[at, :].astype(f32) + other[at, :].astype(f32)).astype(bf16)
            return carry

        lax.fori_loop(0, rows // 64, body, 0)

    def to_second(self):
        wait_all(self.first())
        self.add(self.got_1, 512)
        start_all(self.second())

    def to_third(self):
        wait_all(self.second())
        self.add(self.got_2, 256)
        start_all(self.third())

    def result(self):
        wait_all(self.third())
        total = self.held[0:64, :].astype(f32)
        for z in range(3):
            total = total + self.got_3[z].astype(f32)
        return total


def sum_sems(parts):
    return [
        pltpu.SemaphoreType.DMA((SumPart.slots * parts,)),
        pltpu.SemaphoreType.DMA((SumPart.slots * parts,)),
        pltpu.SemaphoreType.DMA((SumPart.slots * parts,)),
    ]


class SmallSum:
    def __init__(self, refs, sems):
        self.mine, self.got = refs
        self.sems = sems

    @staticmethod
    def scratch():
        return [
            pltpu.VMEM((6, 8, 1024), f32),
            pltpu.VMEM((5, 8, 1024), f32),
            pltpu.SemaphoreType.DMA((5,)),
            pltpu.SemaphoreType.DMA((5,)),
        ]

    def hop(self, k):
        device = sibling() if k == 0 else across((0, 1, 2, 4, 8)[k])
        return send(self.mine.at[k], self.got.at[k], self.sems, k, device)

    def begin(self, rows):
        self.mine[0] = rows
        self.hop(0).start()

    def advance(self, k, both):
        self.hop(k).wait()
        came = self.got[k]
        if k == 0:
            row = lax.broadcasted_iota(jnp.int32, came.shape, 0)
            came = jnp.where(row < both, came, 0.0)
        self.mine[k + 1] = self.mine[k] + came
        if k < 4:
            self.hop(k + 1).start()


class BackwardSum:
    def __init__(self, cols):
        self.cols = cols
        self.ins = len(cols) + 1
        self.outs = len(cols) + 1

    def specs(self, moved):
        vmem = [pl.BlockSpec((8, 1024), lambda g, j, n: (0, 0))]
        sizes = [(64, c) for c in self.cols]
        shapes = [jax.ShapeDtypeStruct(size, f32) for size in sizes]
        outs = [pl.BlockSpec(size, lambda g, j, n: (0, 0)) for size in sizes]
        scratch = []
        for c in self.cols:
            scratch += SumPart.buffers(c // 2) * 2
        scratch += sum_sems(2 * len(self.cols)) + SmallSum.scratch()
        return (
            [ANY] * len(self.cols) + vmem,
            outs + vmem,
            shapes + [jax.ShapeDtypeStruct((8, 1024), f32)],
            scratch,
        )

    def parts(self, ins, scratch):
        count = 2 * len(self.cols)
        sems = scratch[4 * count : 4 * count + 3]
        made = []
        for k in range(count):
            width = self.cols[k // 2] // 2
            refs = scratch[4 * k : 4 * k + 4]
            span = ((k % 2) * width, width)
            made.append(SumPart(ins[k // 2], span, k % 2, refs, sems, SumPart.slots * k))
        rest = scratch[4 * count + 3 :]
        return made, SmallSum(rest[:2], rest[2:])

    def before(self, step, ins, outs, scratch):
        parts, small = self.parts(ins, scratch)

        @pl.when(step == 0)
        def _():
            greet(True)
            small.begin(ins[-1][...])
            for part in parts[:2] + parts[4:]:
                start_all(part.first())

        for k in range(4):

            @pl.when(step == k + 1)
            def _():
                small.advance(k, 4)

        @pl.when(step == 2)
        def _():
            for part in parts[:2] + parts[4:]:
                part.to_second()
            for part in parts[2:4]:
                start_all(part.first())

        @pl.when(step == 5)
        def _():
            small.advance(4, 4)
            outs[-1][...] = small.mine[5]

        @pl.when(step == 6)
        def _():
            for part in parts[:2] + parts[4:]:
                part.to_third()

        @pl.when(step == 7)
        def _():
            for part in parts[2:4]:
                part.to_second()

        @pl.when(step == 8)
        def _():
            for part in parts[2:4]:
                part.to_third()

    def after(self, step, ins, outs, scratch):
        parts, _ = self.parts(ins, scratch)

        @pl.when(step == 11)
        def _():
            for k, part in enumerate(parts):
                width = self.cols[k // 2] // 2
                span = slice((k % 2) * width, (k % 2 + 1) * width)
                outs[k // 2][:, span] = part.result()


def normalized(values):
    average = jnp.mean(values, axis=-1, keepdims=True)
    centred = values - average
    variance = jnp.mean(centred * centred, axis=-1, keepdims=True)
    inverse = lax.rsqrt(variance + norm_eps)
    return centred * inverse, inverse


def column_sum(values):
    return jnp.sum(values.reshape(-1, 8, values.shape[-1]), axis=0)


def turned(values, out_ref):
    flip = values.T
    bits = bits_of_me()
    for a in range(16):
        r = flipped(bits, a)
        slot = r[2] * 8 + r[3] * 4 + r[0] * 2 + r[1]
        out_ref[pl.ds(pl.multiple_of(slot * 64, 64), 64), :] = flip[a * 64 : (a + 1) * 64, :]


def shape(rows, cols, dtype=bf16):
    return jax.ShapeDtypeStruct((rows, cols), dtype)


def row_tile(cols):
    return pl.BlockSpec((BT, cols), lambda i: (i, 0))


def col_tile(rows):
    return pl.BlockSpec((rows, BT), lambda i: (0, i))


def whole(rows, cols):
    return pl.BlockSpec((rows, cols), lambda i: (0, 0))


def weight(cols):
    return pl.BlockSpec((1024, cols), lambda i: (0, 0), pipeline_mode=pl.Buffered(1))


def my_side():
    return lax.axis_index("mp")


def own_tile(cols, tiles):
    return pl.BlockSpec((BT, cols), lambda i: (jnp.clip(i - tiles * my_side(), 0, tiles - 1), 0))


def other_tile(cols, tiles):
    return pl.BlockSpec(
        (BT, cols), lambda i: (jnp.clip(i - tiles * (1 - my_side()), 0, tiles - 1), 0)
    )


def own_of_natural(cols, tiles):
    return pl.BlockSpec((BT, cols), lambda i: (my_side() * tiles + i, 0))


def other_of_natural(cols, tiles):
    return pl.BlockSpec((BT, cols), lambda i: ((1 - my_side()) * tiles + i, 0))


def grid_call(kernel, steps, ins, outs, scratch, flops, name, collective=None, aliases={}):
    arrays = [a for a, _ in ins]
    nbytes = sum(a.size * a.dtype.itemsize for a in arrays)
    nbytes += sum(o.size * o.dtype.itemsize for o, _ in outs)
    return pl.pallas_call(
        kernel,
        grid=(steps,),
        in_specs=[s for _, s in ins],
        out_specs=[s for _, s in outs],
        scratch_shapes=scratch,
        out_shape=[o for o, _ in outs],
        input_output_aliases=aliases,
        compiler_params=params(1, collective),
        cost_estimate=cost(flops, nbytes),
        name=name,
    )(*arrays)


class FirstGather:
    def __init__(self, wq, up, up_out, wo, out_out, sems):
        self.pieces = [(None, wq, (at, width), r) for at, width, r in chunk_halves(wq.shape[3])]
        self.pieces += [(up, up_out, (at, width), r) for at, width, r in halves(up.shape[1])]
        self.pieces += [(wo, out_out, (at, width), r) for at, width, r in halves(wo.shape[1])]
        self.sems = sems

    def z(self, *ks):
        copies = []
        for k in ks:
            src, dst, span, _ = self.pieces[k]
            if src is None:
                bits = bits_of_me()
                place = dst.at[bits[0] * 2 + bits[1], bits[2] * 2 + bits[3], :, pl.ds(*span)]
                copies += [
                    send(place, place, self.sems, 6 * k + hop, across(4 * (hop + 1)))
                    for hop in range(3)
                ]
            else:
                copies += gather_z(src, dst, span, self.sems, 6 * k)
        return copies

    def second(self, *ks):
        copies = []
        for k in ks:
            _, dst, span, route = self.pieces[k]
            copies += gather_second(dst, span, route, self.sems, 6 * k)
        return copies

    def third(self, *ks):
        copies = []
        for k in ks:
            _, dst, span, route = self.pieces[k]
            copies += gather_third(dst, span, route, self.sems, 6 * k)
        return copies


def chunk_halves(cols):
    width = cols // 4
    return [(k * width, width, k % 2) for k in range(4)]


def qkv_kernel(
    tiles,
    own,
    own_all,
    gain,
    shift,
    bias,
    w_mine,
    wo,
    up,
    turned_out,
    out,
    up_out,
    out_out,
    w_out,
    normed,
    came,
    wq,
    swap_send,
    swap_came,
    copy_sem,
    *sems,
):
    step = pl.program_id(0)
    side = my_side()
    moves = FirstGather(wq, up, up_out, wo, out_out, sems)
    local = w_mine.shape[2]

    def swap(k):
        return send(
            own_all.at[pl.ds(k * BT, BT), :], came.at[k], (swap_send, swap_came), k, sibling()
        )

    @pl.when(step == 0)
    def _():
        bits = bits_of_me()
        for c in range(3):
            wq[bits[0] * 2 + bits[1], bits[2] * 2 + bits[3], :, c * local : (c + 1) * local] = (
                w_mine[c]
            )
        greet(True)
        start_all(moves.z(0, 1))
        start_all([swap(k) for k in range(tiles)])

    def norm(values):
        scaled, _ = normalized(values.astype(f32))
        rows = (scaled * gain[...] + shift[...]).astype(bf16)
        first = lax.rem(step + side * tiles, 2 * tiles) * BT
        normed[pl.ds(pl.multiple_of(first, BT), BT), :] = rows
        turned(rows, turned_out)

    @pl.when(step < tiles)
    def _():
        norm(own[...])

    for k in range(tiles):

        @pl.when(step == tiles + k)
        def _():
            swap(k).wait()
            norm(came[k])

    @pl.when(step == 2 * tiles - 2)
    def _():
        wait_all(moves.z(0, 1))
        start_all(moves.second(0, 1))
        start_all(moves.z(2, 3))

    @pl.when(step == 2 * tiles)
    def _():
        wait_all(moves.second(0, 1))
        start_all(moves.third(0, 1))
        wait_all(moves.z(2, 3))
        start_all(moves.z(6, 7))
        wait_all(moves.third(0, 1))
        start_all(moves.second(2, 3))

    @pl.when(step == 2 * tiles + 2)
    def _():
        wait_all(moves.second(2, 3))
        start_all(moves.third(2, 3))
        wait_all(moves.z(6, 7))
        start_all(moves.z(4, 5))

    half = out.shape[1]
    for c in range(2):

        @pl.when((step >= (2 + 2 * c) * tiles) & (step < (4 + 2 * c) * tiles))
        def _():
            @pl.when(step == (2 + 2 * c) * tiles)
            def _():
                if c:
                    wait_all(moves.third(2, 3))
                    start_all(moves.second(6, 7))
                    pltpu.make_async_copy(wq, w_out, copy_sem).start()

            first = (step - (2 + 2 * c) * tiles) * BT
            rows = normed[pl.ds(pl.multiple_of(first, BT), BT), :]
            cols = slice(c * half, (c + 1) * half)
            part = wq[:, :, :, cols].reshape(1024, half)
            out[...] = (dot_nn(rows, part) + bias[:, cols]).astype(bf16)

    @pl.when(step == 5 * tiles)
    def _():
        wait_all(moves.second(6, 7))
        start_all(moves.third(6, 7))

    @pl.when(step == 6 * tiles - 1)
    def _():
        wait_all(moves.third(6, 7))
        wait_all(moves.z(4, 5))
        pltpu.make_async_copy(wq, w_out, copy_sem).wait()


def project_kernel(a, w, out):
    out[...] = dot_nt(a[...], w[...]).astype(bf16)


def project_norm_kernel(a, w, toks, came, bias, gain, shift, hid_out, normed_out):
    partial = dot_nt(a[...], w[...])
    hidden = toks[...].astype(f32) + (partial + came[...].astype(f32) + bias[...])
    hid_out[...] = hidden
    scaled, _ = normalized(hidden)
    normed_out[...] = (scaled * gain[...] + shift[...]).astype(bf16)


def feed_kernel(
    tiles,
    x_all,
    c_all,
    bias,
    wu,
    wd,
    ffn_own,
    norm_own,
    ffn_came,
    norm_came,
    up_out,
    down_out,
    bsum,
    up_total,
    down_total,
    act,
    gpre,
    xt,
    ct,
    xs,
    cs,
    ffn_sent,
    norm_sent,
    local_sems,
    send_sems,
    came_sems,
    out_sems,
):
    step = pl.program_id(0)
    remote = (send_sems, came_sems)

    def rows(k):
        return pl.ds(k * BT, BT)

    def local(k):
        return [
            pltpu.make_async_copy(x_all.at[rows(k), :], xs.at[k], local_sems.at[k]),
            pltpu.make_async_copy(c_all.at[rows(k), :], cs.at[k], local_sems.at[tiles + k]),
        ]

    def swapped(k):
        return [
            send(x_all.at[rows(k), :], xs.at[tiles + k], remote, k, sibling()),
            send(c_all.at[rows(k), :], cs.at[tiles + k], remote, tiles + k, sibling()),
        ]

    def returned(k):
        return [
            send(ffn_sent, ffn_came.at[rows(k), :], remote, 2 * tiles + k, sibling()),
            send(norm_sent, norm_came.at[rows(k), :], remote, 3 * tiles + k, sibling()),
        ]

    @pl.when(step == 0)
    def _():
        for k in range(tiles):
            start_all(local(k))
        bsum[...] = jnp.zeros(bsum.shape, f32)
        greet_sibling()
        for k in range(tiles):
            start_all(swapped(k))

    for k in range(tiles):

        @pl.when(step == k)
        def _():
            wait_all(local(k))

        @pl.when(step == tiles + k)
        def _():
            wait_all(swapped(k))

    x, c = xs[step], cs[step]
    xt[...] = x.T
    ct[...] = c.T
    width = 512
    spans = [slice(at, at + width) for at in range(0, wu.shape[1], width)]
    for cols in spans:
        value = dot_nn(x, wu[:, cols]) + bias[:, cols]
        upstream = dot_nn(c, wd[:, cols])
        square = value * value
        bent = jnp.tanh(value * (gelu_coeff + (gelu_coeff * 0.044715) * square))
        half_up = 0.5 + 0.5 * bent
        act[:, cols] = (value * half_up).astype(bf16)
        slope = half_up + value * (half_up * (1.0 - bent)) * (
            gelu_coeff + (3.0 * 0.044715 * gelu_coeff) * square
        )
        grad = (upstream * slope).astype(bf16)
        gpre[:, cols] = grad
        bsum[:, cols] += column_sum(grad.astype(f32))
    ffn = dot_nt(act[...], wd[...]).astype(bf16)
    norm = dot_nt(gpre[...], wu[...]).astype(bf16)

    @pl.when(step < tiles)
    def _():
        ffn_own[...] = ffn
        norm_own[...] = norm

    for k in range(tiles):

        @pl.when(step == tiles + k)
        def _():
            if k:
                wait_all(returned(k - 1))
            ffn_sent[...] = ffn
            norm_sent[...] = norm
            start_all(returned(k))

    @pl.when(step == 0)
    def _():
        for cols in spans:
            down_total[:, cols] = dot_nn(ct[...], act[:, cols])
        for cols in spans:
            up_total[:, cols] = dot_nn(xt[...], gpre[:, cols])

    @pl.when(step > 0)
    def _():
        for cols in spans:
            down_total[:, cols] += dot_nn(ct[...], act[:, cols])
        for cols in spans:
            up_total[:, cols] += dot_nn(xt[...], gpre[:, cols])

    def leave(total, stage, out, base):
        half = total.shape[1] // 2
        bits = bits_of_me()
        copies = []
        for top in range(2):
            for route in range(2):
                part = total[512 * top : 512 * top + 512, route * half : route * half + half]
                stage[top * 2 + route] = part.astype(bf16)
        for a in range(16):
            r = flipped(bits, a)
            for route in range(2):
                slot = r[2 + route] * 8 + r[3 - route] * 4 + r[0] * 2 + r[1]
                copies.append(
                    pltpu.make_async_copy(
                        stage.at[(a // 8) * 2 + route, pl.ds((a % 8) * 64, 64), :],
                        out.at[
                            pl.ds(pl.multiple_of(slot * 64, 64), 64), pl.ds(route * half, half)
                        ],
                        out_sems.at[base + 2 * a + route],
                    )
                )
        start_all(copies)
        return copies

    @pl.when(step == 2 * tiles - 1)
    def _():
        copies = leave(down_total, cs, down_out, 0)
        copies += leave(up_total, xs, up_out, 32)
        wait_all(copies)
        wait_all(returned(tiles - 1))


def middle_kernel(hid, f_own, f_came, g_own, g_came, cot, bias, gain, out, gattn, sums):
    @pl.when(pl.program_id(0) == 0)
    def _():
        sums[...] = jnp.zeros(sums.shape, f32)

    hidden = hid[...]
    grad_out = cot[...].astype(f32)
    out[...] = (hidden + (f_own[...].astype(f32) + f_came[...].astype(f32) + bias[...])).astype(bf16)
    scaled, inverse = normalized(hidden)
    grad_norm = g_own[...].astype(f32) + g_came[...].astype(f32)
    through = grad_norm * gain[...]
    centre = jnp.mean(through, axis=-1, keepdims=True)
    along = jnp.mean(through * scaled, axis=-1, keepdims=True)
    grad = (grad_out + inverse * (through - centre - scaled * along)).astype(bf16)
    gattn[...] = grad
    sums[0:8, :] += column_sum(grad_norm * scaled)
    sums[8:16, :] += column_sum(grad_norm)
    sums[16:24, :] += column_sum(grad.astype(f32))
    sums[24:32, :] += column_sum(grad_out)


def grad_attended_kernel(tiles, own, other, exact, w, do_out, delta_out, g_turned):
    mine = (pl.program_id(0) // tiles) == my_side()
    grad = jnp.where(mine, own[...], other[...])
    turned(grad, g_turned)
    part = dot_nn(grad, w[...]).astype(bf16)
    do_out[...] = part
    cols = part.shape[1]
    row = lax.broadcasted_iota(jnp.int32, (16, cols), 0)
    head = lax.broadcasted_iota(jnp.int32, (16, cols), 1) // HD
    pick = jnp.where(row == (head // 4) * 8 + head % 4, 1.0, 0.0).astype(f32)
    delta_out[...] = lax.dot_general(
        pick,
        part.astype(f32) * exact[...],
        (((1,), (1,)), ((), ())),
        precision=lax.Precision.HIGHEST,
        preferred_element_type=f32,
    )


class LastSum:
    def __init__(self, cols):
        self.spans = halves(cols, 2)

    def scratch(self):
        made = []
        for _, width, _ in self.spans:
            made += SumPart.buffers(width)
        return made + sum_sems(4) + SmallSum.scratch()

    def parts(self, ins, scratch):
        made = []
        for k, (at, width, route) in enumerate(self.spans):
            refs = scratch[4 * k : 4 * k + 4]
            made.append(
                SumPart(ins[0], (at, width), route, refs, scratch[16:19], SumPart.slots * k)
            )
        return made, SmallSum(scratch[19:21], scratch[21:23])


def last_kernel(tiles, comm, dq, dk, dv, w, toks, gattn, gain, small, *refs):
    ins, refs = refs[:1], refs[1:]
    out, grad_w, small_out = refs[:3]
    sums, sent, came, send_sems, recv_sems = refs[3:8]
    parts, tiny = comm.parts(ins, refs[8:])
    step = pl.program_id(0)

    def swap(k):
        return send(sent.at[k], came.at[k], (send_sems, recv_sems), k, sibling())

    @pl.when(step == 0)
    def _():
        greet(True)
        sums[...] = jnp.zeros(sums.shape, f32)
        for part in parts:
            start_all(part.first())

    @pl.when(step == 2)
    def _():
        for part in parts[:2]:
            part.to_second()

    @pl.when(step == 4)
    def _():
        for part in parts[2:]:
            part.to_second()
        for part in parts[:2]:
            part.to_third()

    grads = jnp.concatenate([dq[...], dk[...], dv[...]], axis=1)
    rows = dot_nt(grads, w[...])

    for k in range(tiles):

        @pl.when(step == k)
        def _():
            sent[k] = rows.astype(bf16)
            swap(k).start()

        @pl.when(step == tiles + k)
        def _():
            swap(k).wait()
            grad_norm = rows + came[k].astype(f32)
            scaled, inverse = normalized(toks[...].astype(f32))
            through = grad_norm * gain[...]
            centre = jnp.mean(through, axis=-1, keepdims=True)
            along = jnp.mean(through * scaled, axis=-1, keepdims=True)
            grad_in = inverse * (through - centre - scaled * along)
            out[...] = (gattn[...].astype(f32) + grad_in).astype(bf16)
            sums[0:8, :] += column_sum(grad_norm * scaled)
            sums[8:16, :] += column_sum(grad_norm)

    @pl.when(step == pl.num_programs(0) - 1)
    def _():
        row = lax.broadcasted_iota(jnp.int32, (8, 1024), 0)
        first = jnp.sum(sums[0:8, :], axis=0, keepdims=True)
        second = jnp.sum(sums[8:16, :], axis=0, keepdims=True)
        tiny.begin(jnp.where(row == 0, first, jnp.where(row == 1, second, small[...])))
        for part in parts[2:]:
            part.to_third()
        for k in range(5):
            tiny.advance(k, 2)
        small_out[...] = tiny.mine[5]
        local = grad_w.shape[2]
        for part, (at, width, _) in zip(parts, comm.spans):
            total = part.result()
            edges = sorted({at, at + width} | {c for c in (local, 2 * local) if at < c < at + width})
            for low, high in zip(edges[:-1], edges[1:]):
                first = low % local
                grad_w[low // local, :, first : first + high - low] = total[:, low - at : high - at]


def weight_grad_kernel(lefts, rights, *refs):
    left, right = refs[:lefts], refs[lefts : lefts * (1 + rights)]
    outs, sums, total = refs[lefts * (1 + rights) : -2], refs[-2], refs[-1]
    step = pl.program_id(0)
    tiles = pl.num_programs(0) // lefts

    def add(k, fresh):
        at = 0
        for r in right[k * rights : (k + 1) * rights]:
            cols = slice(at, at + r.shape[1])
            term = dot_nn(left[k][...], r[...])
            total[:, cols] = term if fresh else total[:, cols] + term
            if rights > 1:
                count = column_sum(r[...].astype(f32))
                sums[:, cols] = count if fresh else sums[:, cols] + count
            at += r.shape[1]

    @pl.when(step == 0)
    def _():
        add(0, True)
        if rights == 1:
            sums[...] = jnp.zeros(sums.shape, f32)

    for k in range(lefts):

        @pl.when((step > 0) & (step // tiles == k))
        def _():
            add(k, False)

    @pl.when(step == pl.num_programs(0) - 1)
    def _():
        half = total.shape[1] // 2
        outs[0][:, :half] = total[:, :half].astype(bf16)
        for to, at in enumerate((0, 2, 1, 3)):
            there, here = slice(256 * to, 256 * to + 256), slice(256 * at, 256 * at + 256)
            outs[0][there, half:] = total[here, half:].astype(bf16)


def weight_grad(lefts, rights, name):
    tiles = lefts[0].shape[1] // BT
    cols = sum(r.shape[1] for r in rights[0])

    def at(i, k):
        return jnp.clip(i - k * tiles, 0, tiles - 1)

    ins = []
    for k, left in enumerate(lefts):
        ins.append((left, pl.BlockSpec((1024, BT), lambda i, k=k: (0, at(i, k)))))
    for k, group in enumerate(rights):
        for r in group:
            ins.append((r, pl.BlockSpec((BT, r.shape[1]), lambda i, k=k: (at(i, k), 0))))
    outs = [(shape(1024, cols), whole(1024, cols)), (shape(8, cols, f32), whole(8, cols))]
    return grid_call(
        functools.partial(weight_grad_kernel, len(lefts), len(rights[0])),
        tiles * len(lefts),
        ins,
        outs,
        [pltpu.VMEM((1024, cols), f32)],
        2 * 1024 * cols * BT * tiles * len(lefts),
        name,
    )


def swap_mp(block):
    return lax.ppermute(block, "mp", [(0, 1), (1, 0)])


def wide(vector):
    return vector.astype(f32).reshape(1, -1)


def layer_on_pairs(
    tokens,
    slot_lengths,
    gain_one,
    shift_one,
    w_qkv,
    bias_qv,
    w_out,
    bias_out,
    gain_two,
    shift_two,
    w_up,
    bias_up,
    w_down,
    bias_down,
    cotangent,
):
    own_rows, width = tokens.shape
    total_rows = 2 * own_rows
    tiles = own_rows // BT
    local = w_qkv.shape[2]
    hidden_cols = w_up.shape[1]
    side_cols = 3 * local
    lengths = slot_lengths[0]
    sums_in = whole(8, width)

    bias = jnp.concatenate([bias_qv[0], jnp.zeros_like(bias_qv[0]), bias_qv[1]])
    half_cols = side_cols // 2
    normed_at = pl.BlockSpec(
        (width, BT),
        lambda i: (0, lax.rem(jnp.minimum(i, 2 * tiles - 1) + my_side() * tiles, 2 * tiles)),
    )
    packed_at = pl.BlockSpec(
        (BT, half_cols),
        lambda i: (
            lax.rem(jnp.maximum(i - 2 * tiles, 0), 2 * tiles),
            jnp.maximum(i - 2 * tiles, 0) // (2 * tiles),
        ),
    )
    rows_turned, packed, up_blocks, out_blocks, qkv_blocks = grid_call(
        functools.partial(qkv_kernel, tiles),
        6 * tiles,
        [
            (tokens, pl.BlockSpec((BT, width), lambda i: (jnp.minimum(i, tiles - 1), 0))),
            (tokens, ANY),
            (wide(gain_one), whole(1, width)),
            (wide(shift_one), whole(1, width)),
            (wide(bias), whole(1, side_cols)),
            (w_qkv.transpose(1, 0, 2), pl.BlockSpec((3, 64, local), lambda i: (0, 0, 0))),
            (w_out.T, ANY),
            (w_up, ANY),
        ],
        [
            (shape(width, total_rows), normed_at),
            (shape(total_rows, side_cols), packed_at),
            (jax.ShapeDtypeStruct((4, 4, 64, hidden_cols), bf16), ANY),
            (jax.ShapeDtypeStruct((4, 4, 64, local), bf16), ANY),
            (jax.ShapeDtypeStruct((4, 4, 64, side_cols), bf16), ANY),
        ],
        [
            pltpu.VMEM((total_rows, width), bf16),
            pltpu.VMEM((tiles, BT, width), bf16),
            pltpu.VMEM((4, 4, 64, side_cols), bf16),
            pltpu.SemaphoreType.DMA((tiles,)),
            pltpu.SemaphoreType.DMA((tiles,)),
            pltpu.SemaphoreType.DMA(()),
        ]
        + gather_sems(8),
        2 * total_rows * width * side_cols,
        "qkv",
        1,
    )
    qkv_w = qkv_blocks.reshape(width, side_cols)
    attended, exact, lse, up_blocks, down_blocks = attend_forward(
        packed,
        lengths,
        AttendGather(),
        (w_down.T, up_blocks),
        jax.ShapeDtypeStruct((4, 4, 64, hidden_cols), bf16),
    )
    up_w = up_blocks.reshape(width, hidden_cols)
    down_w = down_blocks.reshape(width, hidden_cols)
    out_w = out_blocks.reshape(width, local)

    (partial_other,) = grid_call(
        project_kernel,
        tiles,
        [(attended, other_of_natural(local, tiles)), (out_w, weight(local))],
        [(shape(own_rows, width), row_tile(width))],
        [],
        2 * own_rows * width * local,
        "project_other",
    )
    partial_came = swap_mp(partial_other)
    hidden, normed_own = grid_call(
        project_norm_kernel,
        tiles,
        [
            (attended, own_of_natural(local, tiles)),
            (out_w, weight(local)),
            (tokens, row_tile(width)),
            (partial_came, row_tile(width)),
            (wide(bias_out), whole(1, width)),
            (wide(gain_two), whole(1, width)),
            (wide(shift_two), whole(1, width)),
        ],
        [(shape(own_rows, width, f32), row_tile(width)), (shape(own_rows, width), row_tile(width))],
        [],
        2 * own_rows * width * local,
        "project_norm",
    )
    own_at = pl.BlockSpec((BT, width), lambda i: (jnp.minimum(i, tiles - 1), 0))
    ffn_own, norm_own, ffn_came, norm_came, up_grad, down_grad, bsum = grid_call(
        functools.partial(feed_kernel, tiles),
        2 * tiles,
        [
            (normed_own, ANY),
            (cotangent, ANY),
            (wide(bias_up), whole(1, hidden_cols)),
            (up_w, weight(hidden_cols)),
            (down_w, weight(hidden_cols)),
        ],
        [
            (shape(own_rows, width), own_at),
            (shape(own_rows, width), own_at),
            (shape(own_rows, width), ANY),
            (shape(own_rows, width), ANY),
            (shape(width, hidden_cols), ANY),
            (shape(width, hidden_cols), ANY),
            (shape(8, hidden_cols, f32), whole(8, hidden_cols)),
        ],
        [
            pltpu.VMEM((width, hidden_cols), f32),
            pltpu.VMEM((width, hidden_cols), f32),
            pltpu.VMEM((BT, hidden_cols), bf16),
            pltpu.VMEM((BT, hidden_cols), bf16),
            pltpu.VMEM((width, BT), bf16),
            pltpu.VMEM((width, BT), bf16),
            pltpu.VMEM((2 * tiles, BT, width), bf16),
            pltpu.VMEM((2 * tiles, BT, width), bf16),
            pltpu.VMEM((BT, width), bf16),
            pltpu.VMEM((BT, width), bf16),
            pltpu.SemaphoreType.DMA((2 * tiles,)),
            pltpu.SemaphoreType.DMA((4 * tiles,)),
            pltpu.SemaphoreType.DMA((4 * tiles,)),
            pltpu.SemaphoreType.DMA((64,)),
        ],
        24 * own_rows * width * hidden_cols,
        "feed",
        5,
    )
    output, grad_attn, middle_sums = grid_call(
        middle_kernel,
        tiles,
        [
            (hidden, row_tile(width)),
            (ffn_own, row_tile(width)),
            (ffn_came, row_tile(width)),
            (norm_own, row_tile(width)),
            (norm_came, row_tile(width)),
            (cotangent, row_tile(width)),
            (wide(bias_down), whole(1, width)),
            (wide(gain_two), whole(1, width)),
        ],
        [
            (shape(own_rows, width), row_tile(width)),
            (shape(own_rows, width), row_tile(width)),
            (shape(32, width, f32), whole(32, width)),
        ],
        [],
        40 * own_rows * width,
        "middle",
    )
    grad_attn_other = swap_mp(grad_attn)
    grad_attended, delta, g_turned = grid_call(
        functools.partial(grad_attended_kernel, tiles),
        2 * tiles,
        [
            (grad_attn, own_tile(width, tiles)),
            (grad_attn_other, other_tile(width, tiles)),
            (exact, row_tile(local)),
            (out_w, weight(local)),
        ],
        [
            (shape(total_rows, local), row_tile(local)),
            (shape(16, total_rows, f32), col_tile(16)),
            (shape(width, total_rows), col_tile(width)),
        ],
        [],
        2 * total_rows * width * local,
        "grad_attended",
    )
    half = local // 2
    out_grad, _ = weight_grad([g_turned], [[attended]], "out_grad")
    early = middle_sums.reshape(4, 8, width).sum(axis=1)
    up_bias = bsum.sum(axis=0).reshape(-1, width)
    early = jnp.concatenate([early, up_bias, jnp.zeros((2, width), f32)])
    moved = (down_grad, up_grad, out_grad, early)
    grad_q, grad_k, grad_v, grad_down, grad_up, grad_w_out, early = attend_backward(
        packed,
        grad_attended,
        lse,
        delta,
        lengths,
        BackwardSum((hidden_cols, hidden_cols, local)),
        moved,
    )
    qkv_grad, qkv_sums = weight_grad([rows_turned], [[grad_q, grad_k, grad_v]], "qkv_grad")
    qv = jnp.concatenate([qkv_sums[:, :local].sum(axis=0), qkv_sums[:, 2 * local :].sum(axis=0)])
    small = jnp.concatenate(
        [jnp.zeros((2, width), f32), qv.reshape(1, -1), jnp.zeros((5, width), f32)]
    )
    last = LastSum(side_cols)

    def two_way(cols):
        return pl.BlockSpec(
            (BT, cols), lambda i: (lax.rem(i + (1 - my_side()) * tiles, 2 * tiles), 0)
        )

    late_tile = pl.BlockSpec((BT, width), lambda i: (jnp.maximum(i - tiles, 0), 0))
    grad_tokens, grad_w_qkv, late = grid_call(
        functools.partial(last_kernel, tiles, last),
        2 * tiles,
        [(g, two_way(local)) for g in (grad_q, grad_k, grad_v)]
        + [
            (qkv_w, weight(side_cols)),
            (tokens, late_tile),
            (grad_attn, late_tile),
            (wide(gain_one), whole(1, width)),
            (small, sums_in),
        ]
        + [(qkv_grad, ANY)],
        [
            (shape(own_rows, width), late_tile),
            (
                jax.ShapeDtypeStruct((3, 64, local), f32),
                pl.BlockSpec((3, 64, local), lambda i: (0, 0, 0)),
            ),
            (shape(8, width, f32), sums_in),
        ],
        [
            pltpu.VMEM((16, width), f32),
            pltpu.VMEM((tiles, BT, width), bf16),
            pltpu.VMEM((tiles, BT, width), bf16),
            pltpu.SemaphoreType.DMA((tiles,)),
            pltpu.SemaphoreType.DMA((tiles,)),
        ]
        + last.scratch(),
        2 * total_rows * width * side_cols,
        "last",
        4,
    )
    return (
        output,
        grad_tokens,
        late[0],
        late[1],
        grad_w_qkv.transpose(1, 0, 2),
        late[2].reshape(2, local),
        grad_w_out.T,
        early[2],
        early[0],
        early[1],
        grad_up,
        early[4:6].reshape(-1),
        grad_down.T,
        early[3],
    )


def gelu_tanh(values):
    inner = gelu_coeff * (values + 0.044715 * values * values * values)
    return 0.5 * values * (1.0 + jnp.tanh(inner))


def gelu_slope(values):
    inner = gelu_coeff * (values + 0.044715 * values * values * values)
    bent = jnp.tanh(inner)
    return 0.5 * (1.0 + bent) + 0.5 * values * (1.0 - bent * bent) * gelu_coeff * (
        1.0 + 3.0 * 0.044715 * values * values
    )


def norm_forward(values, gain_vec, shift_vec):
    average = jnp.mean(values, axis=-1, keepdims=True)
    centred = values - average
    variance = jnp.mean(centred * centred, axis=-1, keepdims=True)
    inverse = lax.rsqrt(variance + norm_eps)
    scaled = centred * inverse
    return (scaled * gain_vec.astype(f32) + shift_vec.astype(f32), scaled, inverse)


def norm_backward(grad_out, scaled, inverse, gain_vec):
    grad_scaled = grad_out * gain_vec.astype(f32)
    centre_term = jnp.mean(grad_scaled, axis=-1, keepdims=True)
    slope_term = jnp.mean(grad_scaled * scaled, axis=-1, keepdims=True)
    grad_in = inverse * (grad_scaled - centre_term - scaled * slope_term)
    return (grad_in, jnp.sum(grad_out * scaled, axis=0), jnp.sum(grad_out, axis=0))


def layer_by_collectives(
    tokens,
    slot_lengths,
    gain_one,
    shift_one,
    w_qkv,
    bias_qv,
    w_out,
    bias_out,
    gain_two,
    shift_two,
    w_up,
    bias_up,
    w_down,
    bias_down,
    cotangent,
):
    w_qkv, w_out, w_up, w_down = (
        lax.all_gather(w_qkv, "dp", axis=0, tiled=True),
        lax.all_gather(w_out, "dp", axis=1, tiled=True),
        lax.all_gather(w_up, "dp", axis=0, tiled=True),
        lax.all_gather(w_down, "dp", axis=1, tiled=True),
    )
    lengths = slot_lengths[0]
    residual = tokens.astype(f32)
    normed_one, scaled_one, inverse_one = norm_forward(residual, gain_one, shift_one)
    rows_one = lax.all_gather(normed_one.astype(bf16), "mp", axis=0, tiled=True)
    packed = jnp.einsum("td,dcf->tcf", rows_one, w_qkv, preferred_element_type=f32)
    zero_bias = jnp.zeros_like(bias_qv[0])
    packed_bias = jnp.stack([bias_qv[0], zero_bias, bias_qv[1]]).astype(f32)
    packed = (packed + packed_bias[None]).astype(bf16)
    local = packed.shape[2]
    packed_rows = packed.reshape(packed.shape[0], -1)
    attended, exact_out, log_totals = attend_forward(packed_rows, lengths)
    hidden = (
        residual
        + lax.psum_scatter(
            jnp.dot(attended, w_out, preferred_element_type=f32),
            "mp",
            scatter_dimension=0,
            tiled=True,
        )
        + bias_out.astype(f32)
    )
    normed_two, scaled_two, inverse_two = norm_forward(hidden, gain_two, shift_two)
    normed_low = normed_two.astype(bf16)
    rows_two = lax.all_gather(normed_low, "mp", axis=0, tiled=True)
    preact = jnp.dot(rows_two, w_up, preferred_element_type=f32) + bias_up.astype(
        f32
    )
    active = gelu_tanh(preact).astype(bf16)
    ffn_out = lax.psum_scatter(
        jnp.dot(active, w_down, preferred_element_type=f32).astype(bf16),
        "mp",
        scatter_dimension=0,
        tiled=True,
    ).astype(f32)
    output = (hidden + ffn_out + bias_down.astype(f32)).astype(bf16)
    grad_out = cotangent.astype(f32)
    grad_rows = lax.all_gather(cotangent, "mp", axis=0, tiled=True)
    grad_active = jnp.einsum("td,fd->tf", grad_rows, w_down, preferred_element_type=f32)
    grad_pre = (grad_active * gelu_slope(preact)).astype(bf16)
    grad_up = jnp.einsum("td,tf->df", rows_two, grad_pre, preferred_element_type=f32)
    grad_down = jnp.einsum("tf,td->fd", active, grad_rows, preferred_element_type=f32)
    grad_bias_up = jnp.sum(grad_pre.astype(f32), axis=0)
    grad_norm_two = lax.psum_scatter(
        jnp.einsum("tf,df->td", grad_pre, w_up, preferred_element_type=f32),
        "mp",
        scatter_dimension=0,
        tiled=True,
    )
    grad_in_two, grad_gain_two, grad_shift_two = norm_backward(
        grad_norm_two, scaled_two, inverse_two, gain_two
    )
    grad_hidden = grad_out + grad_in_two
    grad_attn = grad_hidden.astype(bf16)
    grad_attn_rows = lax.all_gather(grad_attn, "mp", axis=0, tiled=True)
    grad_w_out = jnp.einsum(
        "tf,td->fd", attended, grad_attn_rows, preferred_element_type=f32
    )
    grad_attended = jnp.einsum(
        "td,fd->tf", grad_attn_rows, w_out, preferred_element_type=f32
    ).astype(bf16)
    product = (grad_attended.astype(f32) * exact_out).reshape(grad_attended.shape[0], -1, HD)
    delta = jnp.sum(product, axis=-1).T
    groups = log_totals.shape[0] // 8
    delta = delta.reshape(groups, -1, delta.shape[1])
    delta = jnp.pad(delta, ((0, 0), (0, 8 - delta.shape[1]), (0, 0))).reshape(8 * groups, -1)
    grads = attend_backward(packed_rows, grad_attended, log_totals, delta, lengths)
    grad_packed = jnp.stack(grads, axis=1)
    grad_w_qkv = jnp.einsum(
        "td,tcf->dcf", rows_one, grad_packed, preferred_element_type=f32
    )
    grad_bias_qv = jnp.stack(
        [
            jnp.sum(grad_packed[:, 0].astype(f32), axis=0),
            jnp.sum(grad_packed[:, 2].astype(f32), axis=0),
        ]
    )
    grad_norm_one = lax.psum_scatter(
        jnp.einsum("tcf,dcf->td", grad_packed, w_qkv, preferred_element_type=f32),
        "mp",
        scatter_dimension=0,
        tiled=True,
    )
    grad_in_one, grad_gain_one, grad_shift_one = norm_backward(
        grad_norm_one, scaled_one, inverse_one, gain_one
    )
    grad_tokens = (grad_hidden + grad_in_one).astype(bf16)
    grad_bias_out = jnp.sum(grad_attn.astype(f32), axis=0)
    grad_bias_down = jnp.sum(grad_out, axis=0)
    grad_w_qkv, grad_w_out, grad_up, grad_down = (
        lax.psum_scatter(grad_w_qkv, "dp", scatter_dimension=0, tiled=True),
        lax.psum_scatter(grad_w_out, "dp", scatter_dimension=1, tiled=True),
        lax.psum_scatter(grad_up, "dp", scatter_dimension=0, tiled=True),
        lax.psum_scatter(grad_down, "dp", scatter_dimension=1, tiled=True),
    )
    small_grads = lax.psum(
        (
            grad_gain_one,
            grad_shift_one,
            grad_bias_out,
            grad_gain_two,
            grad_shift_two,
            grad_bias_down,
        ),
        ("dp", "mp"),
    )
    grad_bias_qv, grad_bias_up = lax.psum((grad_bias_qv, grad_bias_up), "dp")
    return (
        output,
        grad_tokens,
        small_grads[0],
        small_grads[1],
        grad_w_qkv,
        grad_bias_qv,
        grad_w_out,
        small_grads[2],
        small_grads[3],
        small_grads[4],
        grad_up,
        grad_bias_up,
        grad_down,
        small_grads[5],
    )


def solution(mesh):
    pairs = dict(mesh.shape) == {"dp": 16, "mp": 2}
    layer = layer_on_pairs if pairs else layer_by_collectives
    return jax.shard_map(
        layer,
        mesh=mesh,
        in_specs=(
            P(("dp", "mp"), None),
            P("dp", None),
            P(),
            P(),
            P("dp", None, "mp"),
            P(None, "mp"),
            P("mp", "dp"),
            P(),
            P(),
            P(),
            P("dp", "mp"),
            P("mp"),
            P("mp", "dp"),
            P(),
            P(("dp", "mp"), None),
        ),
        out_specs=(
            P(("dp", "mp"), None),
            P(("dp", "mp"), None),
            P(),
            P(),
            P("dp", None, "mp"),
            P(None, "mp"),
            P("mp", "dp"),
            P(),
            P(),
            P(),
            P("dp", "mp"),
            P("mp"),
            P("mp", "dp"),
            P(),
        ),
        check_vma=False,
    )
```

```python
import functools

import jax
import jax.numpy as jnp
from jax import lax
from jax.experimental import pallas as pl
from jax.experimental.pallas import tpu as pltpu
from jax.sharding import PartitionSpec as P

HD = 64
LONG_LEN = 3072
BT = 512
VMEM_CAP = 60 * 1024 * 1024

f32 = jnp.float32
bf16 = jnp.bfloat16
norm_eps = 1e-05
masked_score = -1e30
gelu_coeff = 0.7978845608028654
score_scale = HD ** (-0.5)
safe_sum = 1e30


def dot_nt(left, right):
    return lax.dot_general(left, right, (((1,), (1,)), ((), ())), preferred_element_type=f32)


def dot_nn(left, right):
    return lax.dot_general(left, right, (((1,), (0,)), ((), ())), preferred_element_type=f32)


def dot_tn(left, right):
    return lax.dot_general(left, right, (((0,), (0,)), ((), ())), preferred_element_type=f32)


def params(axes=1, collective=None):
    if collective is None:
        return pltpu.CompilerParams(
            vmem_limit_bytes=VMEM_CAP, dimension_semantics=("arbitrary",) * axes
        )
    return pltpu.CompilerParams(
        vmem_limit_bytes=VMEM_CAP,
        dimension_semantics=("arbitrary",) * axes,
        collective_id=collective,
        has_side_effects=True,
    )


def cost(flops, nbytes, exps=0):
    return pl.CostEstimate(flops=int(flops), bytes_accessed=int(nbytes), transcendentals=int(exps))


ANY = pl.BlockSpec(memory_space=pl.ANY)


def bits_of_me():
    me = lax.axis_index("dp")
    return (me // 8, (me // 4) % 2, (me // 2) % 2, me % 2)


def flipped(bits, which):
    return tuple(1 - b if which & (8 >> k) else b for k, b in enumerate(bits))


def index_of(bits):
    return bits[0] * 8 + bits[1] * 4 + bits[2] * 2 + bits[3]


def across(which):
    return {"dp": index_of(flipped(bits_of_me(), which))}


def sibling():
    return {"mp": 1 - lax.axis_index("mp")}


MESH_ID = pl.DeviceIdType.MESH
HOPS = (1, 2, 4, 8, 12)


def sibling_across(which):
    return {**across(which), **sibling()}


def greet(with_small):
    devices = [across(hop) for hop in HOPS]
    if with_small:
        devices += [across(3), sibling()] + [sibling_across(k) for k in (1, 2, 3)]
    barrier = pltpu.get_barrier_semaphore()
    for device in devices:
        pl.semaphore_signal(barrier, inc=1, device_id=device, device_id_type=MESH_ID)
    pl.semaphore_wait(barrier, len(devices))


def greet_sibling():
    barrier = pltpu.get_barrier_semaphore()
    pl.semaphore_signal(barrier, inc=1, device_id=sibling(), device_id_type=MESH_ID)
    pl.semaphore_wait(barrier, 1)


def send(src, dst, sems, slot, device):
    return pltpu.make_async_remote_copy(
        src_ref=src,
        dst_ref=dst,
        send_sem=sems[0].at[slot],
        recv_sem=sems[1].at[slot],
        device_id=device,
        device_id_type=MESH_ID,
    )


def start_all(copies):
    for copy in copies:
        copy.start()


def wait_all(copies):
    for copy in copies:
        copy.wait()


def gather_z(src, dst, span, sems, base):
    bits = bits_of_me()
    z, yx = bits[0] * 2 + bits[1], bits[2] * 2 + bits[3]
    cols = pl.ds(*span)
    place = dst.at[z, yx, :, cols]
    copies = [
        send(src.at[:, cols], place, sems, base + k, across(4 * (k + 1))) for k in range(3)
    ]
    copies.append(pltpu.make_async_copy(src.at[:, cols], place, sems[2].at[base]))
    return copies


def gather_second(dst, span, route, sems, base):
    bits = bits_of_me()
    part = dst.at[:, bits[2] * 2 + bits[3], :, pl.ds(*span)]
    return [send(part, part, sems, base + 3, across((1, 2)[route]))]


def gather_third(dst, span, route, sems, base):
    copies = []
    for k, which in enumerate((0, (1, 2)[route])):
        bits = flipped(bits_of_me(), which)
        part = dst.at[:, bits[2] * 2 + bits[3], :, pl.ds(*span)]
        copies.append(send(part, part, sems, base + 4 + k, across((2, 1)[route])))
    return copies


def gather_sems(pieces):
    return [
        pltpu.SemaphoreType.DMA((6 * pieces,)),
        pltpu.SemaphoreType.DMA((6 * pieces,)),
        pltpu.SemaphoreType.DMA((6 * pieces,)),
    ]


def halves(cols, parts=1):
    half = cols // 2
    width = half // parts
    return [(r * half + c * width, width, r) for c in range(parts) for r in range(2)]


def head_lanes(block, head):
    lane_head = lax.broadcasted_iota(jnp.int32, block.shape, 1) // HD
    return jnp.where(lane_head == head, block, jnp.zeros_like(block))


def pack_heads(columns):
    lane = lax.broadcasted_iota(jnp.int32, columns[0].shape, 1)
    pairs = [
        jnp.where(lane < HD, columns[2 * i], columns[2 * i + 1]) for i in range(len(columns) // 2)
    ]
    return pairs[0] if len(pairs) == 1 else jnp.concatenate(pairs, axis=1)


def block_probs(scores, top):
    total, parts = None, []
    for t in range(scores.shape[1] // 128):
        part = jnp.exp(scores[:, t * 128 : (t + 1) * 128] - top)
        total = part if total is None else total + part
        parts.append(part.astype(bf16))
    return parts, total


def head_rows(stack, heads, first, count):
    block = stack.shape[0] // heads
    return jnp.concatenate(
        [stack[h * block + first : h * block + first + count, :] for h in range(heads)], axis=0
    )


def attend_block(masked, keys, values, m_ref, l_ref, acc_ref):
    heads, half = len(masked), keys.shape[0] // 2
    for part in range(2):
        rows = slice(part * half, (part + 1) * half)
        seen = (part + 1) * half
        low = []
        for h, query in enumerate(masked):
            scores = dot_nt(query[rows, :], keys[:seen, :])
            row = lax.broadcasted_iota(jnp.int32, scores.shape, 0) + part * half
            col = lax.broadcasted_iota(jnp.int32, scores.shape, 1)
            scores = jnp.where(row >= col, scores, masked_score)
            top = jnp.broadcast_to(jnp.max(scores, axis=1, keepdims=True), (half, 128))
            m_ref[h, rows, :] = top
            parts, l_ref[h, rows, :] = block_probs(scores, top)
            low += parts
        acc_ref[rows, :] = dot_nn(
            jnp.concatenate(low, axis=1), head_rows(values, heads, 0, seen)
        )


def attend_finish(heads, m_ref, l_ref, acc_ref, out_ref, exact_ref, lse_ref):
    block = out_ref.shape[0]
    lane = lax.broadcasted_iota(jnp.int32, (block, 128), 1)
    rows = jnp.zeros((block, 128), f32)
    inverse = []
    for h in range(heads):
        total = jnp.sum(l_ref[h], axis=1, keepdims=True)
        rows = jnp.where(lane == h, m_ref[h][:, :1] + jnp.log(total), rows)
        inverse.append(jnp.broadcast_to(1.0 / total, (block, 128)))
    result = acc_ref[...] * pack_heads(inverse)
    out_ref[...] = result.astype(bf16)
    exact_ref[...] = result
    lse_ref[...] = rows.T[:8, :]


def mask_values(v_ref, vm_ref, heads, block):
    for j in range(v_ref.shape[0] // block):
        value = v_ref[j * block : (j + 1) * block, :]
        for h in range(heads):
            vm_ref[j, h * block : (h + 1) * block, :] = head_lanes(value, h)


def attend_forward_kernel(heads, comm, lens_ref, q_ref, k_ref, v_ref, *refs):
    ins, refs = refs[: comm.ins], refs[comm.ins :]
    out_ref, exact_ref, lse_ref, big_ref = refs[:4]
    outs = refs[4 : 4 + comm.outs]
    vm_ref, m_ref, l_ref, acc_ref = refs[4 + comm.outs : 8 + comm.outs]
    sems = refs[8 + comm.outs :]
    step = pl.program_id(1)
    block = q_ref.shape[0]
    comm.before(pl.program_id(0) * pl.num_programs(1) + step, ins, outs, sems)

    @pl.when(step == 0)
    def _():
        mask_values(v_ref, vm_ref, heads, block)

    @pl.when((step == 0) & (pl.program_id(0) == 0))
    def _():
        big_ref[...] = jnp.zeros(big_ref.shape, f32)

    query = q_ref[...] * jnp.asarray(score_scale, bf16)
    masked = [head_lanes(query, h) for h in range(heads)]

    def key_block(j):
        return k_ref[pl.ds(pl.multiple_of(j * block, block), block), :]

    attend_block(masked, key_block(step), vm_ref[step], m_ref, l_ref, acc_ref)
    away = jnp.where(lens_ref[0] == LONG_LEN, 0.0, 1e30).astype(f32)

    def earlier(j, carry):
        keys = key_block(j)
        low = []
        for h in range(heads):
            parts, total = block_probs(dot_nt(masked[h], keys), m_ref[h] + away)
            l_ref[h] += total
            low += parts
        acc_ref[...] += dot_nn(jnp.concatenate(low, axis=1), vm_ref[j])
        return carry

    lax.fori_loop(0, step, earlier, 0)
    for h in range(heads):
        big_ref[...] = jnp.maximum(
            big_ref[...], jnp.max(l_ref[h].reshape(-1, 8, 128), axis=0)
        )
    attend_finish(heads, m_ref, l_ref, acc_ref, out_ref, exact_ref, lse_ref)
    comm.after(pl.program_id(0) * pl.num_programs(1) + step, ins, outs, sems)


def attend_safe_kernel(
    heads,
    groups,
    lens_ref,
    big_ref,
    packed,
    low_in,
    exact_in,
    lse_in,
    low,
    exact,
    lse,
    q_ref,
    k_ref,
    v_ref,
    out_ref,
    exact_ref,
    lse_ref,
    vm_ref,
    m_ref,
    l_ref,
    acc_ref,
    sem,
):
    block, cols = q_ref.shape
    tokens = k_ref.shape[0]

    def fetch(src, dst):
        copy = pltpu.make_async_copy(src, dst, sem)
        copy.start()
        copy.wait()

    def one_query(group, step):
        rows = pl.ds(pl.multiple_of(step * block, block), block)
        here = pl.ds(group * cols, cols)
        fetch(packed.at[rows, here], q_ref)
        query = q_ref[...] * jnp.asarray(score_scale, bf16)
        masked = [head_lanes(query, h) for h in range(heads)]

        def key_block(j):
            return k_ref[pl.ds(pl.multiple_of(j * block, block), block), :]

        attend_block(masked, key_block(step), vm_ref[step], m_ref, l_ref, acc_ref)

        def earlier(j, carry):
            keys = key_block(j)
            parts_all, shrink = [], []
            for h in range(heads):
                scores = dot_nt(masked[h], keys)
                old = m_ref[h]
                top = jnp.maximum(old, jnp.max(scores, axis=1, keepdims=True))
                factor = jnp.exp(old - top)
                m_ref[h] = top
                parts, total = block_probs(scores, top)
                l_ref[h] = l_ref[h] * factor + total
                parts_all += parts
                shrink.append(factor)
            acc_ref[...] = acc_ref[...] * pack_heads(shrink) + dot_nn(
                jnp.concatenate(parts_all, axis=1), vm_ref[j]
            )
            return carry

        lax.fori_loop(0, jnp.where(lens_ref[0] == LONG_LEN, step, 0), earlier, 0)
        attend_finish(heads, m_ref, l_ref, acc_ref, out_ref, exact_ref, lse_ref)
        fetch(out_ref, low.at[rows, here])
        fetch(exact_ref, exact.at[rows, here])
        fetch(lse_ref, lse.at[pl.ds(group * 8, 8), rows])

    @pl.when(jnp.logical_not(jnp.max(big_ref[...]) < safe_sum))
    def _():
        for group in range(groups):
            fetch(packed.at[:, pl.ds((groups + group) * cols, cols)], k_ref)
            fetch(packed.at[:, pl.ds((2 * groups + group) * cols, cols)], v_ref)
            mask_values(v_ref, vm_ref, heads, block)
            lax.fori_loop(
                0, tokens // block, lambda i, c, group=group: (one_query(group, i), c)[1], 0
            )


class NoTransfers:
    ins = outs = 0

    def before(self, *args):
        pass

    def after(self, *args):
        pass


def attend_specs(tokens, width):
    groups = width // min(256, width)
    cols = width // groups
    ins = [
        pl.BlockSpec((BT, cols), lambda g, i, n: (i, g)),
        pl.BlockSpec((tokens, cols), lambda g, i, n: (0, groups + g)),
        pl.BlockSpec((tokens, cols), lambda g, i, n: (0, 2 * groups + g)),
    ]
    outs = [
        pl.BlockSpec((BT, cols), lambda g, i, n: (i, g)),
        pl.BlockSpec((BT, cols), lambda g, i, n: (i, g)),
        pl.BlockSpec((8, BT), lambda g, i, n: (g, i)),
    ]
    shapes = [
        jax.ShapeDtypeStruct((tokens, width), bf16),
        jax.ShapeDtypeStruct((tokens, width), f32),
        jax.ShapeDtypeStruct((8 * groups, tokens), f32),
    ]
    heads = cols // HD
    scratch = [
        pltpu.VMEM((tokens // BT, heads * BT, cols), bf16),
        pltpu.VMEM((heads, BT, 128), f32),
        pltpu.VMEM((heads, BT, 128), f32),
        pltpu.VMEM((BT, cols), f32),
    ]
    return groups, heads, ins, outs, shapes, scratch


def attend_cost(tokens, width, products):
    pairs = (tokens // BT) * (tokens // BT + 1) // 2
    work = products * 2 * pairs * BT * BT * width
    return cost(4 * work, 10 * tokens * width, pairs * BT * BT * width // HD)


def attend_safe(packed, lengths, big, low, exact, lse):
    tokens, width = packed.shape[0], packed.shape[1] // 3
    groups, heads, _, _, shapes, scratch = attend_specs(tokens, width)
    cols = width // groups
    return pl.pallas_call(
        functools.partial(attend_safe_kernel, heads, groups),
        grid_spec=pltpu.PrefetchScalarGridSpec(
            num_scalar_prefetch=1,
            grid=(1,),
            in_specs=[pl.BlockSpec((8, 128), lambda i, n: (0, 0))] + [ANY] * 4,
            out_specs=[ANY] * 3,
            scratch_shapes=[
                pltpu.VMEM((BT, cols), bf16),
                pltpu.VMEM((tokens, cols), bf16),
                pltpu.VMEM((tokens, cols), bf16),
                pltpu.VMEM((BT, cols), bf16),
                pltpu.VMEM((BT, cols), f32),
                pltpu.VMEM((8, BT), f32),
            ]
            + scratch
            + [pltpu.SemaphoreType.DMA(())],
        ),
        out_shape=shapes,
        input_output_aliases={3: 0, 4: 1, 5: 2},
        compiler_params=params(1),
        cost_estimate=cost(1000, 100000),
        name="attend_safe",
    )(lengths, big, packed, low, exact, lse)


def attend_forward(packed, lengths, comm=NoTransfers(), moved=(), fresh=None):
    tokens, width = packed.shape[0], packed.shape[1] // 3
    groups, heads, ins, outs, shapes, scratch = attend_specs(tokens, width)
    low, exact, lse, big, *rest = pl.pallas_call(
        functools.partial(attend_forward_kernel, heads, comm),
        grid_spec=pltpu.PrefetchScalarGridSpec(
            num_scalar_prefetch=1,
            grid=(groups, tokens // BT),
            in_specs=ins + [ANY] * len(moved),
            out_specs=outs
            + [pl.BlockSpec((8, 128), lambda g, i, n: (0, 0))]
            + [ANY] * comm.outs,
            scratch_shapes=scratch + (comm.scratch() if moved else []),
        ),
        out_shape=shapes
        + [jax.ShapeDtypeStruct((8, 128), f32)]
        + [jax.ShapeDtypeStruct(m.shape, m.dtype) for m in moved[1:]]
        + ([fresh] if moved else []),
        input_output_aliases={5: 4} if moved else {},
        compiler_params=params(2, 2 if moved else None),
        cost_estimate=attend_cost(tokens, width, 2),
        name="attend_forward",
    )(lengths, packed, packed, packed, *moved)
    low, exact, lse = attend_safe(packed, lengths, big, low, exact, lse)
    return [low, exact, lse] + rest


def attend_backward_kernel(heads, comm, lens_ref, q_ref, k_ref, v_ref, do_ref, lse_ref, delta_ref, *refs):
    ins, refs = refs[: comm.ins], refs[comm.ins :]
    dq_ref, dk_ref, dv_ref = refs[:3]
    outs, refs = refs[3 : 3 + comm.outs], refs[3 + comm.outs :]
    qm_ref, dom_ref, km_ref, vm_ref, dqa_ref, dka_ref, dva_ref = refs[:7]
    scratch = refs[7:]
    step = pl.program_id(1)
    count = pl.num_programs(1)
    block = k_ref.shape[0]
    comm.before(pl.program_id(0) * count + step, ins, outs, scratch)

    @pl.when(step == 0)
    def _():
        for t in range(q_ref.shape[0] // block):
            rows = slice(t * block, (t + 1) * block)
            for h in range(heads):
                place = slice(h * block, (h + 1) * block)
                qm_ref[t, place, :] = head_lanes(q_ref[rows, :], h)
                dom_ref[t, place, :] = head_lanes(do_ref[rows, :], h)
        dqa_ref[...] = jnp.zeros(dqa_ref.shape, f32)

    for h in range(heads):
        place = slice(h * block, (h + 1) * block)
        km_ref[place, :] = head_lanes(k_ref[...] * jnp.asarray(score_scale, bf16), h)
        vm_ref[place, :] = head_lanes(v_ref[...], h)
    dka_ref[...] = jnp.zeros(dka_ref.shape, f32)
    dva_ref[...] = jnp.zeros(dva_ref.shape, f32)
    away = jnp.where(lens_ref[0] == LONG_LEN, 0.0, 1e30).astype(f32)

    def pair(i, first, count, seen, on_diagonal):
        rows = pl.ds(pl.multiple_of(i * block + first, count), count)
        query, grad = q_ref[rows, :], do_ref[rows, :]
        low, slopes = [], []
        for h in range(heads):
            place = slice(h * block, h * block + seen)
            scores = dot_nt(km_ref[place, :], query)
            logs = lse_ref[h : h + 1, rows]
            if not on_diagonal:
                logs = logs + away
            prob = jnp.exp(scores - logs)
            if on_diagonal:
                key = lax.broadcasted_iota(jnp.int32, scores.shape, 0)
                tok = lax.broadcasted_iota(jnp.int32, scores.shape, 1) + first
                prob = jnp.where(tok >= key, prob, 0.0)
            grad_prob = dot_nt(vm_ref[place, :], grad)
            slope = prob * (grad_prob - delta_ref[h : h + 1, rows])
            low.append(prob.astype(bf16))
            slopes.append(slope.astype(bf16))
        if on_diagonal:
            grads = head_rows(dom_ref[i], heads, first, count)
            queries = head_rows(qm_ref[i], heads, first, count)
            keys = head_rows(km_ref[...], heads, 0, seen)
        else:
            grads, queries, keys = dom_ref[i], qm_ref[i], km_ref[...]
        dva_ref[0:seen, :] += dot_nn(jnp.concatenate(low, axis=1), grads)
        dka_ref[0:seen, :] += dot_nn(jnp.concatenate(slopes, axis=1), queries)
        dqa_ref[rows, :] += dot_tn(jnp.concatenate(slopes, axis=0), keys)

    half = block // 2
    pair(step, 0, half, half, True)
    pair(step, half, half, block, True)
    lax.fori_loop(step + 1, count, lambda i, c: (pair(i, 0, block, block, False), c)[1], 0)
    dk_ref[...] = (dka_ref[...] * score_scale).astype(bf16)
    dv_ref[...] = dva_ref[...].astype(bf16)

    @pl.when(step == count - 1)
    def _():
        dq_ref[...] = dqa_ref[...].astype(bf16)

    comm.after(pl.program_id(0) * count + step, ins, outs, scratch)


def attend_backward(packed, grad_attended, lse, delta, lengths, comm=NoTransfers(), moved=()):
    tokens, width = grad_attended.shape
    groups = width // min(256, width)
    cols = width // groups
    heads = cols // HD
    blocks = tokens // BT
    column = pl.BlockSpec((tokens, cols), lambda g, j, n: (0, g))
    stats = pl.BlockSpec((8, tokens), lambda g, j, n: (g, 0))
    tile = pl.BlockSpec((BT, cols), lambda g, j, n: (j, g))
    move_ins, move_outs, move_shapes, move_scratch = comm.specs(moved) if moved else ([], [], [], [])
    return pl.pallas_call(
        functools.partial(attend_backward_kernel, heads, comm),
        grid_spec=pltpu.PrefetchScalarGridSpec(
            num_scalar_prefetch=1,
            grid=(groups, blocks),
            in_specs=[
                column,
                pl.BlockSpec((BT, cols), lambda g, j, n: (j, groups + g)),
                pl.BlockSpec((BT, cols), lambda g, j, n: (j, 2 * groups + g)),
                column,
                stats,
                stats,
            ]
            + move_ins,
            out_specs=[column, tile, tile] + move_outs,
            scratch_shapes=[
                pltpu.VMEM((blocks, heads * BT, cols), bf16),
                pltpu.VMEM((blocks, heads * BT, cols), bf16),
                pltpu.VMEM((heads * BT, cols), bf16),
                pltpu.VMEM((heads * BT, cols), bf16),
                pltpu.VMEM((tokens, cols), f32),
                pltpu.VMEM((BT, cols), f32),
                pltpu.VMEM((BT, cols), f32),
            ]
            + move_scratch,
        ),
        out_shape=[jax.ShapeDtypeStruct((tokens, width), bf16)] * 3 + move_shapes,
        compiler_params=params(2, 3 if moved else None),
        cost_estimate=attend_cost(tokens, width, 5),
        name="attend_backward",
    )(lengths, packed, packed, packed, grad_attended, lse, delta, *moved)


class AttendGather:
    ins, outs = 2, 2

    def scratch(self):
        return gather_sems(4)

    def pieces(self, ins, outs):
        up = [(None, outs[0], (at, width), route) for at, width, route in halves(outs[0].shape[3])]
        down = [(ins[0], outs[1], (at, width), route) for at, width, route in halves(ins[0].shape[1])]
        return up + down

    def hops(self, name, ks, ins, outs, sems):
        copies = []
        for k in ks:
            src, dst, span, route = self.pieces(ins, outs)[k]
            if name == "z":
                copies += gather_z(src, dst, span, sems, 6 * k)
            elif name == "second":
                copies += gather_second(dst, span, route, sems, 6 * k)
            else:
                copies += gather_third(dst, span, route, sems, 6 * k)
        return copies

    def before(self, step, ins, outs, sems):
        def hops(name, ks):
            return self.hops(name, ks, ins, outs, sems)

        @pl.when(step == 0)
        def _():
            greet(False)
            start_all(hops("z", (2, 3)))
            start_all(hops("second", (0, 1)))

        @pl.when(step == 3)
        def _():
            wait_all(hops("second", (0, 1)))
            start_all(hops("third", (0, 1)))

        @pl.when(step == 6)
        def _():
            wait_all(hops("z", (2, 3)))
            start_all(hops("second", (2, 3)))

        @pl.when(step == 9)
        def _():
            wait_all(hops("second", (2, 3)))
            start_all(hops("third", (2, 3)))

    def after(self, step, ins, outs, sems):
        @pl.when(step == 11)
        def _():
            wait_all(self.hops("third", (0, 1, 2, 3), ins, outs, sems))


class SumPart:
    slots = 5

    def __init__(self, grad, span, route, refs, sems, base):
        self.keep = grad.at[pl.ds(0, 512), pl.ds(*span)]
        self.sent = grad.at[pl.ds(512, 512), pl.ds(*span)]
        self.held, self.got_1, self.got_2, self.got_3 = refs
        self.sems, self.base = sems, base
        self.hops = ((2, 1), (1, 2))[route]

    @staticmethod
    def buffers(width):
        return [
            pltpu.VMEM((512, width), bf16),
            pltpu.VMEM((512, width), bf16),
            pltpu.VMEM((256, width), bf16),
            pltpu.VMEM((3, 64, width), bf16),
        ]

    def first(self):
        return [
            send(self.sent, self.got_1, self.sems, self.base, across(self.hops[0])),
            pltpu.make_async_copy(self.keep, self.held, self.sems[2].at[self.base]),
        ]

    def second(self):
        return [
            send(
                self.held.at[pl.ds(256, 256), :],
                self.got_2,
                self.sems,
                self.base + 1,
                across(self.hops[1]),
            )
        ]

    def third(self):
        return [
            send(
                self.held.at[pl.ds(64 * z, 64), :],
                self.got_3.at[z - 1],
                self.sems,
                self.base + 1 + z,
                across(4 * z),
            )
            for z in (1, 2, 3)
        ]

    def add(self, other, rows):
        def body(i, carry):
            at = pl.ds(pl.multiple_of(i * 64, 64), 64)
            self.held[at, :] = self.held[at, :] + other[at, :]
            return carry

        lax.fori_loop(0, rows // 64, body, 0)

    def to_second(self):
        wait_all(self.first())
        self.add(self.got_1, 512)
        start_all(self.second())

    def to_third(self):
        wait_all(self.second())
        self.add(self.got_2, 256)
        start_all(self.third())

    def result(self):
        wait_all(self.third())
        total = self.held[0:64, :].astype(f32)
        for z in range(3):
            total = total + self.got_3[z].astype(f32)
        return total


def sum_sems(parts):
    return [
        pltpu.SemaphoreType.DMA((SumPart.slots * parts,)),
        pltpu.SemaphoreType.DMA((SumPart.slots * parts,)),
        pltpu.SemaphoreType.DMA((SumPart.slots * parts,)),
    ]


class SmallSum:
    def __init__(self, refs, sems):
        self.got, self.sems = refs, sems

    @staticmethod
    def scratch():
        return [
            pltpu.VMEM((8, 8, 1024), f32),
            pltpu.VMEM((4, 8, 1024), f32),
            pltpu.SemaphoreType.DMA((10,)),
            pltpu.SemaphoreType.DMA((10,)),
        ]

    def near(self):
        bits = bits_of_me()
        place = self.got[0].at[lax.axis_index("mp") * 4 + bits[2] * 2 + bits[3]]
        devices = [across(k) for k in (1, 2, 3)] + [sibling()]
        devices += [sibling_across(k) for k in (1, 2, 3)]
        return [send(place, place, self.sems, k, device) for k, device in enumerate(devices)]

    def far(self):
        bits = bits_of_me()
        place = self.got[1].at[bits[0] * 2 + bits[1]]
        return [send(place, place, self.sems, 6 + k, across(4 * k)) for k in (1, 2, 3)]

    def begin(self, rows):
        bits = bits_of_me()
        self.got[0][lax.axis_index("mp") * 4 + bits[2] * 2 + bits[3]] = rows
        start_all(self.near())

    def middle(self, both):
        wait_all(self.near())
        row = lax.broadcasted_iota(jnp.int32, (8, 1024), 0)
        total = jnp.zeros((8, 1024), f32)
        for k in range(8):
            counts = (row < both) | (lax.axis_index("mp") == k // 4)
            total = total + jnp.where(counts, self.got[0][k], 0.0)
        bits = bits_of_me()
        self.got[1][bits[0] * 2 + bits[1]] = total
        start_all(self.far())

    def end(self):
        wait_all(self.far())
        return (self.got[1][0] + self.got[1][1]) + (self.got[1][2] + self.got[1][3])


class BackwardSum:
    def __init__(self, cols):
        self.cols = cols
        self.ins = len(cols) + 1
        self.outs = len(cols) + 1

    def specs(self, moved):
        vmem = [pl.BlockSpec((8, 1024), lambda g, j, n: (0, 0))]
        sizes = [(64, c) for c in self.cols]
        shapes = [jax.ShapeDtypeStruct(size, f32) for size in sizes]
        outs = [pl.BlockSpec(size, lambda g, j, n: (0, 0)) for size in sizes]
        scratch = []
        for c in self.cols:
            scratch += SumPart.buffers(c // 2) * 2
        scratch += sum_sems(2 * len(self.cols)) + SmallSum.scratch()
        return (
            [ANY] * len(self.cols) + vmem,
            outs + vmem,
            shapes + [jax.ShapeDtypeStruct((8, 1024), f32)],
            scratch,
        )

    def parts(self, ins, scratch):
        count = 2 * len(self.cols)
        sems = scratch[4 * count : 4 * count + 3]
        made = []
        for k in range(count):
            width = self.cols[k // 2] // 2
            refs = scratch[4 * k : 4 * k + 4]
            span = ((k % 2) * width, width)
            made.append(SumPart(ins[k // 2], span, k % 2, refs, sems, SumPart.slots * k))
        rest = scratch[4 * count + 3 :]
        return made, SmallSum(rest[:2], rest[2:])

    def before(self, step, ins, outs, scratch):
        parts, small = self.parts(ins, scratch)

        @pl.when(step == 0)
        def _():
            greet(True)
            small.begin(ins[-1][...])
            for part in parts[:2] + parts[4:]:
                start_all(part.first())

        @pl.when(step == 1)
        def _():
            small.middle(4)

        @pl.when(step == 2)
        def _():
            for part in parts[:2] + parts[4:]:
                part.to_second()
            for part in parts[2:4]:
                start_all(part.first())

        @pl.when(step == 5)
        def _():
            outs[-1][...] = small.end()

        @pl.when(step == 6)
        def _():
            for part in parts[:2] + parts[4:]:
                part.to_third()

        @pl.when(step == 7)
        def _():
            for part in parts[2:4]:
                part.to_second()

        @pl.when(step == 8)
        def _():
            for part in parts[2:4]:
                part.to_third()

    def after(self, step, ins, outs, scratch):
        parts, _ = self.parts(ins, scratch)

        @pl.when(step == 11)
        def _():
            for k, part in enumerate(parts):
                width = self.cols[k // 2] // 2
                span = slice((k % 2) * width, (k % 2 + 1) * width)
                outs[k // 2][:, span] = part.result()


def normalized(values):
    average = jnp.mean(values, axis=-1, keepdims=True)
    centred = values - average
    variance = jnp.mean(centred * centred, axis=-1, keepdims=True)
    inverse = lax.rsqrt(variance + norm_eps)
    return centred * inverse, inverse


def column_sum(values):
    return jnp.sum(values.reshape(-1, 8, values.shape[-1]), axis=0)


def turned(values, out_ref):
    flip = values.T
    bits = bits_of_me()
    for a in range(16):
        r = flipped(bits, a)
        slot = r[2] * 8 + r[3] * 4 + r[0] * 2 + r[1]
        out_ref[pl.ds(pl.multiple_of(slot * 64, 64), 64), :] = flip[a * 64 : (a + 1) * 64, :]


def shape(rows, cols, dtype=bf16):
    return jax.ShapeDtypeStruct((rows, cols), dtype)


def row_tile(cols):
    return pl.BlockSpec((BT, cols), lambda i: (i, 0))


def col_tile(rows):
    return pl.BlockSpec((rows, BT), lambda i: (0, i))


def whole(rows, cols):
    return pl.BlockSpec((rows, cols), lambda i: (0, 0))


def weight(cols):
    return pl.BlockSpec((1024, cols), lambda i: (0, 0), pipeline_mode=pl.Buffered(1))


def my_side():
    return lax.axis_index("mp")


def grid_call(kernel, steps, ins, outs, scratch, flops, name, collective=None, aliases={}):
    arrays = [a for a, _ in ins]
    nbytes = sum(a.size * a.dtype.itemsize for a in arrays)
    nbytes += sum(o.size * o.dtype.itemsize for o, _ in outs)
    return pl.pallas_call(
        kernel,
        grid=(steps,),
        in_specs=[s for _, s in ins],
        out_specs=[s for _, s in outs],
        scratch_shapes=scratch,
        out_shape=[o for o, _ in outs],
        input_output_aliases=aliases,
        compiler_params=params(1, collective),
        cost_estimate=cost(flops, nbytes),
        name=name,
    )(*arrays)


GAIN_ONE, SHIFT_ONE, BIAS_OUT, GAIN_TWO, SHIFT_TWO, BIAS_DOWN, BIAS_UP = range(7)


VECTORS = 9


def row_of(vectors, at, cols=slice(0, 1024)):
    parts = []
    for k in range(cols.start // 1024, (cols.stop + 1023) // 1024):
        low, high = max(cols.start, 1024 * k), min(cols.stop, 1024 * k + 1024)
        parts.append(vectors[at + k : at + k + 1, low - 1024 * k : high - 1024 * k])
    return parts[0] if len(parts) == 1 else jnp.concatenate(parts, axis=1)


def qkv_bias(vectors, cols):
    last = vectors[VECTORS - 1 : VECTORS, :]
    half = last.shape[1] // 2
    zero = jnp.zeros((1, half), f32)
    return jnp.concatenate([last[:, :half], zero, last[:, half:]], axis=1)[:, cols]


class FirstGather:
    def __init__(self, wq, up, up_out, wo, out_out, sems):
        self.pieces = [(None, wq, (at, width), r) for at, width, r in chunk_halves(wq.shape[3])]
        self.pieces += [(up, up_out, (at, width), r) for at, width, r in halves(up.shape[1])]
        self.pieces += [(wo, out_out, (at, width), r) for at, width, r in halves(wo.shape[1])]
        self.sems = sems

    def z(self, *ks):
        copies = []
        for k in ks:
            src, dst, span, _ = self.pieces[k]
            if src is None:
                bits = bits_of_me()
                place = dst.at[bits[0] * 2 + bits[1], bits[2] * 2 + bits[3], :, pl.ds(*span)]
                copies += [
                    send(place, place, self.sems, 6 * k + hop, across(4 * (hop + 1)))
                    for hop in range(3)
                ]
            else:
                copies += gather_z(src, dst, span, self.sems, 6 * k)
        return copies

    def second(self, *ks):
        copies = []
        for k in ks:
            _, dst, span, route = self.pieces[k]
            copies += gather_second(dst, span, route, self.sems, 6 * k)
        return copies

    def third(self, *ks):
        copies = []
        for k in ks:
            _, dst, span, route = self.pieces[k]
            copies += gather_third(dst, span, route, self.sems, 6 * k)
        return copies


def chunk_halves(cols):
    width = cols // 4
    return [(k * width, width, k % 2) for k in range(4)]


def qkv_kernel(
    tiles,
    own,
    own_all,
    vectors,
    w_mine,
    wo,
    up,
    turned_out,
    out,
    up_out,
    out_out,
    w_out,
    normed,
    came,
    wq,
    swap_send,
    swap_came,
    copy_sem,
    *sems,
):
    step = pl.program_id(0)
    side = my_side()
    moves = FirstGather(wq, up, up_out, wo, out_out, sems)
    local = w_mine.shape[2]

    def swap(k):
        return send(
            own_all.at[pl.ds(k * BT, BT), :], came.at[k], (swap_send, swap_came), k, sibling()
        )

    @pl.when(step == 0)
    def _():
        bits = bits_of_me()
        for c in range(3):
            wq[bits[0] * 2 + bits[1], bits[2] * 2 + bits[3], :, c * local : (c + 1) * local] = (
                w_mine[c]
            )
        greet(True)
        start_all(moves.z(0, 1))
        start_all([swap(k) for k in range(tiles)])

    def norm(values):
        scaled, _ = normalized(values.astype(f32))
        rows = (scaled * row_of(vectors, GAIN_ONE) + row_of(vectors, SHIFT_ONE)).astype(bf16)
        first = lax.rem(step + side * tiles, 2 * tiles) * BT
        normed[pl.ds(pl.multiple_of(first, BT), BT), :] = rows
        turned(rows, turned_out)

    @pl.when(step < tiles)
    def _():
        norm(own[...])

    for k in range(tiles):

        @pl.when(step == tiles + k)
        def _():
            swap(k).wait()
            norm(came[k])

    @pl.when(step == 2 * tiles - 2)
    def _():
        wait_all(moves.z(0, 1))
        start_all(moves.second(0, 1))
        start_all(moves.z(2, 3))

    @pl.when(step == 2 * tiles)
    def _():
        wait_all(moves.second(0, 1))
        start_all(moves.third(0, 1))
        wait_all(moves.z(2, 3))
        start_all(moves.z(6, 7))
        start_all(moves.z(4, 5))
        wait_all(moves.third(0, 1))
        start_all(moves.second(2, 3))

    @pl.when(step == 2 * tiles + 2)
    def _():
        wait_all(moves.second(2, 3))
        start_all(moves.third(2, 3))
        wait_all(moves.z(6, 7))

    half = out.shape[1]
    for c in range(2):

        @pl.when((step >= (2 + 2 * c) * tiles) & (step < (4 + 2 * c) * tiles))
        def _():
            @pl.when(step == (2 + 2 * c) * tiles)
            def _():
                if c:
                    wait_all(moves.third(2, 3))
                    start_all(moves.second(6, 7))
                    pltpu.make_async_copy(wq, w_out, copy_sem).start()

            first = (step - (2 + 2 * c) * tiles) * BT
            rows = normed[pl.ds(pl.multiple_of(first, BT), BT), :]
            cols = slice(c * half, (c + 1) * half)
            part = wq[:, :, :, cols].reshape(1024, half)
            out[...] = (dot_nn(rows, part) + qkv_bias(vectors, cols)).astype(bf16)

    @pl.when(step == 5 * tiles)
    def _():
        wait_all(moves.second(6, 7))
        start_all(moves.third(6, 7))

    @pl.when(step == 6 * tiles - 1)
    def _():
        wait_all(moves.third(6, 7))
        wait_all(moves.z(4, 5))
        pltpu.make_async_copy(wq, w_out, copy_sem).wait()


def project_kernel(tiles, a, w, toks, vectors, hid_out, normed_out, sent, came, sent_sems, came_sems):
    step = pl.program_id(0)

    def swap(k):
        return send(sent.at[k], came.at[k], (sent_sems, came_sems), k, sibling())

    @pl.when(step == 0)
    def _():
        greet_sibling()

    partial = dot_nt(a[...], w[...])
    for k in range(tiles):

        @pl.when(step == k)
        def _():
            sent[k] = partial.astype(bf16)
            swap(k).start()

        @pl.when(step == tiles + k)
        def _():
            swap(k).wait()
            bias = row_of(vectors, BIAS_OUT)
            hidden = toks[...].astype(f32) + (partial + came[k].astype(f32) + bias)
            hid_out[...] = hidden
            scaled, _ = normalized(hidden)
            normed_out[...] = (
                scaled * row_of(vectors, GAIN_TWO) + row_of(vectors, SHIFT_TWO)
            ).astype(bf16)


def feed_kernel(
    tiles,
    x_all,
    c_all,
    vectors,
    wu,
    wd,
    ffn_own,
    norm_own,
    ffn_came,
    norm_came,
    up_out,
    down_out,
    bsum,
    up_total,
    down_total,
    act,
    gpre,
    xt,
    ct,
    xs,
    cs,
    ffn_sent,
    norm_sent,
    local_sems,
    send_sems,
    came_sems,
    out_sems,
):
    step = pl.program_id(0)
    remote = (send_sems, came_sems)

    def rows(k):
        return pl.ds(k * BT, BT)

    def local(k):
        return [
            pltpu.make_async_copy(x_all.at[rows(k), :], xs.at[k], local_sems.at[k]),
            pltpu.make_async_copy(c_all.at[rows(k), :], cs.at[k], local_sems.at[tiles + k]),
        ]

    def swapped(k):
        return [
            send(x_all.at[rows(k), :], xs.at[tiles + k], remote, k, sibling()),
            send(c_all.at[rows(k), :], cs.at[tiles + k], remote, tiles + k, sibling()),
        ]

    def returned(k):
        return [
            send(ffn_sent, ffn_came.at[rows(k), :], remote, 2 * tiles + k, sibling()),
            send(norm_sent, norm_came.at[rows(k), :], remote, 3 * tiles + k, sibling()),
        ]

    @pl.when(step == 0)
    def _():
        for k in range(tiles):
            start_all(local(k))
        bsum[...] = jnp.zeros(bsum.shape, f32)
        greet_sibling()
        for k in range(tiles):
            start_all(swapped(k))

    for k in range(tiles):

        @pl.when(step == k)
        def _():
            wait_all(local(k))

        @pl.when(step == tiles + k)
        def _():
            wait_all(swapped(k))

    x, c = xs[step], cs[step]
    xt[...] = x.T
    ct[...] = c.T
    width = 512
    spans = [slice(at, at + width) for at in range(0, wu.shape[1], width)]
    for cols in spans:
        value = dot_nn(x, wu[:, cols]) + row_of(vectors, BIAS_UP, cols)
        upstream = dot_nn(c, wd[:, cols])
        square = value * value
        bent = jnp.tanh(value * (gelu_coeff + (gelu_coeff * 0.044715) * square))
        half_up = 0.5 + 0.5 * bent
        act[:, cols] = (value * half_up).astype(bf16)
        slope = half_up + value * (half_up * (1.0 - bent)) * (
            gelu_coeff + (3.0 * 0.044715 * gelu_coeff) * square
        )
        grad = (upstream * slope).astype(bf16)
        gpre[:, cols] = grad
        bsum[:, cols] += column_sum(grad.astype(f32))
    ffn = dot_nt(act[...], wd[...]).astype(bf16)
    norm = dot_nt(gpre[...], wu[...]).astype(bf16)

    @pl.when(step < tiles)
    def _():
        ffn_own[...] = ffn
        norm_own[...] = norm

    for k in range(tiles):

        @pl.when(step == tiles + k)
        def _():
            if k:
                wait_all(returned(k - 1))
            ffn_sent[...] = ffn
            norm_sent[...] = norm
            start_all(returned(k))

    @pl.when(step == 0)
    def _():
        for cols in spans:
            down_total[:, cols] = dot_nn(ct[...], act[:, cols])
        for cols in spans:
            up_total[:, cols] = dot_nn(xt[...], gpre[:, cols])

    @pl.when(step > 0)
    def _():
        for cols in spans:
            down_total[:, cols] += dot_nn(ct[...], act[:, cols])
        for cols in spans:
            up_total[:, cols] += dot_nn(xt[...], gpre[:, cols])

    def leave(total, stage, out, base):
        half = total.shape[1] // 2
        bits = bits_of_me()
        copies = []
        for top in range(2):
            for route in range(2):
                part = total[512 * top : 512 * top + 512, route * half : route * half + half]
                stage[top * 2 + route] = part.astype(bf16)
        for a in range(16):
            r = flipped(bits, a)
            for route in range(2):
                slot = r[2 + route] * 8 + r[3 - route] * 4 + r[0] * 2 + r[1]
                copies.append(
                    pltpu.make_async_copy(
                        stage.at[(a // 8) * 2 + route, pl.ds((a % 8) * 64, 64), :],
                        out.at[
                            pl.ds(pl.multiple_of(slot * 64, 64), 64), pl.ds(route * half, half)
                        ],
                        out_sems.at[base + 2 * a + route],
                    )
                )
        start_all(copies)
        return copies

    @pl.when(step == 2 * tiles - 1)
    def _():
        copies = leave(down_total, cs, down_out, 0)
        copies += leave(up_total, xs, up_out, 32)
        wait_all(copies)
        wait_all(returned(tiles - 1))


def middle_kernel(
    tiles,
    hid,
    f_own,
    f_came,
    g_own,
    g_came,
    cot,
    vectors,
    exact,
    attended,
    w,
    out,
    gattn,
    do_out,
    delta_out,
    grad_w,
    sums,
    turned_rows,
    total,
    now,
    sent,
    came,
    sent_sems,
    came_sems,
):
    step = pl.program_id(0)

    def swap(k):
        return send(sent.at[k], came.at[k], (sent_sems, came_sems), k, sibling())

    @pl.when(step == 0)
    def _():
        sums[...] = jnp.zeros(sums.shape, f32)
        total[...] = jnp.zeros(total.shape, f32)
        greet_sibling()

    @pl.when(step < tiles)
    def _():
        hidden = hid[...]
        grad_out = cot[...].astype(f32)
        branch = f_own[...].astype(f32) + f_came[...].astype(f32) + row_of(vectors, BIAS_DOWN)
        out[...] = (hidden + branch).astype(bf16)
        scaled, inverse = normalized(hidden)
        grad_norm = g_own[...].astype(f32) + g_came[...].astype(f32)
        through = grad_norm * row_of(vectors, GAIN_TWO)
        centre = jnp.mean(through, axis=-1, keepdims=True)
        along = jnp.mean(through * scaled, axis=-1, keepdims=True)
        grad = (grad_out + inverse * (through - centre - scaled * along)).astype(bf16)
        gattn[...] = grad
        now[...] = grad
        sums[0:8, :] += column_sum(grad_norm * scaled)
        sums[8:16, :] += column_sum(grad_norm)
        sums[16:24, :] += column_sum(grad.astype(f32))
        sums[24:32, :] += column_sum(grad_out)

    for k in range(tiles):

        @pl.when(step == k)
        def _():
            sent[k] = now[...]
            swap(k).start()

        @pl.when(step == tiles + k)
        def _():
            swap(k).wait()
            now[...] = came[k]

    grad = now[...]
    turned(grad, turned_rows)
    part = dot_nn(grad, w[...]).astype(bf16)
    do_out[...] = part
    product = part.astype(f32) * exact[...]
    head = lax.broadcasted_iota(jnp.int32, (part.shape[1], 128), 0) // HD
    place = lax.broadcasted_iota(jnp.int32, (part.shape[1], 128), 1)
    pick = jnp.where(place == (head // 4) * 8 + head % 4, 1.0, 0.0).astype(bf16)
    high = product.astype(bf16)
    rest = (product - high.astype(f32)).astype(bf16)
    delta_out[...] = (dot_nn(high, pick) + dot_nn(rest, pick)).T[:16, :]
    total[...] += dot_nn(turned_rows[...], attended[...])

    @pl.when(step == 2 * tiles - 1)
    def _():
        write_grad(total, grad_w)


def write_grad(total, out):
    half = total.shape[1] // 2
    out[:, :half] = total[:, :half].astype(bf16)
    for to, at in enumerate((0, 2, 1, 3)):
        there, here = slice(256 * to, 256 * to + 256), slice(256 * at, 256 * at + 256)
        out[there, half:] = total[here, half:].astype(bf16)


class HeldSumPart(SumPart):
    def __init__(self, route, refs, sems, base):
        self.held, self.sent = refs[:2]
        self.got_1, self.got_2, self.got_3 = refs[2:]
        self.sems, self.base = sems, base
        self.hops = ((2, 1), (1, 2))[route]

    @staticmethod
    def buffers(width):
        return [pltpu.VMEM((512, width), bf16)] + SumPart.buffers(width)

    def first(self):
        return [send(self.sent, self.got_1, self.sems, self.base, across(self.hops[0]))]


def last_scratch(cols):
    made = []
    for _ in range(4):
        made += HeldSumPart.buffers(cols // 4)
    return made + sum_sems(4) + SmallSum.scratch()


def last_kernel(
    tiles,
    turned_rows,
    dq,
    dk,
    dv,
    w,
    toks,
    gattn,
    vectors,
    out,
    grad_w,
    small_out,
    sums,
    qv_sums,
    total,
    sent,
    came,
    send_sems,
    recv_sems,
    *refs,
):
    step = pl.program_id(0)
    blocks = 2 * tiles
    parts = [
        HeldSumPart(k % 2, refs[5 * k : 5 * k + 5], refs[20:23], SumPart.slots * k)
        for k in range(4)
    ]
    tiny = SmallSum(refs[23:25], refs[25:27])
    local = dq.shape[1]
    quarter = 3 * local // 4

    def swap(k):
        return send(sent.at[k], came.at[k], (send_sems, recv_sems), k, sibling())

    @pl.when(step == 0)
    def _():
        greet(True)
        sums[...] = jnp.zeros(sums.shape, f32)
        qv_sums[...] = jnp.zeros(qv_sums.shape, f32)

    grads = jnp.concatenate([dq[...], dk[...], dv[...]], axis=1)

    @pl.when(step < blocks)
    def _():
        qv_sums[:, :local] += column_sum(dq[...].astype(f32))
        qv_sums[:, local:] += column_sum(dv[...].astype(f32))

    for c in range(2):

        @pl.when((step >= c * blocks) & (step < (c + 1) * blocks))
        def _():
            spans = [slice(r * 2 * quarter + c * quarter, r * 2 * quarter + (c + 1) * quarter) for r in range(2)]
            term = dot_nn(turned_rows[...], jnp.concatenate([grads[:, s] for s in spans], axis=1))

            @pl.when(step == c * blocks)
            def _():
                total[...] = term

            @pl.when(step > c * blocks)
            def _():
                total[...] += term

            @pl.when(step == (c + 1) * blocks - 1)
            def _():
                one, two = parts[2 * c], parts[2 * c + 1]
                one.held[...] = total[0:512, :quarter].astype(bf16)
                one.sent[...] = total[512:1024, :quarter].astype(bf16)
                two.held[0:256, :] = total[0:256, quarter:].astype(bf16)
                two.held[256:512, :] = total[512:768, quarter:].astype(bf16)
                two.sent[0:256, :] = total[256:512, quarter:].astype(bf16)
                two.sent[256:512, :] = total[768:1024, quarter:].astype(bf16)
                start_all(one.first() + two.first())

    @pl.when(step == 2 * blocks + 1)
    def _():
        for part in parts[:2]:
            part.to_second()

    @pl.when(step == 2 * blocks + 3)
    def _():
        for part in parts[:2]:
            part.to_third()

    @pl.when(step == 2 * blocks + 4)
    def _():
        for part in parts[2:]:
            part.to_second()

    @pl.when(step == 2 * blocks + 5)
    def _():
        for part in parts[2:]:
            part.to_third()

    @pl.when(step >= 2 * blocks)
    def _():
        rows = dot_nt(grads, w[...])
        for k in range(tiles):

            @pl.when(step == 2 * blocks + k)
            def _():
                sent[k] = rows.astype(bf16)
                swap(k).start()

            @pl.when(step == 2 * blocks + tiles + k)
            def _():
                swap(k).wait()
                grad_norm = rows + came[k].astype(f32)
                scaled, inverse = normalized(toks[...].astype(f32))
                through = grad_norm * row_of(vectors, GAIN_ONE)
                centre = jnp.mean(through, axis=-1, keepdims=True)
                along = jnp.mean(through * scaled, axis=-1, keepdims=True)
                grad_in = inverse * (through - centre - scaled * along)
                out[...] = (gattn[...].astype(f32) + grad_in).astype(bf16)
                sums[0:8, :] += column_sum(grad_norm * scaled)
                sums[8:16, :] += column_sum(grad_norm)

    @pl.when(step == pl.num_programs(0) - 1)
    def _():
        row = lax.broadcasted_iota(jnp.int32, (8, 1024), 0)
        first = jnp.sum(sums[0:8, :], axis=0, keepdims=True)
        second = jnp.sum(sums[8:16, :], axis=0, keepdims=True)
        third = jnp.sum(qv_sums[...], axis=0, keepdims=True)
        rows = jnp.where(row == 0, first, jnp.where(row == 1, second, third))
        tiny.begin(jnp.where(row < 3, rows, 0.0))
        tiny.middle(2)
        small_out[...] = tiny.end()
        for k, part in enumerate(parts):
            at = (k % 2) * 2 * quarter + (k // 2) * quarter
            summed = part.result()
            edges = [at] + [c for c in (local, 2 * local) if at < c < at + quarter] + [at + quarter]
            for low, high in zip(edges[:-1], edges[1:]):
                to = low % local
                grad_w[low // local, :, to : to + high - low] = summed[:, low - at : high - at]


def layer_on_pairs(
    tokens,
    slot_lengths,
    gain_one,
    shift_one,
    w_qkv,
    bias_qv,
    w_out,
    bias_out,
    gain_two,
    shift_two,
    w_up,
    bias_up,
    w_down,
    bias_down,
    cotangent,
):
    own_rows, width = tokens.shape
    total_rows = 2 * own_rows
    tiles = own_rows // BT
    local = w_qkv.shape[2]
    hidden_cols = w_up.shape[1]
    side_cols = 3 * local
    lengths = slot_lengths[0]

    vectors = jnp.concatenate(
        [
            gain_one,
            shift_one,
            bias_out,
            gain_two,
            shift_two,
            bias_down,
            bias_up,
            bias_qv.reshape(-1),
        ]
    ).reshape(VECTORS, width).astype(f32)
    half_cols = side_cols // 2
    normed_at = pl.BlockSpec(
        (width, BT),
        lambda i: (0, lax.rem(jnp.minimum(i, 2 * tiles - 1) + my_side() * tiles, 2 * tiles)),
    )
    packed_at = pl.BlockSpec(
        (BT, half_cols),
        lambda i: (
            lax.rem(jnp.maximum(i - 2 * tiles, 0), 2 * tiles),
            jnp.maximum(i - 2 * tiles, 0) // (2 * tiles),
        ),
    )
    rows_turned, packed, up_blocks, out_blocks, qkv_blocks = grid_call(
        functools.partial(qkv_kernel, tiles),
        6 * tiles,
        [
            (tokens, pl.BlockSpec((BT, width), lambda i: (jnp.minimum(i, tiles - 1), 0))),
            (tokens, ANY),
            (vectors, whole(VECTORS, width)),
            (w_qkv.transpose(1, 0, 2), pl.BlockSpec((3, 64, local), lambda i: (0, 0, 0))),
            (w_out.T, ANY),
            (w_up, ANY),
        ],
        [
            (shape(width, total_rows), normed_at),
            (shape(total_rows, side_cols), packed_at),
            (jax.ShapeDtypeStruct((4, 4, 64, hidden_cols), bf16), ANY),
            (jax.ShapeDtypeStruct((4, 4, 64, local), bf16), ANY),
            (jax.ShapeDtypeStruct((4, 4, 64, side_cols), bf16), ANY),
        ],
        [
            pltpu.VMEM((total_rows, width), bf16),
            pltpu.VMEM((tiles, BT, width), bf16),
            pltpu.VMEM((4, 4, 64, side_cols), bf16),
            pltpu.SemaphoreType.DMA((tiles,)),
            pltpu.SemaphoreType.DMA((tiles,)),
            pltpu.SemaphoreType.DMA(()),
        ]
        + gather_sems(8),
        2 * total_rows * width * side_cols,
        "qkv",
        1,
    )
    qkv_w = qkv_blocks.reshape(width, side_cols)
    attended, exact, lse, up_blocks, down_blocks = attend_forward(
        packed,
        lengths,
        AttendGather(),
        (w_down.T, up_blocks),
        jax.ShapeDtypeStruct((4, 4, 64, hidden_cols), bf16),
    )
    up_w = up_blocks.reshape(width, hidden_cols)
    down_w = down_blocks.reshape(width, hidden_cols)
    out_w = out_blocks.reshape(width, local)

    def two_way(cols, skip=0):
        def at(i):
            return lax.rem(jnp.maximum(i - skip, 0) + (1 - my_side()) * tiles, 2 * tiles)

        return pl.BlockSpec((BT, cols), lambda i: (at(i), 0))

    late_tile = pl.BlockSpec((BT, width), lambda i: (jnp.maximum(i - tiles, 0), 0))
    swap_buffers = [
        pltpu.VMEM((tiles, BT, width), bf16),
        pltpu.VMEM((tiles, BT, width), bf16),
        pltpu.SemaphoreType.DMA((tiles,)),
        pltpu.SemaphoreType.DMA((tiles,)),
    ]
    hidden, normed_own = grid_call(
        functools.partial(project_kernel, tiles),
        2 * tiles,
        [
            (attended, two_way(local)),
            (out_w, weight(local)),
            (tokens, late_tile),
            (vectors, whole(VECTORS, width)),
        ],
        [(shape(own_rows, width, f32), late_tile), (shape(own_rows, width), late_tile)],
        swap_buffers,
        4 * own_rows * width * local,
        "project",
        6,
    )
    own_at = pl.BlockSpec((BT, width), lambda i: (jnp.minimum(i, tiles - 1), 0))
    ffn_own, norm_own, ffn_came, norm_came, up_grad, down_grad, bsum = grid_call(
        functools.partial(feed_kernel, tiles),
        2 * tiles,
        [
            (normed_own, ANY),
            (cotangent, ANY),
            (vectors, whole(VECTORS, width)),
            (up_w, weight(hidden_cols)),
            (down_w, weight(hidden_cols)),
        ],
        [
            (shape(own_rows, width), own_at),
            (shape(own_rows, width), own_at),
            (shape(own_rows, width), ANY),
            (shape(own_rows, width), ANY),
            (shape(width, hidden_cols), ANY),
            (shape(width, hidden_cols), ANY),
            (shape(8, hidden_cols, f32), whole(8, hidden_cols)),
        ],
        [
            pltpu.VMEM((width, hidden_cols), f32),
            pltpu.VMEM((width, hidden_cols), f32),
            pltpu.VMEM((BT, hidden_cols), bf16),
            pltpu.VMEM((BT, hidden_cols), bf16),
            pltpu.VMEM((width, BT), bf16),
            pltpu.VMEM((width, BT), bf16),
            pltpu.VMEM((2 * tiles, BT, width), bf16),
            pltpu.VMEM((2 * tiles, BT, width), bf16),
            pltpu.VMEM((BT, width), bf16),
            pltpu.VMEM((BT, width), bf16),
            pltpu.SemaphoreType.DMA((2 * tiles,)),
            pltpu.SemaphoreType.DMA((4 * tiles,)),
            pltpu.SemaphoreType.DMA((4 * tiles,)),
            pltpu.SemaphoreType.DMA((64,)),
        ],
        24 * own_rows * width * hidden_cols,
        "feed",
        5,
    )
    def mine_first(i):
        return lax.rem(i + my_side() * tiles, 2 * tiles)

    natural_tile = pl.BlockSpec((BT, local), lambda i: (mine_first(i), 0))
    output, grad_attn, grad_attended, delta, out_grad, middle_sums = grid_call(
        functools.partial(middle_kernel, tiles),
        2 * tiles,
        [
            (hidden, own_at),
            (ffn_own, own_at),
            (ffn_came, own_at),
            (norm_own, own_at),
            (norm_came, own_at),
            (cotangent, own_at),
            (vectors, whole(VECTORS, width)),
            (exact, natural_tile),
            (attended, natural_tile),
            (out_w, weight(local)),
        ],
        [
            (shape(own_rows, width), own_at),
            (shape(own_rows, width), own_at),
            (shape(total_rows, local), natural_tile),
            (shape(16, total_rows, f32), pl.BlockSpec((16, BT), lambda i: (0, mine_first(i)))),
            (shape(width, local), whole(width, local)),
            (shape(32, width, f32), whole(32, width)),
        ],
        [
            pltpu.VMEM((width, BT), bf16),
            pltpu.VMEM((width, local), f32),
            pltpu.VMEM((BT, width), bf16),
        ]
        + swap_buffers,
        4 * total_rows * width * local,
        "middle",
        7,
    )
    early = middle_sums.reshape(4, 8, width).sum(axis=1)
    up_bias = bsum.sum(axis=0).reshape(-1, width)
    early = jnp.concatenate([early, up_bias, jnp.zeros((2, width), f32)])
    moved = (down_grad, up_grad, out_grad, early)
    grad_q, grad_k, grad_v, grad_down, grad_up, grad_w_out, early = attend_backward(
        packed,
        grad_attended,
        lse,
        delta,
        lengths,
        BackwardSum((hidden_cols, hidden_cols, local)),
        moved,
    )
    blocks = 2 * tiles

    def grad_at(i):
        later = lax.rem(jnp.maximum(i - 2 * blocks, 0) + (1 - my_side()) * tiles, blocks)
        return jnp.where(i < 2 * blocks, lax.rem(i, blocks), later)

    grad_tile = pl.BlockSpec((BT, local), lambda i: (grad_at(i), 0))
    turned_tile = pl.BlockSpec(
        (width, BT), lambda i: (0, jnp.where(i < 2 * blocks, lax.rem(i, blocks), blocks - 1))
    )
    last_tile = pl.BlockSpec(
        (BT, width), lambda i: (jnp.maximum(i - 2 * blocks - tiles, 0), 0)
    )
    grad_tokens, grad_w_qkv, late = grid_call(
        functools.partial(last_kernel, tiles),
        3 * blocks,
        [(rows_turned, turned_tile)]
        + [(g, grad_tile) for g in (grad_q, grad_k, grad_v)]
        + [
            (qkv_w, weight(side_cols)),
            (tokens, last_tile),
            (grad_attn, last_tile),
            (vectors, whole(VECTORS, width)),
        ],
        [
            (shape(own_rows, width), last_tile),
            (
                jax.ShapeDtypeStruct((3, 64, local), f32),
                pl.BlockSpec((3, 64, local), lambda i: (0, 0, 0)),
            ),
            (shape(8, width, f32), whole(8, width)),
        ],
        [
            pltpu.VMEM((16, width), f32),
            pltpu.VMEM((8, width), f32),
            pltpu.VMEM((width, side_cols // 2), f32),
        ]
        + swap_buffers
        + last_scratch(side_cols),
        4 * total_rows * width * side_cols,
        "last",
        4,
    )
    return (
        output,
        grad_tokens,
        late[0],
        late[1],
        grad_w_qkv.transpose(1, 0, 2),
        late[2].reshape(2, local),
        grad_w_out.T,
        early[2],
        early[0],
        early[1],
        grad_up,
        early[4:6].reshape(-1),
        grad_down.T,
        early[3],
    )


def gelu_tanh(values):
    inner = gelu_coeff * (values + 0.044715 * values * values * values)
    return 0.5 * values * (1.0 + jnp.tanh(inner))


def gelu_slope(values):
    inner = gelu_coeff * (values + 0.044715 * values * values * values)
    bent = jnp.tanh(inner)
    return 0.5 * (1.0 + bent) + 0.5 * values * (1.0 - bent * bent) * gelu_coeff * (
        1.0 + 3.0 * 0.044715 * values * values
    )


def norm_forward(values, gain_vec, shift_vec):
    average = jnp.mean(values, axis=-1, keepdims=True)
    centred = values - average
    variance = jnp.mean(centred * centred, axis=-1, keepdims=True)
    inverse = lax.rsqrt(variance + norm_eps)
    scaled = centred * inverse
    return (scaled * gain_vec.astype(f32) + shift_vec.astype(f32), scaled, inverse)


def norm_backward(grad_out, scaled, inverse, gain_vec):
    grad_scaled = grad_out * gain_vec.astype(f32)
    centre_term = jnp.mean(grad_scaled, axis=-1, keepdims=True)
    slope_term = jnp.mean(grad_scaled * scaled, axis=-1, keepdims=True)
    grad_in = inverse * (grad_scaled - centre_term - scaled * slope_term)
    return (grad_in, jnp.sum(grad_out * scaled, axis=0), jnp.sum(grad_out, axis=0))


def layer_by_collectives(
    tokens,
    slot_lengths,
    gain_one,
    shift_one,
    w_qkv,
    bias_qv,
    w_out,
    bias_out,
    gain_two,
    shift_two,
    w_up,
    bias_up,
    w_down,
    bias_down,
    cotangent,
):
    w_qkv, w_out, w_up, w_down = (
        lax.all_gather(w_qkv, "dp", axis=0, tiled=True),
        lax.all_gather(w_out, "dp", axis=1, tiled=True),
        lax.all_gather(w_up, "dp", axis=0, tiled=True),
        lax.all_gather(w_down, "dp", axis=1, tiled=True),
    )
    lengths = slot_lengths[0]
    residual = tokens.astype(f32)
    normed_one, scaled_one, inverse_one = norm_forward(residual, gain_one, shift_one)
    rows_one = lax.all_gather(normed_one.astype(bf16), "mp", axis=0, tiled=True)
    packed = jnp.einsum("td,dcf->tcf", rows_one, w_qkv, preferred_element_type=f32)
    zero_bias = jnp.zeros_like(bias_qv[0])
    packed_bias = jnp.stack([bias_qv[0], zero_bias, bias_qv[1]]).astype(f32)
    packed = (packed + packed_bias[None]).astype(bf16)
    local = packed.shape[2]
    packed_rows = packed.reshape(packed.shape[0], -1)
    attended, exact_out, log_totals = attend_forward(packed_rows, lengths)
    hidden = (
        residual
        + lax.psum_scatter(
            jnp.dot(attended, w_out, preferred_element_type=f32),
            "mp",
            scatter_dimension=0,
            tiled=True,
        )
        + bias_out.astype(f32)
    )
    normed_two, scaled_two, inverse_two = norm_forward(hidden, gain_two, shift_two)
    normed_low = normed_two.astype(bf16)
    rows_two = lax.all_gather(normed_low, "mp", axis=0, tiled=True)
    preact = jnp.dot(rows_two, w_up, preferred_element_type=f32) + bias_up.astype(
        f32
    )
    active = gelu_tanh(preact).astype(bf16)
    ffn_out = lax.psum_scatter(
        jnp.dot(active, w_down, preferred_element_type=f32).astype(bf16),
        "mp",
        scatter_dimension=0,
        tiled=True,
    ).astype(f32)
    output = (hidden + ffn_out + bias_down.astype(f32)).astype(bf16)
    grad_out = cotangent.astype(f32)
    grad_rows = lax.all_gather(cotangent, "mp", axis=0, tiled=True)
    grad_active = jnp.einsum("td,fd->tf", grad_rows, w_down, preferred_element_type=f32)
    grad_pre = (grad_active * gelu_slope(preact)).astype(bf16)
    grad_up = jnp.einsum("td,tf->df", rows_two, grad_pre, preferred_element_type=f32)
    grad_down = jnp.einsum("tf,td->fd", active, grad_rows, preferred_element_type=f32)
    grad_bias_up = jnp.sum(grad_pre.astype(f32), axis=0)
    grad_norm_two = lax.psum_scatter(
        jnp.einsum("tf,df->td", grad_pre, w_up, preferred_element_type=f32),
        "mp",
        scatter_dimension=0,
        tiled=True,
    )
    grad_in_two, grad_gain_two, grad_shift_two = norm_backward(
        grad_norm_two, scaled_two, inverse_two, gain_two
    )
    grad_hidden = grad_out + grad_in_two
    grad_attn = grad_hidden.astype(bf16)
    grad_attn_rows = lax.all_gather(grad_attn, "mp", axis=0, tiled=True)
    grad_w_out = jnp.einsum(
        "tf,td->fd", attended, grad_attn_rows, preferred_element_type=f32
    )
    grad_attended = jnp.einsum(
        "td,fd->tf", grad_attn_rows, w_out, preferred_element_type=f32
    ).astype(bf16)
    product = (grad_attended.astype(f32) * exact_out).reshape(grad_attended.shape[0], -1, HD)
    delta = jnp.sum(product, axis=-1).T
    groups = log_totals.shape[0] // 8
    delta = delta.reshape(groups, -1, delta.shape[1])
    delta = jnp.pad(delta, ((0, 0), (0, 8 - delta.shape[1]), (0, 0))).reshape(8 * groups, -1)
    grads = attend_backward(packed_rows, grad_attended, log_totals, delta, lengths)
    grad_packed = jnp.stack(grads, axis=1)
    grad_w_qkv = jnp.einsum(
        "td,tcf->dcf", rows_one, grad_packed, preferred_element_type=f32
    )
    grad_bias_qv = jnp.stack(
        [
            jnp.sum(grad_packed[:, 0].astype(f32), axis=0),
            jnp.sum(grad_packed[:, 2].astype(f32), axis=0),
        ]
    )
    grad_norm_one = lax.psum_scatter(
        jnp.einsum("tcf,dcf->td", grad_packed, w_qkv, preferred_element_type=f32),
        "mp",
        scatter_dimension=0,
        tiled=True,
    )
    grad_in_one, grad_gain_one, grad_shift_one = norm_backward(
        grad_norm_one, scaled_one, inverse_one, gain_one
    )
    grad_tokens = (grad_hidden + grad_in_one).astype(bf16)
    grad_bias_out = jnp.sum(grad_attn.astype(f32), axis=0)
    grad_bias_down = jnp.sum(grad_out, axis=0)
    grad_w_qkv, grad_w_out, grad_up, grad_down = (
        lax.psum_scatter(grad_w_qkv, "dp", scatter_dimension=0, tiled=True),
        lax.psum_scatter(grad_w_out, "dp", scatter_dimension=1, tiled=True),
        lax.psum_scatter(grad_up, "dp", scatter_dimension=0, tiled=True),
        lax.psum_scatter(grad_down, "dp", scatter_dimension=1, tiled=True),
    )
    small_grads = lax.psum(
        (
            grad_gain_one,
            grad_shift_one,
            grad_bias_out,
            grad_gain_two,
            grad_shift_two,
            grad_bias_down,
        ),
        ("dp", "mp"),
    )
    grad_bias_qv, grad_bias_up = lax.psum((grad_bias_qv, grad_bias_up), "dp")
    return (
        output,
        grad_tokens,
        small_grads[0],
        small_grads[1],
        grad_w_qkv,
        grad_bias_qv,
        grad_w_out,
        small_grads[2],
        small_grads[3],
        small_grads[4],
        grad_up,
        grad_bias_up,
        grad_down,
        small_grads[5],
    )


def solution(mesh):
    pairs = dict(mesh.shape) == {"dp": 16, "mp": 2}
    layer = layer_on_pairs if pairs else layer_by_collectives
    return jax.shard_map(
        layer,
        mesh=mesh,
        in_specs=(
            P(("dp", "mp"), None),
            P("dp", None),
            P(),
            P(),
            P("dp", None, "mp"),
            P(None, "mp"),
            P("mp", "dp"),
            P(),
            P(),
            P(),
            P("dp", "mp"),
            P("mp"),
            P("mp", "dp"),
            P(),
            P(("dp", "mp"), None),
        ),
        out_specs=(
            P(("dp", "mp"), None),
            P(("dp", "mp"), None),
            P(),
            P(),
            P("dp", None, "mp"),
            P(None, "mp"),
            P("mp", "dp"),
            P(),
            P(),
            P(),
            P("dp", "mp"),
            P("mp"),
            P("mp", "dp"),
            P(),
        ),
        check_vma=False,
    )
```

```python
import functools

import jax
import jax.numpy as jnp
from jax import lax
from jax.experimental import pallas as pl
from jax.experimental.pallas import tpu as pltpu
from jax.sharding import PartitionSpec as P

HD = 64
LONG_LEN = 3072
BT = 512
VMEM_CAP = 60 * 1024 * 1024

f32 = jnp.float32
bf16 = jnp.bfloat16
norm_eps = 1e-05
masked_score = -1e30
gelu_coeff = 0.7978845608028654
score_scale = HD ** (-0.5)
safe_sum = 1e30


def dot_nt(left, right):
    return lax.dot_general(left, right, (((1,), (1,)), ((), ())), preferred_element_type=f32)


def dot_nn(left, right):
    return lax.dot_general(left, right, (((1,), (0,)), ((), ())), preferred_element_type=f32)


def dot_tn(left, right):
    return lax.dot_general(left, right, (((0,), (0,)), ((), ())), preferred_element_type=f32)


def params(axes=1, collective=None):
    if collective is None:
        return pltpu.CompilerParams(
            vmem_limit_bytes=VMEM_CAP, dimension_semantics=("arbitrary",) * axes
        )
    return pltpu.CompilerParams(
        vmem_limit_bytes=VMEM_CAP,
        dimension_semantics=("arbitrary",) * axes,
        collective_id=collective,
        has_side_effects=True,
    )


def cost(flops, nbytes, exps=0):
    return pl.CostEstimate(flops=int(flops), bytes_accessed=int(nbytes), transcendentals=int(exps))


ANY = pl.BlockSpec(memory_space=pl.ANY)


def bits_of_me():
    me = lax.axis_index("dp")
    return (me // 8, (me // 4) % 2, (me // 2) % 2, me % 2)


def flipped(bits, which):
    return tuple(1 - b if which & (8 >> k) else b for k, b in enumerate(bits))


def index_of(bits):
    return bits[0] * 8 + bits[1] * 4 + bits[2] * 2 + bits[3]


def across(which):
    return {"dp": index_of(flipped(bits_of_me(), which))}


def sibling():
    return {"mp": 1 - lax.axis_index("mp")}


MESH_ID = pl.DeviceIdType.MESH
HOPS = (1, 2, 4, 8, 12)


def sibling_across(which):
    return {**across(which), **sibling()}


def greet(with_small):
    devices = [across(hop) for hop in HOPS]
    if with_small:
        devices += [across(3), sibling()] + [sibling_across(k) for k in (1, 2, 3)]
    greet_only(devices)


def greet_only(devices):
    barrier = pltpu.get_barrier_semaphore()
    for device in devices:
        pl.semaphore_signal(barrier, inc=1, device_id=device, device_id_type=MESH_ID)
    pl.semaphore_wait(barrier, len(devices))


def greet_sibling():
    greet_only([sibling()])


def send(src, dst, sems, slot, device):
    return pltpu.make_async_remote_copy(
        src_ref=src,
        dst_ref=dst,
        send_sem=sems[0].at[slot],
        recv_sem=sems[1].at[slot],
        device_id=device,
        device_id_type=MESH_ID,
    )


def start_all(copies):
    for copy in copies:
        copy.start()


def wait_all(copies):
    for copy in copies:
        copy.wait()


def gather_z(src, dst, span, sems, base):
    bits = bits_of_me()
    z, yx = bits[0] * 2 + bits[1], bits[2] * 2 + bits[3]
    cols = pl.ds(*span)
    place = dst.at[z, yx, :, cols]
    copies = [
        send(src.at[:, cols], place, sems, base + k, across(4 * (k + 1))) for k in range(3)
    ]
    copies.append(pltpu.make_async_copy(src.at[:, cols], place, sems[2].at[base]))
    return copies


def gather_second(dst, span, route, sems, base):
    bits = bits_of_me()
    part = dst.at[:, bits[2] * 2 + bits[3], :, pl.ds(*span)]
    return [send(part, part, sems, base + 3, across((1, 2)[route]))]


def gather_third(dst, span, route, sems, base):
    copies = []
    for k, which in enumerate((0, (1, 2)[route])):
        bits = flipped(bits_of_me(), which)
        part = dst.at[:, bits[2] * 2 + bits[3], :, pl.ds(*span)]
        copies.append(send(part, part, sems, base + 4 + k, across((2, 1)[route])))
    return copies


def late_z_first(src, dst, span, route, sems, base):
    bits = bits_of_me()
    cols = pl.ds(*span)
    place = dst.at[bits[0] * 2 + bits[1], bits[2] * 2 + bits[3], :, cols]
    return [
        send(src.at[:, cols], place, sems, base, across((1, 2)[route])),
        pltpu.make_async_copy(src.at[:, cols], place, sems[2].at[base]),
    ]


def late_z_second(dst, span, route, sems, base):
    z = bits_of_me()[0] * 2 + bits_of_me()[1]
    copies = []
    for k, which in enumerate((0, (1, 2)[route])):
        bits = flipped(bits_of_me(), which)
        part = dst.at[z, bits[2] * 2 + bits[3], :, pl.ds(*span)]
        copies.append(send(part, part, sems, base + 1 + k, across((2, 1)[route])))
    return copies


def late_z_third(dst, span, sems, base):
    part = dst.at[bits_of_me()[0] * 2 + bits_of_me()[1], :, :, pl.ds(*span)]
    return [send(part, part, sems, base + 3 + k, across(4 * (k + 1))) for k in range(3)]


def gather_sems(pieces):
    return [
        pltpu.SemaphoreType.DMA((6 * pieces,)),
        pltpu.SemaphoreType.DMA((6 * pieces,)),
        pltpu.SemaphoreType.DMA((6 * pieces,)),
    ]


def halves(cols, parts=1):
    half = cols // 2
    width = half // parts
    return [(r * half + c * width, width, r) for c in range(parts) for r in range(2)]


def head_lanes(block, head):
    lane_head = lax.broadcasted_iota(jnp.int32, block.shape, 1) // HD
    return jnp.where(lane_head == head, block, jnp.zeros_like(block))


def pack_heads(columns):
    lane = lax.broadcasted_iota(jnp.int32, columns[0].shape, 1)
    pairs = [
        jnp.where(lane < HD, columns[2 * i], columns[2 * i + 1]) for i in range(len(columns) // 2)
    ]
    return pairs[0] if len(pairs) == 1 else jnp.concatenate(pairs, axis=1)


def block_probs(scores, top):
    total, parts = None, []
    for t in range(scores.shape[1] // 128):
        part = jnp.exp(scores[:, t * 128 : (t + 1) * 128] - top)
        total = part if total is None else total + part
        parts.append(part.astype(bf16))
    return parts, total


def head_rows(stack, heads, first, count):
    block = stack.shape[0] // heads
    return jnp.concatenate(
        [stack[h * block + first : h * block + first + count, :] for h in range(heads)], axis=0
    )


def attend_block(masked, keys, values, m_ref, l_ref, acc_ref):
    heads, half = len(masked), keys.shape[0] // 2
    for part in range(2):
        rows = slice(part * half, (part + 1) * half)
        seen = (part + 1) * half
        low = []
        for h, query in enumerate(masked):
            scores = dot_nt(query[rows, :], keys[:seen, :])
            row = lax.broadcasted_iota(jnp.int32, scores.shape, 0) + part * half
            col = lax.broadcasted_iota(jnp.int32, scores.shape, 1)
            scores = jnp.where(row >= col, scores, masked_score)
            top = jnp.broadcast_to(jnp.max(scores, axis=1, keepdims=True), (half, 128))
            m_ref[h, rows, :] = top
            parts, l_ref[h, rows, :] = block_probs(scores, top)
            low += parts
        acc_ref[rows, :] = dot_nn(
            jnp.concatenate(low, axis=1), head_rows(values, heads, 0, seen)
        )


def attend_finish(heads, m_ref, l_ref, acc_ref, out_ref, exact_ref, lse_ref):
    block = out_ref.shape[0]
    lane = lax.broadcasted_iota(jnp.int32, (block, 128), 1)
    rows = jnp.zeros((block, 128), f32)
    inverse = []
    for h in range(heads):
        total = jnp.sum(l_ref[h], axis=1, keepdims=True)
        rows = jnp.where(lane == h, m_ref[h][:, :1] + jnp.log(total), rows)
        inverse.append(jnp.broadcast_to(1.0 / total, (block, 128)))
    result = acc_ref[...] * pack_heads(inverse)
    out_ref[...] = result.astype(bf16)
    exact_ref[...] = result
    lse_ref[...] = rows.T[:8, :]


def mask_values(v_ref, vm_ref, heads, block):
    for j in range(v_ref.shape[0] // block):
        value = v_ref[j * block : (j + 1) * block, :]
        for h in range(heads):
            vm_ref[j, h * block : (h + 1) * block, :] = head_lanes(value, h)


def attend_forward_kernel(heads, comm, lens_ref, q_ref, k_ref, v_ref, *refs):
    ins, refs = refs[: comm.ins], refs[comm.ins :]
    out_ref, exact_ref, lse_ref, big_ref = refs[:4]
    outs = refs[4 : 4 + comm.outs]
    vm_ref, m_ref, l_ref, acc_ref = refs[4 + comm.outs : 8 + comm.outs]
    sems = refs[8 + comm.outs :]
    step = pl.program_id(0)
    block = q_ref.shape[0]
    cols = heads * HD
    groups = q_ref.shape[1] // cols
    comm.before(step, ins, outs, sems)
    spans = [slice(g * cols, (g + 1) * cols) for g in range(groups)]
    stats = [pl.ds(g * heads, heads) for g in range(groups)]

    @pl.when(step == 0)
    def _():
        for g in range(groups):
            mask_values(v_ref.at[:, spans[g]], vm_ref.at[g], heads, block)
        big_ref[...] = jnp.zeros(big_ref.shape, f32)

    masked = []
    for g in range(groups):
        query = q_ref[:, spans[g]] * jnp.asarray(score_scale, bf16)
        masked.append([head_lanes(query, h) for h in range(heads)])

    def key_block(j, g):
        return k_ref[pl.ds(pl.multiple_of(j * block, block), block), spans[g]]

    for g in range(groups):
        attend_block(
            masked[g],
            key_block(step, g),
            vm_ref[g, step],
            m_ref.at[stats[g]],
            l_ref.at[stats[g]],
            acc_ref.at[:, spans[g]],
        )
    away = jnp.where(lens_ref[0] == LONG_LEN, 0.0, 1e30).astype(f32)

    def earlier(j, carry):
        for g in range(groups):
            keys = key_block(j, g)
            low = []
            for h in range(heads):
                at = g * heads + h
                parts, total = block_probs(dot_nt(masked[g][h], keys), m_ref[at] + away)
                l_ref[at] += total
                low += parts
            acc_ref[:, spans[g]] += dot_nn(jnp.concatenate(low, axis=1), vm_ref[g, j])
        return carry

    lax.fori_loop(0, step, earlier, 0)
    big = big_ref[...]
    for h in range(groups * heads):
        big = jnp.maximum(big, jnp.max(l_ref[h].reshape(-1, 8, 128), axis=0))
    big_ref[...] = big
    for g in range(groups):
        attend_finish(
            heads,
            m_ref.at[stats[g]],
            l_ref.at[stats[g]],
            acc_ref.at[:, spans[g]],
            out_ref.at[:, spans[g]],
            exact_ref.at[:, spans[g]],
            lse_ref.at[pl.ds(8 * g, 8), :],
        )
    comm.after(step, ins, outs, sems)


def attend_safe_kernel(
    heads,
    groups,
    lens_ref,
    big_ref,
    packed,
    low_in,
    exact_in,
    lse_in,
    low,
    exact,
    lse,
    q_ref,
    k_ref,
    v_ref,
    out_ref,
    exact_ref,
    lse_ref,
    vm_ref,
    m_ref,
    l_ref,
    acc_ref,
    sem,
):
    block, cols = q_ref.shape
    tokens = k_ref.shape[0]

    def fetch(src, dst):
        copy = pltpu.make_async_copy(src, dst, sem)
        copy.start()
        copy.wait()

    def one_query(group, step):
        rows = pl.ds(pl.multiple_of(step * block, block), block)
        here = pl.ds(group * cols, cols)
        fetch(packed.at[rows, here], q_ref)
        query = q_ref[...] * jnp.asarray(score_scale, bf16)
        masked = [head_lanes(query, h) for h in range(heads)]

        def key_block(j):
            return k_ref[pl.ds(pl.multiple_of(j * block, block), block), :]

        attend_block(masked, key_block(step), vm_ref[step], m_ref, l_ref, acc_ref)

        def earlier(j, carry):
            keys = key_block(j)
            parts_all, shrink = [], []
            for h in range(heads):
                scores = dot_nt(masked[h], keys)
                old = m_ref[h]
                top = jnp.maximum(old, jnp.max(scores, axis=1, keepdims=True))
                factor = jnp.exp(old - top)
                m_ref[h] = top
                parts, total = block_probs(scores, top)
                l_ref[h] = l_ref[h] * factor + total
                parts_all += parts
                shrink.append(factor)
            acc_ref[...] = acc_ref[...] * pack_heads(shrink) + dot_nn(
                jnp.concatenate(parts_all, axis=1), vm_ref[j]
            )
            return carry

        lax.fori_loop(0, jnp.where(lens_ref[0] == LONG_LEN, step, 0), earlier, 0)
        attend_finish(heads, m_ref, l_ref, acc_ref, out_ref, exact_ref, lse_ref)
        fetch(out_ref, low.at[rows, here])
        fetch(exact_ref, exact.at[rows, here])
        fetch(lse_ref, lse.at[pl.ds(group * 8, 8), rows])

    @pl.when(jnp.logical_not(jnp.max(big_ref[...]) < safe_sum))
    def _():
        for group in range(groups):
            fetch(packed.at[:, pl.ds((groups + group) * cols, cols)], k_ref)
            fetch(packed.at[:, pl.ds((2 * groups + group) * cols, cols)], v_ref)
            mask_values(v_ref, vm_ref, heads, block)
            lax.fori_loop(
                0, tokens // block, lambda i, c, group=group: (one_query(group, i), c)[1], 0
            )


class NoTransfers:
    ins = outs = 0

    def before(self, *args):
        pass

    def after(self, *args):
        pass


def attend_shapes(tokens, width):
    groups = width // min(256, width)
    cols = width // groups
    shapes = [
        jax.ShapeDtypeStruct((tokens, width), bf16),
        jax.ShapeDtypeStruct((tokens, width), f32),
        jax.ShapeDtypeStruct((8 * groups, tokens), f32),
    ]
    return groups, cols, cols // HD, shapes


def attend_cost(tokens, width, products):
    pairs = (tokens // BT) * (tokens // BT + 1) // 2
    work = products * 2 * pairs * BT * BT * width
    return cost(4 * work, 10 * tokens * width, pairs * BT * BT * width // HD)


def attend_safe(packed, lengths, big, low, exact, lse):
    tokens, width = packed.shape[0], packed.shape[1] // 3
    groups, cols, heads, shapes = attend_shapes(tokens, width)
    return pl.pallas_call(
        functools.partial(attend_safe_kernel, heads, groups),
        grid_spec=pltpu.PrefetchScalarGridSpec(
            num_scalar_prefetch=1,
            grid=(1,),
            in_specs=[pl.BlockSpec((8, 128), lambda i, n: (0, 0))] + [ANY] * 4,
            out_specs=[ANY] * 3,
            scratch_shapes=[
                pltpu.VMEM((BT, cols), bf16),
                pltpu.VMEM((tokens, cols), bf16),
                pltpu.VMEM((tokens, cols), bf16),
                pltpu.VMEM((BT, cols), bf16),
                pltpu.VMEM((BT, cols), f32),
                pltpu.VMEM((8, BT), f32),
                pltpu.VMEM((tokens // BT, heads * BT, cols), bf16),
                pltpu.VMEM((heads, BT, 128), f32),
                pltpu.VMEM((heads, BT, 128), f32),
                pltpu.VMEM((BT, cols), f32),
                pltpu.SemaphoreType.DMA(()),
            ],
        ),
        out_shape=shapes,
        input_output_aliases={3: 0, 4: 1, 5: 2},
        compiler_params=params(1),
        cost_estimate=cost(1000, 100000),
        name="attend_safe",
    )(lengths, big, packed, low, exact, lse)


def attend_forward(packed, lengths, comm=NoTransfers(), moved=(), fresh=None):
    tokens, width = packed.shape[0], packed.shape[1] // 3
    groups, cols, heads, shapes = attend_shapes(tokens, width)
    tile = pl.BlockSpec((BT, width), lambda i, n: (i, 0))
    low, exact, lse, big, *rest = pl.pallas_call(
        functools.partial(attend_forward_kernel, heads, comm),
        grid_spec=pltpu.PrefetchScalarGridSpec(
            num_scalar_prefetch=1,
            grid=(tokens // BT,),
            in_specs=[
                tile,
                pl.BlockSpec((tokens, width), lambda i, n: (0, 1), pipeline_mode=pl.Buffered(1)),
                pl.BlockSpec((tokens, width), lambda i, n: (0, 2), pipeline_mode=pl.Buffered(1)),
            ]
            + [ANY] * len(moved),
            out_specs=[
                tile,
                tile,
                pl.BlockSpec((8 * groups, BT), lambda i, n: (0, i)),
                pl.BlockSpec((8, 128), lambda i, n: (0, 0)),
            ]
            + [ANY] * comm.outs,
            scratch_shapes=[
                pltpu.VMEM((groups, tokens // BT, heads * BT, cols), bf16),
                pltpu.VMEM((groups * heads, BT, 128), f32),
                pltpu.VMEM((groups * heads, BT, 128), f32),
                pltpu.VMEM((BT, width), f32),
            ]
            + (comm.scratch() if moved else []),
        ),
        out_shape=shapes
        + [jax.ShapeDtypeStruct((8, 128), f32)]
        + [jax.ShapeDtypeStruct(m.shape, m.dtype) for m in moved[1:]]
        + ([fresh] if moved else []),
        input_output_aliases={5: 4} if moved else {},
        compiler_params=params(1, 2 if moved else None),
        cost_estimate=attend_cost(tokens, width, 2),
        name="attend_forward",
    )(lengths, packed, packed, packed, *moved)
    low, exact, lse = attend_safe(packed, lengths, big, low, exact, lse)
    return [low, exact, lse] + rest


def attend_backward_kernel(heads, comm, lens_ref, q_ref, k_ref, v_ref, do_ref, lse_ref, delta_ref, *refs):
    ins, refs = refs[: comm.ins], refs[comm.ins :]
    dq_ref, dk_ref, dv_ref = refs[:3]
    outs, refs = refs[3 : 3 + comm.outs], refs[3 + comm.outs :]
    qm_ref, dom_ref, km_ref, vm_ref, dqa_ref, dka_ref, dva_ref = refs[:7]
    scratch = refs[7:]
    step = pl.program_id(1)
    count = pl.num_programs(1)
    block = k_ref.shape[0]
    comm.before(pl.program_id(0) * count + step, ins, outs, scratch)

    @pl.when(step == 0)
    def _():
        for t in range(q_ref.shape[0] // block):
            rows = slice(t * block, (t + 1) * block)
            for h in range(heads):
                place = slice(h * block, (h + 1) * block)
                qm_ref[t, place, :] = head_lanes(q_ref[rows, :], h)
                dom_ref[t, place, :] = head_lanes(do_ref[rows, :], h)
        dqa_ref[...] = jnp.zeros(dqa_ref.shape, f32)

    for h in range(heads):
        place = slice(h * block, (h + 1) * block)
        km_ref[place, :] = head_lanes(k_ref[...] * jnp.asarray(score_scale, bf16), h)
        vm_ref[place, :] = head_lanes(v_ref[...], h)
    dka_ref[...] = jnp.zeros(dka_ref.shape, f32)
    dva_ref[...] = jnp.zeros(dva_ref.shape, f32)
    away = jnp.where(lens_ref[0] == LONG_LEN, 0.0, 1e30).astype(f32)

    def pair(i, first, count, seen, on_diagonal):
        rows = pl.ds(pl.multiple_of(i * block + first, count), count)
        query, grad = q_ref[rows, :], do_ref[rows, :]
        low, slopes = [], []
        for h in range(heads):
            place = slice(h * block, h * block + seen)
            scores = dot_nt(km_ref[place, :], query)
            logs = lse_ref[h : h + 1, rows]
            if not on_diagonal:
                logs = logs + away
            prob = jnp.exp(scores - logs)
            if on_diagonal:
                key = lax.broadcasted_iota(jnp.int32, scores.shape, 0)
                tok = lax.broadcasted_iota(jnp.int32, scores.shape, 1) + first
                prob = jnp.where(tok >= key, prob, 0.0)
            grad_prob = dot_nt(vm_ref[place, :], grad)
            slope = prob * (grad_prob - delta_ref[h : h + 1, rows])
            low.append(prob.astype(bf16))
            slopes.append(slope.astype(bf16))
        if on_diagonal:
            grads = head_rows(dom_ref[i], heads, first, count)
            queries = head_rows(qm_ref[i], heads, first, count)
            keys = head_rows(km_ref[...], heads, 0, seen)
        else:
            grads, queries, keys = dom_ref[i], qm_ref[i], km_ref[...]
        dva_ref[0:seen, :] += dot_nn(jnp.concatenate(low, axis=1), grads)
        dka_ref[0:seen, :] += dot_nn(jnp.concatenate(slopes, axis=1), queries)
        dqa_ref[rows, :] += dot_tn(jnp.concatenate(slopes, axis=0), keys)

    half = block // 2
    pair(step, 0, half, half, True)
    pair(step, half, half, block, True)
    lax.fori_loop(step + 1, count, lambda i, c: (pair(i, 0, block, block, False), c)[1], 0)
    dk_ref[...] = (dka_ref[...] * score_scale).astype(bf16)
    dv_ref[...] = dva_ref[...].astype(bf16)

    @pl.when(step == count - 1)
    def _():
        dq_ref[...] = dqa_ref[...].astype(bf16)

    comm.after(pl.program_id(0) * count + step, ins, outs, scratch)


def attend_backward(packed, grad_attended, lse, delta, lengths, comm=NoTransfers(), moved=()):
    tokens, width = grad_attended.shape
    groups = width // min(256, width)
    cols = width // groups
    heads = cols // HD
    blocks = tokens // BT
    column = pl.BlockSpec((tokens, cols), lambda g, j, n: (0, g))
    stats = pl.BlockSpec((8, tokens), lambda g, j, n: (g, 0))
    tile = pl.BlockSpec((BT, cols), lambda g, j, n: (j, g))
    move_ins, move_outs, move_shapes, move_scratch = comm.specs(moved) if moved else ([], [], [], [])
    return pl.pallas_call(
        functools.partial(attend_backward_kernel, heads, comm),
        grid_spec=pltpu.PrefetchScalarGridSpec(
            num_scalar_prefetch=1,
            grid=(groups, blocks),
            in_specs=[
                column,
                pl.BlockSpec((BT, cols), lambda g, j, n: (j, groups + g)),
                pl.BlockSpec((BT, cols), lambda g, j, n: (j, 2 * groups + g)),
                column,
                stats,
                stats,
            ]
            + move_ins,
            out_specs=[column, tile, tile] + move_outs,
            scratch_shapes=[
                pltpu.VMEM((blocks, heads * BT, cols), bf16),
                pltpu.VMEM((blocks, heads * BT, cols), bf16),
                pltpu.VMEM((heads * BT, cols), bf16),
                pltpu.VMEM((heads * BT, cols), bf16),
                pltpu.VMEM((tokens, cols), f32),
                pltpu.VMEM((BT, cols), f32),
                pltpu.VMEM((BT, cols), f32),
            ]
            + move_scratch,
        ),
        out_shape=[jax.ShapeDtypeStruct((tokens, width), bf16)] * 3 + move_shapes,
        compiler_params=params(2, 3 if moved else None),
        cost_estimate=attend_cost(tokens, width, 5),
        name="attend_backward",
    )(lengths, packed, packed, packed, grad_attended, lse, delta, *moved)


class AttendGather:
    ins, outs = 2, 2

    def scratch(self):
        return gather_sems(6)

    def pieces(self, ins, outs):
        up = [(None, outs[0], (at, width), route) for at, width, route in halves(outs[0].shape[3])]
        down = [(ins[0], outs[1], (at, w), route) for at, w, route in halves(ins[0].shape[1], 2)]
        return up + down

    def hops(self, name, ks, ins, outs, sems):
        copies = []
        for k in ks:
            src, dst, span, route = self.pieces(ins, outs)[k]
            if name == "z":
                copies += gather_z(src, dst, span, sems, 6 * k)
            elif name == "second":
                copies += gather_second(dst, span, route, sems, 6 * k)
            elif name == "third":
                copies += gather_third(dst, span, route, sems, 6 * k)
            elif name == "late 1":
                copies += late_z_first(src, dst, span, route, sems, 6 * k)
            elif name == "late 2":
                copies += late_z_second(dst, span, route, sems, 6 * k)
            else:
                copies += late_z_third(dst, span, sems, 6 * k)
        return copies

    def before(self, step, ins, outs, sems):
        def hops(name, *ks):
            return self.hops(name, ks, ins, outs, sems)

        @pl.when(step == 0)
        def _():
            greet(False)
            start_all(hops("late 1", 4, 5))
            start_all(hops("second", 0, 1))
            start_all(hops("z", 2, 3))

        @pl.when(step == 1)
        def _():
            wait_all(hops("late 1", 4, 5))
            start_all(hops("late 2", 4, 5))

        @pl.when(step == 2)
        def _():
            wait_all(hops("second", 0, 1))
            wait_all(hops("late 2", 4, 5))
            start_all(hops("third", 0, 1))
            start_all(hops("late 3", 4, 5))

        @pl.when(step == 4)
        def _():
            wait_all(hops("z", 2, 3))
            start_all(hops("second", 2, 3))

        @pl.when(step == 5)
        def _():
            wait_all(hops("second", 2, 3))
            start_all(hops("third", 2, 3))

    def after(self, step, ins, outs, sems):
        @pl.when(step == 5)
        def _():
            wait_all(self.hops("third", (0, 1, 2, 3), ins, outs, sems))
            wait_all(self.hops("late 3", (4, 5), ins, outs, sems))


class SumPart:
    slots = 5

    def __init__(self, grad, span, route, refs, sems, base):
        self.keep = grad.at[pl.ds(0, 512), pl.ds(*span)]
        self.sent = grad.at[pl.ds(512, 512), pl.ds(*span)]
        self.held, self.got_1, self.got_2, self.got_3 = refs
        self.sems, self.base = sems, base
        self.hops = ((2, 1), (1, 2))[route]

    @staticmethod
    def buffers(width):
        return [
            pltpu.VMEM((512, width), bf16),
            pltpu.VMEM((512, width), bf16),
            pltpu.VMEM((256, width), bf16),
            pltpu.VMEM((3, 64, width), bf16),
        ]

    def first(self):
        return [
            send(self.sent, self.got_1, self.sems, self.base, across(self.hops[0])),
            pltpu.make_async_copy(self.keep, self.held, self.sems[2].at[self.base]),
        ]

    def second(self):
        return [
            send(
                self.held.at[pl.ds(256, 256), :],
                self.got_2,
                self.sems,
                self.base + 1,
                across(self.hops[1]),
            )
        ]

    def third(self):
        return [
            send(
                self.held.at[pl.ds(64 * z, 64), :],
                self.got_3.at[z - 1],
                self.sems,
                self.base + 1 + z,
                across(4 * z),
            )
            for z in (1, 2, 3)
        ]

    def add(self, other, rows):
        def body(i, carry):
            at = pl.ds(pl.multiple_of(i * 64, 64), 64)
            self.held[at, :] = self.held[at, :] + other[at, :]
            return carry

        lax.fori_loop(0, rows // 64, body, 0)

    def to_second(self):
        wait_all(self.first())
        self.add(self.got_1, 512)
        start_all(self.second())

    def to_third(self):
        wait_all(self.second())
        self.add(self.got_2, 256)
        start_all(self.third())

    def result(self):
        wait_all(self.third())
        total = self.held[0:64, :].astype(f32)
        for z in range(3):
            total = total + self.got_3[z].astype(f32)
        return total


def sum_sems(parts):
    return [
        pltpu.SemaphoreType.DMA((SumPart.slots * parts,)),
        pltpu.SemaphoreType.DMA((SumPart.slots * parts,)),
        pltpu.SemaphoreType.DMA((SumPart.slots * parts,)),
    ]


class SmallSum:
    def __init__(self, refs, sems):
        self.got, self.sems = refs, sems

    @staticmethod
    def scratch():
        return [
            pltpu.VMEM((8, 8, 1024), f32),
            pltpu.VMEM((4, 8, 1024), f32),
            pltpu.SemaphoreType.DMA((10,)),
            pltpu.SemaphoreType.DMA((10,)),
        ]

    def near(self):
        bits = bits_of_me()
        place = self.got[0].at[lax.axis_index("mp") * 4 + bits[2] * 2 + bits[3]]
        devices = [across(k) for k in (1, 2, 3)] + [sibling()]
        devices += [sibling_across(k) for k in (1, 2, 3)]
        return [send(place, place, self.sems, k, device) for k, device in enumerate(devices)]

    def far(self):
        bits = bits_of_me()
        place = self.got[1].at[bits[0] * 2 + bits[1]]
        return [send(place, place, self.sems, 6 + k, across(4 * k)) for k in (1, 2, 3)]

    def begin(self, rows):
        bits = bits_of_me()
        self.got[0][lax.axis_index("mp") * 4 + bits[2] * 2 + bits[3]] = rows
        start_all(self.near())

    def middle(self, both):
        wait_all(self.near())
        row = lax.broadcasted_iota(jnp.int32, (8, 1024), 0)
        total = jnp.zeros((8, 1024), f32)
        for k in range(8):
            counts = (row < both) | (lax.axis_index("mp") == k // 4)
            total = total + jnp.where(counts, self.got[0][k], 0.0)
        bits = bits_of_me()
        self.got[1][bits[0] * 2 + bits[1]] = total
        start_all(self.far())

    def end(self):
        wait_all(self.far())
        return (self.got[1][0] + self.got[1][1]) + (self.got[1][2] + self.got[1][3])


class BackwardSum:
    def __init__(self, cols):
        self.cols = cols
        self.ins = len(cols) + 1
        self.outs = len(cols) + 1

    def specs(self, moved):
        vmem = [pl.BlockSpec((8, 1024), lambda g, j, n: (0, 0))]
        sizes = [(64, c) for c in self.cols]
        shapes = [jax.ShapeDtypeStruct(size, f32) for size in sizes]
        outs = [pl.BlockSpec(size, lambda g, j, n: (0, 0)) for size in sizes]
        scratch = []
        for c in self.cols:
            scratch += SumPart.buffers(c // 2) * 2
        scratch += sum_sems(2 * len(self.cols)) + SmallSum.scratch()
        return (
            [ANY] * len(self.cols) + vmem,
            outs + vmem,
            shapes + [jax.ShapeDtypeStruct((8, 1024), f32)],
            scratch,
        )

    def parts(self, ins, scratch):
        count = 2 * len(self.cols)
        sems = scratch[4 * count : 4 * count + 3]
        made = []
        for k in range(count):
            width = self.cols[k // 2] // 2
            refs = scratch[4 * k : 4 * k + 4]
            span = ((k % 2) * width, width)
            made.append(SumPart(ins[k // 2], span, k % 2, refs, sems, SumPart.slots * k))
        rest = scratch[4 * count + 3 :]
        return made, SmallSum(rest[:2], rest[2:])

    def before(self, step, ins, outs, scratch):
        parts, small = self.parts(ins, scratch)

        @pl.when(step == 0)
        def _():
            greet(True)
            small.begin(ins[-1][...])
            for part in parts[:2] + parts[4:]:
                start_all(part.first())

        @pl.when(step == 1)
        def _():
            small.middle(4)

        @pl.when(step == 2)
        def _():
            for part in parts[:2] + parts[4:]:
                part.to_second()
            for part in parts[2:4]:
                start_all(part.first())

        @pl.when(step == 5)
        def _():
            outs[-1][...] = small.end()

        @pl.when(step == 6)
        def _():
            for part in parts[:2] + parts[4:]:
                part.to_third()

        @pl.when(step == 7)
        def _():
            for part in parts[2:4]:
                part.to_second()

        @pl.when(step == 8)
        def _():
            for part in parts[2:4]:
                part.to_third()

    def after(self, step, ins, outs, scratch):
        parts, _ = self.parts(ins, scratch)

        @pl.when(step == 11)
        def _():
            for k, part in enumerate(parts):
                width = self.cols[k // 2] // 2
                span = slice((k % 2) * width, (k % 2 + 1) * width)
                outs[k // 2][:, span] = part.result()


def normalized(values):
    average = jnp.mean(values, axis=-1, keepdims=True)
    centred = values - average
    variance = jnp.mean(centred * centred, axis=-1, keepdims=True)
    inverse = lax.rsqrt(variance + norm_eps)
    return centred * inverse, inverse


def column_sum(values):
    return jnp.sum(values.reshape(-1, 8, values.shape[-1]), axis=0)


def turned(values, out_ref):
    flip = values.T
    bits = bits_of_me()
    for a in range(16):
        r = flipped(bits, a)
        slot = r[2] * 8 + r[3] * 4 + r[0] * 2 + r[1]
        out_ref[pl.ds(pl.multiple_of(slot * 64, 64), 64), :] = flip[a * 64 : (a + 1) * 64, :]


def shape(rows, cols, dtype=bf16):
    return jax.ShapeDtypeStruct((rows, cols), dtype)


def row_tile(cols):
    return pl.BlockSpec((BT, cols), lambda i: (i, 0))


def col_tile(rows):
    return pl.BlockSpec((rows, BT), lambda i: (0, i))


def whole(rows, cols):
    return pl.BlockSpec((rows, cols), lambda i: (0, 0))


def weight(cols):
    return pl.BlockSpec((1024, cols), lambda i: (0, 0), pipeline_mode=pl.Buffered(1))


def my_side():
    return lax.axis_index("mp")


def grid_call(kernel, steps, ins, outs, scratch, flops, name, collective=None, aliases={}):
    arrays = [a for a, _ in ins]
    nbytes = sum(a.size * a.dtype.itemsize for a in arrays)
    nbytes += sum(o.size * o.dtype.itemsize for o, _ in outs)
    return pl.pallas_call(
        kernel,
        grid=(steps,),
        in_specs=[s for _, s in ins],
        out_specs=[s for _, s in outs],
        scratch_shapes=scratch,
        out_shape=[o for o, _ in outs],
        input_output_aliases=aliases,
        compiler_params=params(1, collective),
        cost_estimate=cost(flops, nbytes),
        name=name,
    )(*arrays)


def vector(values):
    rows = values.shape[0] // 128
    return (values.reshape(rows, 128), whole(rows, 128))


def spread(ref, at=0, cols=1024):
    rows = ref[...].astype(f32)
    low, count = at // 128, cols // 128
    return jnp.concatenate([rows[k : k + 1, :] for k in range(low, low + count)], axis=1)


def qkv_bias(ref, cols):
    bias = ref[...].astype(f32)
    zero = jnp.zeros((1, bias.shape[1]), f32)
    return jnp.concatenate([bias[0:1, :], zero, bias[1:2, :]], axis=1)[:, cols]


class FirstGather:
    def __init__(self, wq, up, up_out, wo, out_out, sems):
        self.pieces = [(None, wq, (at, width), r) for at, width, r in chunk_halves(wq.shape[3])]
        self.pieces += [(up, up_out, (at, width), r) for at, width, r in halves(up.shape[1])]
        self.pieces += [(wo, out_out, (at, width), r) for at, width, r in halves(wo.shape[1])]
        self.sems = sems

    def z(self, *ks):
        copies = []
        for k in ks:
            src, dst, span, _ = self.pieces[k]
            if src is None:
                bits = bits_of_me()
                place = dst.at[bits[0] * 2 + bits[1], bits[2] * 2 + bits[3], :, pl.ds(*span)]
                copies += [
                    send(place, place, self.sems, 6 * k + hop, across(4 * (hop + 1)))
                    for hop in range(3)
                ]
            else:
                copies += gather_z(src, dst, span, self.sems, 6 * k)
        return copies

    def second(self, *ks):
        copies = []
        for k in ks:
            _, dst, span, route = self.pieces[k]
            copies += gather_second(dst, span, route, self.sems, 6 * k)
        return copies

    def third(self, *ks):
        copies = []
        for k in ks:
            _, dst, span, route = self.pieces[k]
            copies += gather_third(dst, span, route, self.sems, 6 * k)
        return copies


def chunk_halves(cols):
    width = cols // 4
    return [(k * width, width, k % 2) for k in range(4)]


def qkv_kernel(
    tiles,
    own,
    own_all,
    gain,
    shift,
    bias,
    w_mine,
    wo,
    up,
    turned_out,
    out,
    up_out,
    out_out,
    w_out,
    normed,
    came,
    wq,
    swap_send,
    swap_came,
    copy_sem,
    *sems,
):
    step = pl.program_id(0)
    side = my_side()
    moves = FirstGather(wq, up, up_out, wo, out_out, sems)
    local = w_mine.shape[2]

    def swap(k):
        return send(
            own_all.at[pl.ds(k * BT, BT), :], came.at[k], (swap_send, swap_came), k, sibling()
        )

    @pl.when(step == 0)
    def _():
        bits = bits_of_me()
        for c in range(3):
            wq[bits[0] * 2 + bits[1], bits[2] * 2 + bits[3], :, c * local : (c + 1) * local] = (
                w_mine[c]
            )
        greet(True)
        start_all(moves.z(0, 1))
        start_all([swap(k) for k in range(tiles)])

    def norm(values):
        scaled, _ = normalized(values.astype(f32))
        rows = (scaled * spread(gain) + spread(shift)).astype(bf16)
        first = lax.rem(step + side * tiles, 2 * tiles) * BT
        normed[pl.ds(pl.multiple_of(first, BT), BT), :] = rows
        turned(rows, turned_out)

    @pl.when(step < tiles)
    def _():
        norm(own[...])

    for k in range(tiles):

        @pl.when(step == tiles + k)
        def _():
            swap(k).wait()
            norm(came[k])

    @pl.when(step == 2 * tiles - 2)
    def _():
        wait_all(moves.z(0, 1))
        start_all(moves.second(0, 1))
        start_all(moves.z(2, 3))

    @pl.when(step == 2 * tiles)
    def _():
        wait_all(moves.second(0, 1))
        start_all(moves.third(0, 1))
        wait_all(moves.z(2, 3))
        start_all(moves.second(2, 3))
        start_all(moves.z(6, 7))
        start_all(moves.z(4, 5))
        wait_all(moves.third(0, 1))

    @pl.when(step == 2 * tiles + 1)
    def _():
        wait_all(moves.second(2, 3))
        start_all(moves.third(2, 3))

    half = out.shape[1]
    for c in range(2):

        @pl.when((step >= (2 + 2 * c) * tiles) & (step < (4 + 2 * c) * tiles))
        def _():
            @pl.when(step == (2 + 2 * c) * tiles)
            def _():
                if c:
                    wait_all(moves.third(2, 3))
                    wait_all(moves.z(6, 7))
                    start_all(moves.second(6, 7))
                    pltpu.make_async_copy(wq, w_out, copy_sem).start()

            first = (step - (2 + 2 * c) * tiles) * BT
            rows = normed[pl.ds(pl.multiple_of(first, BT), BT), :]
            cols = slice(c * half, (c + 1) * half)
            part = wq[:, :, :, cols].reshape(1024, half)
            out[...] = (dot_nn(rows, part) + qkv_bias(bias, cols)).astype(bf16)

    @pl.when(step == 5 * tiles)
    def _():
        wait_all(moves.second(6, 7))
        start_all(moves.third(6, 7))

    @pl.when(step == 6 * tiles - 1)
    def _():
        wait_all(moves.third(6, 7))
        wait_all(moves.z(4, 5))
        pltpu.make_async_copy(wq, w_out, copy_sem).wait()


def project_kernel(
    tiles,
    a,
    w,
    toks,
    bias,
    gain,
    shift,
    hid_out,
    normed_out,
    sent,
    came,
    sent_sems,
    came_sems,
):
    step = pl.program_id(0)

    def swap(k):
        return send(sent.at[k], came.at[k], (sent_sems, came_sems), k, sibling())

    @pl.when(step == 0)
    def _():
        greet_sibling()

    partial = dot_nt(a[...], w[...])
    for k in range(tiles):

        @pl.when(step == k)
        def _():
            sent[k] = partial.astype(bf16)
            swap(k).start()

        @pl.when(step == tiles + k)
        def _():
            swap(k).wait()
            hidden = toks[...].astype(f32) + (partial + came[k].astype(f32) + spread(bias))
            hid_out[...] = hidden
            scaled, _ = normalized(hidden)
            normed_out[...] = (scaled * spread(gain) + spread(shift)).astype(bf16)


def feed_kernel(
    tiles,
    x_all,
    c_all,
    bias,
    wu,
    wd,
    ffn_own,
    norm_own,
    ffn_came,
    norm_came,
    up_out,
    down_out,
    bsum,
    up_total,
    down_total,
    act,
    gpre,
    xt,
    ct,
    xs,
    cs,
    ffn_sent,
    norm_sent,
    local_sems,
    send_sems,
    came_sems,
    out_sems,
):
    step = pl.program_id(0)
    remote = (send_sems, came_sems)

    def rows(k):
        return pl.ds(k * BT, BT)

    def local(k):
        return [
            pltpu.make_async_copy(x_all.at[rows(k), :], xs.at[k], local_sems.at[k]),
            pltpu.make_async_copy(c_all.at[rows(k), :], cs.at[k], local_sems.at[tiles + k]),
        ]

    def swapped(k):
        return [
            send(x_all.at[rows(k), :], xs.at[tiles + k], remote, k, sibling()),
            send(c_all.at[rows(k), :], cs.at[tiles + k], remote, tiles + k, sibling()),
        ]

    def returned(k):
        return [
            send(ffn_sent, ffn_came.at[rows(k), :], remote, 2 * tiles + k, sibling()),
            send(norm_sent, norm_came.at[rows(k), :], remote, 3 * tiles + k, sibling()),
        ]

    @pl.when(step == 0)
    def _():
        for k in range(tiles):
            start_all(local(k))
        bsum[...] = jnp.zeros(bsum.shape, f32)
        greet_sibling()
        for k in range(tiles):
            start_all(swapped(k))

    for k in range(tiles):

        @pl.when(step == k)
        def _():
            wait_all(local(k))

        @pl.when(step == tiles + k)
        def _():
            wait_all(swapped(k))

    x, c = xs[step], cs[step]
    xt[...] = x.T
    ct[...] = c.T
    width = 512
    spans = [slice(at, at + width) for at in range(0, wu.shape[1], width)]
    for cols in spans:
        value = dot_nn(x, wu[:, cols]) + spread(bias, cols.start, width)
        upstream = dot_nn(c, wd[:, cols])
        square = value * value
        bent = jnp.tanh(value * (gelu_coeff + (gelu_coeff * 0.044715) * square))
        half_up = 0.5 + 0.5 * bent
        act[:, cols] = (value * half_up).astype(bf16)
        slope = half_up + value * (half_up * (1.0 - bent)) * (
            gelu_coeff + (3.0 * 0.044715 * gelu_coeff) * square
        )
        grad = (upstream * slope).astype(bf16)
        gpre[:, cols] = grad
        bsum[:, cols] += column_sum(grad.astype(f32))
    ffn = dot_nt(act[...], wd[...]).astype(bf16)
    norm = dot_nt(gpre[...], wu[...]).astype(bf16)

    @pl.when(step < tiles)
    def _():
        ffn_own[...] = ffn
        norm_own[...] = norm

    for k in range(tiles):

        @pl.when(step == tiles + k)
        def _():
            if k:
                wait_all(returned(k - 1))
            ffn_sent[...] = ffn
            norm_sent[...] = norm
            start_all(returned(k))

    @pl.when(step == 0)
    def _():
        for cols in spans:
            down_total[:, cols] = dot_nn(ct[...], act[:, cols])
        for cols in spans:
            up_total[:, cols] = dot_nn(xt[...], gpre[:, cols])

    @pl.when(step > 0)
    def _():
        for cols in spans:
            down_total[:, cols] += dot_nn(ct[...], act[:, cols])
        for cols in spans:
            up_total[:, cols] += dot_nn(xt[...], gpre[:, cols])

    def leave(total, stage, out, base):
        half = total.shape[1] // 2
        bits = bits_of_me()
        copies = []
        for top in range(2):
            for route in range(2):
                part = total[512 * top : 512 * top + 512, route * half : route * half + half]
                stage[top * 2 + route] = part.astype(bf16)
        for a in range(16):
            r = flipped(bits, a)
            for route in range(2):
                slot = r[2 + route] * 8 + r[3 - route] * 4 + r[0] * 2 + r[1]
                copies.append(
                    pltpu.make_async_copy(
                        stage.at[(a // 8) * 2 + route, pl.ds((a % 8) * 64, 64), :],
                        out.at[
                            pl.ds(pl.multiple_of(slot * 64, 64), 64), pl.ds(route * half, half)
                        ],
                        out_sems.at[base + 2 * a + route],
                    )
                )
        start_all(copies)
        return copies

    @pl.when(step == 2 * tiles - 1)
    def _():
        copies = leave(down_total, cs, down_out, 0)
        copies += leave(up_total, xs, up_out, 32)
        wait_all(copies)
        wait_all(returned(tiles - 1))


def middle_kernel(
    tiles,
    hid,
    f_own,
    f_came,
    g_own,
    g_came,
    cot,
    bias,
    gain,
    exact,
    attended,
    w,
    out,
    gattn,
    do_out,
    delta_out,
    grad_w,
    sums,
    turned_rows,
    total,
    now,
    sent,
    came,
    sent_sems,
    came_sems,
):
    step = pl.program_id(0)

    def swap(k):
        return send(sent.at[k], came.at[k], (sent_sems, came_sems), k, sibling())

    @pl.when(step == 0)
    def _():
        sums[...] = jnp.zeros(sums.shape, f32)
        total[...] = jnp.zeros(total.shape, f32)
        greet_sibling()

    @pl.when(step < tiles)
    def _():
        hidden = hid[...]
        grad_out = cot[...].astype(f32)
        branch = f_own[...].astype(f32) + f_came[...].astype(f32) + spread(bias)
        out[...] = (hidden + branch).astype(bf16)
        scaled, inverse = normalized(hidden)
        grad_norm = g_own[...].astype(f32) + g_came[...].astype(f32)
        through = grad_norm * spread(gain)
        centre = jnp.mean(through, axis=-1, keepdims=True)
        along = jnp.mean(through * scaled, axis=-1, keepdims=True)
        grad = (grad_out + inverse * (through - centre - scaled * along)).astype(bf16)
        gattn[...] = grad
        now[...] = grad
        sums[0:8, :] += column_sum(grad_norm * scaled)
        sums[8:16, :] += column_sum(grad_norm)
        sums[16:24, :] += column_sum(grad.astype(f32))
        sums[24:32, :] += column_sum(grad_out)

    for k in range(tiles):

        @pl.when(step == k)
        def _():
            sent[k] = now[...]
            swap(k).start()

        @pl.when(step == tiles + k)
        def _():
            swap(k).wait()
            now[...] = came[k]

    grad = now[...]
    turned(grad, turned_rows)
    part = dot_nn(grad, w[...]).astype(bf16)
    do_out[...] = part
    product = part.astype(f32) * exact[...]
    head = lax.broadcasted_iota(jnp.int32, (part.shape[1], 128), 0) // HD
    place = lax.broadcasted_iota(jnp.int32, (part.shape[1], 128), 1)
    pick = jnp.where(place == (head // 4) * 8 + head % 4, 1.0, 0.0).astype(bf16)
    high = product.astype(bf16)
    rest = (product - high.astype(f32)).astype(bf16)
    delta_out[...] = (dot_nn(high, pick) + dot_nn(rest, pick)).T[:16, :]
    total[...] += dot_nn(turned_rows[...], attended[...])

    @pl.when(step == 2 * tiles - 1)
    def _():
        write_grad(total, grad_w)


def write_grad(total, out):
    half = total.shape[1] // 2
    out[:, :half] = total[:, :half].astype(bf16)
    for to, at in enumerate((0, 2, 1, 3)):
        there, here = slice(256 * to, 256 * to + 256), slice(256 * at, 256 * at + 256)
        out[there, half:] = total[here, half:].astype(bf16)


class HeldSumPart(SumPart):
    def __init__(self, route, refs, sems, base):
        self.held, self.sent = refs[:2]
        self.got_1, self.got_2, self.got_3 = refs[2:]
        self.sems, self.base = sems, base
        self.hops = ((2, 1), (1, 2))[route]

    @staticmethod
    def buffers(width):
        return [pltpu.VMEM((512, width), bf16)] + SumPart.buffers(width)

    def first(self):
        return [send(self.sent, self.got_1, self.sems, self.base, across(self.hops[0]))]


def last_scratch(cols):
    made = []
    for _ in range(4):
        made += HeldSumPart.buffers(cols // 4)
    return made + sum_sems(4) + SmallSum.scratch()


def last_kernel(
    tiles,
    turned_rows,
    dq,
    dk,
    dv,
    w,
    toks,
    gattn,
    gain,
    out,
    grad_w,
    small_out,
    sums,
    qv_sums,
    total,
    sent,
    came,
    send_sems,
    recv_sems,
    *refs,
):
    step = pl.program_id(0)
    blocks = 2 * tiles
    parts = [
        HeldSumPart(k % 2, refs[5 * k : 5 * k + 5], refs[20:23], SumPart.slots * k)
        for k in range(4)
    ]
    tiny = SmallSum(refs[23:25], refs[25:27])
    local = dq.shape[1]
    quarter = 3 * local // 4

    def swap(k):
        return send(sent.at[k], came.at[k], (send_sems, recv_sems), k, sibling())

    @pl.when(step == 0)
    def _():
        greet(True)
        sums[...] = jnp.zeros(sums.shape, f32)
        qv_sums[...] = jnp.zeros(qv_sums.shape, f32)

    grads = jnp.concatenate([dq[...], dk[...], dv[...]], axis=1)

    @pl.when(step < blocks)
    def _():
        qv_sums[:, :local] += column_sum(dq[...].astype(f32))
        qv_sums[:, local:] += column_sum(dv[...].astype(f32))

    for c in range(2):

        @pl.when((step >= c * blocks) & (step < (c + 1) * blocks))
        def _():
            spans = [slice(r * 2 * quarter + c * quarter, r * 2 * quarter + (c + 1) * quarter) for r in range(2)]
            term = dot_nn(turned_rows[...], jnp.concatenate([grads[:, s] for s in spans], axis=1))

            @pl.when(step == c * blocks)
            def _():
                total[...] = term

            @pl.when(step > c * blocks)
            def _():
                total[...] += term

            @pl.when(step == (c + 1) * blocks - 1)
            def _():
                one, two = parts[2 * c], parts[2 * c + 1]
                one.held[...] = total[0:512, :quarter].astype(bf16)
                one.sent[...] = total[512:1024, :quarter].astype(bf16)
                two.held[0:256, :] = total[0:256, quarter:].astype(bf16)
                two.held[256:512, :] = total[512:768, quarter:].astype(bf16)
                two.sent[0:256, :] = total[256:512, quarter:].astype(bf16)
                two.sent[256:512, :] = total[768:1024, quarter:].astype(bf16)
                start_all(one.first() + two.first())

    @pl.when(step == 2 * blocks + 1)
    def _():
        for part in parts[:2]:
            part.to_second()

    @pl.when(step == 2 * blocks + 3)
    def _():
        for part in parts[:2]:
            part.to_third()

    @pl.when(step == 2 * blocks + 4)
    def _():
        for part in parts[2:]:
            part.to_second()

    @pl.when(step == 2 * blocks + 5)
    def _():
        for part in parts[2:]:
            part.to_third()

    @pl.when(step >= 2 * blocks)
    def _():
        rows = dot_nt(grads, w[...])
        for k in range(tiles):

            @pl.when(step == 2 * blocks + k)
            def _():
                sent[k] = rows.astype(bf16)
                swap(k).start()

            @pl.when(step == 2 * blocks + tiles + k)
            def _():
                swap(k).wait()
                grad_norm = rows + came[k].astype(f32)
                scaled, inverse = normalized(toks[...].astype(f32))
                through = grad_norm * spread(gain)
                centre = jnp.mean(through, axis=-1, keepdims=True)
                along = jnp.mean(through * scaled, axis=-1, keepdims=True)
                grad_in = inverse * (through - centre - scaled * along)
                out[...] = (gattn[...].astype(f32) + grad_in).astype(bf16)
                sums[0:8, :] += column_sum(grad_norm * scaled)
                sums[8:16, :] += column_sum(grad_norm)

    @pl.when(step == pl.num_programs(0) - 1)
    def _():
        row = lax.broadcasted_iota(jnp.int32, (8, 1024), 0)
        first = jnp.sum(sums[0:8, :], axis=0, keepdims=True)
        second = jnp.sum(sums[8:16, :], axis=0, keepdims=True)
        third = jnp.sum(qv_sums[...], axis=0, keepdims=True)
        rows = jnp.where(row == 0, first, jnp.where(row == 1, second, third))
        tiny.begin(jnp.where(row < 3, rows, 0.0))
        tiny.middle(2)
        small_out[...] = tiny.end()
        for k, part in enumerate(parts):
            at = (k % 2) * 2 * quarter + (k // 2) * quarter
            summed = part.result()
            edges = [at] + [c for c in (local, 2 * local) if at < c < at + quarter] + [at + quarter]
            for low, high in zip(edges[:-1], edges[1:]):
                to = low % local
                grad_w[low // local, :, to : to + high - low] = summed[:, low - at : high - at]


def layer_on_pairs(
    tokens,
    slot_lengths,
    gain_one,
    shift_one,
    w_qkv,
    bias_qv,
    w_out,
    bias_out,
    gain_two,
    shift_two,
    w_up,
    bias_up,
    w_down,
    bias_down,
    cotangent,
):
    own_rows, width = tokens.shape
    total_rows = 2 * own_rows
    tiles = own_rows // BT
    local = w_qkv.shape[2]
    hidden_cols = w_up.shape[1]
    side_cols = 3 * local
    lengths = slot_lengths[0]

    half_cols = side_cols // 2
    normed_at = pl.BlockSpec(
        (width, BT),
        lambda i: (0, lax.rem(jnp.minimum(i, 2 * tiles - 1) + my_side() * tiles, 2 * tiles)),
    )
    packed_at = pl.BlockSpec(
        (BT, half_cols),
        lambda i: (
            lax.rem(jnp.maximum(i - 2 * tiles, 0), 2 * tiles),
            jnp.maximum(i - 2 * tiles, 0) // (2 * tiles),
        ),
    )
    rows_turned, packed, up_blocks, out_blocks, qkv_blocks = grid_call(
        functools.partial(qkv_kernel, tiles),
        6 * tiles,
        [
            (tokens, pl.BlockSpec((BT, width), lambda i: (jnp.minimum(i, tiles - 1), 0))),
            (tokens, ANY),
            vector(gain_one),
            vector(shift_one),
            (bias_qv, whole(2, local)),
            (w_qkv.transpose(1, 0, 2), pl.BlockSpec((3, 64, local), lambda i: (0, 0, 0))),
            (w_out.T, ANY),
            (w_up, ANY),
        ],
        [
            (shape(width, total_rows), normed_at),
            (shape(total_rows, side_cols), packed_at),
            (jax.ShapeDtypeStruct((4, 4, 64, hidden_cols), bf16), ANY),
            (jax.ShapeDtypeStruct((4, 4, 64, local), bf16), ANY),
            (jax.ShapeDtypeStruct((4, 4, 64, side_cols), bf16), ANY),
        ],
        [
            pltpu.VMEM((total_rows, width), bf16),
            pltpu.VMEM((tiles, BT, width), bf16),
            pltpu.VMEM((4, 4, 64, side_cols), bf16),
            pltpu.SemaphoreType.DMA((tiles,)),
            pltpu.SemaphoreType.DMA((tiles,)),
            pltpu.SemaphoreType.DMA(()),
        ]
        + gather_sems(8),
        2 * total_rows * width * side_cols,
        "qkv",
        1,
    )
    qkv_w = qkv_blocks.reshape(width, side_cols)
    attended, exact, lse, up_blocks, down_blocks = attend_forward(
        packed,
        lengths,
        AttendGather(),
        (w_down.T, up_blocks),
        jax.ShapeDtypeStruct((4, 4, 64, hidden_cols), bf16),
    )
    up_w = up_blocks.reshape(width, hidden_cols)
    out_w = out_blocks.reshape(width, local)

    def two_way(cols, skip=0):
        def at(i):
            return lax.rem(jnp.maximum(i - skip, 0) + (1 - my_side()) * tiles, 2 * tiles)

        return pl.BlockSpec((BT, cols), lambda i: (at(i), 0))

    late_tile = pl.BlockSpec((BT, width), lambda i: (jnp.maximum(i - tiles, 0), 0))
    swap_buffers = [
        pltpu.VMEM((tiles, BT, width), bf16),
        pltpu.VMEM((tiles, BT, width), bf16),
        pltpu.SemaphoreType.DMA((tiles,)),
        pltpu.SemaphoreType.DMA((tiles,)),
    ]
    hidden, normed_own = grid_call(
        functools.partial(project_kernel, tiles),
        2 * tiles,
        [
            (attended, two_way(local)),
            (out_w, weight(local)),
            (tokens, late_tile),
            vector(bias_out),
            vector(gain_two),
            vector(shift_two),
        ],
        [
            (shape(own_rows, width, f32), late_tile),
            (shape(own_rows, width), late_tile),
        ],
        swap_buffers,
        4 * own_rows * width * local,
        "project",
        6,
    )
    down_w = down_blocks.reshape(width, hidden_cols)
    own_at = pl.BlockSpec((BT, width), lambda i: (jnp.minimum(i, tiles - 1), 0))
    ffn_own, norm_own, ffn_came, norm_came, up_grad, down_grad, bsum = grid_call(
        functools.partial(feed_kernel, tiles),
        2 * tiles,
        [
            (normed_own, ANY),
            (cotangent, ANY),
            vector(bias_up),
            (up_w, weight(hidden_cols)),
            (down_w, weight(hidden_cols)),
        ],
        [
            (shape(own_rows, width), own_at),
            (shape(own_rows, width), own_at),
            (shape(own_rows, width), ANY),
            (shape(own_rows, width), ANY),
            (shape(width, hidden_cols), ANY),
            (shape(width, hidden_cols), ANY),
            (shape(8, hidden_cols, f32), whole(8, hidden_cols)),
        ],
        [
            pltpu.VMEM((width, hidden_cols), f32),
            pltpu.VMEM((width, hidden_cols), f32),
            pltpu.VMEM((BT, hidden_cols), bf16),
            pltpu.VMEM((BT, hidden_cols), bf16),
            pltpu.VMEM((width, BT), bf16),
            pltpu.VMEM((width, BT), bf16),
            pltpu.VMEM((2 * tiles, BT, width), bf16),
            pltpu.VMEM((2 * tiles, BT, width), bf16),
            pltpu.VMEM((BT, width), bf16),
            pltpu.VMEM((BT, width), bf16),
            pltpu.SemaphoreType.DMA((2 * tiles,)),
            pltpu.SemaphoreType.DMA((4 * tiles,)),
            pltpu.SemaphoreType.DMA((4 * tiles,)),
            pltpu.SemaphoreType.DMA((64,)),
        ],
        24 * own_rows * width * hidden_cols,
        "feed",
        5,
    )
    def mine_first(i):
        return lax.rem(i + my_side() * tiles, 2 * tiles)

    natural_tile = pl.BlockSpec((BT, local), lambda i: (mine_first(i), 0))
    output, grad_attn, grad_attended, delta, out_grad, middle_sums = grid_call(
        functools.partial(middle_kernel, tiles),
        2 * tiles,
        [
            (hidden, own_at),
            (ffn_own, own_at),
            (ffn_came, own_at),
            (norm_own, own_at),
            (norm_came, own_at),
            (cotangent, own_at),
            vector(bias_down),
            vector(gain_two),
            (exact, natural_tile),
            (attended, natural_tile),
            (out_w, weight(local)),
        ],
        [
            (shape(own_rows, width), own_at),
            (shape(own_rows, width), own_at),
            (shape(total_rows, local), natural_tile),
            (shape(16, total_rows, f32), pl.BlockSpec((16, BT), lambda i: (0, mine_first(i)))),
            (shape(width, local), whole(width, local)),
            (shape(32, width, f32), whole(32, width)),
        ],
        [
            pltpu.VMEM((width, BT), bf16),
            pltpu.VMEM((width, local), f32),
            pltpu.VMEM((BT, width), bf16),
        ]
        + swap_buffers,
        4 * total_rows * width * local,
        "middle",
        7,
    )
    early = middle_sums.reshape(4, 8, width).sum(axis=1)
    up_bias = bsum.sum(axis=0).reshape(-1, width)
    early = jnp.concatenate([early, up_bias, jnp.zeros((2, width), f32)])
    moved = (down_grad, up_grad, out_grad, early)
    grad_q, grad_k, grad_v, grad_down, grad_up, grad_w_out, early = attend_backward(
        packed,
        grad_attended,
        lse,
        delta,
        lengths,
        BackwardSum((hidden_cols, hidden_cols, local)),
        moved,
    )
    blocks = 2 * tiles

    def grad_at(i):
        later = lax.rem(jnp.maximum(i - 2 * blocks, 0) + (1 - my_side()) * tiles, blocks)
        return jnp.where(i < 2 * blocks, lax.rem(i, blocks), later)

    grad_tile = pl.BlockSpec((BT, local), lambda i: (grad_at(i), 0))
    turned_tile = pl.BlockSpec(
        (width, BT), lambda i: (0, jnp.where(i < 2 * blocks, lax.rem(i, blocks), blocks - 1))
    )
    last_tile = pl.BlockSpec(
        (BT, width), lambda i: (jnp.maximum(i - 2 * blocks - tiles, 0), 0)
    )
    grad_tokens, grad_w_qkv, late = grid_call(
        functools.partial(last_kernel, tiles),
        3 * blocks,
        [(rows_turned, turned_tile)]
        + [(g, grad_tile) for g in (grad_q, grad_k, grad_v)]
        + [
            (qkv_w, weight(side_cols)),
            (tokens, last_tile),
            (grad_attn, last_tile),
            vector(gain_one),
        ],
        [
            (shape(own_rows, width), last_tile),
            (
                jax.ShapeDtypeStruct((3, 64, local), f32),
                pl.BlockSpec((3, 64, local), lambda i: (0, 0, 0)),
            ),
            (shape(8, width, f32), whole(8, width)),
        ],
        [
            pltpu.VMEM((16, width), f32),
            pltpu.VMEM((8, width), f32),
            pltpu.VMEM((width, side_cols // 2), f32),
        ]
        + swap_buffers
        + last_scratch(side_cols),
        4 * total_rows * width * side_cols,
        "last",
        4,
    )
    return (
        output,
        grad_tokens,
        late[0],
        late[1],
        grad_w_qkv.transpose(1, 0, 2),
        late[2].reshape(2, local),
        grad_w_out.T,
        early[2],
        early[0],
        early[1],
        grad_up,
        early[4:6].reshape(-1),
        grad_down.T,
        early[3],
    )


def gelu_tanh(values):
    inner = gelu_coeff * (values + 0.044715 * values * values * values)
    return 0.5 * values * (1.0 + jnp.tanh(inner))


def gelu_slope(values):
    inner = gelu_coeff * (values + 0.044715 * values * values * values)
    bent = jnp.tanh(inner)
    return 0.5 * (1.0 + bent) + 0.5 * values * (1.0 - bent * bent) * gelu_coeff * (
        1.0 + 3.0 * 0.044715 * values * values
    )


def norm_forward(values, gain_vec, shift_vec):
    average = jnp.mean(values, axis=-1, keepdims=True)
    centred = values - average
    variance = jnp.mean(centred * centred, axis=-1, keepdims=True)
    inverse = lax.rsqrt(variance + norm_eps)
    scaled = centred * inverse
    return (scaled * gain_vec.astype(f32) + shift_vec.astype(f32), scaled, inverse)


def norm_backward(grad_out, scaled, inverse, gain_vec):
    grad_scaled = grad_out * gain_vec.astype(f32)
    centre_term = jnp.mean(grad_scaled, axis=-1, keepdims=True)
    slope_term = jnp.mean(grad_scaled * scaled, axis=-1, keepdims=True)
    grad_in = inverse * (grad_scaled - centre_term - scaled * slope_term)
    return (grad_in, jnp.sum(grad_out * scaled, axis=0), jnp.sum(grad_out, axis=0))


def layer_by_collectives(
    tokens,
    slot_lengths,
    gain_one,
    shift_one,
    w_qkv,
    bias_qv,
    w_out,
    bias_out,
    gain_two,
    shift_two,
    w_up,
    bias_up,
    w_down,
    bias_down,
    cotangent,
):
    w_qkv, w_out, w_up, w_down = (
        lax.all_gather(w_qkv, "dp", axis=0, tiled=True),
        lax.all_gather(w_out, "dp", axis=1, tiled=True),
        lax.all_gather(w_up, "dp", axis=0, tiled=True),
        lax.all_gather(w_down, "dp", axis=1, tiled=True),
    )
    lengths = slot_lengths[0]
    residual = tokens.astype(f32)
    normed_one, scaled_one, inverse_one = norm_forward(residual, gain_one, shift_one)
    rows_one = lax.all_gather(normed_one.astype(bf16), "mp", axis=0, tiled=True)
    packed = jnp.einsum("td,dcf->tcf", rows_one, w_qkv, preferred_element_type=f32)
    zero_bias = jnp.zeros_like(bias_qv[0])
    packed_bias = jnp.stack([bias_qv[0], zero_bias, bias_qv[1]]).astype(f32)
    packed = (packed + packed_bias[None]).astype(bf16)
    local = packed.shape[2]
    packed_rows = packed.reshape(packed.shape[0], -1)
    attended, exact_out, log_totals = attend_forward(packed_rows, lengths)
    hidden = (
        residual
        + lax.psum_scatter(
            jnp.dot(attended, w_out, preferred_element_type=f32),
            "mp",
            scatter_dimension=0,
            tiled=True,
        )
        + bias_out.astype(f32)
    )
    normed_two, scaled_two, inverse_two = norm_forward(hidden, gain_two, shift_two)
    normed_low = normed_two.astype(bf16)
    rows_two = lax.all_gather(normed_low, "mp", axis=0, tiled=True)
    preact = jnp.dot(rows_two, w_up, preferred_element_type=f32) + bias_up.astype(
        f32
    )
    active = gelu_tanh(preact).astype(bf16)
    ffn_out = lax.psum_scatter(
        jnp.dot(active, w_down, preferred_element_type=f32).astype(bf16),
        "mp",
        scatter_dimension=0,
        tiled=True,
    ).astype(f32)
    output = (hidden + ffn_out + bias_down.astype(f32)).astype(bf16)
    grad_out = cotangent.astype(f32)
    grad_rows = lax.all_gather(cotangent, "mp", axis=0, tiled=True)
    grad_active = jnp.einsum("td,fd->tf", grad_rows, w_down, preferred_element_type=f32)
    grad_pre = (grad_active * gelu_slope(preact)).astype(bf16)
    grad_up = jnp.einsum("td,tf->df", rows_two, grad_pre, preferred_element_type=f32)
    grad_down = jnp.einsum("tf,td->fd", active, grad_rows, preferred_element_type=f32)
    grad_bias_up = jnp.sum(grad_pre.astype(f32), axis=0)
    grad_norm_two = lax.psum_scatter(
        jnp.einsum("tf,df->td", grad_pre, w_up, preferred_element_type=f32),
        "mp",
        scatter_dimension=0,
        tiled=True,
    )
    grad_in_two, grad_gain_two, grad_shift_two = norm_backward(
        grad_norm_two, scaled_two, inverse_two, gain_two
    )
    grad_hidden = grad_out + grad_in_two
    grad_attn = grad_hidden.astype(bf16)
    grad_attn_rows = lax.all_gather(grad_attn, "mp", axis=0, tiled=True)
    grad_w_out = jnp.einsum(
        "tf,td->fd", attended, grad_attn_rows, preferred_element_type=f32
    )
    grad_attended = jnp.einsum(
        "td,fd->tf", grad_attn_rows, w_out, preferred_element_type=f32
    ).astype(bf16)
    product = (grad_attended.astype(f32) * exact_out).reshape(grad_attended.shape[0], -1, HD)
    delta = jnp.sum(product, axis=-1).T
    groups = log_totals.shape[0] // 8
    delta = delta.reshape(groups, -1, delta.shape[1])
    delta = jnp.pad(delta, ((0, 0), (0, 8 - delta.shape[1]), (0, 0))).reshape(8 * groups, -1)
    grads = attend_backward(packed_rows, grad_attended, log_totals, delta, lengths)
    grad_packed = jnp.stack(grads, axis=1)
    grad_w_qkv = jnp.einsum(
        "td,tcf->dcf", rows_one, grad_packed, preferred_element_type=f32
    )
    grad_bias_qv = jnp.stack(
        [
            jnp.sum(grad_packed[:, 0].astype(f32), axis=0),
            jnp.sum(grad_packed[:, 2].astype(f32), axis=0),
        ]
    )
    grad_norm_one = lax.psum_scatter(
        jnp.einsum("tcf,dcf->td", grad_packed, w_qkv, preferred_element_type=f32),
        "mp",
        scatter_dimension=0,
        tiled=True,
    )
    grad_in_one, grad_gain_one, grad_shift_one = norm_backward(
        grad_norm_one, scaled_one, inverse_one, gain_one
    )
    grad_tokens = (grad_hidden + grad_in_one).astype(bf16)
    grad_bias_out = jnp.sum(grad_attn.astype(f32), axis=0)
    grad_bias_down = jnp.sum(grad_out, axis=0)
    grad_w_qkv, grad_w_out, grad_up, grad_down = (
        lax.psum_scatter(grad_w_qkv, "dp", scatter_dimension=0, tiled=True),
        lax.psum_scatter(grad_w_out, "dp", scatter_dimension=1, tiled=True),
        lax.psum_scatter(grad_up, "dp", scatter_dimension=0, tiled=True),
        lax.psum_scatter(grad_down, "dp", scatter_dimension=1, tiled=True),
    )
    small_grads = lax.psum(
        (
            grad_gain_one,
            grad_shift_one,
            grad_bias_out,
            grad_gain_two,
            grad_shift_two,
            grad_bias_down,
        ),
        ("dp", "mp"),
    )
    grad_bias_qv, grad_bias_up = lax.psum((grad_bias_qv, grad_bias_up), "dp")
    return (
        output,
        grad_tokens,
        small_grads[0],
        small_grads[1],
        grad_w_qkv,
        grad_bias_qv,
        grad_w_out,
        small_grads[2],
        small_grads[3],
        small_grads[4],
        grad_up,
        grad_bias_up,
        grad_down,
        small_grads[5],
    )


def solution(mesh):
    pairs = dict(mesh.shape) == {"dp": 16, "mp": 2}
    layer = layer_on_pairs if pairs else layer_by_collectives
    return jax.shard_map(
        layer,
        mesh=mesh,
        in_specs=(
            P(("dp", "mp"), None),
            P("dp", None),
            P(),
            P(),
            P("dp", None, "mp"),
            P(None, "mp"),
            P("mp", "dp"),
            P(),
            P(),
            P(),
            P("dp", "mp"),
            P("mp"),
            P("mp", "dp"),
            P(),
            P(("dp", "mp"), None),
        ),
        out_specs=(
            P(("dp", "mp"), None),
            P(("dp", "mp"), None),
            P(),
            P(),
            P("dp", None, "mp"),
            P(None, "mp"),
            P("mp", "dp"),
            P(),
            P(),
            P(),
            P("dp", "mp"),
            P("mp"),
            P("mp", "dp"),
            P(),
        ),
        check_vma=False,
    )
```

```python
import functools

import jax
import jax.numpy as jnp
from jax import lax
from jax.experimental import pallas as pl
from jax.experimental.pallas import tpu as pltpu
from jax.sharding import PartitionSpec as P

HD = 64
LONG_LEN = 3072
BT = 512
VMEM_CAP = 60 * 1024 * 1024

f32 = jnp.float32
bf16 = jnp.bfloat16
norm_eps = 1e-05
masked_score = -1e30
gelu_coeff = 0.7978845608028654
score_scale = HD ** (-0.5)
safe_sum = 1e30


def dot_nt(left, right):
    return lax.dot_general(left, right, (((1,), (1,)), ((), ())), preferred_element_type=f32)


def dot_nn(left, right):
    return lax.dot_general(left, right, (((1,), (0,)), ((), ())), preferred_element_type=f32)


def dot_tn(left, right):
    return lax.dot_general(left, right, (((0,), (0,)), ((), ())), preferred_element_type=f32)


def params(axes=1, collective=None):
    if collective is None:
        return pltpu.CompilerParams(
            vmem_limit_bytes=VMEM_CAP, dimension_semantics=("arbitrary",) * axes
        )
    return pltpu.CompilerParams(
        vmem_limit_bytes=VMEM_CAP,
        dimension_semantics=("arbitrary",) * axes,
        collective_id=collective,
        has_side_effects=True,
    )


def cost(flops, nbytes, exps=0):
    return pl.CostEstimate(flops=int(flops), bytes_accessed=int(nbytes), transcendentals=int(exps))


ANY = pl.BlockSpec(memory_space=pl.ANY)


def bits_of_me():
    me = lax.axis_index("dp")
    return (me // 8, (me // 4) % 2, (me // 2) % 2, me % 2)


def flipped(bits, which):
    return tuple(1 - b if which & (8 >> k) else b for k, b in enumerate(bits))


def index_of(bits):
    return bits[0] * 8 + bits[1] * 4 + bits[2] * 2 + bits[3]


def across(which):
    return {"dp": index_of(flipped(bits_of_me(), which))}


def sibling():
    return {"mp": 1 - lax.axis_index("mp")}


MESH_ID = pl.DeviceIdType.MESH
HOPS = (1, 2, 4, 8, 12)


def sibling_across(which):
    return {**across(which), **sibling()}


def greet(with_small):
    devices = [across(hop) for hop in HOPS]
    if with_small:
        devices += [across(3), sibling()] + [sibling_across(k) for k in (1, 2, 3)]
    greet_only(devices)


def greet_only(devices):
    barrier = pltpu.get_barrier_semaphore()
    for device in devices:
        pl.semaphore_signal(barrier, inc=1, device_id=device, device_id_type=MESH_ID)
    pl.semaphore_wait(barrier, len(devices))


def greet_sibling():
    greet_only([sibling()])


def send(src, dst, sems, slot, device):
    return pltpu.make_async_remote_copy(
        src_ref=src,
        dst_ref=dst,
        send_sem=sems[0].at[slot],
        recv_sem=sems[1].at[slot],
        device_id=device,
        device_id_type=MESH_ID,
    )


def start_all(copies):
    for copy in copies:
        copy.start()


def wait_all(copies):
    for copy in copies:
        copy.wait()


def gather_z(src, dst, span, sems, base):
    bits = bits_of_me()
    z, yx = bits[0] * 2 + bits[1], bits[2] * 2 + bits[3]
    cols = pl.ds(*span)
    place = dst.at[z, yx, :, cols]
    copies = [
        send(src.at[:, cols], place, sems, base + k, across(4 * (k + 1))) for k in range(3)
    ]
    copies.append(pltpu.make_async_copy(src.at[:, cols], place, sems[2].at[base]))
    return copies


def gather_second(dst, span, route, sems, base):
    bits = bits_of_me()
    part = dst.at[:, bits[2] * 2 + bits[3], :, pl.ds(*span)]
    return [send(part, part, sems, base + 3, across((1, 2)[route]))]


def gather_third(dst, span, route, sems, base):
    copies = []
    for k, which in enumerate((0, (1, 2)[route])):
        bits = flipped(bits_of_me(), which)
        part = dst.at[:, bits[2] * 2 + bits[3], :, pl.ds(*span)]
        copies.append(send(part, part, sems, base + 4 + k, across((2, 1)[route])))
    return copies


def gather_sems(pieces):
    return [
        pltpu.SemaphoreType.DMA((6 * pieces,)),
        pltpu.SemaphoreType.DMA((6 * pieces,)),
        pltpu.SemaphoreType.DMA((6 * pieces,)),
    ]


def halves(cols, parts=1):
    half = cols // 2
    width = half // parts
    return [(r * half + c * width, width, r) for c in range(parts) for r in range(2)]


def head_lanes(block, head):
    lane_head = lax.broadcasted_iota(jnp.int32, block.shape, 1) // HD
    return jnp.where(lane_head == head, block, jnp.zeros_like(block))


def pack_heads(columns):
    lane = lax.broadcasted_iota(jnp.int32, columns[0].shape, 1)
    pairs = [
        jnp.where(lane < HD, columns[2 * i], columns[2 * i + 1]) for i in range(len(columns) // 2)
    ]
    return pairs[0] if len(pairs) == 1 else jnp.concatenate(pairs, axis=1)


def block_probs(scores, top):
    total, parts = None, []
    for t in range(scores.shape[1] // 128):
        part = jnp.exp(scores[:, t * 128 : (t + 1) * 128] - top)
        total = part if total is None else total + part
        parts.append(part.astype(bf16))
    return parts, total


def head_rows(stack, heads, first, count):
    block = stack.shape[0] // heads
    return jnp.concatenate(
        [stack[h * block + first : h * block + first + count, :] for h in range(heads)], axis=0
    )


def attend_block(masked, keys, values, m_ref, l_ref, acc_ref):
    heads, half = len(masked), keys.shape[0] // 2
    for part in range(2):
        rows = slice(part * half, (part + 1) * half)
        seen = (part + 1) * half
        low = []
        for h, query in enumerate(masked):
            scores = dot_nt(query[rows, :], keys[:seen, :])
            row = lax.broadcasted_iota(jnp.int32, scores.shape, 0) + part * half
            col = lax.broadcasted_iota(jnp.int32, scores.shape, 1)
            scores = jnp.where(row >= col, scores, masked_score)
            top = jnp.broadcast_to(jnp.max(scores, axis=1, keepdims=True), (half, 128))
            m_ref[h, rows, :] = top
            parts, l_ref[h, rows, :] = block_probs(scores, top)
            low += parts
        acc_ref[rows, :] = dot_nn(
            jnp.concatenate(low, axis=1), head_rows(values, heads, 0, seen)
        )


def attend_finish(heads, m_ref, l_ref, acc_ref, out_ref, exact_ref, lse_ref):
    block = out_ref.shape[0]
    lane = lax.broadcasted_iota(jnp.int32, (block, 128), 1)
    rows = jnp.zeros((block, 128), f32)
    inverse = []
    for h in range(heads):
        total = jnp.sum(l_ref[h], axis=1, keepdims=True)
        rows = jnp.where(lane == h, m_ref[h][:, :1] + jnp.log(total), rows)
        inverse.append(jnp.broadcast_to(1.0 / total, (block, 128)))
    result = acc_ref[...] * pack_heads(inverse)
    out_ref[...] = result.astype(bf16)
    exact_ref[...] = result
    lse_ref[...] = rows.T[:8, :]


def mask_values(v_ref, vm_ref, heads, block):
    for j in range(v_ref.shape[0] // block):
        value = v_ref[j * block : (j + 1) * block, :]
        for h in range(heads):
            vm_ref[j, h * block : (h + 1) * block, :] = head_lanes(value, h)


def attend_forward_kernel(heads, comm, lens_ref, q_ref, k_ref, v_ref, *refs):
    ins, refs = refs[: comm.ins], refs[comm.ins :]
    out_ref, exact_ref, lse_ref, big_ref = refs[:4]
    outs = refs[4 : 4 + comm.outs]
    vm_ref, m_ref, l_ref, acc_ref = refs[4 + comm.outs : 8 + comm.outs]
    sems = refs[8 + comm.outs :]
    step = pl.program_id(1)
    block = q_ref.shape[0]
    comm.before(pl.program_id(0) * pl.num_programs(1) + step, ins, outs, sems)

    @pl.when(step == 0)
    def _():
        mask_values(v_ref, vm_ref, heads, block)

    @pl.when((step == 0) & (pl.program_id(0) == 0))
    def _():
        big_ref[...] = jnp.zeros(big_ref.shape, f32)

    query = q_ref[...] * jnp.asarray(score_scale, bf16)
    masked = [head_lanes(query, h) for h in range(heads)]

    def key_block(j):
        return k_ref[pl.ds(pl.multiple_of(j * block, block), block), :]

    attend_block(masked, key_block(step), vm_ref[step], m_ref, l_ref, acc_ref)
    away = jnp.where(lens_ref[0] == LONG_LEN, 0.0, 1e30).astype(f32)

    def earlier(j, carry):
        keys = key_block(j)
        low = []
        for h in range(heads):
            parts, total = block_probs(dot_nt(masked[h], keys), m_ref[h] + away)
            l_ref[h] += total
            low += parts
        acc_ref[...] += dot_nn(jnp.concatenate(low, axis=1), vm_ref[j])
        return carry

    lax.fori_loop(0, step, earlier, 0)
    for h in range(heads):
        big_ref[...] = jnp.maximum(
            big_ref[...], jnp.max(l_ref[h].reshape(-1, 8, 128), axis=0)
        )
    attend_finish(heads, m_ref, l_ref, acc_ref, out_ref, exact_ref, lse_ref)
    comm.after(pl.program_id(0) * pl.num_programs(1) + step, ins, outs, sems)


def attend_safe_kernel(
    heads,
    groups,
    lens_ref,
    big_ref,
    packed,
    low_in,
    exact_in,
    lse_in,
    low,
    exact,
    lse,
    q_ref,
    k_ref,
    v_ref,
    out_ref,
    exact_ref,
    lse_ref,
    vm_ref,
    m_ref,
    l_ref,
    acc_ref,
    sem,
):
    block, cols = q_ref.shape
    tokens = k_ref.shape[0]

    def fetch(src, dst):
        copy = pltpu.make_async_copy(src, dst, sem)
        copy.start()
        copy.wait()

    def one_query(group, step):
        rows = pl.ds(pl.multiple_of(step * block, block), block)
        here = pl.ds(group * cols, cols)
        fetch(packed.at[rows, here], q_ref)
        query = q_ref[...] * jnp.asarray(score_scale, bf16)
        masked = [head_lanes(query, h) for h in range(heads)]

        def key_block(j):
            return k_ref[pl.ds(pl.multiple_of(j * block, block), block), :]

        attend_block(masked, key_block(step), vm_ref[step], m_ref, l_ref, acc_ref)

        def earlier(j, carry):
            keys = key_block(j)
            parts_all, shrink = [], []
            for h in range(heads):
                scores = dot_nt(masked[h], keys)
                old = m_ref[h]
                top = jnp.maximum(old, jnp.max(scores, axis=1, keepdims=True))
                factor = jnp.exp(old - top)
                m_ref[h] = top
                parts, total = block_probs(scores, top)
                l_ref[h] = l_ref[h] * factor + total
                parts_all += parts
                shrink.append(factor)
            acc_ref[...] = acc_ref[...] * pack_heads(shrink) + dot_nn(
                jnp.concatenate(parts_all, axis=1), vm_ref[j]
            )
            return carry

        lax.fori_loop(0, jnp.where(lens_ref[0] == LONG_LEN, step, 0), earlier, 0)
        attend_finish(heads, m_ref, l_ref, acc_ref, out_ref, exact_ref, lse_ref)
        fetch(out_ref, low.at[rows, here])
        fetch(exact_ref, exact.at[rows, here])
        fetch(lse_ref, lse.at[pl.ds(group * 8, 8), rows])

    @pl.when(jnp.logical_not(jnp.max(big_ref[...]) < safe_sum))
    def _():
        for group in range(groups):
            fetch(packed.at[:, pl.ds((groups + group) * cols, cols)], k_ref)
            fetch(packed.at[:, pl.ds((2 * groups + group) * cols, cols)], v_ref)
            mask_values(v_ref, vm_ref, heads, block)
            lax.fori_loop(
                0, tokens // block, lambda i, c, group=group: (one_query(group, i), c)[1], 0
            )


class NoTransfers:
    ins = outs = 0

    def before(self, *args):
        pass

    def after(self, *args):
        pass


def attend_shapes(tokens, width):
    groups = width // min(256, width)
    cols = width // groups
    shapes = [
        jax.ShapeDtypeStruct((tokens, width), bf16),
        jax.ShapeDtypeStruct((tokens, width), f32),
        jax.ShapeDtypeStruct((8 * groups, tokens), f32),
    ]
    return groups, cols, cols // HD, shapes


def attend_specs(tokens, width):
    groups = width // min(256, width)
    cols = width // groups
    ins = [
        pl.BlockSpec((BT, cols), lambda g, i, n: (i, g)),
        pl.BlockSpec((tokens, cols), lambda g, i, n: (0, groups + g)),
        pl.BlockSpec((tokens, cols), lambda g, i, n: (0, 2 * groups + g)),
    ]
    outs = [
        pl.BlockSpec((BT, cols), lambda g, i, n: (i, g)),
        pl.BlockSpec((BT, cols), lambda g, i, n: (i, g)),
        pl.BlockSpec((8, BT), lambda g, i, n: (g, i)),
    ]
    shapes = [
        jax.ShapeDtypeStruct((tokens, width), bf16),
        jax.ShapeDtypeStruct((tokens, width), f32),
        jax.ShapeDtypeStruct((8 * groups, tokens), f32),
    ]
    heads = cols // HD
    scratch = [
        pltpu.VMEM((tokens // BT, heads * BT, cols), bf16),
        pltpu.VMEM((heads, BT, 128), f32),
        pltpu.VMEM((heads, BT, 128), f32),
        pltpu.VMEM((BT, cols), f32),
    ]
    return groups, heads, ins, outs, shapes, scratch


def attend_cost(tokens, width, products):
    pairs = (tokens // BT) * (tokens // BT + 1) // 2
    work = products * 2 * pairs * BT * BT * width
    return cost(4 * work, 10 * tokens * width, pairs * BT * BT * width // HD)


def attend_safe(packed, lengths, big, low, exact, lse):
    tokens, width = packed.shape[0], packed.shape[1] // 3
    groups, cols, heads, shapes = attend_shapes(tokens, width)
    return pl.pallas_call(
        functools.partial(attend_safe_kernel, heads, groups),
        grid_spec=pltpu.PrefetchScalarGridSpec(
            num_scalar_prefetch=1,
            grid=(1,),
            in_specs=[pl.BlockSpec((8, 128), lambda i, n: (0, 0))] + [ANY] * 4,
            out_specs=[ANY] * 3,
            scratch_shapes=[
                pltpu.VMEM((BT, cols), bf16),
                pltpu.VMEM((tokens, cols), bf16),
                pltpu.VMEM((tokens, cols), bf16),
                pltpu.VMEM((BT, cols), bf16),
                pltpu.VMEM((BT, cols), f32),
                pltpu.VMEM((8, BT), f32),
                pltpu.VMEM((tokens // BT, heads * BT, cols), bf16),
                pltpu.VMEM((heads, BT, 128), f32),
                pltpu.VMEM((heads, BT, 128), f32),
                pltpu.VMEM((BT, cols), f32),
                pltpu.SemaphoreType.DMA(()),
            ],
        ),
        out_shape=shapes,
        input_output_aliases={3: 0, 4: 1, 5: 2},
        compiler_params=params(1),
        cost_estimate=cost(1000, 100000),
        name="attend_safe",
    )(lengths, big, packed, low, exact, lse)


def attend_forward(packed, lengths, comm=NoTransfers(), moved=(), fresh=None):
    tokens, width = packed.shape[0], packed.shape[1] // 3
    groups, heads, ins, outs, shapes, scratch = attend_specs(tokens, width)
    low, exact, lse, big, *rest = pl.pallas_call(
        functools.partial(attend_forward_kernel, heads, comm),
        grid_spec=pltpu.PrefetchScalarGridSpec(
            num_scalar_prefetch=1,
            grid=(groups, tokens // BT),
            in_specs=ins + [ANY] * len(moved),
            out_specs=outs
            + [pl.BlockSpec((8, 128), lambda g, i, n: (0, 0))]
            + [ANY] * comm.outs,
            scratch_shapes=scratch + (comm.scratch() if moved else []),
        ),
        out_shape=shapes
        + [jax.ShapeDtypeStruct((8, 128), f32)]
        + [jax.ShapeDtypeStruct(m.shape, m.dtype) for m in moved[1:]]
        + ([fresh] if moved else []),
        input_output_aliases={5: 4} if moved else {},
        compiler_params=params(2, 2 if moved else None),
        cost_estimate=attend_cost(tokens, width, 2),
        name="attend_forward",
    )(lengths, packed, packed, packed, *moved)
    low, exact, lse = attend_safe(packed, lengths, big, low, exact, lse)
    return [low, exact, lse] + rest


def attend_backward_kernel(heads, comm, lens_ref, q_ref, k_ref, v_ref, do_ref, lse_ref, delta_ref, *refs):
    ins, refs = refs[: comm.ins], refs[comm.ins :]
    dq_ref, dk_ref, dv_ref = refs[:3]
    outs, refs = refs[3 : 3 + comm.outs], refs[3 + comm.outs :]
    qm_ref, dom_ref, km_ref, vm_ref, dqa_ref, dka_ref, dva_ref = refs[:7]
    scratch = refs[7:]
    step = pl.program_id(1)
    count = pl.num_programs(1)
    block = k_ref.shape[0]
    comm.before(pl.program_id(0) * count + step, ins, outs, scratch)

    @pl.when(step == 0)
    def _():
        for t in range(q_ref.shape[0] // block):
            rows = slice(t * block, (t + 1) * block)
            for h in range(heads):
                place = slice(h * block, (h + 1) * block)
                qm_ref[t, place, :] = head_lanes(q_ref[rows, :], h)
                dom_ref[t, place, :] = head_lanes(do_ref[rows, :], h)
        dqa_ref[...] = jnp.zeros(dqa_ref.shape, f32)

    for h in range(heads):
        place = slice(h * block, (h + 1) * block)
        km_ref[place, :] = head_lanes(k_ref[...] * jnp.asarray(score_scale, bf16), h)
        vm_ref[place, :] = head_lanes(v_ref[...], h)
    dka_ref[...] = jnp.zeros(dka_ref.shape, f32)
    dva_ref[...] = jnp.zeros(dva_ref.shape, f32)
    away = jnp.where(lens_ref[0] == LONG_LEN, 0.0, 1e30).astype(f32)

    def pair(i, first, count, seen, on_diagonal):
        rows = pl.ds(pl.multiple_of(i * block + first, count), count)
        query, grad = q_ref[rows, :], do_ref[rows, :]
        low, slopes = [], []
        for h in range(heads):
            place = slice(h * block, h * block + seen)
            scores = dot_nt(km_ref[place, :], query)
            logs = lse_ref[h : h + 1, rows]
            if not on_diagonal:
                logs = logs + away
            prob = jnp.exp(scores - logs)
            if on_diagonal:
                key = lax.broadcasted_iota(jnp.int32, scores.shape, 0)
                tok = lax.broadcasted_iota(jnp.int32, scores.shape, 1) + first
                prob = jnp.where(tok >= key, prob, 0.0)
            grad_prob = dot_nt(vm_ref[place, :], grad)
            slope = prob * (grad_prob - delta_ref[h : h + 1, rows])
            low.append(prob.astype(bf16))
            slopes.append(slope.astype(bf16))
        if on_diagonal:
            grads = head_rows(dom_ref[i], heads, first, count)
            queries = head_rows(qm_ref[i], heads, first, count)
            keys = head_rows(km_ref[...], heads, 0, seen)
        else:
            grads, queries, keys = dom_ref[i], qm_ref[i], km_ref[...]
        dva_ref[0:seen, :] += dot_nn(jnp.concatenate(low, axis=1), grads)
        dka_ref[0:seen, :] += dot_nn(jnp.concatenate(slopes, axis=1), queries)
        dqa_ref[rows, :] += dot_tn(jnp.concatenate(slopes, axis=0), keys)

    half = block // 2
    pair(step, 0, half, half, True)
    pair(step, half, half, block, True)
    lax.fori_loop(step + 1, count, lambda i, c: (pair(i, 0, block, block, False), c)[1], 0)
    dk_ref[...] = (dka_ref[...] * score_scale).astype(bf16)
    dv_ref[...] = dva_ref[...].astype(bf16)

    @pl.when(step == count - 1)
    def _():
        dq_ref[...] = dqa_ref[...].astype(bf16)

    comm.after(pl.program_id(0) * count + step, ins, outs, scratch)


def attend_backward(packed, grad_attended, lse, delta, lengths, comm=NoTransfers(), moved=()):
    tokens, width = grad_attended.shape
    groups = width // min(256, width)
    cols = width // groups
    heads = cols // HD
    blocks = tokens // BT
    column = pl.BlockSpec((tokens, cols), lambda g, j, n: (0, g))
    stats = pl.BlockSpec((8, tokens), lambda g, j, n: (g, 0))
    tile = pl.BlockSpec((BT, cols), lambda g, j, n: (j, g))
    move_ins, move_outs, move_shapes, move_scratch = comm.specs(moved) if moved else ([], [], [], [])
    return pl.pallas_call(
        functools.partial(attend_backward_kernel, heads, comm),
        grid_spec=pltpu.PrefetchScalarGridSpec(
            num_scalar_prefetch=1,
            grid=(groups, blocks),
            in_specs=[
                column,
                pl.BlockSpec((BT, cols), lambda g, j, n: (j, groups + g)),
                pl.BlockSpec((BT, cols), lambda g, j, n: (j, 2 * groups + g)),
                column,
                stats,
                stats,
            ]
            + move_ins,
            out_specs=[column, tile, tile] + move_outs,
            scratch_shapes=[
                pltpu.VMEM((blocks, heads * BT, cols), bf16),
                pltpu.VMEM((blocks, heads * BT, cols), bf16),
                pltpu.VMEM((heads * BT, cols), bf16),
                pltpu.VMEM((heads * BT, cols), bf16),
                pltpu.VMEM((tokens, cols), f32),
                pltpu.VMEM((BT, cols), f32),
                pltpu.VMEM((BT, cols), f32),
            ]
            + move_scratch,
        ),
        out_shape=[jax.ShapeDtypeStruct((tokens, width), bf16)] * 3 + move_shapes,
        compiler_params=params(2, 3 if moved else None),
        cost_estimate=attend_cost(tokens, width, 5),
        name="attend_backward",
    )(lengths, packed, packed, packed, grad_attended, lse, delta, *moved)


class AttendGather:
    ins, outs = 2, 2

    def scratch(self):
        return gather_sems(4)

    def pieces(self, ins, outs):
        up = [(None, outs[0], (at, width), route) for at, width, route in halves(outs[0].shape[3])]
        down = [(ins[0], outs[1], (at, width), route) for at, width, route in halves(ins[0].shape[1])]
        return up + down

    def hops(self, name, ks, ins, outs, sems):
        copies = []
        for k in ks:
            src, dst, span, route = self.pieces(ins, outs)[k]
            if name == "z":
                copies += gather_z(src, dst, span, sems, 6 * k)
            elif name == "second":
                copies += gather_second(dst, span, route, sems, 6 * k)
            else:
                copies += gather_third(dst, span, route, sems, 6 * k)
        return copies

    def before(self, step, ins, outs, sems):
        def hops(name, ks):
            return self.hops(name, ks, ins, outs, sems)

        @pl.when(step == 0)
        def _():
            greet(False)
            start_all(hops("z", (2, 3)))
            start_all(hops("second", (0, 1)))

        @pl.when(step == 3)
        def _():
            wait_all(hops("second", (0, 1)))
            start_all(hops("third", (0, 1)))

        @pl.when(step == 6)
        def _():
            wait_all(hops("z", (2, 3)))
            start_all(hops("second", (2, 3)))

        @pl.when(step == 9)
        def _():
            wait_all(hops("second", (2, 3)))
            start_all(hops("third", (2, 3)))

    def after(self, step, ins, outs, sems):
        @pl.when(step == 11)
        def _():
            wait_all(self.hops("third", (0, 1, 2, 3), ins, outs, sems))


class SumPart:
    slots = 5

    def __init__(self, grad, span, route, refs, sems, base):
        self.keep = grad.at[pl.ds(0, 512), pl.ds(*span)]
        self.sent = grad.at[pl.ds(512, 512), pl.ds(*span)]
        self.held, self.got_1, self.got_2, self.got_3 = refs
        self.sems, self.base = sems, base
        self.hops = ((2, 1), (1, 2))[route]

    @staticmethod
    def buffers(width):
        return [
            pltpu.VMEM((512, width), bf16),
            pltpu.VMEM((512, width), bf16),
            pltpu.VMEM((256, width), bf16),
            pltpu.VMEM((3, 64, width), bf16),
        ]

    def first(self):
        return [
            send(self.sent, self.got_1, self.sems, self.base, across(self.hops[0])),
            pltpu.make_async_copy(self.keep, self.held, self.sems[2].at[self.base]),
        ]

    def second(self):
        return [
            send(
                self.held.at[pl.ds(256, 256), :],
                self.got_2,
                self.sems,
                self.base + 1,
                across(self.hops[1]),
            )
        ]

    def third(self):
        return [
            send(
                self.held.at[pl.ds(64 * z, 64), :],
                self.got_3.at[z - 1],
                self.sems,
                self.base + 1 + z,
                across(4 * z),
            )
            for z in (1, 2, 3)
        ]

    def add(self, other, rows):
        def body(i, carry):
            at = pl.ds(pl.multiple_of(i * 64, 64), 64)
            self.held[at, :] = self.held[at, :] + other[at, :]
            return carry

        lax.fori_loop(0, rows // 64, body, 0)

    def to_second(self):
        wait_all(self.first())
        self.add(self.got_1, 512)
        start_all(self.second())

    def to_third(self):
        wait_all(self.second())
        self.add(self.got_2, 256)
        start_all(self.third())

    def result(self):
        wait_all(self.third())
        total = self.held[0:64, :].astype(f32)
        for z in range(3):
            total = total + self.got_3[z].astype(f32)
        return total


def sum_sems(parts):
    return [
        pltpu.SemaphoreType.DMA((SumPart.slots * parts,)),
        pltpu.SemaphoreType.DMA((SumPart.slots * parts,)),
        pltpu.SemaphoreType.DMA((SumPart.slots * parts,)),
    ]


class SmallSum:
    def __init__(self, refs, sems):
        self.got, self.sems = refs, sems

    @staticmethod
    def scratch():
        return [
            pltpu.VMEM((8, 8, 1024), f32),
            pltpu.VMEM((4, 8, 1024), f32),
            pltpu.SemaphoreType.DMA((10,)),
            pltpu.SemaphoreType.DMA((10,)),
        ]

    def near(self):
        bits = bits_of_me()
        place = self.got[0].at[lax.axis_index("mp") * 4 + bits[2] * 2 + bits[3]]
        devices = [across(k) for k in (1, 2, 3)] + [sibling()]
        devices += [sibling_across(k) for k in (1, 2, 3)]
        return [send(place, place, self.sems, k, device) for k, device in enumerate(devices)]

    def far(self):
        bits = bits_of_me()
        place = self.got[1].at[bits[0] * 2 + bits[1]]
        return [send(place, place, self.sems, 6 + k, across(4 * k)) for k in (1, 2, 3)]

    def begin(self, rows):
        bits = bits_of_me()
        self.got[0][lax.axis_index("mp") * 4 + bits[2] * 2 + bits[3]] = rows
        start_all(self.near())

    def middle(self, both):
        wait_all(self.near())
        row = lax.broadcasted_iota(jnp.int32, (8, 1024), 0)
        total = jnp.zeros((8, 1024), f32)
        for k in range(8):
            counts = (row < both) | (lax.axis_index("mp") == k // 4)
            total = total + jnp.where(counts, self.got[0][k], 0.0)
        bits = bits_of_me()
        self.got[1][bits[0] * 2 + bits[1]] = total
        start_all(self.far())

    def end(self):
        wait_all(self.far())
        return (self.got[1][0] + self.got[1][1]) + (self.got[1][2] + self.got[1][3])


class BackwardSum:
    def __init__(self, cols):
        self.cols = cols
        self.ins = len(cols) + 1
        self.outs = len(cols) + 1

    def specs(self, moved):
        vmem = [pl.BlockSpec((8, 1024), lambda g, j, n: (0, 0))]
        sizes = [(64, c) for c in self.cols]
        shapes = [jax.ShapeDtypeStruct(size, f32) for size in sizes]
        outs = [pl.BlockSpec(size, lambda g, j, n: (0, 0)) for size in sizes]
        scratch = []
        for c in self.cols:
            scratch += SumPart.buffers(c // 2) * 2
        scratch += sum_sems(2 * len(self.cols)) + SmallSum.scratch()
        return (
            [ANY] * len(self.cols) + vmem,
            outs + vmem,
            shapes + [jax.ShapeDtypeStruct((8, 1024), f32)],
            scratch,
        )

    def parts(self, ins, scratch):
        count = 2 * len(self.cols)
        sems = scratch[4 * count : 4 * count + 3]
        made = []
        for k in range(count):
            width = self.cols[k // 2] // 2
            refs = scratch[4 * k : 4 * k + 4]
            span = ((k % 2) * width, width)
            made.append(SumPart(ins[k // 2], span, k % 2, refs, sems, SumPart.slots * k))
        rest = scratch[4 * count + 3 :]
        return made, SmallSum(rest[:2], rest[2:])

    def before(self, step, ins, outs, scratch):
        parts, small = self.parts(ins, scratch)

        @pl.when(step == 0)
        def _():
            greet(True)
            small.begin(ins[-1][...])
            for part in parts[:2] + parts[4:]:
                start_all(part.first())

        @pl.when(step == 1)
        def _():
            small.middle(4)

        @pl.when(step == 2)
        def _():
            for part in parts[:2] + parts[4:]:
                part.to_second()
            for part in parts[2:4]:
                start_all(part.first())

        @pl.when(step == 5)
        def _():
            outs[-1][...] = small.end()

        @pl.when(step == 6)
        def _():
            for part in parts[:2] + parts[4:]:
                part.to_third()

        @pl.when(step == 7)
        def _():
            for part in parts[2:4]:
                part.to_second()

        @pl.when(step == 8)
        def _():
            for part in parts[2:4]:
                part.to_third()

    def after(self, step, ins, outs, scratch):
        parts, _ = self.parts(ins, scratch)

        @pl.when(step == 11)
        def _():
            for k, part in enumerate(parts):
                width = self.cols[k // 2] // 2
                span = slice((k % 2) * width, (k % 2 + 1) * width)
                outs[k // 2][:, span] = part.result()


def normalized(values):
    average = jnp.mean(values, axis=-1, keepdims=True)
    centred = values - average
    variance = jnp.mean(centred * centred, axis=-1, keepdims=True)
    inverse = lax.rsqrt(variance + norm_eps)
    return centred * inverse, inverse


def column_sum(values):
    return jnp.sum(values.reshape(-1, 8, values.shape[-1]), axis=0)


def turned(values, out_ref):
    flip = values.T
    bits = bits_of_me()
    for a in range(16):
        r = flipped(bits, a)
        slot = r[2] * 8 + r[3] * 4 + r[0] * 2 + r[1]
        out_ref[pl.ds(pl.multiple_of(slot * 64, 64), 64), :] = flip[a * 64 : (a + 1) * 64, :]


def shape(rows, cols, dtype=bf16):
    return jax.ShapeDtypeStruct((rows, cols), dtype)


def row_tile(cols):
    return pl.BlockSpec((BT, cols), lambda i: (i, 0))


def col_tile(rows):
    return pl.BlockSpec((rows, BT), lambda i: (0, i))


def whole(rows, cols):
    return pl.BlockSpec((rows, cols), lambda i: (0, 0))


def weight(cols):
    return pl.BlockSpec((1024, cols), lambda i: (0, 0), pipeline_mode=pl.Buffered(1))


def my_side():
    return lax.axis_index("mp")


def grid_call(kernel, steps, ins, outs, scratch, flops, name, collective=None, aliases={}):
    arrays = [a for a, _ in ins]
    nbytes = sum(a.size * a.dtype.itemsize for a in arrays)
    nbytes += sum(o.size * o.dtype.itemsize for o, _ in outs)
    return pl.pallas_call(
        kernel,
        grid=(steps,),
        in_specs=[s for _, s in ins],
        out_specs=[s for _, s in outs],
        scratch_shapes=scratch,
        out_shape=[o for o, _ in outs],
        input_output_aliases=aliases,
        compiler_params=params(1, collective),
        cost_estimate=cost(flops, nbytes),
        name=name,
    )(*arrays)


def vector(values):
    rows = values.shape[0] // 128
    return (values.reshape(rows, 128), whole(rows, 128))


def spread(ref, at=0, cols=1024):
    rows = ref[...].astype(f32)
    low, count = at // 128, cols // 128
    return jnp.concatenate([rows[k : k + 1, :] for k in range(low, low + count)], axis=1)


def qkv_bias(ref, cols):
    bias = ref[...].astype(f32)
    zero = jnp.zeros((1, bias.shape[1]), f32)
    return jnp.concatenate([bias[0:1, :], zero, bias[1:2, :]], axis=1)[:, cols]


class FirstGather:
    def __init__(self, wq, up, up_out, wo, out_out, sems):
        self.pieces = [(None, wq, (at, width), r) for at, width, r in chunk_halves(wq.shape[3])]
        self.pieces += [(up, up_out, (at, width), r) for at, width, r in halves(up.shape[1])]
        self.pieces += [(wo, out_out, (at, width), r) for at, width, r in halves(wo.shape[1])]
        self.sems = sems

    def z(self, *ks):
        copies = []
        for k in ks:
            src, dst, span, _ = self.pieces[k]
            if src is None:
                bits = bits_of_me()
                place = dst.at[bits[0] * 2 + bits[1], bits[2] * 2 + bits[3], :, pl.ds(*span)]
                copies += [
                    send(place, place, self.sems, 6 * k + hop, across(4 * (hop + 1)))
                    for hop in range(3)
                ]
            else:
                copies += gather_z(src, dst, span, self.sems, 6 * k)
        return copies

    def second(self, *ks):
        copies = []
        for k in ks:
            _, dst, span, route = self.pieces[k]
            copies += gather_second(dst, span, route, self.sems, 6 * k)
        return copies

    def third(self, *ks):
        copies = []
        for k in ks:
            _, dst, span, route = self.pieces[k]
            copies += gather_third(dst, span, route, self.sems, 6 * k)
        return copies


def chunk_halves(cols):
    width = cols // 4
    return [(k * width, width, k % 2) for k in range(4)]


def qkv_kernel(
    tiles,
    own,
    own_all,
    gain,
    shift,
    bias,
    w_mine,
    wo,
    up,
    turned_out,
    out,
    up_out,
    out_out,
    w_out,
    normed,
    came,
    wq,
    swap_send,
    swap_came,
    copy_sem,
    *sems,
):
    step = pl.program_id(0)
    side = my_side()
    moves = FirstGather(wq, up, up_out, wo, out_out, sems)
    local = w_mine.shape[2]

    def swap(k):
        return send(
            own_all.at[pl.ds(k * BT, BT), :], came.at[k], (swap_send, swap_came), k, sibling()
        )

    @pl.when(step == 0)
    def _():
        bits = bits_of_me()
        for c in range(3):
            wq[bits[0] * 2 + bits[1], bits[2] * 2 + bits[3], :, c * local : (c + 1) * local] = (
                w_mine[c]
            )
        greet(True)
        start_all(moves.z(0, 1))
        start_all([swap(k) for k in range(tiles)])

    def norm(values):
        scaled, _ = normalized(values.astype(f32))
        rows = (scaled * spread(gain) + spread(shift)).astype(bf16)
        first = lax.rem(step + side * tiles, 2 * tiles) * BT
        normed[pl.ds(pl.multiple_of(first, BT), BT), :] = rows
        turned(rows, turned_out)

    @pl.when(step < tiles)
    def _():
        norm(own[...])

    for k in range(tiles):

        @pl.when(step == tiles + k)
        def _():
            swap(k).wait()
            norm(came[k])

    @pl.when(step == 2 * tiles - 2)
    def _():
        wait_all(moves.z(0, 1))
        start_all(moves.second(0, 1))
        start_all(moves.z(2, 3))

    @pl.when(step == 2 * tiles)
    def _():
        wait_all(moves.second(0, 1))
        start_all(moves.third(0, 1))
        wait_all(moves.z(2, 3))
        start_all(moves.second(2, 3))
        start_all(moves.z(6, 7))
        start_all(moves.z(4, 5))
        wait_all(moves.third(0, 1))

    @pl.when(step == 2 * tiles + 1)
    def _():
        wait_all(moves.second(2, 3))
        start_all(moves.third(2, 3))

    half = out.shape[1]
    for c in range(2):

        @pl.when((step >= (2 + 2 * c) * tiles) & (step < (4 + 2 * c) * tiles))
        def _():
            @pl.when(step == (2 + 2 * c) * tiles)
            def _():
                if c:
                    wait_all(moves.third(2, 3))
                    wait_all(moves.z(6, 7))
                    start_all(moves.second(6, 7))
                    pltpu.make_async_copy(wq, w_out, copy_sem).start()

            first = (step - (2 + 2 * c) * tiles) * BT
            rows = normed[pl.ds(pl.multiple_of(first, BT), BT), :]
            cols = slice(c * half, (c + 1) * half)
            part = wq[:, :, :, cols].reshape(1024, half)
            out[...] = (dot_nn(rows, part) + qkv_bias(bias, cols)).astype(bf16)

    @pl.when(step == 5 * tiles)
    def _():
        wait_all(moves.second(6, 7))
        start_all(moves.third(6, 7))

    @pl.when(step == 6 * tiles - 1)
    def _():
        wait_all(moves.third(6, 7))
        wait_all(moves.z(4, 5))
        pltpu.make_async_copy(wq, w_out, copy_sem).wait()


def project_kernel(
    tiles,
    a,
    w,
    toks,
    bias,
    gain,
    shift,
    hid_out,
    normed_out,
    sent,
    came,
    sent_sems,
    came_sems,
):
    step = pl.program_id(0)

    def swap(k):
        return send(sent.at[k], came.at[k], (sent_sems, came_sems), k, sibling())

    @pl.when(step == 0)
    def _():
        greet_sibling()

    partial = dot_nt(a[...], w[...])
    for k in range(tiles):

        @pl.when(step == k)
        def _():
            sent[k] = partial.astype(bf16)
            swap(k).start()

        @pl.when(step == tiles + k)
        def _():
            swap(k).wait()
            hidden = toks[...].astype(f32) + (partial + came[k].astype(f32) + spread(bias))
            hid_out[...] = hidden
            scaled, _ = normalized(hidden)
            normed_out[...] = (scaled * spread(gain) + spread(shift)).astype(bf16)


def feed_kernel(
    tiles,
    x_all,
    c_all,
    bias,
    wu,
    wd,
    ffn_own,
    norm_own,
    ffn_came,
    norm_came,
    up_out,
    down_out,
    bsum,
    up_total,
    down_total,
    act,
    gpre,
    xt,
    ct,
    xs,
    cs,
    ffn_sent,
    norm_sent,
    local_sems,
    send_sems,
    came_sems,
    out_sems,
):
    step = pl.program_id(0)
    remote = (send_sems, came_sems)

    def rows(k):
        return pl.ds(k * BT, BT)

    def local(k):
        return [
            pltpu.make_async_copy(x_all.at[rows(k), :], xs.at[k], local_sems.at[k]),
            pltpu.make_async_copy(c_all.at[rows(k), :], cs.at[k], local_sems.at[tiles + k]),
        ]

    def swapped(k):
        return [
            send(x_all.at[rows(k), :], xs.at[tiles + k], remote, k, sibling()),
            send(c_all.at[rows(k), :], cs.at[tiles + k], remote, tiles + k, sibling()),
        ]

    def returned(k):
        return [
            send(ffn_sent, ffn_came.at[rows(k), :], remote, 2 * tiles + k, sibling()),
            send(norm_sent, norm_came.at[rows(k), :], remote, 3 * tiles + k, sibling()),
        ]

    @pl.when(step == 0)
    def _():
        for k in range(tiles):
            start_all(local(k))
        bsum[...] = jnp.zeros(bsum.shape, f32)
        greet_sibling()
        for k in range(tiles):
            start_all(swapped(k))

    for k in range(tiles):

        @pl.when(step == k)
        def _():
            wait_all(local(k))

        @pl.when(step == tiles + k)
        def _():
            wait_all(swapped(k))

    x, c = xs[step], cs[step]
    xt[...] = x.T
    ct[...] = c.T
    width = 512
    spans = [slice(at, at + width) for at in range(0, wu.shape[1], width)]
    for cols in spans:
        value = dot_nn(x, wu[:, cols]) + spread(bias, cols.start, width)
        upstream = dot_nn(c, wd[:, cols])
        square = value * value
        bent = jnp.tanh(value * (gelu_coeff + (gelu_coeff * 0.044715) * square))
        half_up = 0.5 + 0.5 * bent
        act[:, cols] = (value * half_up).astype(bf16)
        slope = half_up + value * (half_up * (1.0 - bent)) * (
            gelu_coeff + (3.0 * 0.044715 * gelu_coeff) * square
        )
        grad = (upstream * slope).astype(bf16)
        gpre[:, cols] = grad
        bsum[:, cols] += column_sum(grad.astype(f32))
    ffn = dot_nt(act[...], wd[...]).astype(bf16)
    norm = dot_nt(gpre[...], wu[...]).astype(bf16)

    @pl.when(step < tiles)
    def _():
        ffn_own[...] = ffn
        norm_own[...] = norm

    for k in range(tiles):

        @pl.when(step == tiles + k)
        def _():
            if k:
                wait_all(returned(k - 1))
            ffn_sent[...] = ffn
            norm_sent[...] = norm
            start_all(returned(k))

    @pl.when(step == 0)
    def _():
        for cols in spans:
            down_total[:, cols] = dot_nn(ct[...], act[:, cols])
        for cols in spans:
            up_total[:, cols] = dot_nn(xt[...], gpre[:, cols])

    @pl.when(step > 0)
    def _():
        for cols in spans:
            down_total[:, cols] += dot_nn(ct[...], act[:, cols])
        for cols in spans:
            up_total[:, cols] += dot_nn(xt[...], gpre[:, cols])

    def leave(total, stage, out, base):
        half = total.shape[1] // 2
        bits = bits_of_me()
        copies = []
        for top in range(2):
            for route in range(2):
                part = total[512 * top : 512 * top + 512, route * half : route * half + half]
                stage[top * 2 + route] = part.astype(bf16)
        for a in range(16):
            r = flipped(bits, a)
            for route in range(2):
                slot = r[2 + route] * 8 + r[3 - route] * 4 + r[0] * 2 + r[1]
                copies.append(
                    pltpu.make_async_copy(
                        stage.at[(a // 8) * 2 + route, pl.ds((a % 8) * 64, 64), :],
                        out.at[
                            pl.ds(pl.multiple_of(slot * 64, 64), 64), pl.ds(route * half, half)
                        ],
                        out_sems.at[base + 2 * a + route],
                    )
                )
        start_all(copies)
        return copies

    @pl.when(step == 2 * tiles - 1)
    def _():
        copies = leave(down_total, cs, down_out, 0)
        copies += leave(up_total, xs, up_out, 32)
        wait_all(copies)
        wait_all(returned(tiles - 1))


def middle_kernel(
    tiles,
    hid,
    f_own,
    f_came,
    g_own,
    g_came,
    cot,
    bias,
    gain,
    exact,
    attended,
    w,
    out,
    gattn,
    do_out,
    delta_out,
    grad_w,
    sums,
    turned_rows,
    total,
    now,
    sent,
    came,
    sent_sems,
    came_sems,
):
    step = pl.program_id(0)

    def swap(k):
        return send(sent.at[k], came.at[k], (sent_sems, came_sems), k, sibling())

    @pl.when(step == 0)
    def _():
        sums[...] = jnp.zeros(sums.shape, f32)
        total[...] = jnp.zeros(total.shape, f32)
        greet_sibling()

    @pl.when(step < tiles)
    def _():
        hidden = hid[...]
        grad_out = cot[...].astype(f32)
        branch = f_own[...].astype(f32) + f_came[...].astype(f32) + spread(bias)
        out[...] = (hidden + branch).astype(bf16)
        scaled, inverse = normalized(hidden)
        grad_norm = g_own[...].astype(f32) + g_came[...].astype(f32)
        through = grad_norm * spread(gain)
        centre = jnp.mean(through, axis=-1, keepdims=True)
        along = jnp.mean(through * scaled, axis=-1, keepdims=True)
        grad = (grad_out + inverse * (through - centre - scaled * along)).astype(bf16)
        gattn[...] = grad
        now[...] = grad
        sums[0:8, :] += column_sum(grad_norm * scaled)
        sums[8:16, :] += column_sum(grad_norm)
        sums[16:24, :] += column_sum(grad.astype(f32))
        sums[24:32, :] += column_sum(grad_out)

    for k in range(tiles):

        @pl.when(step == k)
        def _():
            sent[k] = now[...]
            swap(k).start()

        @pl.when(step == tiles + k)
        def _():
            swap(k).wait()
            now[...] = came[k]

    grad = now[...]
    turned(grad, turned_rows)
    part = dot_nn(grad, w[...]).astype(bf16)
    do_out[...] = part
    product = part.astype(f32) * exact[...]
    head = lax.broadcasted_iota(jnp.int32, (part.shape[1], 128), 0) // HD
    place = lax.broadcasted_iota(jnp.int32, (part.shape[1], 128), 1)
    pick = jnp.where(place == (head // 4) * 8 + head % 4, 1.0, 0.0).astype(bf16)
    high = product.astype(bf16)
    rest = (product - high.astype(f32)).astype(bf16)
    delta_out[...] = (dot_nn(high, pick) + dot_nn(rest, pick)).T[:16, :]
    total[...] += dot_nn(turned_rows[...], attended[...])

    @pl.when(step == 2 * tiles - 1)
    def _():
        write_grad(total, grad_w)


def write_grad(total, out):
    half = total.shape[1] // 2
    out[:, :half] = total[:, :half].astype(bf16)
    for to, at in enumerate((0, 2, 1, 3)):
        there, here = slice(256 * to, 256 * to + 256), slice(256 * at, 256 * at + 256)
        out[there, half:] = total[here, half:].astype(bf16)


class HeldSumPart(SumPart):
    def __init__(self, route, refs, sems, base):
        self.held, self.sent = refs[:2]
        self.got_1, self.got_2, self.got_3 = refs[2:]
        self.sems, self.base = sems, base
        self.hops = ((2, 1), (1, 2))[route]

    @staticmethod
    def buffers(width):
        return [pltpu.VMEM((512, width), bf16)] + SumPart.buffers(width)

    def first(self):
        return [send(self.sent, self.got_1, self.sems, self.base, across(self.hops[0]))]


def last_scratch(cols):
    made = []
    for _ in range(4):
        made += HeldSumPart.buffers(cols // 4)
    return made + sum_sems(4) + SmallSum.scratch()


def last_kernel(
    tiles,
    turned_rows,
    dq,
    dk,
    dv,
    w,
    toks,
    gattn,
    gain,
    out,
    grad_w,
    small_out,
    sums,
    qv_sums,
    total,
    sent,
    came,
    send_sems,
    recv_sems,
    *refs,
):
    step = pl.program_id(0)
    blocks = 2 * tiles
    parts = [
        HeldSumPart(k % 2, refs[5 * k : 5 * k + 5], refs[20:23], SumPart.slots * k)
        for k in range(4)
    ]
    tiny = SmallSum(refs[23:25], refs[25:27])
    local = dq.shape[1]
    quarter = 3 * local // 4

    def swap(k):
        return send(sent.at[k], came.at[k], (send_sems, recv_sems), k, sibling())

    @pl.when(step == 0)
    def _():
        greet(True)
        sums[...] = jnp.zeros(sums.shape, f32)
        qv_sums[...] = jnp.zeros(qv_sums.shape, f32)

    grads = jnp.concatenate([dq[...], dk[...], dv[...]], axis=1)

    @pl.when(step < blocks)
    def _():
        qv_sums[:, :local] += column_sum(dq[...].astype(f32))
        qv_sums[:, local:] += column_sum(dv[...].astype(f32))

    for c in range(2):

        @pl.when((step >= c * blocks) & (step < (c + 1) * blocks))
        def _():
            spans = [slice(r * 2 * quarter + c * quarter, r * 2 * quarter + (c + 1) * quarter) for r in range(2)]
            term = dot_nn(turned_rows[...], jnp.concatenate([grads[:, s] for s in spans], axis=1))

            @pl.when(step == c * blocks)
            def _():
                total[...] = term

            @pl.when(step > c * blocks)
            def _():
                total[...] += term

            @pl.when(step == (c + 1) * blocks - 1)
            def _():
                one, two = parts[2 * c], parts[2 * c + 1]
                one.held[...] = total[0:512, :quarter].astype(bf16)
                one.sent[...] = total[512:1024, :quarter].astype(bf16)
                two.held[0:256, :] = total[0:256, quarter:].astype(bf16)
                two.held[256:512, :] = total[512:768, quarter:].astype(bf16)
                two.sent[0:256, :] = total[256:512, quarter:].astype(bf16)
                two.sent[256:512, :] = total[768:1024, quarter:].astype(bf16)
                start_all(one.first() + two.first())

    @pl.when(step == 2 * blocks + 1)
    def _():
        for part in parts[:2]:
            part.to_second()

    @pl.when(step == 2 * blocks + 3)
    def _():
        for part in parts[:2]:
            part.to_third()

    @pl.when(step == 2 * blocks + 4)
    def _():
        for part in parts[2:]:
            part.to_second()

    @pl.when(step == 2 * blocks + 5)
    def _():
        for part in parts[2:]:
            part.to_third()

    @pl.when(step >= 2 * blocks)
    def _():
        rows = dot_nt(grads, w[...])
        for k in range(tiles):

            @pl.when(step == 2 * blocks + k)
            def _():
                sent[k] = rows.astype(bf16)
                swap(k).start()

            @pl.when(step == 2 * blocks + tiles + k)
            def _():
                swap(k).wait()
                grad_norm = rows + came[k].astype(f32)
                scaled, inverse = normalized(toks[...].astype(f32))
                through = grad_norm * spread(gain)
                centre = jnp.mean(through, axis=-1, keepdims=True)
                along = jnp.mean(through * scaled, axis=-1, keepdims=True)
                grad_in = inverse * (through - centre - scaled * along)
                out[...] = (gattn[...].astype(f32) + grad_in).astype(bf16)
                sums[0:8, :] += column_sum(grad_norm * scaled)
                sums[8:16, :] += column_sum(grad_norm)

    @pl.when(step == pl.num_programs(0) - 1)
    def _():
        row = lax.broadcasted_iota(jnp.int32, (8, 1024), 0)
        first = jnp.sum(sums[0:8, :], axis=0, keepdims=True)
        second = jnp.sum(sums[8:16, :], axis=0, keepdims=True)
        third = jnp.sum(qv_sums[...], axis=0, keepdims=True)
        rows = jnp.where(row == 0, first, jnp.where(row == 1, second, third))
        tiny.begin(jnp.where(row < 3, rows, 0.0))
        tiny.middle(2)
        small_out[...] = tiny.end()
        for k, part in enumerate(parts):
            at = (k % 2) * 2 * quarter + (k // 2) * quarter
            summed = part.result()
            edges = [at] + [c for c in (local, 2 * local) if at < c < at + quarter] + [at + quarter]
            for low, high in zip(edges[:-1], edges[1:]):
                to = low % local
                grad_w[low // local, :, to : to + high - low] = summed[:, low - at : high - at]


def layer_on_pairs(
    tokens,
    slot_lengths,
    gain_one,
    shift_one,
    w_qkv,
    bias_qv,
    w_out,
    bias_out,
    gain_two,
    shift_two,
    w_up,
    bias_up,
    w_down,
    bias_down,
    cotangent,
):
    own_rows, width = tokens.shape
    total_rows = 2 * own_rows
    tiles = own_rows // BT
    local = w_qkv.shape[2]
    hidden_cols = w_up.shape[1]
    side_cols = 3 * local
    lengths = slot_lengths[0]

    half_cols = side_cols // 2
    normed_at = pl.BlockSpec(
        (width, BT),
        lambda i: (0, lax.rem(jnp.minimum(i, 2 * tiles - 1) + my_side() * tiles, 2 * tiles)),
    )
    packed_at = pl.BlockSpec(
        (BT, half_cols),
        lambda i: (
            lax.rem(jnp.maximum(i - 2 * tiles, 0), 2 * tiles),
            jnp.maximum(i - 2 * tiles, 0) // (2 * tiles),
        ),
    )
    rows_turned, packed, up_blocks, out_blocks, qkv_blocks = grid_call(
        functools.partial(qkv_kernel, tiles),
        6 * tiles,
        [
            (tokens, pl.BlockSpec((BT, width), lambda i: (jnp.minimum(i, tiles - 1), 0))),
            (tokens, ANY),
            vector(gain_one),
            vector(shift_one),
            (bias_qv, whole(2, local)),
            (w_qkv.transpose(1, 0, 2), pl.BlockSpec((3, 64, local), lambda i: (0, 0, 0))),
            (w_out.T, ANY),
            (w_up, ANY),
        ],
        [
            (shape(width, total_rows), normed_at),
            (shape(total_rows, side_cols), packed_at),
            (jax.ShapeDtypeStruct((4, 4, 64, hidden_cols), bf16), ANY),
            (jax.ShapeDtypeStruct((4, 4, 64, local), bf16), ANY),
            (jax.ShapeDtypeStruct((4, 4, 64, side_cols), bf16), ANY),
        ],
        [
            pltpu.VMEM((total_rows, width), bf16),
            pltpu.VMEM((tiles, BT, width), bf16),
            pltpu.VMEM((4, 4, 64, side_cols), bf16),
            pltpu.SemaphoreType.DMA((tiles,)),
            pltpu.SemaphoreType.DMA((tiles,)),
            pltpu.SemaphoreType.DMA(()),
        ]
        + gather_sems(8),
        2 * total_rows * width * side_cols,
        "qkv",
        1,
    )
    qkv_w = qkv_blocks.reshape(width, side_cols)
    attended, exact, lse, up_blocks, down_blocks = attend_forward(
        packed,
        lengths,
        AttendGather(),
        (w_down.T, up_blocks),
        jax.ShapeDtypeStruct((4, 4, 64, hidden_cols), bf16),
    )
    up_w = up_blocks.reshape(width, hidden_cols)
    out_w = out_blocks.reshape(width, local)

    def two_way(cols, skip=0):
        def at(i):
            return lax.rem(jnp.maximum(i - skip, 0) + (1 - my_side()) * tiles, 2 * tiles)

        return pl.BlockSpec((BT, cols), lambda i: (at(i), 0))

    late_tile = pl.BlockSpec((BT, width), lambda i: (jnp.maximum(i - tiles, 0), 0))
    swap_buffers = [
        pltpu.VMEM((tiles, BT, width), bf16),
        pltpu.VMEM((tiles, BT, width), bf16),
        pltpu.SemaphoreType.DMA((tiles,)),
        pltpu.SemaphoreType.DMA((tiles,)),
    ]
    hidden, normed_own = grid_call(
        functools.partial(project_kernel, tiles),
        2 * tiles,
        [
            (attended, two_way(local)),
            (out_w, weight(local)),
            (tokens, late_tile),
            vector(bias_out),
            vector(gain_two),
            vector(shift_two),
        ],
        [
            (shape(own_rows, width, f32), late_tile),
            (shape(own_rows, width), late_tile),
        ],
        swap_buffers,
        4 * own_rows * width * local,
        "project",
        6,
    )
    down_w = down_blocks.reshape(width, hidden_cols)
    own_at = pl.BlockSpec((BT, width), lambda i: (jnp.minimum(i, tiles - 1), 0))
    ffn_own, norm_own, ffn_came, norm_came, up_grad, down_grad, bsum = grid_call(
        functools.partial(feed_kernel, tiles),
        2 * tiles,
        [
            (normed_own, ANY),
            (cotangent, ANY),
            vector(bias_up),
            (up_w, weight(hidden_cols)),
            (down_w, weight(hidden_cols)),
        ],
        [
            (shape(own_rows, width), own_at),
            (shape(own_rows, width), own_at),
            (shape(own_rows, width), ANY),
            (shape(own_rows, width), ANY),
            (shape(width, hidden_cols), ANY),
            (shape(width, hidden_cols), ANY),
            (shape(8, hidden_cols, f32), whole(8, hidden_cols)),
        ],
        [
            pltpu.VMEM((width, hidden_cols), f32),
            pltpu.VMEM((width, hidden_cols), f32),
            pltpu.VMEM((BT, hidden_cols), bf16),
            pltpu.VMEM((BT, hidden_cols), bf16),
            pltpu.VMEM((width, BT), bf16),
            pltpu.VMEM((width, BT), bf16),
            pltpu.VMEM((2 * tiles, BT, width), bf16),
            pltpu.VMEM((2 * tiles, BT, width), bf16),
            pltpu.VMEM((BT, width), bf16),
            pltpu.VMEM((BT, width), bf16),
            pltpu.SemaphoreType.DMA((2 * tiles,)),
            pltpu.SemaphoreType.DMA((4 * tiles,)),
            pltpu.SemaphoreType.DMA((4 * tiles,)),
            pltpu.SemaphoreType.DMA((64,)),
        ],
        24 * own_rows * width * hidden_cols,
        "feed",
        5,
    )
    def mine_first(i):
        return lax.rem(i + my_side() * tiles, 2 * tiles)

    natural_tile = pl.BlockSpec((BT, local), lambda i: (mine_first(i), 0))
    output, grad_attn, grad_attended, delta, out_grad, middle_sums = grid_call(
        functools.partial(middle_kernel, tiles),
        2 * tiles,
        [
            (hidden, own_at),
            (ffn_own, own_at),
            (ffn_came, own_at),
            (norm_own, own_at),
            (norm_came, own_at),
            (cotangent, own_at),
            vector(bias_down),
            vector(gain_two),
            (exact, natural_tile),
            (attended, natural_tile),
            (out_w, weight(local)),
        ],
        [
            (shape(own_rows, width), own_at),
            (shape(own_rows, width), own_at),
            (shape(total_rows, local), natural_tile),
            (shape(16, total_rows, f32), pl.BlockSpec((16, BT), lambda i: (0, mine_first(i)))),
            (shape(width, local), whole(width, local)),
            (shape(32, width, f32), whole(32, width)),
        ],
        [
            pltpu.VMEM((width, BT), bf16),
            pltpu.VMEM((width, local), f32),
            pltpu.VMEM((BT, width), bf16),
        ]
        + swap_buffers,
        4 * total_rows * width * local,
        "middle",
        7,
    )
    early = middle_sums.reshape(4, 8, width).sum(axis=1)
    up_bias = bsum.sum(axis=0).reshape(-1, width)
    early = jnp.concatenate([early, up_bias, jnp.zeros((2, width), f32)])
    moved = (down_grad, up_grad, out_grad, early)
    grad_q, grad_k, grad_v, grad_down, grad_up, grad_w_out, early = attend_backward(
        packed,
        grad_attended,
        lse,
        delta,
        lengths,
        BackwardSum((hidden_cols, hidden_cols, local)),
        moved,
    )
    blocks = 2 * tiles

    def grad_at(i):
        later = lax.rem(jnp.maximum(i - 2 * blocks, 0) + (1 - my_side()) * tiles, blocks)
        return jnp.where(i < 2 * blocks, lax.rem(i, blocks), later)

    grad_tile = pl.BlockSpec((BT, local), lambda i: (grad_at(i), 0))
    turned_tile = pl.BlockSpec(
        (width, BT), lambda i: (0, jnp.where(i < 2 * blocks, lax.rem(i, blocks), blocks - 1))
    )
    last_tile = pl.BlockSpec(
        (BT, width), lambda i: (jnp.maximum(i - 2 * blocks - tiles, 0), 0)
    )
    grad_tokens, grad_w_qkv, late = grid_call(
        functools.partial(last_kernel, tiles),
        3 * blocks,
        [(rows_turned, turned_tile)]
        + [(g, grad_tile) for g in (grad_q, grad_k, grad_v)]
        + [
            (qkv_w, weight(side_cols)),
            (tokens, last_tile),
            (grad_attn, last_tile),
            vector(gain_one),
        ],
        [
            (shape(own_rows, width), last_tile),
            (
                jax.ShapeDtypeStruct((3, 64, local), f32),
                pl.BlockSpec((3, 64, local), lambda i: (0, 0, 0)),
            ),
            (shape(8, width, f32), whole(8, width)),
        ],
        [
            pltpu.VMEM((16, width), f32),
            pltpu.VMEM((8, width), f32),
            pltpu.VMEM((width, side_cols // 2), f32),
        ]
        + swap_buffers
        + last_scratch(side_cols),
        4 * total_rows * width * side_cols,
        "last",
        4,
    )
    return (
        output,
        grad_tokens,
        late[0],
        late[1],
        grad_w_qkv.transpose(1, 0, 2),
        late[2].reshape(2, local),
        grad_w_out.T,
        early[2],
        early[0],
        early[1],
        grad_up,
        early[4:6].reshape(-1),
        grad_down.T,
        early[3],
    )


def gelu_tanh(values):
    inner = gelu_coeff * (values + 0.044715 * values * values * values)
    return 0.5 * values * (1.0 + jnp.tanh(inner))


def gelu_slope(values):
    inner = gelu_coeff * (values + 0.044715 * values * values * values)
    bent = jnp.tanh(inner)
    return 0.5 * (1.0 + bent) + 0.5 * values * (1.0 - bent * bent) * gelu_coeff * (
        1.0 + 3.0 * 0.044715 * values * values
    )


def norm_forward(values, gain_vec, shift_vec):
    average = jnp.mean(values, axis=-1, keepdims=True)
    centred = values - average
    variance = jnp.mean(centred * centred, axis=-1, keepdims=True)
    inverse = lax.rsqrt(variance + norm_eps)
    scaled = centred * inverse
    return (scaled * gain_vec.astype(f32) + shift_vec.astype(f32), scaled, inverse)


def norm_backward(grad_out, scaled, inverse, gain_vec):
    grad_scaled = grad_out * gain_vec.astype(f32)
    centre_term = jnp.mean(grad_scaled, axis=-1, keepdims=True)
    slope_term = jnp.mean(grad_scaled * scaled, axis=-1, keepdims=True)
    grad_in = inverse * (grad_scaled - centre_term - scaled * slope_term)
    return (grad_in, jnp.sum(grad_out * scaled, axis=0), jnp.sum(grad_out, axis=0))


def layer_by_collectives(
    tokens,
    slot_lengths,
    gain_one,
    shift_one,
    w_qkv,
    bias_qv,
    w_out,
    bias_out,
    gain_two,
    shift_two,
    w_up,
    bias_up,
    w_down,
    bias_down,
    cotangent,
):
    w_qkv, w_out, w_up, w_down = (
        lax.all_gather(w_qkv, "dp", axis=0, tiled=True),
        lax.all_gather(w_out, "dp", axis=1, tiled=True),
        lax.all_gather(w_up, "dp", axis=0, tiled=True),
        lax.all_gather(w_down, "dp", axis=1, tiled=True),
    )
    lengths = slot_lengths[0]
    residual = tokens.astype(f32)
    normed_one, scaled_one, inverse_one = norm_forward(residual, gain_one, shift_one)
    rows_one = lax.all_gather(normed_one.astype(bf16), "mp", axis=0, tiled=True)
    packed = jnp.einsum("td,dcf->tcf", rows_one, w_qkv, preferred_element_type=f32)
    zero_bias = jnp.zeros_like(bias_qv[0])
    packed_bias = jnp.stack([bias_qv[0], zero_bias, bias_qv[1]]).astype(f32)
    packed = (packed + packed_bias[None]).astype(bf16)
    local = packed.shape[2]
    packed_rows = packed.reshape(packed.shape[0], -1)
    attended, exact_out, log_totals = attend_forward(packed_rows, lengths)
    hidden = (
        residual
        + lax.psum_scatter(
            jnp.dot(attended, w_out, preferred_element_type=f32),
            "mp",
            scatter_dimension=0,
            tiled=True,
        )
        + bias_out.astype(f32)
    )
    normed_two, scaled_two, inverse_two = norm_forward(hidden, gain_two, shift_two)
    normed_low = normed_two.astype(bf16)
    rows_two = lax.all_gather(normed_low, "mp", axis=0, tiled=True)
    preact = jnp.dot(rows_two, w_up, preferred_element_type=f32) + bias_up.astype(
        f32
    )
    active = gelu_tanh(preact).astype(bf16)
    ffn_out = lax.psum_scatter(
        jnp.dot(active, w_down, preferred_element_type=f32).astype(bf16),
        "mp",
        scatter_dimension=0,
        tiled=True,
    ).astype(f32)
    output = (hidden + ffn_out + bias_down.astype(f32)).astype(bf16)
    grad_out = cotangent.astype(f32)
    grad_rows = lax.all_gather(cotangent, "mp", axis=0, tiled=True)
    grad_active = jnp.einsum("td,fd->tf", grad_rows, w_down, preferred_element_type=f32)
    grad_pre = (grad_active * gelu_slope(preact)).astype(bf16)
    grad_up = jnp.einsum("td,tf->df", rows_two, grad_pre, preferred_element_type=f32)
    grad_down = jnp.einsum("tf,td->fd", active, grad_rows, preferred_element_type=f32)
    grad_bias_up = jnp.sum(grad_pre.astype(f32), axis=0)
    grad_norm_two = lax.psum_scatter(
        jnp.einsum("tf,df->td", grad_pre, w_up, preferred_element_type=f32),
        "mp",
        scatter_dimension=0,
        tiled=True,
    )
    grad_in_two, grad_gain_two, grad_shift_two = norm_backward(
        grad_norm_two, scaled_two, inverse_two, gain_two
    )
    grad_hidden = grad_out + grad_in_two
    grad_attn = grad_hidden.astype(bf16)
    grad_attn_rows = lax.all_gather(grad_attn, "mp", axis=0, tiled=True)
    grad_w_out = jnp.einsum(
        "tf,td->fd", attended, grad_attn_rows, preferred_element_type=f32
    )
    grad_attended = jnp.einsum(
        "td,fd->tf", grad_attn_rows, w_out, preferred_element_type=f32
    ).astype(bf16)
    product = (grad_attended.astype(f32) * exact_out).reshape(grad_attended.shape[0], -1, HD)
    delta = jnp.sum(product, axis=-1).T
    groups = log_totals.shape[0] // 8
    delta = delta.reshape(groups, -1, delta.shape[1])
    delta = jnp.pad(delta, ((0, 0), (0, 8 - delta.shape[1]), (0, 0))).reshape(8 * groups, -1)
    grads = attend_backward(packed_rows, grad_attended, log_totals, delta, lengths)
    grad_packed = jnp.stack(grads, axis=1)
    grad_w_qkv = jnp.einsum(
        "td,tcf->dcf", rows_one, grad_packed, preferred_element_type=f32
    )
    grad_bias_qv = jnp.stack(
        [
            jnp.sum(grad_packed[:, 0].astype(f32), axis=0),
            jnp.sum(grad_packed[:, 2].astype(f32), axis=0),
        ]
    )
    grad_norm_one = lax.psum_scatter(
        jnp.einsum("tcf,dcf->td", grad_packed, w_qkv, preferred_element_type=f32),
        "mp",
        scatter_dimension=0,
        tiled=True,
    )
    grad_in_one, grad_gain_one, grad_shift_one = norm_backward(
        grad_norm_one, scaled_one, inverse_one, gain_one
    )
    grad_tokens = (grad_hidden + grad_in_one).astype(bf16)
    grad_bias_out = jnp.sum(grad_attn.astype(f32), axis=0)
    grad_bias_down = jnp.sum(grad_out, axis=0)
    grad_w_qkv, grad_w_out, grad_up, grad_down = (
        lax.psum_scatter(grad_w_qkv, "dp", scatter_dimension=0, tiled=True),
        lax.psum_scatter(grad_w_out, "dp", scatter_dimension=1, tiled=True),
        lax.psum_scatter(grad_up, "dp", scatter_dimension=0, tiled=True),
        lax.psum_scatter(grad_down, "dp", scatter_dimension=1, tiled=True),
    )
    small_grads = lax.psum(
        (
            grad_gain_one,
            grad_shift_one,
            grad_bias_out,
            grad_gain_two,
            grad_shift_two,
            grad_bias_down,
        ),
        ("dp", "mp"),
    )
    grad_bias_qv, grad_bias_up = lax.psum((grad_bias_qv, grad_bias_up), "dp")
    return (
        output,
        grad_tokens,
        small_grads[0],
        small_grads[1],
        grad_w_qkv,
        grad_bias_qv,
        grad_w_out,
        small_grads[2],
        small_grads[3],
        small_grads[4],
        grad_up,
        grad_bias_up,
        grad_down,
        small_grads[5],
    )


def solution(mesh):
    pairs = dict(mesh.shape) == {"dp": 16, "mp": 2}
    layer = layer_on_pairs if pairs else layer_by_collectives
    return jax.shard_map(
        layer,
        mesh=mesh,
        in_specs=(
            P(("dp", "mp"), None),
            P("dp", None),
            P(),
            P(),
            P("dp", None, "mp"),
            P(None, "mp"),
            P("mp", "dp"),
            P(),
            P(),
            P(),
            P("dp", "mp"),
            P("mp"),
            P("mp", "dp"),
            P(),
            P(("dp", "mp"), None),
        ),
        out_specs=(
            P(("dp", "mp"), None),
            P(("dp", "mp"), None),
            P(),
            P(),
            P("dp", None, "mp"),
            P(None, "mp"),
            P("mp", "dp"),
            P(),
            P(),
            P(),
            P("dp", "mp"),
            P("mp"),
            P("mp", "dp"),
            P(),
        ),
        check_vma=False,
    )
```

```python
import functools

import jax
import jax.numpy as jnp
from jax import lax
from jax.experimental import pallas as pl
from jax.experimental.pallas import tpu as pltpu
from jax.sharding import PartitionSpec as P

HD = 64
LONG_LEN = 3072
BT = 512
VMEM_CAP = 60 * 1024 * 1024

f32 = jnp.float32
bf16 = jnp.bfloat16
norm_eps = 1e-05
masked_score = -1e30
gelu_coeff = 0.7978845608028654
score_scale = HD ** (-0.5)
safe_sum = 1e30


def dot_nt(left, right):
    return lax.dot_general(left, right, (((1,), (1,)), ((), ())), preferred_element_type=f32)


def dot_nn(left, right):
    return lax.dot_general(left, right, (((1,), (0,)), ((), ())), preferred_element_type=f32)


def dot_tn(left, right):
    return lax.dot_general(left, right, (((0,), (0,)), ((), ())), preferred_element_type=f32)


def params(axes=1, collective=None):
    if collective is None:
        return pltpu.CompilerParams(
            vmem_limit_bytes=VMEM_CAP, dimension_semantics=("arbitrary",) * axes
        )
    return pltpu.CompilerParams(
        vmem_limit_bytes=VMEM_CAP,
        dimension_semantics=("arbitrary",) * axes,
        collective_id=collective,
        has_side_effects=True,
    )


def cost(flops, nbytes, exps=0):
    return pl.CostEstimate(flops=int(flops), bytes_accessed=int(nbytes), transcendentals=int(exps))


ANY = pl.BlockSpec(memory_space=pl.ANY)


def bits_of_me():
    me = lax.axis_index("dp")
    return (me // 8, (me // 4) % 2, (me // 2) % 2, me % 2)


def flipped(bits, which):
    return tuple(1 - b if which & (8 >> k) else b for k, b in enumerate(bits))


def index_of(bits):
    return bits[0] * 8 + bits[1] * 4 + bits[2] * 2 + bits[3]


def across(which):
    return {"dp": index_of(flipped(bits_of_me(), which))}


def sibling():
    return {"mp": 1 - lax.axis_index("mp")}


MESH_ID = pl.DeviceIdType.MESH
HOPS = (1, 2, 4, 8, 12)


def sibling_across(which):
    return {**across(which), **sibling()}


def greet(with_small):
    devices = [across(hop) for hop in HOPS]
    if with_small:
        devices += [across(3), sibling()] + [sibling_across(k) for k in (1, 2, 3)]
    greet_only(devices)


def greet_only(devices):
    barrier = pltpu.get_barrier_semaphore()
    for device in devices:
        pl.semaphore_signal(barrier, inc=1, device_id=device, device_id_type=MESH_ID)
    pl.semaphore_wait(barrier, len(devices))


def greet_sibling():
    greet_only([sibling()])


def send(src, dst, sems, slot, device):
    return pltpu.make_async_remote_copy(
        src_ref=src,
        dst_ref=dst,
        send_sem=sems[0].at[slot],
        recv_sem=sems[1].at[slot],
        device_id=device,
        device_id_type=MESH_ID,
    )


def start_all(copies):
    for copy in copies:
        copy.start()


def wait_all(copies):
    for copy in copies:
        copy.wait()


def gather_z(src, dst, span, sems, base):
    bits = bits_of_me()
    z, yx = bits[0] * 2 + bits[1], bits[2] * 2 + bits[3]
    cols = pl.ds(*span)
    place = dst.at[z, yx, :, cols]
    copies = [
        send(src.at[:, cols], place, sems, base + k, across(4 * (k + 1))) for k in range(3)
    ]
    copies.append(pltpu.make_async_copy(src.at[:, cols], place, sems[2].at[base]))
    return copies


def gather_second(dst, span, route, sems, base):
    bits = bits_of_me()
    part = dst.at[:, bits[2] * 2 + bits[3], :, pl.ds(*span)]
    return [send(part, part, sems, base + 3, across((1, 2)[route]))]


def gather_third(dst, span, route, sems, base):
    copies = []
    for k, which in enumerate((0, (1, 2)[route])):
        bits = flipped(bits_of_me(), which)
        part = dst.at[:, bits[2] * 2 + bits[3], :, pl.ds(*span)]
        copies.append(send(part, part, sems, base + 4 + k, across((2, 1)[route])))
    return copies


def gather_sems(pieces):
    return [
        pltpu.SemaphoreType.DMA((6 * pieces,)),
        pltpu.SemaphoreType.DMA((6 * pieces,)),
        pltpu.SemaphoreType.DMA((6 * pieces,)),
    ]


def halves(cols, parts=1):
    half = cols // 2
    width = half // parts
    return [(r * half + c * width, width, r) for c in range(parts) for r in range(2)]


def head_lanes(block, head):
    lane_head = lax.broadcasted_iota(jnp.int32, block.shape, 1) // HD
    return jnp.where(lane_head == head, block, jnp.zeros_like(block))


def pack_heads(columns):
    lane = lax.broadcasted_iota(jnp.int32, columns[0].shape, 1)
    pairs = [
        jnp.where(lane < HD, columns[2 * i], columns[2 * i + 1]) for i in range(len(columns) // 2)
    ]
    return pairs[0] if len(pairs) == 1 else jnp.concatenate(pairs, axis=1)


def block_probs(scores, top):
    total, parts = None, []
    for t in range(scores.shape[1] // 128):
        part = jnp.exp(scores[:, t * 128 : (t + 1) * 128] - top)
        total = part if total is None else total + part
        parts.append(part.astype(bf16))
    return parts, total


def head_rows(stack, heads, first, count):
    block = stack.shape[0] // heads
    return jnp.concatenate(
        [stack[h * block + first : h * block + first + count, :] for h in range(heads)], axis=0
    )


def attend_block(masked, keys, values, m_ref, l_ref, acc_ref):
    heads, half = len(masked), keys.shape[0] // 2
    for part in range(2):
        rows = slice(part * half, (part + 1) * half)
        seen = (part + 1) * half
        low = []
        for h, query in enumerate(masked):
            scores = dot_nt(query[rows, :], keys[:seen, :])
            row = lax.broadcasted_iota(jnp.int32, scores.shape, 0) + part * half
            col = lax.broadcasted_iota(jnp.int32, scores.shape, 1)
            scores = jnp.where(row >= col, scores, masked_score)
            top = jnp.broadcast_to(jnp.max(scores, axis=1, keepdims=True), (half, 128))
            m_ref[h, rows, :] = top
            parts, l_ref[h, rows, :] = block_probs(scores, top)
            low += parts
        acc_ref[rows, :] = dot_nn(
            jnp.concatenate(low, axis=1), head_rows(values, heads, 0, seen)
        )


def attend_finish(heads, m_ref, l_ref, acc_ref, out_ref, exact_ref, lse_ref):
    block = out_ref.shape[0]
    lane = lax.broadcasted_iota(jnp.int32, (block, 128), 1)
    tops, totals = jnp.zeros((block, 128), f32), jnp.ones((block, 128), f32)
    inverse = []
    for h in range(heads):
        total = jnp.broadcast_to(jnp.sum(l_ref[h], axis=1, keepdims=True), (block, 128))
        tops = jnp.where(lane == h, m_ref[h], tops)
        totals = jnp.where(lane == h, total, totals)
        inverse.append(total)
    inverse = [1.0 / pack_heads(inverse[k : k + 2]) for k in range(0, heads, 2)]
    result = acc_ref[...] * jnp.concatenate(inverse, axis=1)
    out_ref[...] = result.astype(bf16)
    exact_ref[...] = result
    lse_ref[...] = (tops + jnp.log(totals)).T[:8, :]


def mask_values(v_ref, vm_ref, heads, block):
    for j in range(v_ref.shape[0] // block):
        value = v_ref[j * block : (j + 1) * block, :]
        for h in range(heads):
            vm_ref[j, h * block : (h + 1) * block, :] = head_lanes(value, h)


def attend_forward_kernel(heads, comm, lens_ref, q_ref, k_ref, v_ref, *refs):
    ins, refs = refs[: comm.ins], refs[comm.ins :]
    out_ref, exact_ref, lse_ref, big_ref = refs[:4]
    outs = refs[4 : 4 + comm.outs]
    vm_ref, m_ref, l_ref, acc_ref = refs[4 + comm.outs : 8 + comm.outs]
    sems = refs[8 + comm.outs :]
    step = pl.program_id(1)
    block = q_ref.shape[0]
    comm.before(pl.program_id(0) * pl.num_programs(1) + step, ins, outs, sems)

    @pl.when(step == 0)
    def _():
        mask_values(v_ref, vm_ref, heads, block)

    @pl.when((step == 0) & (pl.program_id(0) == 0))
    def _():
        big_ref[...] = jnp.zeros(big_ref.shape, f32)

    query = q_ref[...] * jnp.asarray(score_scale, bf16)
    masked = [head_lanes(query, h) for h in range(heads)]

    def key_block(j):
        return k_ref[pl.ds(pl.multiple_of(j * block, block), block), :]

    attend_block(masked, key_block(step), vm_ref[step], m_ref, l_ref, acc_ref)
    away = jnp.where(lens_ref[0] == LONG_LEN, 0.0, 1e30).astype(f32)

    def earlier(j, carry):
        keys = key_block(j)
        low = []
        for h in range(heads):
            parts, total = block_probs(dot_nt(masked[h], keys), m_ref[h] + away)
            l_ref[h] += total
            low += parts
        acc_ref[...] += dot_nn(jnp.concatenate(low, axis=1), vm_ref[j])
        return carry

    lax.fori_loop(0, step, earlier, 0)
    for h in range(heads):
        big_ref[...] = jnp.maximum(
            big_ref[...], jnp.max(l_ref[h].reshape(-1, 8, 128), axis=0)
        )
    attend_finish(heads, m_ref, l_ref, acc_ref, out_ref, exact_ref, lse_ref)
    comm.after(pl.program_id(0) * pl.num_programs(1) + step, ins, outs, sems)


def attend_safe_kernel(
    heads,
    groups,
    lens_ref,
    big_ref,
    packed,
    low_in,
    exact_in,
    lse_in,
    low,
    exact,
    lse,
    q_ref,
    k_ref,
    v_ref,
    out_ref,
    exact_ref,
    lse_ref,
    vm_ref,
    m_ref,
    l_ref,
    acc_ref,
    sem,
):
    block, cols = q_ref.shape
    tokens = k_ref.shape[0]

    def fetch(src, dst):
        copy = pltpu.make_async_copy(src, dst, sem)
        copy.start()
        copy.wait()

    def one_query(group, step):
        rows = pl.ds(pl.multiple_of(step * block, block), block)
        here = pl.ds(group * cols, cols)
        fetch(packed.at[rows, here], q_ref)
        query = q_ref[...] * jnp.asarray(score_scale, bf16)
        masked = [head_lanes(query, h) for h in range(heads)]

        def key_block(j):
            return k_ref[pl.ds(pl.multiple_of(j * block, block), block), :]

        attend_block(masked, key_block(step), vm_ref[step], m_ref, l_ref, acc_ref)

        def earlier(j, carry):
            keys = key_block(j)
            parts_all, shrink = [], []
            for h in range(heads):
                scores = dot_nt(masked[h], keys)
                old = m_ref[h]
                top = jnp.maximum(old, jnp.max(scores, axis=1, keepdims=True))
                factor = jnp.exp(old - top)
                m_ref[h] = top
                parts, total = block_probs(scores, top)
                l_ref[h] = l_ref[h] * factor + total
                parts_all += parts
                shrink.append(factor)
            acc_ref[...] = acc_ref[...] * pack_heads(shrink) + dot_nn(
                jnp.concatenate(parts_all, axis=1), vm_ref[j]
            )
            return carry

        lax.fori_loop(0, jnp.where(lens_ref[0] == LONG_LEN, step, 0), earlier, 0)
        attend_finish(heads, m_ref, l_ref, acc_ref, out_ref, exact_ref, lse_ref)
        fetch(out_ref, low.at[rows, here])
        fetch(exact_ref, exact.at[rows, here])
        fetch(lse_ref, lse.at[pl.ds(group * 8, 8), rows])

    @pl.when(jnp.logical_not(jnp.max(big_ref[...]) < safe_sum))
    def _():
        for group in range(groups):
            fetch(packed.at[:, pl.ds((groups + group) * cols, cols)], k_ref)
            fetch(packed.at[:, pl.ds((2 * groups + group) * cols, cols)], v_ref)
            mask_values(v_ref, vm_ref, heads, block)
            lax.fori_loop(
                0, tokens // block, lambda i, c, group=group: (one_query(group, i), c)[1], 0
            )


class NoTransfers:
    ins = outs = 0

    def before(self, *args):
        pass

    def after(self, *args):
        pass


def attend_shapes(tokens, width):
    groups = width // min(256, width)
    cols = width // groups
    shapes = [
        jax.ShapeDtypeStruct((tokens, width), bf16),
        jax.ShapeDtypeStruct((tokens, width), f32),
        jax.ShapeDtypeStruct((8 * groups, tokens), f32),
    ]
    return groups, cols, cols // HD, shapes


def attend_specs(tokens, width):
    groups = width // min(256, width)
    cols = width // groups
    ins = [
        pl.BlockSpec((BT, cols), lambda g, i, n: (i, g)),
        pl.BlockSpec((tokens, cols), lambda g, i, n: (0, groups + g)),
        pl.BlockSpec((tokens, cols), lambda g, i, n: (0, 2 * groups + g)),
    ]
    outs = [
        pl.BlockSpec((BT, cols), lambda g, i, n: (i, g)),
        pl.BlockSpec((BT, cols), lambda g, i, n: (i, g)),
        pl.BlockSpec((8, BT), lambda g, i, n: (g, i)),
    ]
    shapes = [
        jax.ShapeDtypeStruct((tokens, width), bf16),
        jax.ShapeDtypeStruct((tokens, width), f32),
        jax.ShapeDtypeStruct((8 * groups, tokens), f32),
    ]
    heads = cols // HD
    scratch = [
        pltpu.VMEM((tokens // BT, heads * BT, cols), bf16),
        pltpu.VMEM((heads, BT, 128), f32),
        pltpu.VMEM((heads, BT, 128), f32),
        pltpu.VMEM((BT, cols), f32),
    ]
    return groups, heads, ins, outs, shapes, scratch


def attend_cost(tokens, width, products):
    pairs = (tokens // BT) * (tokens // BT + 1) // 2
    work = products * 2 * pairs * BT * BT * width
    return cost(4 * work, 10 * tokens * width, pairs * BT * BT * width // HD)


def attend_safe(packed, lengths, big, low, exact, lse):
    tokens, width = packed.shape[0], packed.shape[1] // 3
    groups, cols, heads, shapes = attend_shapes(tokens, width)
    return pl.pallas_call(
        functools.partial(attend_safe_kernel, heads, groups),
        grid_spec=pltpu.PrefetchScalarGridSpec(
            num_scalar_prefetch=1,
            grid=(1,),
            in_specs=[pl.BlockSpec((8, 128), lambda i, n: (0, 0))] + [ANY] * 4,
            out_specs=[ANY] * 3,
            scratch_shapes=[
                pltpu.VMEM((BT, cols), bf16),
                pltpu.VMEM((tokens, cols), bf16),
                pltpu.VMEM((tokens, cols), bf16),
                pltpu.VMEM((BT, cols), bf16),
                pltpu.VMEM((BT, cols), f32),
                pltpu.VMEM((8, BT), f32),
                pltpu.VMEM((tokens // BT, heads * BT, cols), bf16),
                pltpu.VMEM((heads, BT, 128), f32),
                pltpu.VMEM((heads, BT, 128), f32),
                pltpu.VMEM((BT, cols), f32),
                pltpu.SemaphoreType.DMA(()),
            ],
        ),
        out_shape=shapes,
        input_output_aliases={3: 0, 4: 1, 5: 2},
        compiler_params=params(1),
        cost_estimate=cost(1000, 100000),
        name="attend_safe",
    )(lengths, big, packed, low, exact, lse)


def attend_forward(packed, lengths, comm=NoTransfers(), moved=(), fresh=None):
    tokens, width = packed.shape[0], packed.shape[1] // 3
    groups, heads, ins, outs, shapes, scratch = attend_specs(tokens, width)
    low, exact, lse, big, *rest = pl.pallas_call(
        functools.partial(attend_forward_kernel, heads, comm),
        grid_spec=pltpu.PrefetchScalarGridSpec(
            num_scalar_prefetch=1,
            grid=(groups, tokens // BT),
            in_specs=ins + [ANY] * len(moved),
            out_specs=outs
            + [pl.BlockSpec((8, 128), lambda g, i, n: (0, 0))]
            + [ANY] * comm.outs,
            scratch_shapes=scratch + (comm.scratch() if moved else []),
        ),
        out_shape=shapes
        + [jax.ShapeDtypeStruct((8, 128), f32)]
        + [jax.ShapeDtypeStruct(m.shape, m.dtype) for m in moved[1:]]
        + ([fresh] if moved else []),
        input_output_aliases={5: 4} if moved else {},
        compiler_params=params(2, 2 if moved else None),
        cost_estimate=attend_cost(tokens, width, 2),
        name="attend_forward",
    )(lengths, packed, packed, packed, *moved)
    low, exact, lse = attend_safe(packed, lengths, big, low, exact, lse)
    return [low, exact, lse] + rest


def attend_backward_kernel(heads, comm, lens_ref, q_ref, k_ref, v_ref, do_ref, lse_ref, delta_ref, *refs):
    ins, refs = refs[: comm.ins], refs[comm.ins :]
    dq_ref, dk_ref, dv_ref = refs[:3]
    outs, refs = refs[3 : 3 + comm.outs], refs[3 + comm.outs :]
    qm_ref, dom_ref, km_ref, vm_ref, dqa_ref, dka_ref, dva_ref = refs[:7]
    scratch = refs[7:]
    step = pl.program_id(1)
    count = pl.num_programs(1)
    block = k_ref.shape[0]
    comm.before(pl.program_id(0) * count + step, ins, outs, scratch)

    @pl.when(step == 0)
    def _():
        for t in range(q_ref.shape[0] // block):
            rows = slice(t * block, (t + 1) * block)
            for h in range(heads):
                place = slice(h * block, (h + 1) * block)
                qm_ref[t, place, :] = head_lanes(q_ref[rows, :], h)
                dom_ref[t, place, :] = head_lanes(do_ref[rows, :], h)
        dqa_ref[...] = jnp.zeros(dqa_ref.shape, f32)

    for h in range(heads):
        place = slice(h * block, (h + 1) * block)
        km_ref[place, :] = head_lanes(k_ref[...] * jnp.asarray(score_scale, bf16), h)
        vm_ref[place, :] = head_lanes(v_ref[...], h)
    dka_ref[...] = jnp.zeros(dka_ref.shape, f32)
    dva_ref[...] = jnp.zeros(dva_ref.shape, f32)
    away = jnp.where(lens_ref[0] == LONG_LEN, 0.0, 1e30).astype(f32)

    def pair(i, first, count, seen, on_diagonal):
        rows = pl.ds(pl.multiple_of(i * block + first, count), count)
        query, grad = q_ref[rows, :], do_ref[rows, :]
        low, slopes = [], []
        for h in range(heads):
            place = slice(h * block, h * block + seen)
            scores = dot_nt(km_ref[place, :], query)
            logs = lse_ref[h : h + 1, rows]
            if not on_diagonal:
                logs = logs + away
            prob = jnp.exp(scores - logs)
            if on_diagonal:
                key = lax.broadcasted_iota(jnp.int32, scores.shape, 0)
                tok = lax.broadcasted_iota(jnp.int32, scores.shape, 1) + first
                prob = jnp.where(tok >= key, prob, 0.0)
            grad_prob = dot_nt(vm_ref[place, :], grad)
            slope = prob * (grad_prob - delta_ref[h : h + 1, rows])
            low.append(prob.astype(bf16))
            slopes.append(slope.astype(bf16))
        if on_diagonal:
            grads = head_rows(dom_ref[i], heads, first, count)
            queries = head_rows(qm_ref[i], heads, first, count)
            keys = head_rows(km_ref[...], heads, 0, seen)
        else:
            grads, queries, keys = dom_ref[i], qm_ref[i], km_ref[...]
        dva_ref[0:seen, :] += dot_nn(jnp.concatenate(low, axis=1), grads)
        dka_ref[0:seen, :] += dot_nn(jnp.concatenate(slopes, axis=1), queries)
        dqa_ref[rows, :] += dot_tn(jnp.concatenate(slopes, axis=0), keys)

    half = block // 2
    pair(step, 0, half, half, True)
    pair(step, half, half, block, True)
    lax.fori_loop(step + 1, count, lambda i, c: (pair(i, 0, block, block, False), c)[1], 0)
    dk_ref[...] = (dka_ref[...] * score_scale).astype(bf16)
    dv_ref[...] = dva_ref[...].astype(bf16)

    @pl.when(step == count - 1)
    def _():
        dq_ref[...] = dqa_ref[...].astype(bf16)

    comm.after(pl.program_id(0) * count + step, ins, outs, scratch)


def attend_backward(packed, grad_attended, lse, delta, lengths, comm=NoTransfers(), moved=()):
    tokens, width = grad_attended.shape
    groups = width // min(256, width)
    cols = width // groups
    heads = cols // HD
    blocks = tokens // BT
    column = pl.BlockSpec((tokens, cols), lambda g, j, n: (0, g))
    stats = pl.BlockSpec((8, tokens), lambda g, j, n: (g, 0))
    tile = pl.BlockSpec((BT, cols), lambda g, j, n: (j, g))
    move_ins, move_outs, move_shapes, move_scratch = comm.specs(moved) if moved else ([], [], [], [])
    return pl.pallas_call(
        functools.partial(attend_backward_kernel, heads, comm),
        grid_spec=pltpu.PrefetchScalarGridSpec(
            num_scalar_prefetch=1,
            grid=(groups, blocks),
            in_specs=[
                column,
                pl.BlockSpec((BT, cols), lambda g, j, n: (j, groups + g)),
                pl.BlockSpec((BT, cols), lambda g, j, n: (j, 2 * groups + g)),
                column,
                stats,
                stats,
            ]
            + move_ins,
            out_specs=[column, tile, tile] + move_outs,
            scratch_shapes=[
                pltpu.VMEM((blocks, heads * BT, cols), bf16),
                pltpu.VMEM((blocks, heads * BT, cols), bf16),
                pltpu.VMEM((heads * BT, cols), bf16),
                pltpu.VMEM((heads * BT, cols), bf16),
                pltpu.VMEM((tokens, cols), f32),
                pltpu.VMEM((BT, cols), f32),
                pltpu.VMEM((BT, cols), f32),
            ]
            + move_scratch,
        ),
        out_shape=[jax.ShapeDtypeStruct((tokens, width), bf16)] * 3 + move_shapes,
        compiler_params=params(2, 3 if moved else None),
        cost_estimate=attend_cost(tokens, width, 5),
        name="attend_backward",
    )(lengths, packed, packed, packed, grad_attended, lse, delta, *moved)


class AttendGather:
    ins, outs = 2, 2

    def scratch(self):
        return gather_sems(4)

    def pieces(self, ins, outs):
        up = [(None, outs[0], (at, width), route) for at, width, route in halves(outs[0].shape[3])]
        down = [(ins[0], outs[1], (at, width), route) for at, width, route in halves(ins[0].shape[1])]
        return up + down

    def hops(self, name, ks, ins, outs, sems):
        copies = []
        for k in ks:
            src, dst, span, route = self.pieces(ins, outs)[k]
            if name == "z":
                copies += gather_z(src, dst, span, sems, 6 * k)
            elif name == "second":
                copies += gather_second(dst, span, route, sems, 6 * k)
            else:
                copies += gather_third(dst, span, route, sems, 6 * k)
        return copies

    def before(self, step, ins, outs, sems):
        def hops(name, ks):
            return self.hops(name, ks, ins, outs, sems)

        @pl.when(step == 0)
        def _():
            greet(False)
            start_all(hops("z", (2, 3)))
            start_all(hops("second", (0, 1)))

        @pl.when(step == 3)
        def _():
            wait_all(hops("second", (0, 1)))
            start_all(hops("third", (0, 1)))

        @pl.when(step == 6)
        def _():
            wait_all(hops("z", (2, 3)))
            start_all(hops("second", (2, 3)))

        @pl.when(step == 9)
        def _():
            wait_all(hops("second", (2, 3)))
            start_all(hops("third", (2, 3)))

    def after(self, step, ins, outs, sems):
        @pl.when(step == 11)
        def _():
            wait_all(self.hops("third", (0, 1, 2, 3), ins, outs, sems))


class SumPart:
    slots = 5

    def __init__(self, grad, span, route, refs, sems, base):
        self.keep = grad.at[pl.ds(0, 512), pl.ds(*span)]
        self.sent = grad.at[pl.ds(512, 512), pl.ds(*span)]
        self.held, self.got_1, self.got_2, self.got_3 = refs
        self.sems, self.base = sems, base
        self.hops = ((2, 1), (1, 2))[route]

    @staticmethod
    def buffers(width):
        return [
            pltpu.VMEM((512, width), bf16),
            pltpu.VMEM((512, width), bf16),
            pltpu.VMEM((256, width), bf16),
            pltpu.VMEM((3, 64, width), bf16),
        ]

    def first(self):
        return [
            send(self.sent, self.got_1, self.sems, self.base, across(self.hops[0])),
            pltpu.make_async_copy(self.keep, self.held, self.sems[2].at[self.base]),
        ]

    def second(self):
        return [
            send(
                self.held.at[pl.ds(256, 256), :],
                self.got_2,
                self.sems,
                self.base + 1,
                across(self.hops[1]),
            )
        ]

    def third(self):
        return [
            send(
                self.held.at[pl.ds(64 * z, 64), :],
                self.got_3.at[z - 1],
                self.sems,
                self.base + 1 + z,
                across(4 * z),
            )
            for z in (1, 2, 3)
        ]

    def add(self, other, rows):
        def body(i, carry):
            at = pl.ds(pl.multiple_of(i * 64, 64), 64)
            self.held[at, :] = self.held[at, :] + other[at, :]
            return carry

        lax.fori_loop(0, rows // 64, body, 0)

    def to_second(self):
        wait_all(self.first())
        self.add(self.got_1, 512)
        start_all(self.second())

    def to_third(self):
        wait_all(self.second())
        self.add(self.got_2, 256)
        start_all(self.third())

    def result(self):
        wait_all(self.third())
        total = self.held[0:64, :].astype(f32)
        for z in range(3):
            total = total + self.got_3[z].astype(f32)
        return total


def sum_sems(parts):
    return [
        pltpu.SemaphoreType.DMA((SumPart.slots * parts,)),
        pltpu.SemaphoreType.DMA((SumPart.slots * parts,)),
        pltpu.SemaphoreType.DMA((SumPart.slots * parts,)),
    ]


class SmallSum:
    def __init__(self, refs, sems):
        self.got, self.sems = refs, sems

    @staticmethod
    def scratch():
        return [
            pltpu.VMEM((8, 8, 1024), f32),
            pltpu.VMEM((4, 8, 1024), f32),
            pltpu.SemaphoreType.DMA((10,)),
            pltpu.SemaphoreType.DMA((10,)),
        ]

    def near(self):
        bits = bits_of_me()
        place = self.got[0].at[lax.axis_index("mp") * 4 + bits[2] * 2 + bits[3]]
        devices = [across(k) for k in (1, 2, 3)] + [sibling()]
        devices += [sibling_across(k) for k in (1, 2, 3)]
        return [send(place, place, self.sems, k, device) for k, device in enumerate(devices)]

    def far(self):
        bits = bits_of_me()
        place = self.got[1].at[bits[0] * 2 + bits[1]]
        return [send(place, place, self.sems, 6 + k, across(4 * k)) for k in (1, 2, 3)]

    def begin(self, rows):
        bits = bits_of_me()
        self.got[0][lax.axis_index("mp") * 4 + bits[2] * 2 + bits[3]] = rows
        start_all(self.near())

    def middle(self, both):
        wait_all(self.near())
        row = lax.broadcasted_iota(jnp.int32, (8, 1024), 0)
        total = jnp.zeros((8, 1024), f32)
        for k in range(8):
            counts = (row < both) | (lax.axis_index("mp") == k // 4)
            total = total + jnp.where(counts, self.got[0][k], 0.0)
        bits = bits_of_me()
        self.got[1][bits[0] * 2 + bits[1]] = total
        start_all(self.far())

    def end(self):
        wait_all(self.far())
        return (self.got[1][0] + self.got[1][1]) + (self.got[1][2] + self.got[1][3])


class BackwardSum:
    def __init__(self, cols):
        self.cols = cols
        self.ins = len(cols) + 2
        self.outs = len(cols) + 1

    def specs(self, moved):
        vmem = [pl.BlockSpec((8, 1024), lambda g, j, n: (0, 0))]
        sizes = [(64, c) for c in self.cols]
        shapes = [jax.ShapeDtypeStruct(size, f32) for size in sizes]
        outs = [pl.BlockSpec(size, lambda g, j, n: (0, 0)) for size in sizes]
        scratch = []
        for c in self.cols:
            scratch += SumPart.buffers(c // 2) * 2
        scratch += sum_sems(2 * len(self.cols)) + SmallSum.scratch()
        return (
            [ANY] * len(self.cols)
            + [
                pl.BlockSpec((32, 1024), lambda g, j, n: (0, 0)),
                pl.BlockSpec((8, 2048), lambda g, j, n: (0, 0)),
            ],
            outs + vmem,
            shapes + [jax.ShapeDtypeStruct((8, 1024), f32)],
            scratch,
        )

    def parts(self, ins, scratch):
        count = 2 * len(self.cols)
        sems = scratch[4 * count : 4 * count + 3]
        made = []
        for k in range(count):
            width = self.cols[k // 2] // 2
            refs = scratch[4 * k : 4 * k + 4]
            span = ((k % 2) * width, width)
            made.append(SumPart(ins[k // 2], span, k % 2, refs, sems, SumPart.slots * k))
        rest = scratch[4 * count + 3 :]
        return made, SmallSum(rest[:2], rest[2:])

    def before(self, step, ins, outs, scratch):
        parts, small = self.parts(ins, scratch)

        @pl.when(step == 0)
        def _():
            greet(True)
            ups = jnp.sum(ins[-1][...], axis=0, keepdims=True)
            rows = [
                jnp.sum(ins[-2][8 * k : 8 * k + 8, :], axis=0, keepdims=True) for k in range(4)
            ]
            rows += [ups[:, :1024], ups[:, 1024:], jnp.zeros((2, 1024), f32)]
            small.begin(jnp.concatenate(rows, axis=0))
            for part in parts[:2] + parts[4:]:
                start_all(part.first())

        @pl.when(step == 1)
        def _():
            small.middle(4)

        @pl.when(step == 2)
        def _():
            for part in parts[:2] + parts[4:]:
                part.to_second()
            for part in parts[2:4]:
                start_all(part.first())

        @pl.when(step == 5)
        def _():
            outs[-1][...] = small.end()

        @pl.when(step == 6)
        def _():
            for part in parts[:2] + parts[4:]:
                part.to_third()

        @pl.when(step == 7)
        def _():
            for part in parts[2:4]:
                part.to_second()

        @pl.when(step == 8)
        def _():
            for part in parts[2:4]:
                part.to_third()

    def after(self, step, ins, outs, scratch):
        parts, _ = self.parts(ins, scratch)

        @pl.when(step == 11)
        def _():
            for k, part in enumerate(parts):
                width = self.cols[k // 2] // 2
                span = slice((k % 2) * width, (k % 2 + 1) * width)
                outs[k // 2][:, span] = part.result()


def normalized(values):
    average = jnp.mean(values, axis=-1, keepdims=True)
    centred = values - average
    variance = jnp.mean(centred * centred, axis=-1, keepdims=True)
    inverse = lax.rsqrt(variance + norm_eps)
    return centred * inverse, inverse


def column_sum(values):
    return jnp.sum(values.reshape(-1, 8, values.shape[-1]), axis=0)


def turned(values, out_ref):
    flip = values.T
    bits = bits_of_me()
    for a in range(16):
        r = flipped(bits, a)
        slot = r[2] * 8 + r[3] * 4 + r[0] * 2 + r[1]
        out_ref[pl.ds(pl.multiple_of(slot * 64, 64), 64), :] = flip[a * 64 : (a + 1) * 64, :]


def shape(rows, cols, dtype=bf16):
    return jax.ShapeDtypeStruct((rows, cols), dtype)


def row_tile(cols):
    return pl.BlockSpec((BT, cols), lambda i: (i, 0))


def col_tile(rows):
    return pl.BlockSpec((rows, BT), lambda i: (0, i))


def whole(rows, cols):
    return pl.BlockSpec((rows, cols), lambda i: (0, 0))


def weight(cols):
    return pl.BlockSpec((1024, cols), lambda i: (0, 0), pipeline_mode=pl.Buffered(1))


def my_side():
    return lax.axis_index("mp")


def grid_call(kernel, steps, ins, outs, scratch, flops, name, collective=None, aliases={}):
    arrays = [a for a, _ in ins]
    nbytes = sum(a.size * a.dtype.itemsize for a in arrays)
    nbytes += sum(o.size * o.dtype.itemsize for o, _ in outs)
    return pl.pallas_call(
        kernel,
        grid=(steps,),
        in_specs=[s for _, s in ins],
        out_specs=[s for _, s in outs],
        scratch_shapes=scratch,
        out_shape=[o for o, _ in outs],
        input_output_aliases=aliases,
        compiler_params=params(1, collective),
        cost_estimate=cost(flops, nbytes),
        name=name,
    )(*arrays)


def vector(values):
    rows = values.shape[0] // 128
    return (values.reshape(rows, 128), whole(rows, 128))


def spread(ref, at=0, cols=1024):
    rows = ref[...].astype(f32)
    low, count = at // 128, cols // 128
    return jnp.concatenate([rows[k : k + 1, :] for k in range(low, low + count)], axis=1)


def qkv_bias(ref, cols):
    bias = ref[...].astype(f32)
    zero = jnp.zeros((1, bias.shape[1]), f32)
    return jnp.concatenate([bias[0:1, :], zero, bias[1:2, :]], axis=1)[:, cols]


class FirstGather:
    def __init__(self, wq, up, up_out, wo, out_out, sems):
        self.pieces = [(None, wq, (at, width), r) for at, width, r in chunk_halves(wq.shape[3])]
        self.pieces += [(up, up_out, (at, width), r) for at, width, r in halves(up.shape[1])]
        self.pieces += [(wo, out_out, (at, width), r) for at, width, r in halves(wo.shape[1])]
        self.sems = sems

    def z(self, *ks):
        copies = []
        for k in ks:
            src, dst, span, _ = self.pieces[k]
            if src is None:
                bits = bits_of_me()
                place = dst.at[bits[0] * 2 + bits[1], bits[2] * 2 + bits[3], :, pl.ds(*span)]
                copies += [
                    send(place, place, self.sems, 6 * k + hop, across(4 * (hop + 1)))
                    for hop in range(3)
                ]
            else:
                copies += gather_z(src, dst, span, self.sems, 6 * k)
        return copies

    def second(self, *ks):
        copies = []
        for k in ks:
            _, dst, span, route = self.pieces[k]
            copies += gather_second(dst, span, route, self.sems, 6 * k)
        return copies

    def third(self, *ks):
        copies = []
        for k in ks:
            _, dst, span, route = self.pieces[k]
            copies += gather_third(dst, span, route, self.sems, 6 * k)
        return copies


def chunk_halves(cols):
    width = cols // 4
    return [(k * width, width, k % 2) for k in range(4)]


def qkv_kernel(
    tiles,
    own,
    own_all,
    gain,
    shift,
    bias,
    w_mine,
    wo,
    up,
    turned_out,
    out,
    up_out,
    out_out,
    w_out,
    normed,
    came,
    wq,
    swap_send,
    swap_came,
    copy_sem,
    *sems,
):
    step = pl.program_id(0)
    side = my_side()
    moves = FirstGather(wq, up, up_out, wo, out_out, sems)
    local = w_mine.shape[2]

    def swap(k):
        return send(
            own_all.at[pl.ds(k * BT, BT), :], came.at[k], (swap_send, swap_came), k, sibling()
        )

    @pl.when(step == 0)
    def _():
        bits = bits_of_me()
        for c in range(3):
            wq[bits[0] * 2 + bits[1], bits[2] * 2 + bits[3], :, c * local : (c + 1) * local] = (
                w_mine[c]
            )
        greet(True)
        start_all(moves.z(0, 1))
        start_all([swap(k) for k in range(tiles)])

    def norm(values):
        scaled, _ = normalized(values.astype(f32))
        rows = (scaled * spread(gain) + spread(shift)).astype(bf16)
        first = lax.rem(step + side * tiles, 2 * tiles) * BT
        normed[pl.ds(pl.multiple_of(first, BT), BT), :] = rows
        turned(rows, turned_out)

    @pl.when(step < tiles)
    def _():
        norm(own[...])

    for k in range(tiles):

        @pl.when(step == tiles + k)
        def _():
            swap(k).wait()
            norm(came[k])

    @pl.when(step == 2 * tiles - 2)
    def _():
        wait_all(moves.z(0, 1))
        start_all(moves.second(0, 1))
        start_all(moves.z(2, 3))

    @pl.when(step == 2 * tiles)
    def _():
        wait_all(moves.second(0, 1))
        start_all(moves.third(0, 1))
        wait_all(moves.z(2, 3))
        start_all(moves.second(2, 3))
        start_all(moves.z(6, 7))
        start_all(moves.z(4, 5))
        wait_all(moves.third(0, 1))

    @pl.when(step == 2 * tiles + 1)
    def _():
        wait_all(moves.second(2, 3))
        start_all(moves.third(2, 3))

    half = out.shape[1]
    for c in range(2):

        @pl.when((step >= (2 + 2 * c) * tiles) & (step < (4 + 2 * c) * tiles))
        def _():
            @pl.when(step == (2 + 2 * c) * tiles)
            def _():
                if c:
                    wait_all(moves.third(2, 3))
                    wait_all(moves.z(6, 7))
                    start_all(moves.second(6, 7))
                    pltpu.make_async_copy(wq, w_out, copy_sem).start()

            first = (step - (2 + 2 * c) * tiles) * BT
            rows = normed[pl.ds(pl.multiple_of(first, BT), BT), :]
            cols = slice(c * half, (c + 1) * half)
            part = wq[:, :, :, cols].reshape(1024, half)
            out[...] = (dot_nn(rows, part) + qkv_bias(bias, cols)).astype(bf16)

    @pl.when(step == 5 * tiles)
    def _():
        wait_all(moves.second(6, 7))
        start_all(moves.third(6, 7))

    @pl.when(step == 6 * tiles - 1)
    def _():
        wait_all(moves.third(6, 7))
        wait_all(moves.z(4, 5))
        pltpu.make_async_copy(wq, w_out, copy_sem).wait()


def project_kernel(
    tiles,
    a,
    w,
    toks,
    bias,
    gain,
    shift,
    hid_out,
    normed_out,
    sent,
    came,
    sent_sems,
    came_sems,
):
    step = pl.program_id(0)

    def swap(k):
        return send(sent.at[k], came.at[k], (sent_sems, came_sems), k, sibling())

    @pl.when(step == 0)
    def _():
        greet_sibling()

    partial = dot_nt(a[...], w[...])
    for k in range(tiles):

        @pl.when(step == k)
        def _():
            sent[k] = partial.astype(bf16)
            swap(k).start()

        @pl.when(step == tiles + k)
        def _():
            swap(k).wait()
            hidden = toks[...].astype(f32) + (partial + came[k].astype(f32) + spread(bias))
            hid_out[...] = hidden
            scaled, _ = normalized(hidden)
            normed_out[...] = (scaled * spread(gain) + spread(shift)).astype(bf16)


def feed_kernel(
    tiles,
    x_all,
    c_all,
    bias,
    wu,
    wd,
    ffn_own,
    norm_own,
    ffn_came,
    norm_came,
    up_out,
    down_out,
    bsum,
    up_total,
    down_total,
    act,
    gpre,
    xt,
    ct,
    xs,
    cs,
    ffn_sent,
    norm_sent,
    local_sems,
    send_sems,
    came_sems,
    out_sems,
):
    step = pl.program_id(0)
    remote = (send_sems, came_sems)

    def rows(k):
        return pl.ds(k * BT, BT)

    def local(k):
        return [
            pltpu.make_async_copy(x_all.at[rows(k), :], xs.at[k], local_sems.at[k]),
            pltpu.make_async_copy(c_all.at[rows(k), :], cs.at[k], local_sems.at[tiles + k]),
        ]

    def swapped(k):
        return [
            send(x_all.at[rows(k), :], xs.at[tiles + k], remote, k, sibling()),
            send(c_all.at[rows(k), :], cs.at[tiles + k], remote, tiles + k, sibling()),
        ]

    def returned(k):
        return [
            send(ffn_sent, ffn_came.at[rows(k), :], remote, 2 * tiles + k, sibling()),
            send(norm_sent, norm_came.at[rows(k), :], remote, 3 * tiles + k, sibling()),
        ]

    @pl.when(step == 0)
    def _():
        for k in range(tiles):
            start_all(local(k))
        bsum[...] = jnp.zeros(bsum.shape, f32)
        greet_sibling()
        for k in range(tiles):
            start_all(swapped(k))

    for k in range(tiles):

        @pl.when(step == k)
        def _():
            wait_all(local(k))

        @pl.when(step == tiles + k)
        def _():
            wait_all(swapped(k))

    x, c = xs[step], cs[step]
    xt[...] = x.T
    ct[...] = c.T
    width = 512
    spans = [slice(at, at + width) for at in range(0, wu.shape[1], width)]
    for cols in spans:
        value = dot_nn(x, wu[:, cols]) + spread(bias, cols.start, width)
        upstream = dot_nn(c, wd[:, cols])
        square = value * value
        bent = jnp.tanh(value * (gelu_coeff + (gelu_coeff * 0.044715) * square))
        half_up = 0.5 + 0.5 * bent
        act[:, cols] = (value * half_up).astype(bf16)
        slope = half_up + value * (half_up * (1.0 - bent)) * (
            gelu_coeff + (3.0 * 0.044715 * gelu_coeff) * square
        )
        grad = (upstream * slope).astype(bf16)
        gpre[:, cols] = grad
        bsum[:, cols] += column_sum(grad.astype(f32))
    ffn = dot_nt(act[...], wd[...]).astype(bf16)
    norm = dot_nt(gpre[...], wu[...]).astype(bf16)

    @pl.when(step < tiles)
    def _():
        ffn_own[...] = ffn
        norm_own[...] = norm

    for k in range(tiles):

        @pl.when(step == tiles + k)
        def _():
            if k:
                wait_all(returned(k - 1))
            ffn_sent[...] = ffn
            norm_sent[...] = norm
            start_all(returned(k))

    @pl.when(step == 0)
    def _():
        for cols in spans:
            down_total[:, cols] = dot_nn(ct[...], act[:, cols])
        for cols in spans:
            up_total[:, cols] = dot_nn(xt[...], gpre[:, cols])

    @pl.when(step > 0)
    def _():
        for cols in spans:
            down_total[:, cols] += dot_nn(ct[...], act[:, cols])
        for cols in spans:
            up_total[:, cols] += dot_nn(xt[...], gpre[:, cols])

    def leave(total, stage, out, base):
        half = total.shape[1] // 2
        bits = bits_of_me()
        copies = []
        for top in range(2):
            for route in range(2):
                part = total[512 * top : 512 * top + 512, route * half : route * half + half]
                stage[top * 2 + route] = part.astype(bf16)
        for a in range(16):
            r = flipped(bits, a)
            for route in range(2):
                slot = r[2 + route] * 8 + r[3 - route] * 4 + r[0] * 2 + r[1]
                copies.append(
                    pltpu.make_async_copy(
                        stage.at[(a // 8) * 2 + route, pl.ds((a % 8) * 64, 64), :],
                        out.at[
                            pl.ds(pl.multiple_of(slot * 64, 64), 64), pl.ds(route * half, half)
                        ],
                        out_sems.at[base + 2 * a + route],
                    )
                )
        start_all(copies)
        return copies

    @pl.when(step == 2 * tiles - 1)
    def _():
        copies = leave(down_total, cs, down_out, 0)
        copies += leave(up_total, xs, up_out, 32)
        wait_all(copies)
        wait_all(returned(tiles - 1))


def middle_kernel(
    tiles,
    hid,
    f_own,
    f_came,
    g_own,
    g_came,
    cot,
    bias,
    gain,
    exact,
    attended,
    w,
    out,
    gattn,
    do_out,
    delta_out,
    grad_w,
    sums,
    turned_rows,
    total,
    now,
    sent,
    came,
    sent_sems,
    came_sems,
):
    step = pl.program_id(0)

    def swap(k):
        return send(sent.at[k], came.at[k], (sent_sems, came_sems), k, sibling())

    @pl.when(step == 0)
    def _():
        sums[...] = jnp.zeros(sums.shape, f32)
        total[...] = jnp.zeros(total.shape, f32)
        greet_sibling()

    @pl.when(step < tiles)
    def _():
        hidden = hid[...]
        grad_out = cot[...].astype(f32)
        branch = f_own[...].astype(f32) + f_came[...].astype(f32) + spread(bias)
        out[...] = (hidden + branch).astype(bf16)
        scaled, inverse = normalized(hidden)
        grad_norm = g_own[...].astype(f32) + g_came[...].astype(f32)
        through = grad_norm * spread(gain)
        centre = jnp.mean(through, axis=-1, keepdims=True)
        along = jnp.mean(through * scaled, axis=-1, keepdims=True)
        grad = (grad_out + inverse * (through - centre - scaled * along)).astype(bf16)
        gattn[...] = grad
        now[...] = grad
        sums[0:8, :] += column_sum(grad_norm * scaled)
        sums[8:16, :] += column_sum(grad_norm)
        sums[16:24, :] += column_sum(grad.astype(f32))
        sums[24:32, :] += column_sum(grad_out)

    for k in range(tiles):

        @pl.when(step == k)
        def _():
            sent[k] = now[...]
            swap(k).start()

        @pl.when(step == tiles + k)
        def _():
            swap(k).wait()
            now[...] = came[k]

    grad = now[...]
    turned(grad, turned_rows)
    part = dot_nn(grad, w[...]).astype(bf16)
    do_out[...] = part
    product = part.astype(f32) * exact[...]
    head = lax.broadcasted_iota(jnp.int32, (part.shape[1], 128), 0) // HD
    place = lax.broadcasted_iota(jnp.int32, (part.shape[1], 128), 1)
    pick = jnp.where(place == (head // 4) * 8 + head % 4, 1.0, 0.0).astype(bf16)
    high = product.astype(bf16)
    rest = (product - high.astype(f32)).astype(bf16)
    delta_out[...] = (dot_nn(high, pick) + dot_nn(rest, pick)).T[:16, :]
    total[...] += dot_nn(turned_rows[...], attended[...])

    @pl.when(step == 2 * tiles - 1)
    def _():
        write_grad(total, grad_w)


def write_grad(total, out):
    half = total.shape[1] // 2
    out[:, :half] = total[:, :half].astype(bf16)
    for to, at in enumerate((0, 2, 1, 3)):
        there, here = slice(256 * to, 256 * to + 256), slice(256 * at, 256 * at + 256)
        out[there, half:] = total[here, half:].astype(bf16)


class HeldSumPart(SumPart):
    def __init__(self, route, refs, sems, base):
        self.held, self.sent = refs[:2]
        self.got_1, self.got_2, self.got_3 = refs[2:]
        self.sems, self.base = sems, base
        self.hops = ((2, 1), (1, 2))[route]

    @staticmethod
    def buffers(width):
        return [pltpu.VMEM((512, width), bf16)] + SumPart.buffers(width)

    def first(self):
        return [send(self.sent, self.got_1, self.sems, self.base, across(self.hops[0]))]


def last_scratch(cols):
    made = []
    for _ in range(4):
        made += HeldSumPart.buffers(cols // 4)
    return made + sum_sems(4) + SmallSum.scratch()


def last_kernel(
    tiles,
    turned_rows,
    dq,
    dk,
    dv,
    w,
    toks,
    gattn,
    gain,
    out,
    grad_w,
    small_out,
    sums,
    qv_sums,
    total,
    sent,
    came,
    send_sems,
    recv_sems,
    *refs,
):
    step = pl.program_id(0)
    blocks = 2 * tiles
    parts = [
        HeldSumPart(k % 2, refs[5 * k : 5 * k + 5], refs[20:23], SumPart.slots * k)
        for k in range(4)
    ]
    tiny = SmallSum(refs[23:25], refs[25:27])
    local = dq.shape[1]
    quarter = 3 * local // 4

    def swap(k):
        return send(sent.at[k], came.at[k], (send_sems, recv_sems), k, sibling())

    @pl.when(step == 0)
    def _():
        greet(True)
        sums[...] = jnp.zeros(sums.shape, f32)
        qv_sums[...] = jnp.zeros(qv_sums.shape, f32)

    grads = jnp.concatenate([dq[...], dk[...], dv[...]], axis=1)

    @pl.when(step < blocks)
    def _():
        qv_sums[:, :local] += column_sum(dq[...].astype(f32))
        qv_sums[:, local:] += column_sum(dv[...].astype(f32))

    for c in range(2):

        @pl.when((step >= c * blocks) & (step < (c + 1) * blocks))
        def _():
            spans = [slice(r * 2 * quarter + c * quarter, r * 2 * quarter + (c + 1) * quarter) for r in range(2)]
            term = dot_nn(turned_rows[...], jnp.concatenate([grads[:, s] for s in spans], axis=1))

            @pl.when(step == c * blocks)
            def _():
                total[...] = term

            @pl.when(step > c * blocks)
            def _():
                total[...] += term

            @pl.when(step == (c + 1) * blocks - 1)
            def _():
                one, two = parts[2 * c], parts[2 * c + 1]
                one.held[...] = total[0:512, :quarter].astype(bf16)
                one.sent[...] = total[512:1024, :quarter].astype(bf16)
                two.held[0:256, :] = total[0:256, quarter:].astype(bf16)
                two.held[256:512, :] = total[512:768, quarter:].astype(bf16)
                two.sent[0:256, :] = total[256:512, quarter:].astype(bf16)
                two.sent[256:512, :] = total[768:1024, quarter:].astype(bf16)
                start_all(one.first() + two.first())

    @pl.when(step == 2 * blocks + 1)
    def _():
        for part in parts[:2]:
            part.to_second()

    @pl.when(step == 2 * blocks + 3)
    def _():
        for part in parts[:2]:
            part.to_third()

    @pl.when(step == 2 * blocks + 4)
    def _():
        for part in parts[2:]:
            part.to_second()

    @pl.when(step == 2 * blocks + 5)
    def _():
        for part in parts[2:]:
            part.to_third()

    @pl.when(step >= 2 * blocks)
    def _():
        rows = dot_nt(grads, w[...])
        for k in range(tiles):

            @pl.when(step == 2 * blocks + k)
            def _():
                sent[k] = rows.astype(bf16)
                swap(k).start()

            @pl.when(step == 2 * blocks + tiles + k)
            def _():
                swap(k).wait()
                grad_norm = rows + came[k].astype(f32)
                scaled, inverse = normalized(toks[...].astype(f32))
                through = grad_norm * spread(gain)
                centre = jnp.mean(through, axis=-1, keepdims=True)
                along = jnp.mean(through * scaled, axis=-1, keepdims=True)
                grad_in = inverse * (through - centre - scaled * along)
                out[...] = (gattn[...].astype(f32) + grad_in).astype(bf16)
                sums[0:8, :] += column_sum(grad_norm * scaled)
                sums[8:16, :] += column_sum(grad_norm)

    @pl.when(step == pl.num_programs(0) - 1)
    def _():
        row = lax.broadcasted_iota(jnp.int32, (8, 1024), 0)
        first = jnp.sum(sums[0:8, :], axis=0, keepdims=True)
        second = jnp.sum(sums[8:16, :], axis=0, keepdims=True)
        third = jnp.sum(qv_sums[...], axis=0, keepdims=True)
        rows = jnp.where(row == 0, first, jnp.where(row == 1, second, third))
        tiny.begin(jnp.where(row < 3, rows, 0.0))
        tiny.middle(2)
        small_out[...] = tiny.end()
        for k, part in enumerate(parts):
            at = (k % 2) * 2 * quarter + (k // 2) * quarter
            summed = part.result()
            edges = [at] + [c for c in (local, 2 * local) if at < c < at + quarter] + [at + quarter]
            for low, high in zip(edges[:-1], edges[1:]):
                to = low % local
                grad_w[low // local, :, to : to + high - low] = summed[:, low - at : high - at]


def layer_on_pairs(
    tokens,
    slot_lengths,
    gain_one,
    shift_one,
    w_qkv,
    bias_qv,
    w_out,
    bias_out,
    gain_two,
    shift_two,
    w_up,
    bias_up,
    w_down,
    bias_down,
    cotangent,
):
    own_rows, width = tokens.shape
    total_rows = 2 * own_rows
    tiles = own_rows // BT
    local = w_qkv.shape[2]
    hidden_cols = w_up.shape[1]
    side_cols = 3 * local
    lengths = slot_lengths[0]

    half_cols = side_cols // 2
    normed_at = pl.BlockSpec(
        (width, BT),
        lambda i: (0, lax.rem(jnp.minimum(i, 2 * tiles - 1) + my_side() * tiles, 2 * tiles)),
    )
    packed_at = pl.BlockSpec(
        (BT, half_cols),
        lambda i: (
            lax.rem(jnp.maximum(i - 2 * tiles, 0), 2 * tiles),
            jnp.maximum(i - 2 * tiles, 0) // (2 * tiles),
        ),
    )
    rows_turned, packed, up_blocks, out_blocks, qkv_blocks = grid_call(
        functools.partial(qkv_kernel, tiles),
        6 * tiles,
        [
            (tokens, pl.BlockSpec((BT, width), lambda i: (jnp.minimum(i, tiles - 1), 0))),
            (tokens, ANY),
            vector(gain_one),
            vector(shift_one),
            (bias_qv, whole(2, local)),
            (w_qkv.transpose(1, 0, 2), pl.BlockSpec((3, 64, local), lambda i: (0, 0, 0))),
            (w_out.T, ANY),
            (w_up, ANY),
        ],
        [
            (shape(width, total_rows), normed_at),
            (shape(total_rows, side_cols), packed_at),
            (jax.ShapeDtypeStruct((4, 4, 64, hidden_cols), bf16), ANY),
            (jax.ShapeDtypeStruct((4, 4, 64, local), bf16), ANY),
            (jax.ShapeDtypeStruct((4, 4, 64, side_cols), bf16), ANY),
        ],
        [
            pltpu.VMEM((total_rows, width), bf16),
            pltpu.VMEM((tiles, BT, width), bf16),
            pltpu.VMEM((4, 4, 64, side_cols), bf16),
            pltpu.SemaphoreType.DMA((tiles,)),
            pltpu.SemaphoreType.DMA((tiles,)),
            pltpu.SemaphoreType.DMA(()),
        ]
        + gather_sems(8),
        2 * total_rows * width * side_cols,
        "qkv",
        1,
    )
    qkv_w = qkv_blocks.reshape(width, side_cols)
    attended, exact, lse, up_blocks, down_blocks = attend_forward(
        packed,
        lengths,
        AttendGather(),
        (w_down.T, up_blocks),
        jax.ShapeDtypeStruct((4, 4, 64, hidden_cols), bf16),
    )
    up_w = up_blocks.reshape(width, hidden_cols)
    out_w = out_blocks.reshape(width, local)

    def two_way(cols, skip=0):
        def at(i):
            return lax.rem(jnp.maximum(i - skip, 0) + (1 - my_side()) * tiles, 2 * tiles)

        return pl.BlockSpec((BT, cols), lambda i: (at(i), 0))

    late_tile = pl.BlockSpec((BT, width), lambda i: (jnp.maximum(i - tiles, 0), 0))
    swap_buffers = [
        pltpu.VMEM((tiles, BT, width), bf16),
        pltpu.VMEM((tiles, BT, width), bf16),
        pltpu.SemaphoreType.DMA((tiles,)),
        pltpu.SemaphoreType.DMA((tiles,)),
    ]
    hidden, normed_own = grid_call(
        functools.partial(project_kernel, tiles),
        2 * tiles,
        [
            (attended, two_way(local)),
            (out_w, weight(local)),
            (tokens, late_tile),
            vector(bias_out),
            vector(gain_two),
            vector(shift_two),
        ],
        [
            (shape(own_rows, width, f32), late_tile),
            (shape(own_rows, width), late_tile),
        ],
        swap_buffers,
        4 * own_rows * width * local,
        "project",
        6,
    )
    down_w = down_blocks.reshape(width, hidden_cols)
    own_at = pl.BlockSpec((BT, width), lambda i: (jnp.minimum(i, tiles - 1), 0))
    ffn_own, norm_own, ffn_came, norm_came, up_grad, down_grad, bsum = grid_call(
        functools.partial(feed_kernel, tiles),
        2 * tiles,
        [
            (normed_own, ANY),
            (cotangent, ANY),
            vector(bias_up),
            (up_w, weight(hidden_cols)),
            (down_w, weight(hidden_cols)),
        ],
        [
            (shape(own_rows, width), own_at),
            (shape(own_rows, width), own_at),
            (shape(own_rows, width), ANY),
            (shape(own_rows, width), ANY),
            (shape(width, hidden_cols), ANY),
            (shape(width, hidden_cols), ANY),
            (shape(8, hidden_cols, f32), whole(8, hidden_cols)),
        ],
        [
            pltpu.VMEM((width, hidden_cols), f32),
            pltpu.VMEM((width, hidden_cols), f32),
            pltpu.VMEM((BT, hidden_cols), bf16),
            pltpu.VMEM((BT, hidden_cols), bf16),
            pltpu.VMEM((width, BT), bf16),
            pltpu.VMEM((width, BT), bf16),
            pltpu.VMEM((2 * tiles, BT, width), bf16),
            pltpu.VMEM((2 * tiles, BT, width), bf16),
            pltpu.VMEM((BT, width), bf16),
            pltpu.VMEM((BT, width), bf16),
            pltpu.SemaphoreType.DMA((2 * tiles,)),
            pltpu.SemaphoreType.DMA((4 * tiles,)),
            pltpu.SemaphoreType.DMA((4 * tiles,)),
            pltpu.SemaphoreType.DMA((64,)),
        ],
        24 * own_rows * width * hidden_cols,
        "feed",
        5,
    )
    def mine_first(i):
        return lax.rem(i + my_side() * tiles, 2 * tiles)

    natural_tile = pl.BlockSpec((BT, local), lambda i: (mine_first(i), 0))
    output, grad_attn, grad_attended, delta, out_grad, middle_sums = grid_call(
        functools.partial(middle_kernel, tiles),
        2 * tiles,
        [
            (hidden, own_at),
            (ffn_own, own_at),
            (ffn_came, own_at),
            (norm_own, own_at),
            (norm_came, own_at),
            (cotangent, own_at),
            vector(bias_down),
            vector(gain_two),
            (exact, natural_tile),
            (attended, natural_tile),
            (out_w, weight(local)),
        ],
        [
            (shape(own_rows, width), own_at),
            (shape(own_rows, width), own_at),
            (shape(total_rows, local), natural_tile),
            (shape(16, total_rows, f32), pl.BlockSpec((16, BT), lambda i: (0, mine_first(i)))),
            (shape(width, local), whole(width, local)),
            (shape(32, width, f32), whole(32, width)),
        ],
        [
            pltpu.VMEM((width, BT), bf16),
            pltpu.VMEM((width, local), f32),
            pltpu.VMEM((BT, width), bf16),
        ]
        + swap_buffers,
        4 * total_rows * width * local,
        "middle",
        7,
    )
    moved = (down_grad, up_grad, out_grad, middle_sums, bsum)
    grad_q, grad_k, grad_v, grad_down, grad_up, grad_w_out, early = attend_backward(
        packed,
        grad_attended,
        lse,
        delta,
        lengths,
        BackwardSum((hidden_cols, hidden_cols, local)),
        moved,
    )
    blocks = 2 * tiles

    def grad_at(i):
        later = lax.rem(jnp.maximum(i - 2 * blocks, 0) + (1 - my_side()) * tiles, blocks)
        return jnp.where(i < 2 * blocks, lax.rem(i, blocks), later)

    grad_tile = pl.BlockSpec((BT, local), lambda i: (grad_at(i), 0))
    turned_tile = pl.BlockSpec(
        (width, BT), lambda i: (0, jnp.where(i < 2 * blocks, lax.rem(i, blocks), blocks - 1))
    )
    last_tile = pl.BlockSpec(
        (BT, width), lambda i: (jnp.maximum(i - 2 * blocks - tiles, 0), 0)
    )
    grad_tokens, grad_w_qkv, late = grid_call(
        functools.partial(last_kernel, tiles),
        3 * blocks,
        [(rows_turned, turned_tile)]
        + [(g, grad_tile) for g in (grad_q, grad_k, grad_v)]
        + [
            (qkv_w, weight(side_cols)),
            (tokens, last_tile),
            (grad_attn, last_tile),
            vector(gain_one),
        ],
        [
            (shape(own_rows, width), last_tile),
            (
                jax.ShapeDtypeStruct((3, 64, local), f32),
                pl.BlockSpec((3, 64, local), lambda i: (0, 0, 0)),
            ),
            (shape(8, width, f32), whole(8, width)),
        ],
        [
            pltpu.VMEM((16, width), f32),
            pltpu.VMEM((8, width), f32),
            pltpu.VMEM((width, side_cols // 2), f32),
        ]
        + swap_buffers
        + last_scratch(side_cols),
        4 * total_rows * width * side_cols,
        "last",
        4,
    )
    return (
        output,
        grad_tokens,
        late[0],
        late[1],
        grad_w_qkv.transpose(1, 0, 2),
        late[2].reshape(2, local),
        grad_w_out.T,
        early[2],
        early[0],
        early[1],
        grad_up,
        early[4:6].reshape(-1),
        grad_down.T,
        early[3],
    )


def gelu_tanh(values):
    inner = gelu_coeff * (values + 0.044715 * values * values * values)
    return 0.5 * values * (1.0 + jnp.tanh(inner))


def gelu_slope(values):
    inner = gelu_coeff * (values + 0.044715 * values * values * values)
    bent = jnp.tanh(inner)
    return 0.5 * (1.0 + bent) + 0.5 * values * (1.0 - bent * bent) * gelu_coeff * (
        1.0 + 3.0 * 0.044715 * values * values
    )


def norm_forward(values, gain_vec, shift_vec):
    average = jnp.mean(values, axis=-1, keepdims=True)
    centred = values - average
    variance = jnp.mean(centred * centred, axis=-1, keepdims=True)
    inverse = lax.rsqrt(variance + norm_eps)
    scaled = centred * inverse
    return (scaled * gain_vec.astype(f32) + shift_vec.astype(f32), scaled, inverse)


def norm_backward(grad_out, scaled, inverse, gain_vec):
    grad_scaled = grad_out * gain_vec.astype(f32)
    centre_term = jnp.mean(grad_scaled, axis=-1, keepdims=True)
    slope_term = jnp.mean(grad_scaled * scaled, axis=-1, keepdims=True)
    grad_in = inverse * (grad_scaled - centre_term - scaled * slope_term)
    return (grad_in, jnp.sum(grad_out * scaled, axis=0), jnp.sum(grad_out, axis=0))


def layer_by_collectives(
    tokens,
    slot_lengths,
    gain_one,
    shift_one,
    w_qkv,
    bias_qv,
    w_out,
    bias_out,
    gain_two,
    shift_two,
    w_up,
    bias_up,
    w_down,
    bias_down,
    cotangent,
):
    w_qkv, w_out, w_up, w_down = (
        lax.all_gather(w_qkv, "dp", axis=0, tiled=True),
        lax.all_gather(w_out, "dp", axis=1, tiled=True),
        lax.all_gather(w_up, "dp", axis=0, tiled=True),
        lax.all_gather(w_down, "dp", axis=1, tiled=True),
    )
    lengths = slot_lengths[0]
    residual = tokens.astype(f32)
    normed_one, scaled_one, inverse_one = norm_forward(residual, gain_one, shift_one)
    rows_one = lax.all_gather(normed_one.astype(bf16), "mp", axis=0, tiled=True)
    packed = jnp.einsum("td,dcf->tcf", rows_one, w_qkv, preferred_element_type=f32)
    zero_bias = jnp.zeros_like(bias_qv[0])
    packed_bias = jnp.stack([bias_qv[0], zero_bias, bias_qv[1]]).astype(f32)
    packed = (packed + packed_bias[None]).astype(bf16)
    local = packed.shape[2]
    packed_rows = packed.reshape(packed.shape[0], -1)
    attended, exact_out, log_totals = attend_forward(packed_rows, lengths)
    hidden = (
        residual
        + lax.psum_scatter(
            jnp.dot(attended, w_out, preferred_element_type=f32),
            "mp",
            scatter_dimension=0,
            tiled=True,
        )
        + bias_out.astype(f32)
    )
    normed_two, scaled_two, inverse_two = norm_forward(hidden, gain_two, shift_two)
    normed_low = normed_two.astype(bf16)
    rows_two = lax.all_gather(normed_low, "mp", axis=0, tiled=True)
    preact = jnp.dot(rows_two, w_up, preferred_element_type=f32) + bias_up.astype(
        f32
    )
    active = gelu_tanh(preact).astype(bf16)
    ffn_out = lax.psum_scatter(
        jnp.dot(active, w_down, preferred_element_type=f32).astype(bf16),
        "mp",
        scatter_dimension=0,
        tiled=True,
    ).astype(f32)
    output = (hidden + ffn_out + bias_down.astype(f32)).astype(bf16)
    grad_out = cotangent.astype(f32)
    grad_rows = lax.all_gather(cotangent, "mp", axis=0, tiled=True)
    grad_active = jnp.einsum("td,fd->tf", grad_rows, w_down, preferred_element_type=f32)
    grad_pre = (grad_active * gelu_slope(preact)).astype(bf16)
    grad_up = jnp.einsum("td,tf->df", rows_two, grad_pre, preferred_element_type=f32)
    grad_down = jnp.einsum("tf,td->fd", active, grad_rows, preferred_element_type=f32)
    grad_bias_up = jnp.sum(grad_pre.astype(f32), axis=0)
    grad_norm_two = lax.psum_scatter(
        jnp.einsum("tf,df->td", grad_pre, w_up, preferred_element_type=f32),
        "mp",
        scatter_dimension=0,
        tiled=True,
    )
    grad_in_two, grad_gain_two, grad_shift_two = norm_backward(
        grad_norm_two, scaled_two, inverse_two, gain_two
    )
    grad_hidden = grad_out + grad_in_two
    grad_attn = grad_hidden.astype(bf16)
    grad_attn_rows = lax.all_gather(grad_attn, "mp", axis=0, tiled=True)
    grad_w_out = jnp.einsum(
        "tf,td->fd", attended, grad_attn_rows, preferred_element_type=f32
    )
    grad_attended = jnp.einsum(
        "td,fd->tf", grad_attn_rows, w_out, preferred_element_type=f32
    ).astype(bf16)
    product = (grad_attended.astype(f32) * exact_out).reshape(grad_attended.shape[0], -1, HD)
    delta = jnp.sum(product, axis=-1).T
    groups = log_totals.shape[0] // 8
    delta = delta.reshape(groups, -1, delta.shape[1])
    delta = jnp.pad(delta, ((0, 0), (0, 8 - delta.shape[1]), (0, 0))).reshape(8 * groups, -1)
    grads = attend_backward(packed_rows, grad_attended, log_totals, delta, lengths)
    grad_packed = jnp.stack(grads, axis=1)
    grad_w_qkv = jnp.einsum(
        "td,tcf->dcf", rows_one, grad_packed, preferred_element_type=f32
    )
    grad_bias_qv = jnp.stack(
        [
            jnp.sum(grad_packed[:, 0].astype(f32), axis=0),
            jnp.sum(grad_packed[:, 2].astype(f32), axis=0),
        ]
    )
    grad_norm_one = lax.psum_scatter(
        jnp.einsum("tcf,dcf->td", grad_packed, w_qkv, preferred_element_type=f32),
        "mp",
        scatter_dimension=0,
        tiled=True,
    )
    grad_in_one, grad_gain_one, grad_shift_one = norm_backward(
        grad_norm_one, scaled_one, inverse_one, gain_one
    )
    grad_tokens = (grad_hidden + grad_in_one).astype(bf16)
    grad_bias_out = jnp.sum(grad_attn.astype(f32), axis=0)
    grad_bias_down = jnp.sum(grad_out, axis=0)
    grad_w_qkv, grad_w_out, grad_up, grad_down = (
        lax.psum_scatter(grad_w_qkv, "dp", scatter_dimension=0, tiled=True),
        lax.psum_scatter(grad_w_out, "dp", scatter_dimension=1, tiled=True),
        lax.psum_scatter(grad_up, "dp", scatter_dimension=0, tiled=True),
        lax.psum_scatter(grad_down, "dp", scatter_dimension=1, tiled=True),
    )
    small_grads = lax.psum(
        (
            grad_gain_one,
            grad_shift_one,
            grad_bias_out,
            grad_gain_two,
            grad_shift_two,
            grad_bias_down,
        ),
        ("dp", "mp"),
    )
    grad_bias_qv, grad_bias_up = lax.psum((grad_bias_qv, grad_bias_up), "dp")
    return (
        output,
        grad_tokens,
        small_grads[0],
        small_grads[1],
        grad_w_qkv,
        grad_bias_qv,
        grad_w_out,
        small_grads[2],
        small_grads[3],
        small_grads[4],
        grad_up,
        grad_bias_up,
        grad_down,
        small_grads[5],
    )


def solution(mesh):
    pairs = dict(mesh.shape) == {"dp": 16, "mp": 2}
    layer = layer_on_pairs if pairs else layer_by_collectives
    return jax.shard_map(
        layer,
        mesh=mesh,
        in_specs=(
            P(("dp", "mp"), None),
            P("dp", None),
            P(),
            P(),
            P("dp", None, "mp"),
            P(None, "mp"),
            P("mp", "dp"),
            P(),
            P(),
            P(),
            P("dp", "mp"),
            P("mp"),
            P("mp", "dp"),
            P(),
            P(("dp", "mp"), None),
        ),
        out_specs=(
            P(("dp", "mp"), None),
            P(("dp", "mp"), None),
            P(),
            P(),
            P("dp", None, "mp"),
            P(None, "mp"),
            P("mp", "dp"),
            P(),
            P(),
            P(),
            P("dp", "mp"),
            P("mp"),
            P("mp", "dp"),
            P(),
        ),
        check_vma=False,
    )
```
